32 devices in a mesh: dp: 8 (over z, x), head: 4 (over y, core).
Axes of the slice: x: 2, y: 2, z: 4, core: 2. Of those that a mesh axis runs over, the one named last changes fastest.
Arguments:
- tokens: bfloat16 [32, 196, 216], P('dp'), may hold values from -6 to 6
- cotangent: float32 [32, 196, 216], P('dp'), may hold values from -6 to 6
- image_count: int32 [8], P('dp'), may hold values from 1 to 4, as said below
- subnet_heads: int32 [1], replicated, may hold values from 6 to 12
- subnet_width: int32 [1], replicated, may hold values from 432 to 864
- block_slot: int32 [12], replicated, may hold values from 0 to 15, as said below
- master: float32 [16, 54, 864], P('dp', None, 'head'), may hold values from -0.8164966 to 0.8164966
- master_m1: float32 [16, 54, 864], P('dp', None, 'head'), may hold values from -187.82971 to 187.82971
- master_m2: float32 [16, 54, 864], P('dp', None, 'head'), may hold values from 78 to 15680
- norm_params: float32 [4, 216], replicated, may hold values from -0.9 to 1.45
- norm_m1: float32 [4, 216], replicated, may hold values from -265.63132 to 265.63132
- norm_m2: float32 [4, 216], replicated, may hold values from 3920 to 35280
- talk: float32 [2, 12, 12], replicated, may hold values from -0.45 to 1.45
- talk_m1: float32 [2, 12, 12], replicated, may hold values from -831.55756 to 831.55756
- talk_m2: float32 [2, 12, 12], replicated, may hold values from 38416 to 307328
- conv: float32 [9, 864], P(None, 'head'), may hold values from -1 to 1
- conv_m1: float32 [9, 864], P(None, 'head'), may hold values from -108.41586 to 108.41586
- conv_m2: float32 [9, 864], P(None, 'head'), may hold values from 653 to 5226
Outputs:
- output: float32 [32, 196, 216], P('dp')
- token_grad: float32 [32, 196, 216], P('dp')
- new_master: float32 [16, 54, 864], P('dp', None, 'head')
- new_master_m1: float32 [16, 54, 864], P('dp', None, 'head')
- new_master_m2: float32 [16, 54, 864], P('dp', None, 'head')
- master_copy: bfloat16 [16, 54, 864], P('dp', None, 'head')
- new_norm: float32 [4, 216], replicated
- new_norm_m1: float32 [4, 216], replicated
- new_norm_m2: float32 [4, 216], replicated
- new_talk: float32 [2, 12, 12], replicated
- new_talk_m1: float32 [2, 12, 12], replicated
- new_talk_m2: float32 [2, 12, 12], replicated
- new_conv: float32 [9, 864], P(None, 'head')
- new_conv_m1: float32 [9, 864], P(None, 'head')
- new_conv_m2: float32 [9, 864], P(None, 'head')
The draws below stay inside these ranges and needn't reach their ends.
Inputs may be any that keep to these rules, and one draw needn't show every extreme that they name: `image_count`: image slots at or beyond a dp index's count are padding; some dp index holds exactly 4 images and some exactly 1. `block_slot`: the twelve slots are distinct.
All inputs are finite; a program needn't handle non-finite values.
Results may differ from the reference program's by a relative error of at most 0.012.
The reference program's roundings to bfloat16 on the way count: a program that leaves them out, or rounds other values in their place, can miss the bound.
Values may be sent and summed in bfloat16 or wider, within the bound.
No kernel may reach another device: no remote copies, remote signals or barrier semaphores. Data moves between devices by JAX's collectives and lax.ppermute only.
A program may use at most 64 MiB of HBM per device.

```python
import math
import jax
import jax.numpy as jnp
from jax import lax

D = 216
HEADS = 12
HD = 18
FF = 864
SIDE = 14
IMG_CAP = 4
SEQ = 196
IMAGES = 32
BROWS = 54
SLOTS_ALL = 16
NVALID = 3920
N_DP = 8
N_HEAD = 4


def slot_table(key):
    order = jax.random.permutation(jax.random.fold_in(key, 101), SLOTS_ALL).astype(jnp.int32)
    first_target = jax.random.randint(jax.random.fold_in(key, 102), (), 0, 12)
    second_target = (first_target + 1 + jax.random.randint(jax.random.fold_in(key, 103), (), 0, 11)) % 12
    for wanted, target in ((SLOTS_ALL - 1, first_target), (0, second_target)):
        where_now = jnp.argmax(order == wanted)
        old_value = order[target]
        order = order.at[target].set(wanted).at[where_now].set(old_value)
    return order


def slot_kinds(key):
    return jnp.minimum(jnp.argsort(slot_table(key)), 12)


def draw_block_slot(key, part):
    return slot_table(key)[:12].astype(jnp.int32)


def draw_master(key, part):
    scale_table = jnp.array([1.2, 1.2, 1.0, 4.0, 1.0, 1.0, 1.0, 1.0] + [2.0 * (D / FF) ** 0.5] * 4 + [1.0], jnp.float32) * D ** (-0.5)
    scales = scale_table[slot_kinds(key)]
    normal = jnp.clip(jax.random.normal(jax.random.fold_in(key, 111), (SLOTS_ALL, BROWS, N_HEAD * D), jnp.float32), -3.0, 3.0)
    return normal * scales[:, None, None]


def grad_scales(key):
    scale_table = jnp.array([1.0, 1.0, 0.8, 0.2, 0.7, 0.7, 0.7, 0.7, 0.6, 0.6, 0.6, 0.6, 0.5], jnp.float32) * NVALID ** 0.5
    return scale_table[slot_kinds(key)]


def draw_master_m1(key, part):
    normal = jnp.clip(jax.random.normal(jax.random.fold_in(key, 121), (SLOTS_ALL, BROWS, N_HEAD * D), jnp.float32), -3.0, 3.0)
    return normal * grad_scales(key)[:, None, None]


def draw_master_m2(key, part):
    factor = jnp.exp(jax.random.uniform(jax.random.fold_in(key, 131), (SLOTS_ALL, BROWS, N_HEAD * D), jnp.float32, jnp.log(0.5), jnp.log(4.0)))
    return factor * (grad_scales(key) ** 2)[:, None, None]


def draw_norm_params(key, part):
    normal = jnp.clip(jax.random.normal(jax.random.fold_in(key, 141), (4, D), jnp.float32), -3.0, 3.0)
    is_gain = (jnp.arange(4) % 2 == 0)[:, None]
    return jnp.where(is_gain, 1.0 + 0.15 * normal, 0.3 * normal)


def draw_talk(key, part):
    normal = jnp.clip(jax.random.normal(jax.random.fold_in(key, 151), (2, HEADS, HEADS), jnp.float32), -3.0, 3.0)
    return jnp.eye(HEADS, dtype=jnp.float32)[None] + 0.15 * normal


def draw_image_count(key, part):
    counts_drawn = jax.random.randint(jax.random.fold_in(key, 161), (N_DP,), 1, IMG_CAP + 1)
    full_place = jax.random.randint(jax.random.fold_in(key, 162), (), 0, N_DP)
    places = jnp.arange(N_DP)
    counts_drawn = jnp.where(places == full_place, IMG_CAP, counts_drawn)
    counts_drawn = jnp.where(places == (full_place + 1) % N_DP, 1, counts_drawn)
    return counts_drawn.astype(jnp.int32)


def block_scale(key, shape, split, smallest, largest):
    def one(dim, parts):
        heights = jax.random.uniform(jax.random.fold_in(jax.random.fold_in(key, 6), dim), (parts,), jnp.float32, smallest / len(split), largest / len(split))
        return jnp.repeat(jnp.exp(heights), shape[dim] // parts).reshape((-1,) + (1,) * (len(shape) - dim - 1))

    loudness = one(*split[0])
    for cut in split[1:]:
        loudness = loudness * one(*cut)
    return loudness


def bell_draw(rng, extent, width, limit, shards=(), kind=jnp.bfloat16):
    level = block_scale(rng, extent, shards, -0.22, 0.18) if shards else 1.0
    drawn = jax.random.normal(rng, extent, jnp.float32) * width * level
    return jnp.minimum(jnp.maximum(drawn, -limit), limit).astype(kind)


def setup_inputs(seed: int = 0) -> dict:
    key_list = jax.random.split(jax.random.key(seed), 19)
    tokens = bell_draw(key_list[0], (IMAGES, SEQ, D), 1.0, 6.0, ((0, 8),))
    cotangent = bell_draw(key_list[1], (IMAGES, SEQ, D), 1.0, 6.0, ((0, 8),), jnp.float32)
    image_count = draw_image_count(jax.random.fold_in(key_list[18], 71), 0)
    subnet_heads = jax.random.randint(key_list[3], (1,), HEADS // 2, HEADS + 1).astype(jnp.int32)
    subnet_width = jax.random.randint(key_list[4], (1,), FF // 2, FF + 1).astype(jnp.int32)
    block_slot = draw_block_slot(jax.random.fold_in(key_list[18], 71), 0)
    master = draw_master(jax.random.fold_in(key_list[18], 71), 0)
    master_m1 = draw_master_m1(jax.random.fold_in(key_list[18], 71), 0)
    master_m2 = draw_master_m2(jax.random.fold_in(key_list[18], 71), 0)
    norm_params = draw_norm_params(jax.random.fold_in(key_list[18], 71), 0)
    norm_m1 = bell_draw(key_list[10], (4, D), ((2 * NVALID) ** 0.5), 265.63132, (), jnp.float32)
    norm_m2 = jnp.clip(jnp.exp(jax.random.uniform(key_list[11], (4, D), jnp.float32, math.log(3920.0), math.log(35280.0))), 3920.0, 35280.0)
    talk = draw_talk(jax.random.fold_in(key_list[18], 71), 0)
    talk_m1 = bell_draw(key_list[13], (2, HEADS, HEADS), ((NVALID * SEQ // 10) ** 0.5), 831.55756, (), jnp.float32)
    talk_m2 = jnp.clip(jnp.exp(jax.random.uniform(key_list[14], (2, HEADS, HEADS), jnp.float32, math.log(38416.0), math.log(307328.0))), 38416.0, 307328.0)
    conv = bell_draw(key_list[15], (9, FF), (3 ** -1), 1.0, ((1, 4),), jnp.float32)
    conv_m1 = bell_draw(key_list[16], (9, FF), ((NVALID // 3) ** 0.5), 108.41586, ((1, 4),), jnp.float32)
    conv_m2 = jnp.clip(jnp.exp(math.log(5226.0) - 2.0798243 * jax.random.uniform(key_list[17], (9, FF), jnp.float32) ** block_scale(key_list[17], (9, FF), ((1, 4),), -0.2, 0.2)), 653.0, 5226.0)
    return {"tokens": tokens, "cotangent": cotangent, "image_count": image_count, "subnet_heads": subnet_heads, "subnet_width": subnet_width, "block_slot": block_slot, "master": master, "master_m1": master_m1, "master_m2": master_m2, "norm_params": norm_params, "norm_m1": norm_m1, "norm_m2": norm_m2, "talk": talk, "talk_m1": talk_m1, "talk_m2": talk_m2, "conv": conv, "conv_m1": conv_m1, "conv_m2": conv_m2}


@jax.custom_vjp
def low(v):
    return lax.optimization_barrier(v.astype(jnp.bfloat16)).astype(jnp.float32)

@jax.custom_vjp
def low_back(v):
    return v

def low_keep(v):
    return (low(v), None)

def low_pass(kept, grad):
    return (grad,)

def back_keep(v):
    return (v, None)

def back_low(kept, grad):
    return (low(grad),)
low.defvjp(low_keep, low_pass)
low_back.defvjp(back_keep, back_low)
norm_eps = 1e-05
beta_first = 0.5
beta_second = 0.5
adam_eps = 1e-08
rate_matrix = 0.06
rate_small = 0.2
decay_matrix = 0.05
adam_steps = 3
highest = lax.Precision.HIGHEST

def layer_norm(values, gain_row, bias_row):
    centred = values - lax.optimization_barrier(jnp.mean(values, axis=-1, keepdims=True))
    spread_sq = lax.optimization_barrier(jnp.mean(centred * centred, axis=-1, keepdims=True))
    return centred * lax.rsqrt(spread_sq + norm_eps) * gain_row + bias_row

def conv_grid(hidden, kernel):
    images, length, channels = hidden.shape
    grid_view = hidden.reshape(images, SIDE, SIDE, channels)
    padded = jnp.pad(grid_view, ((0, 0), (1, 1), (1, 1), (0, 0)))
    summed = jnp.zeros_like(grid_view)
    for tap_index in range(9):
        row_off = tap_index // 3
        col_off = tap_index % 3
        summed = summed + kernel[tap_index] * padded[:, row_off:row_off + SIDE, col_off:col_off + SIDE, :]
    return summed.reshape(images, length, channels)

def block_to_matrix(block):
    block_rows = block.shape[0]
    return block.reshape(block_rows, N_HEAD, D).transpose(1, 0, 2).reshape(N_HEAD * block_rows, D)

def wide_to_matrix(blocks_four):
    block_rows = blocks_four.shape[1]
    return blocks_four.reshape(4, block_rows, N_HEAD, D).transpose(2, 0, 1, 3).reshape(FF, D)

def matrix_to_block(matrix):
    block_rows = matrix.shape[0] // N_HEAD
    return matrix.reshape(N_HEAD, block_rows, D).transpose(1, 0, 2).reshape(1, block_rows, N_HEAD * D)

def matrix_to_wide(matrix):
    block_rows = matrix.shape[0] // (4 * N_HEAD)
    return matrix.reshape(N_HEAD, 4, block_rows, D).transpose(1, 2, 0, 3).reshape(4, block_rows, N_HEAD * D)

def forward(params, token_values, image_valid, head_keep, unit_keep):
    w_query, w_key, w_value, w_out, w_in, w_down, norm_params, talk, conv = params
    images = token_values.shape[0]
    normed = low(layer_norm(token_values, norm_params[0], norm_params[1]))
    queries = low(low_back(jnp.einsum('gsd,fd->gsf', normed, w_query, precision=highest))).reshape(images, SEQ, HEADS, HD)
    key_vecs = low(low_back(jnp.einsum('gsd,fd->gsf', normed, w_key, precision=highest))).reshape(images, SEQ, HEADS, HD)
    value_vecs = low(low_back(jnp.einsum('gsd,fd->gsf', normed, w_value, precision=highest))).reshape(images, SEQ, HEADS, HD)
    scores = low(low_back(jnp.einsum('gqhe,gkhe->ghqk', queries, key_vecs, precision=highest) * HD ** (-0.5)))
    pre_mixed = jnp.einsum('mn,gnqk->gmqk', talk[0], scores, precision=highest)
    softmaxed = jax.nn.softmax(pre_mixed, axis=-1)
    post_mixed = low(low_back(jnp.einsum('jm,gmqk->gjqk', talk[1], softmaxed, precision=highest)))
    attended = jnp.einsum('ghqk,gkhe->gqhe', post_mixed, value_vecs, precision=highest) * head_keep[None, None, :, None]
    attended = low(low_back(attended.reshape(images, SEQ, HEADS * HD)))
    branch_one = low_back(jnp.einsum('gsf,fd->gsd', attended, w_out, precision=highest))
    middle = token_values + branch_one
    second = low(layer_norm(middle, norm_params[2], norm_params[3]))
    hidden = low_back(jnp.einsum('gsd,ud->gsu', second, w_in, precision=highest))
    activated = conv_grid(hidden, conv)
    gated = low(activated * jax.nn.sigmoid(activated) * unit_keep)
    branch_two = low_back(jnp.einsum('gsu,ud->gsd', gated, w_down, precision=highest))
    return (middle + branch_two) * image_valid[:, None, None]

def adamw(weights_old, gradient, moment_one, moment_two, step_rate, decay_rate):
    one_new = beta_first * moment_one + (1.0 - beta_first) * gradient
    two_new = beta_second * moment_two + (1.0 - beta_second) * gradient * gradient
    hat_one = one_new / (1.0 - beta_first ** adam_steps)
    hat_two = two_new / (1.0 - beta_second ** adam_steps)
    weights_new = weights_old - step_rate * (hat_one / (jnp.sqrt(hat_two) + adam_eps) + decay_rate * weights_old)
    return (weights_new, one_new, two_new)

def reference(tokens, cotangent, image_count, subnet_heads, subnet_width, block_slot, master, master_m1, master_m2, norm_params, norm_m1, norm_m2, talk, talk_m1, talk_m2, conv, conv_m1, conv_m2):
    valid_all = (jnp.arange(IMG_CAP)[None, :] < image_count[:, None]).astype(jnp.float32).reshape(IMAGES)
    head_keep = (jnp.arange(HEADS) < subnet_heads[0]).astype(jnp.float32)
    unit_keep = (jnp.arange(FF) < subnet_width[0]).astype(jnp.float32)
    blocks = master[block_slot].astype(jnp.bfloat16).astype(jnp.float32)
    weights = (block_to_matrix(blocks[0]), block_to_matrix(blocks[1]), block_to_matrix(blocks[2]), block_to_matrix(blocks[3]), wide_to_matrix(blocks[4:8]), wide_to_matrix(blocks[8:12]), norm_params, talk, conv)
    group_size = 2 * IMG_CAP
    group_count = IMAGES // group_size
    token_groups = tokens.astype(jnp.float32).reshape(group_count, group_size, SEQ, D)
    cot_groups = cotangent.reshape(group_count, group_size, SEQ, D)
    valid_groups = valid_all.reshape(group_count, group_size)

    def one_group(running, inputs):
        token_block, cot_block, valid_block = inputs

        def run(params, token_values):
            return forward(params, token_values, valid_block, head_keep, unit_keep)
        result, pullback = jax.vjp(run, weights, token_block)
        param_grads, token_back = pullback(cot_block)
        running = jax.tree.map(lambda summed, extra: summed + extra, running, param_grads)
        return (running, (result, token_back))
    zero_grads = jax.tree.map(jnp.zeros_like, weights)
    grads, (outputs, token_backs) = lax.scan(one_group, zero_grads, (token_groups, cot_groups, valid_groups))
    grad_q, grad_k, grad_v, grad_o, grad_in, grad_down, grad_norm, grad_talk, grad_conv = grads
    block_grads = jnp.concatenate([matrix_to_block(grad_q), matrix_to_block(grad_k), matrix_to_block(grad_v), matrix_to_block(grad_o), matrix_to_wide(grad_in), matrix_to_wide(grad_down)], axis=0)
    slot_grads = jnp.zeros(master.shape, master.dtype).at[block_slot].set(block_grads)
    new_master, new_master_m1, new_master_m2 = adamw(master, slot_grads, master_m1, master_m2, rate_matrix, decay_matrix)
    new_norm, new_norm_m1, new_norm_m2 = adamw(norm_params, grad_norm, norm_m1, norm_m2, rate_small, 0.0)
    new_talk, new_talk_m1, new_talk_m2 = adamw(talk, grad_talk, talk_m1, talk_m2, rate_small, 0.0)
    new_conv, new_conv_m1, new_conv_m2 = adamw(conv, grad_conv, conv_m1, conv_m2, rate_small, decay_matrix)
    output = outputs.reshape(IMAGES, SEQ, D)
    token_grad = token_backs.reshape(IMAGES, SEQ, D)
    return (output, token_grad, new_master, new_master_m1, new_master_m2, new_master.astype(jnp.bfloat16), new_norm, new_norm_m1, new_norm_m2, new_talk, new_talk_m1, new_talk_m2, new_conv, new_conv_m1, new_conv_m2)
```

```python
import jax
import jax.numpy as jnp
from jax import lax
from jax.sharding import PartitionSpec as P

HD = 18
SIDE = 14


norm_eps = 1e-05
beta_first = 0.5
beta_second = 0.5
adam_eps = 1e-08
rate_matrix = 0.06
rate_small = 0.2
decay_matrix = 0.05
adam_steps = 3
highest = lax.Precision.HIGHEST


def normalize(values, gain_row, bias_row):
    centred = values - jnp.mean(values, axis=-1, keepdims=True)
    inverse = lax.rsqrt(jnp.mean(centred * centred, axis=-1, keepdims=True) + norm_eps)
    scaled = centred * inverse
    return (scaled, inverse, scaled * gain_row + bias_row)


def normalize_back(grad_normed, scaled, inverse, gain_row):
    grad_scaled = grad_normed * gain_row
    centred_grad = grad_scaled - jnp.mean(grad_scaled, axis=-1, keepdims=True)
    return inverse * (
        centred_grad - scaled * jnp.mean(grad_scaled * scaled, axis=-1, keepdims=True)
    )


def pad_grid(values):
    images, length, channels = values.shape
    return jnp.pad(values.reshape(images, SIDE, SIDE, channels), ((0, 0), (1, 1), (1, 1), (0, 0)))


def shifted(padded, row_off, col_off):
    return padded[:, 1 + row_off : 1 + row_off + SIDE, 1 + col_off : 1 + col_off + SIDE, :]


def conv_grid(hidden, kernel):
    padded = pad_grid(hidden)
    summed = jnp.zeros_like(shifted(padded, 0, 0))
    for tap_index in range(9):
        summed = summed + kernel[tap_index] * shifted(padded, tap_index // 3 - 1, tap_index % 3 - 1)
    return summed.reshape(hidden.shape)


def conv_back(grad_act, hidden, kernel):
    padded_grad = pad_grid(grad_act)
    padded_hidden = pad_grid(hidden)
    grad_grid = shifted(padded_grad, 0, 0)
    grad_hidden = jnp.zeros_like(grad_grid)
    kernel_rows = []
    for tap_index in range(9):
        row_off = tap_index // 3 - 1
        col_off = tap_index % 3 - 1
        grad_hidden = grad_hidden + kernel[tap_index] * shifted(padded_grad, -row_off, -col_off)
        kernel_rows.append(
            jnp.sum(grad_grid * shifted(padded_hidden, row_off, col_off), axis=(0, 1, 2))
        )
    return (grad_hidden.reshape(hidden.shape), jnp.stack(kernel_rows))


def mix_scores(received, talk):
    pre_mixed = jnp.einsum(
        "mn,gnqk->gmqk", talk[0], received.astype(jnp.float32), precision=highest
    )
    softmaxed = jax.nn.softmax(pre_mixed, axis=-1)
    post_mixed = jnp.einsum("jm,gmqk->gjqk", talk[1], softmaxed, precision=highest).astype(
        jnp.bfloat16
    )
    return (softmaxed, post_mixed)


def mix_back(grad_post_all, softmaxed, received, talk):
    grad_soft = jnp.einsum("jm,gjqk->gmqk", talk[1], grad_post_all, precision=highest)
    talk_post = jnp.einsum("gjqk,gmqk->jm", grad_post_all, softmaxed, precision=highest)
    grad_mixed = softmaxed * (grad_soft - jnp.sum(grad_soft * softmaxed, axis=-1, keepdims=True))
    talk_pre = jnp.einsum(
        "gmqk,gnqk->mn", grad_mixed, received.astype(jnp.float32), precision=highest
    )
    grad_scores = jnp.einsum("mn,gmqk->gnqk", talk[0], grad_mixed, precision=highest).astype(
        jnp.bfloat16
    )
    return (grad_scores, talk_pre, talk_post)


def adamw(weights_old, gradient, moment_one, moment_two, step_rate, decay_rate):
    one_new = beta_first * moment_one + (1.0 - beta_first) * gradient
    two_new = beta_second * moment_two + (1.0 - beta_second) * gradient * gradient
    hat_one = one_new / (1.0 - beta_first**adam_steps)
    hat_two = two_new / (1.0 - beta_second**adam_steps)
    weights_new = weights_old - step_rate * (
        hat_one / (jnp.sqrt(hat_two) + adam_eps) + decay_rate * weights_old
    )
    return (weights_new, one_new, two_new)


def gather_blocks(master, block_slot):
    mine = master.astype(jnp.bfloat16)
    data_devices = lax.axis_size("dp")
    every = lax.all_to_all(
        jnp.broadcast_to(mine[None], (data_devices,) + mine.shape), "dp", split_axis=0, concat_axis=0, tiled=True
    )
    every = every.reshape((data_devices * mine.shape[0],) + mine.shape[1:])
    return jnp.take(every, block_slot, axis=0)


def split_pair(values):
    high = lax.reduce_precision(values, exponent_bits=8, mantissa_bits=7)
    low = values - high
    return jnp.concatenate([high.astype(jnp.bfloat16), low.astype(jnp.bfloat16)], axis=-2)


def join_pair(values):
    rows = values.shape[-2] // 2
    return values[..., :rows, :].astype(jnp.float32) + values[..., rows:, :].astype(jnp.float32)


def local(
    tokens,
    cotangent,
    image_count,
    subnet_heads,
    subnet_width,
    block_slot,
    master,
    master_m1,
    master_m2,
    norm_params,
    norm_m1,
    norm_m2,
    talk,
    talk_m1,
    talk_m2,
    conv,
    conv_m1,
    conv_m2,
):
    slot_count = master.shape[0]
    block_rows = master.shape[1]
    model_width = master.shape[2]
    capacity = tokens.shape[0]
    seq_len = tokens.shape[1]
    head_devices = lax.axis_size("head")
    data_devices = lax.axis_size("dp")
    head_place = lax.axis_index("head")
    images = capacity // head_devices
    heads = head_devices * (block_rows // HD)
    hidden_all = head_devices * 4 * block_rows
    scale_factor = HD ** (-0.5)
    first_image = head_place * images
    blocks = gather_blocks(master, block_slot)
    attn_blocks = lax.all_gather(blocks[0:4], "head", axis=0)
    ffn_blocks = lax.all_gather(blocks[4:12], "head", axis=0)
    conv_full = lax.all_gather(conv, "head", axis=1, tiled=True)
    w_query, w_key, w_value, w_out = [
        attn_blocks[:, i].reshape(head_devices * block_rows, model_width) for i in range(4)
    ]
    w_in = ffn_blocks[:, 0:4].reshape(hidden_all, model_width)
    w_down = ffn_blocks[:, 4:8].reshape(hidden_all, model_width)
    image_valid = (first_image + jnp.arange(images) < image_count[0]).astype(jnp.float32)
    head_keep = (jnp.arange(heads) < subnet_heads[0]).astype(jnp.float32)
    unit_keep = (jnp.arange(hidden_all) < subnet_width[0]).astype(jnp.float32)
    token_values = lax.dynamic_slice_in_dim(tokens, first_image, images, 0).astype(jnp.float32)
    my_cotangent = lax.dynamic_slice_in_dim(cotangent, first_image, images, 0)
    scaled_one, inverse_one, normed_full = normalize(token_values, norm_params[0], norm_params[1])
    normed_one = normed_full.astype(jnp.bfloat16)

    def project(weight):
        return (
            jnp.einsum("gsd,fd->gsf", normed_one, weight, preferred_element_type=jnp.float32)
            .astype(jnp.bfloat16)
            .reshape(images, seq_len, heads, HD)
        )

    queries, key_vecs, value_vecs = project(w_query), project(w_key), project(w_value)
    scores = (
        jnp.einsum("gqhe,gkhe->ghqk", queries, key_vecs, preferred_element_type=jnp.float32)
        * scale_factor
    ).astype(jnp.bfloat16)
    softmaxed, post_mixed = mix_scores(scores, talk)
    attended = (
        jnp.einsum("ghqk,gkhe->gqhe", post_mixed, value_vecs, preferred_element_type=jnp.float32)
        * head_keep[None, None, :, None]
    )
    attended = attended.astype(jnp.bfloat16).reshape(images, seq_len, heads * HD)
    middle = token_values + jnp.einsum(
        "gsf,fd->gsd", attended, w_out, preferred_element_type=jnp.float32
    )
    scaled_two, inverse_two, normed_full_two = normalize(middle, norm_params[2], norm_params[3])
    normed_two = normed_full_two.astype(jnp.bfloat16)
    hidden = jnp.einsum("gsd,ud->gsu", normed_two, w_in, preferred_element_type=jnp.float32)
    activated = conv_grid(hidden, conv_full)
    sigmoid_act = jax.nn.sigmoid(activated)
    gated = (activated * sigmoid_act * unit_keep).astype(jnp.bfloat16)
    down = jnp.einsum("gsu,ud->gsd", gated, w_down, preferred_element_type=jnp.float32)
    my_output = (middle + down) * image_valid[:, None, None]
    output = lax.all_gather(my_output.astype(jnp.bfloat16), "head", axis=0, tiled=True).astype(
        jnp.float32
    )
    grad_output = my_cotangent * image_valid[:, None, None]
    grad_low = grad_output.astype(jnp.bfloat16)
    grad_down = jnp.einsum("gsu,gsd->ud", gated, grad_low, preferred_element_type=jnp.float32)
    grad_gated = (
        jnp.einsum("gsd,ud->gsu", grad_low, w_down, preferred_element_type=jnp.float32) * unit_keep
    )
    grad_act = grad_gated * sigmoid_act * (1.0 + activated * (1.0 - sigmoid_act))
    grad_hidden, grad_kernel = conv_back(grad_act, hidden, conv_full)
    grad_hidden_low = grad_hidden.astype(jnp.bfloat16)
    grad_in = jnp.einsum(
        "gsu,gsd->ud", grad_hidden_low, normed_two, preferred_element_type=jnp.float32
    )
    grad_normed_two = jnp.einsum(
        "gsu,ud->gsd", grad_hidden_low, w_in, preferred_element_type=jnp.float32
    )
    grad_middle = grad_output + normalize_back(
        grad_normed_two, scaled_two, inverse_two, norm_params[2]
    )
    grad_branch = grad_middle.astype(jnp.bfloat16)
    grad_out_proj = jnp.einsum(
        "gsf,gsd->fd", attended, grad_branch, preferred_element_type=jnp.float32
    )
    grad_attended = jnp.einsum(
        "gsd,fd->gsf", grad_branch, w_out, preferred_element_type=jnp.float32
    ).reshape(images, seq_len, heads, HD)
    grad_att_low = (grad_attended * head_keep[None, None, :, None]).astype(jnp.bfloat16)
    grad_values = jnp.einsum(
        "ghqk,gqhe->gkhe", post_mixed, grad_att_low, preferred_element_type=jnp.float32
    ).astype(jnp.bfloat16)
    grad_post = jnp.einsum(
        "gqhe,gkhe->ghqk", grad_att_low, value_vecs, preferred_element_type=jnp.float32
    ).astype(jnp.bfloat16)
    grad_scores, talk_pre, talk_post = mix_back(
        grad_post.astype(jnp.float32), softmaxed, scores, talk
    )
    grad_queries = (
        jnp.einsum("ghqk,gkhe->gqhe", grad_scores, key_vecs, preferred_element_type=jnp.float32)
        * scale_factor
    ).astype(jnp.bfloat16)
    grad_keys = (
        jnp.einsum("ghqk,gqhe->gkhe", grad_scores, queries, preferred_element_type=jnp.float32)
        * scale_factor
    ).astype(jnp.bfloat16)
    grad_parts = [
        part.reshape(images, seq_len, heads * HD) for part in (grad_queries, grad_keys, grad_values)
    ]
    grad_projs = [
        jnp.einsum("gsf,gsd->fd", part, normed_one, preferred_element_type=jnp.float32)
        for part in grad_parts
    ]
    grad_normed_one = sum(
        jnp.einsum("gsf,fd->gsd", part, weight, preferred_element_type=jnp.float32)
        for part, weight in zip(grad_parts, (w_query, w_key, w_value))
    )
    my_token_grad = grad_middle + normalize_back(
        grad_normed_one, scaled_one, inverse_one, norm_params[0]
    )
    token_grad = lax.all_gather(
        my_token_grad.astype(jnp.bfloat16), "head", axis=0, tiled=True
    ).astype(jnp.float32)
    norm_part = jnp.stack(
        [
            jnp.sum(grad_normed_one * scaled_one, axis=(0, 1)),
            jnp.sum(grad_normed_one, axis=(0, 1)),
            jnp.sum(grad_normed_two * scaled_two, axis=(0, 1)),
            jnp.sum(grad_normed_two, axis=(0, 1)),
        ]
    )
    talk_part = jnp.stack([talk_pre, talk_post]).reshape(2, heads * heads)
    talk_part = jnp.pad(talk_part, ((0, 0), (0, model_width - heads * heads)))
    every_head = jnp.broadcast_to(
        jnp.concatenate([norm_part, talk_part])[None], (head_devices, 6, model_width)
    )
    conv_part = grad_kernel.reshape(9, head_devices, model_width).transpose(1, 0, 2)
    small = split_pair(jnp.concatenate([every_head, conv_part], axis=1))

    def by_head(matrix):
        return matrix.reshape(head_devices, -1, model_width)

    message = jnp.concatenate(
        [by_head(m).astype(jnp.bfloat16) for m in (*grad_projs, grad_out_proj, grad_in, grad_down)]
        + [small],
        axis=1,
    )
    received = lax.all_to_all(message, "head", split_axis=0, concat_axis=0, tiled=True)
    matrix_rows = 12 * block_rows
    block_grads = jnp.sum(received[:, :matrix_rows].astype(jnp.float32), axis=0).reshape(
        12, block_rows, model_width
    )
    small_sum = jnp.sum(join_pair(received[:, matrix_rows:]), axis=0)
    all_slots = slot_count * data_devices
    spread_grads = (
        jnp.zeros((all_slots, block_rows, model_width), jnp.bfloat16)
        .at[block_slot]
        .set(block_grads.astype(jnp.bfloat16))
        .reshape(data_devices, slot_count * block_rows, model_width)
    )
    small_pair = split_pair(small_sum)
    message_two = jnp.concatenate(
        [spread_grads, jnp.broadcast_to(small_pair[None], (data_devices,) + small_pair.shape)],
        axis=1,
    )
    received_two = lax.all_to_all(message_two, "dp", split_axis=0, concat_axis=0, tiled=True)
    slot_rows = slot_count * block_rows
    slot_grads = jnp.sum(received_two[:, :slot_rows].astype(jnp.float32), axis=0).reshape(
        slot_count, block_rows, model_width
    )
    small_total = jnp.sum(join_pair(received_two[:, slot_rows:]), axis=0)
    norm_grad = small_total[0:4]
    talk_grad = small_total[4:6, : heads * heads].reshape(2, heads, heads)
    conv_grad = small_total[6:15]
    new_master, new_master_m1, new_master_m2 = adamw(
        master, slot_grads, master_m1, master_m2, rate_matrix, decay_matrix
    )
    new_norm, new_norm_m1, new_norm_m2 = adamw(
        norm_params, norm_grad, norm_m1, norm_m2, rate_small, 0.0
    )
    new_talk, new_talk_m1, new_talk_m2 = adamw(talk, talk_grad, talk_m1, talk_m2, rate_small, 0.0)
    new_conv, new_conv_m1, new_conv_m2 = adamw(
        conv, conv_grad, conv_m1, conv_m2, rate_small, decay_matrix
    )
    return (
        output,
        token_grad,
        new_master,
        new_master_m1,
        new_master_m2,
        new_master.astype(jnp.bfloat16),
        new_norm,
        new_norm_m1,
        new_norm_m2,
        new_talk,
        new_talk_m1,
        new_talk_m2,
        new_conv,
        new_conv_m1,
        new_conv_m2,
    )


def solution(mesh):
    in_specs = (
        P("dp", None, None),
        P("dp", None, None),
        P("dp"),
        P(),
        P(),
        P(),
        P("dp", None, "head"),
        P("dp", None, "head"),
        P("dp", None, "head"),
        P(),
        P(),
        P(),
        P(),
        P(),
        P(),
        P(None, "head"),
        P(None, "head"),
        P(None, "head"),
    )
    out_specs = (
        P("dp", None, None),
        P("dp", None, None),
        P("dp", None, "head"),
        P("dp", None, "head"),
        P("dp", None, "head"),
        P("dp", None, "head"),
        P(),
        P(),
        P(),
        P(),
        P(),
        P(),
        P(None, "head"),
        P(None, "head"),
        P(None, "head"),
    )
    return jax.shard_map(local, mesh=mesh, in_specs=in_specs, out_specs=out_specs, check_vma=False)
```

```python
import functools
import jax
import jax.numpy as jnp
from jax import lax
from jax.experimental import pallas as pl
from jax.experimental.pallas import tpu as pltpu
from jax.sharding import PartitionSpec as P

HD = 18
SIDE = 14
PITCH = 16
MARGIN = 24
norm_eps = 1e-05
bf16 = jnp.bfloat16
f32 = jnp.float32


def nn(a, b):
    return lax.dot_general(a, b, (((1,), (0,)), ((), ())), preferred_element_type=f32)


def nt(a, b):
    return lax.dot_general(a, b, (((1,), (1,)), ((), ())), preferred_element_type=f32)


def tn(a, b):
    return lax.dot_general(a, b, (((0,), (0,)), ((), ())), preferred_element_type=f32)


def iota(shape, dim):
    return lax.broadcasted_iota(jnp.int32, shape, dim)


def split2(v):
    hi = v.astype(bf16)
    return hi, (v - hi.astype(f32)).astype(bf16)


def real_rows(shape):
    return (iota(shape, 0) & (PITCH - 1)) < SIDE


def head_mask(rows_heads, keep_heads=None):
    shape = (rows_heads * PITCH, 256)
    row_head = iota(shape, 0) >> 4
    lane = iota(shape, 1)
    rest = lane & 63
    lane_head = (lane >> 6) * 3 + (rest >= 18).astype(jnp.int32) + (rest >= 36).astype(jnp.int32)
    on = (row_head == lane_head) & (rest < 54)
    if keep_heads is not None:
        on = on & (row_head < keep_heads)
    return on


def true_head(rows, place):
    return ((rows // (3 * PITCH)) ^ place) * 3 + (rows // PITCH) % 3


def prep_kernel(scal, tok_ref, cot_ref, norm_ref, talk_ref, x_ref, a_ref, dy_ref, kron_ref, mask_ref, bias_ref, tmp_ref):
    x_ref[...] = jnp.zeros_like(x_ref)
    dy_ref[...] = jnp.zeros_like(dy_ref)
    valid = (scal[0] < scal[1]).astype(f32)
    tmp_ref[...] = tok_ref[0].astype(f32)
    for y in range(SIDE):
        x_ref[PITCH * y : PITCH * y + SIDE, :] = tmp_ref[SIDE * y : SIDE * (y + 1), :]
        dy_ref[PITCH * y : PITCH * y + SIDE, :] = cot_ref[0, SIDE * y : SIDE * (y + 1), :] * valid
    x = x_ref[...]
    centred = x - jnp.mean(x, axis=-1, keepdims=True)
    inv = lax.rsqrt(jnp.mean(centred * centred, axis=-1, keepdims=True) + norm_eps)
    a = centred * inv * norm_ref[0:1, :] + norm_ref[1:2, :]
    a_ref[...] = jnp.where(real_rows(a.shape), a, 0.0).astype(bf16)
    heads = talk_ref.shape[1]
    n = heads * PITCH
    ex = (true_head(iota((n, heads), 0), scal[0]) == iota((n, heads), 1)).astype(bf16)
    same = ((iota((n, n), 0) & (PITCH - 1)) == (iota((n, n), 1) & (PITCH - 1)))
    for i in range(2):
        for j, part in enumerate(split2(talk_ref[i])):
            if i == 0:
                half = nt(ex, part).astype(bf16)
            else:
                half = nn(ex, part).astype(bf16)
            kron_ref[2 * i + j] = jnp.where(same, nt(half, ex), 0.0).astype(bf16)
    mask_ref[...] = head_mask(heads).astype(bf16)
    bias_ref[...] = jnp.where(real_rows(bias_ref.shape), 0.0, -1e30)


def load_weight(dst_ref, w_refs, b):
    for k, w_ref in enumerate(w_refs):
        dst_ref[64 * k : 64 * k + 54, :] = w_ref[b]


def attn_fwd_kernel(
    scal, x_ref, a_ref, kron_ref, mask_ref, bias_ref, *refs, parts, unroll
):
    w_refs, refs = refs[:parts], refs[parts:]
    mid_ref, q_ref, k_ref, v_ref, o_ref, s_ref, p_ref, ws_ref, keep_ref = refs
    heads = kron_ref.shape[1] // PITCH
    n = heads * PITCH
    a = a_ref[...]
    ws_ref[...] = jnp.zeros_like(ws_ref)
    for b, dst in enumerate((q_ref, k_ref, v_ref)):
        load_weight(ws_ref.at[b], w_refs, b)
        dst[...] = nt(a, ws_ref[b]).astype(bf16)
    load_weight(ws_ref.at[3], w_refs, 3)
    scale = HD ** (-0.5)
    keep_rows = (true_head(iota((n, 1), 0), scal[0]) < scal[2]).astype(f32)
    keep_ref[...] = mask_ref[...].astype(f32) * keep_rows

    def group(y, _):
        rows = pl.ds(pl.multiple_of(y * PITCH, PITCH), PITCH)
        mask = mask_ref[...]
        qx = jnp.concatenate([q_ref[rows, :]] * heads, axis=0) * mask
        s = (nt(k_ref[...], qx) * scale).astype(bf16)
        s_ref[y] = s
        t = nn(s, kron_ref[0]) + nn(s, kron_ref[1])
        t = t + bias_ref[...]
        e = jnp.exp(t - jnp.max(t, axis=0, keepdims=True))
        p = e * (1.0 / jnp.sum(e, axis=0, keepdims=True))
        p_ref[y] = p
        ph, plo = split2(p)
        r = nt(kron_ref[2], ph).astype(bf16)
        o = nn(r, v_ref[...]) * keep_ref[...]
        o_ref[rows, :] = jnp.sum(o.reshape(heads, PITCH, 256), axis=0).astype(bf16)
        return 0

    lax.fori_loop(0, SIDE, group, 0, unroll=unroll)
    mid_ref[...] = x_ref[...] + nn(o_ref[...], ws_ref[3])


def ln_stats(v):
    centred = v - jnp.mean(v, axis=-1, keepdims=True)
    inv = lax.rsqrt(jnp.mean(centred * centred, axis=-1, keepdims=True) + norm_eps)
    return centred * inv, inv


def ln_back(grad, scaled, inv, gain):
    gs = grad * gain
    return inv * (
        gs - jnp.mean(gs, axis=-1, keepdims=True) - scaled * jnp.mean(gs * scaled, axis=-1, keepdims=True)
    )


def place(rows=216):
    shape = (rows, 256)
    lane = iota(shape, 1)
    rest = lane & 63
    return ((iota(shape, 0) == (lane >> 6) * 54 + rest) & (rest < 54)).astype(bf16)


def ffn_kernel(
    scal, mid_ref, dy_ref, norm_ref, *refs, parts
):
    w_refs, refs = refs[:parts], refs[parts:]
    out_ref, dmid_ref, gn_ref = refs[:3]
    gw_refs, refs = refs[3 : 3 + parts], refs[3 + parts :]
    win_ref, wdn_ref, h_ref, d_ref, gate_ref, dh_ref, cv_ref, gcv_ref, tmp_ref = refs
    hd = parts
    lanes = hd * 256
    win_ref[...] = jnp.zeros_like(win_ref)
    wdn_ref[...] = jnp.zeros_like(wdn_ref)
    pm = place()
    for h in range(hd):
        for j in range(4):
            at = 256 * h + 64 * j
            win_ref[at : at + 54, :] = w_refs[h][j]
            wdn_ref[at : at + 54, :] = w_refs[h][4 + j]
        both = nn(w_refs[h][8], pm)
        cv_ref[:, 256 * h : 256 * (h + 1)] = both[0:9] + both[16:25]
    mid = mid_ref[...]
    z, inv = ln_stats(mid)
    rows = real_rows(mid.shape)
    w = jnp.where(rows, z * norm_ref[2:3, :] + norm_ref[3:4, :], 0.0).astype(bf16)
    dy = dy_ref[...]
    e = dy.astype(bf16)
    tokens = mid.shape[0]
    pad = MARGIN
    zero = jnp.zeros((pad, lanes), f32)
    h_ref[0:pad, :] = zero
    h_ref[pad + tokens :, :] = zero
    d_ref[0:pad, :] = zero
    d_ref[pad + tokens :, :] = zero
    h_ref[pad : pad + tokens, :] = nt(w, win_ref[...])
    d_ref[pad : pad + tokens, :] = nt(e, wdn_ref[...])
    lane = iota((1, 128), 1)
    rmask = real_rows((tokens, 128))
    for c in range(lanes // 128):
        cols = slice(128 * c, 128 * (c + 1))
        glane = lane + 128 * c
        rest = glane & 63
        unit = (((glane >> 8) ^ scal[0]) * 4 + ((glane >> 6) & 3)) * 54 + rest
        keep = ((rest < 54) & (unit < scal[3])).astype(f32)
        act = jnp.zeros((tokens, 128), f32)
        for t in range(9):
            off = PITCH * (t // 3 - 1) + t % 3 - 1
            act = act + cv_ref[t : t + 1, cols] * h_ref[pad + off : pad + off + tokens, cols]
        sig = 1.0 / (1.0 + jnp.exp(-act))
        gate_ref[:, cols] = (act * sig * keep).astype(bf16)
        dact = d_ref[pad : pad + tokens, cols] * keep * sig * (1.0 + act * (1.0 - sig))
        d_ref[pad : pad + tokens, cols] = dact
        dh = jnp.zeros((tokens, 128), f32)
        for t in range(9):
            off = PITCH * (t // 3 - 1) + t % 3 - 1
            gcv_ref[t : t + 1, cols] = jnp.sum(
                dact * h_ref[pad + off : pad + off + tokens, cols], axis=0, keepdims=True
            )
            dh = dh + cv_ref[t : t + 1, cols] * d_ref[pad - off : pad - off + tokens, cols]
        dh_ref[:, cols] = jnp.where(rmask, dh, 0.0).astype(bf16)
    valid = (scal[0] < scal[1]).astype(f32)
    down = nn(gate_ref[...], wdn_ref[...])
    tmp_ref[...] = (mid + down) * valid
    for y in range(SIDE):
        out_ref[SIDE * y : SIDE * (y + 1), :] = tmp_ref[PITCH * y : PITCH * y + SIDE, :].astype(bf16)
    dw = nn(dh_ref[...], win_ref[...])
    gn_ref[...] = jnp.zeros_like(gn_ref)
    gn_ref[0:1, :] = jnp.sum(dw * z, axis=0, keepdims=True)
    gn_ref[1:2, :] = jnp.sum(dw, axis=0, keepdims=True)
    dmid_ref[...] = dy + ln_back(dw, z, inv, norm_ref[2:3, :])
    for h in range(hd):
        cols = slice(256 * h, 256 * (h + 1))
        gi = tn(dh_ref[:, cols], w).astype(bf16)
        gd = tn(gate_ref[:, cols], e).astype(bf16)
        for j in range(4):
            gw_refs[h][j] = gi[64 * j : 64 * j + 54]
            gw_refs[h][4 + j] = gd[64 * j : 64 * j + 54]
        hi, lo = split2(gcv_ref[:, cols])
        gw_refs[h][8] = jnp.zeros_like(gw_refs[h][8])
        gw_refs[h][8, 0:9] = nt(hi, pm).astype(bf16)
        gw_refs[h][8, 16:25] = nt(lo, pm).astype(bf16)


def attn_bwd_kernel(
    scal, x_ref, a_ref, dmid_ref, norm_ref, gn2_ref, kron_ref, mask_ref, q_ref, k_ref, v_ref, o_ref, s_ref, p_ref,
    *refs, parts, unroll
):
    w_refs, refs = refs[:parts], refs[parts:]
    tg_ref, gw_refs, refs = refs[0], refs[1 : 1 + parts], refs[1 + parts :]
    ws_ref, do_ref, gq_ref, gk_ref, gv_ref, g0_ref, g1_ref, tmp_ref, fm_ref, small_ref = refs
    heads = kron_ref.shape[1] // PITCH
    n = heads * PITCH
    hd = parts
    scale = HD ** (-0.5)
    ws_ref[...] = jnp.zeros_like(ws_ref)
    for b in range(4):
        load_weight(ws_ref.at[b], w_refs, b)
    f = dmid_ref[...].astype(bf16)
    lane = iota((1, 256), 1)
    rest = lane & 63
    lane_head = ((lane >> 6) ^ scal[0]) * 3 + (rest >= 18).astype(jnp.int32) + (rest >= 36).astype(jnp.int32)
    lane_keep = ((lane_head < scal[2]) & (rest < 54)).astype(f32)
    do_ref[...] = (nt(f, ws_ref[3]) * lane_keep).astype(bf16)
    g0_ref[...] = jnp.zeros_like(g0_ref)
    g1_ref[...] = jnp.zeros_like(g1_ref)
    gk_ref[...] = jnp.zeros_like(gk_ref)
    gv_ref[...] = jnp.zeros_like(gv_ref)
    fm_ref[...] = mask_ref[...].astype(f32)

    def group(y, _):
        rows = pl.ds(pl.multiple_of(y * PITCH, PITCH), PITCH)
        mask = mask_ref[...]
        qx = jnp.concatenate([q_ref[rows, :]] * heads, axis=0) * mask
        dx = jnp.concatenate([do_ref[rows, :]] * heads, axis=0) * mask
        v = v_ref[...]
        k = k_ref[...]
        p = p_ref[y]
        ph, plo = split2(p)
        dr = nt(dx, v).astype(bf16)
        drt = nt(v, dx).astype(bf16)
        dp = nn(drt, kron_ref[2])
        dt = p * (dp - jnp.sum(dp * p, axis=0, keepdims=True))
        dth, dtl = split2(dt)
        g1_ref[...] += nn(dr, ph)
        srow = (nt(qx, k) * scale).astype(bf16)
        g0_ref[...] += nn(srow, dth)
        dst = nt(dth, kron_ref[0]).astype(bf16)
        dsr = nt(kron_ref[0], dth).astype(bf16)
        gk_ref[...] += nn(dst, qx)
        gq = nn(dsr, k) * fm_ref[...]
        gq_ref[rows, :] = (jnp.sum(gq.reshape(heads, PITCH, 256), axis=0) * scale).astype(bf16)
        rt = nt(ph, kron_ref[2]).astype(bf16)
        gv_ref[...] += nn(rt, dx)
        return 0

    lax.fori_loop(0, SIDE, group, 0, unroll=unroll)
    gq = gq_ref[...]
    gk = (gk_ref[...] * scale).astype(bf16)
    gv = gv_ref[...].astype(bf16)
    a = a_ref[...]
    da = nn(gq, ws_ref[0]) + nn(gk, ws_ref[1]) + nn(gv, ws_ref[2])
    for b, (g, t) in enumerate(((gq, a), (gk, a), (gv, a), (o_ref[...], f))):
        gw = tn(g, t).astype(bf16)
        for h in range(hd):
            gw_refs[h][b] = gw[64 * h : 64 * h + 54]
    z, inv = ln_stats(x_ref[...])
    small_ref[...] = jnp.zeros_like(small_ref)
    small_ref[0:1, :] = jnp.sum(da * z, axis=0, keepdims=True)
    small_ref[1:2, :] = jnp.sum(da, axis=0, keepdims=True)
    small_ref[2:4, :] = gn2_ref[0:2, :]
    tmp_ref[...] = dmid_ref[...] + ln_back(da, z, inv, norm_ref[0:1, :])
    for y in range(SIDE):
        tg_ref[SIDE * y : SIDE * (y + 1), :] = tmp_ref[PITCH * y : PITCH * y + SIDE, :].astype(bf16)
    same = (iota((n, n), 0) & (PITCH - 1)) == (iota((n, n), 1) & (PITCH - 1))
    ex = (true_head(iota((n, heads), 0), scal[0]) == iota((n, heads), 1)).astype(bf16)
    for i, ref in enumerate((g0_ref, g1_ref)):
        g = jnp.where(same, ref[...], 0.0)
        hi, lo = split2(g)
        cols = nn(hi, ex) + nn(lo, ex)
        hi, lo = split2(cols)
        if i == 0:
            small_ref[8:20, 0:heads] = tn(hi, ex) + tn(lo, ex)
        else:
            small_ref[8:20, 128 : 128 + heads] = tn(ex, hi) + tn(ex, lo)
    hi, lo = split2(small_ref[...])
    for h in range(hd):
        gw_refs[h][4, 0:24] = hi
        gw_refs[h][4, 24:48] = lo
        gw_refs[h][4, 48:54] = jnp.zeros((6, hi.shape[1]), bf16)


def cast_kernel(m_ref, out_ref):
    low = m_ref[...].astype(bf16)
    for i in range(out_ref.shape[0]):
        out_ref[i] = low


def select_kernel(slot_ref, every_ref, conv_ref, attn_ref, ffn_ref):
    per = every_ref.shape[1]
    for b in range(12):
        slot = slot_ref[b]
        block = every_ref[slot // per, slot % per]
        if b < 4:
            attn_ref[b] = block
        else:
            ffn_ref[b - 4] = block
    hi, lo = split2(conv_ref[...])
    ffn_ref[8] = jnp.zeros_like(ffn_ref[8])
    ffn_ref[8, 0:9] = hi
    ffn_ref[8, 16:25] = lo


def total(refs, at):
    acc = refs[0][at].astype(f32)
    for ref in refs[1:]:
        acc = acc + ref[at].astype(f32)
    return acc


def spread_kernel(slot_ref, *refs, parts):
    attn, ffn_refs, out_ref = refs[:parts], refs[parts : 2 * parts], refs[2 * parts]
    ranks, per = out_ref.shape[0], out_ref.shape[1] - 1
    out_ref[...] = jnp.zeros_like(out_ref)
    for b in range(12):
        slot = slot_ref[b]
        block = total(attn, b) if b < 4 else total(ffn_refs, b - 4)
        out_ref[slot // per, slot % per] = block.astype(bf16)
    norm = total(attn, 4)
    norm_hi, norm_lo = split2(norm[0:24] + norm[24:48])
    conv = total(ffn_refs, 8)
    conv_hi, conv_lo = split2(conv[0:9] + conv[16:25])
    for i in range(ranks):
        out_ref[i, per, 0:20] = norm_hi[0:20]
        out_ref[i, per, 20:29] = conv_hi
        out_ref[i, per, 29:38] = conv_lo
        out_ref[i, per, 38:42] = norm_lo[0:4]
        out_ref[i, per, 42:54] = norm_lo[8:20]


def adam(w, g, one, two, rate, decay):
    one_new = 0.5 * one + 0.5 * g
    two_new = 0.5 * two + 0.5 * g * g
    hat_one = one_new / (1.0 - 0.5**3)
    hat_two = two_new / (1.0 - 0.5**3)
    return w - rate * (hat_one / (jnp.sqrt(hat_two) + 1e-08) + decay * w), one_new, two_new


def update_kernel(*refs):
    got_ref, ins, outs = refs[0], refs[1:13], refs[13:]
    ranks, per = got_ref.shape[0], got_ref.shape[1] - 1
    for i in range(per):
        g = got_ref[0, i].astype(f32)
        for r in range(1, ranks):
            g = g + got_ref[r, i].astype(f32)
        w, one, two = adam(ins[0][i], g, ins[1][i], ins[2][i], 0.06, 0.05)
        outs[0][i], outs[1][i], outs[2][i], outs[3][i] = w, one, two, w.astype(bf16)
    g = got_ref[0, per].astype(f32)
    for r in range(1, ranks):
        g = g + got_ref[r, per].astype(f32)
    heads = ins[6].shape[1]
    norm = g[0:4] + g[38:42]
    mix = g[8:20] + g[42:54]
    conv = g[20:29] + g[29:38]
    outs[4][...], outs[5][...], outs[6][...] = adam(ins[3][...], norm, ins[4][...], ins[5][...], 0.2, 0.0)
    for i in range(2):
        w, one, two = adam(ins[6][i], mix[:, 128 * i : 128 * i + heads], ins[7][i], ins[8][i], 0.2, 0.0)
        outs[7][i], outs[8][i], outs[9][i] = w, one, two
    outs[10][...], outs[11][...], outs[12][...] = adam(ins[9][...], conv, ins[10][...], ins[11][...], 0.2, 0.05)


def assemble_kernel(scal, *refs, parts):
    for i, out_ref in enumerate(refs[2 * parts :]):
        for k in range(parts):
            out_ref[scal[0] ^ k] = refs[parts * i + k][...].astype(f32)


VM = pl.BlockSpec(memory_space=pltpu.VMEM)
SM = pl.BlockSpec(memory_space=pltpu.SMEM)
SDS = jax.ShapeDtypeStruct


def call(body, name, n_scalar, n_in, out_shape, scratch=(), mb=16, micros=1, **kw):
    return pl.pallas_call(
        functools.partial(body, **kw) if kw else body,
        in_specs=[SM] * n_scalar + [VM] * n_in,
        out_specs=[VM] * len(out_shape),
        out_shape=out_shape,
        scratch_shapes=scratch,
        compiler_params=pltpu.CompilerParams(vmem_limit_bytes=mb << 20),
        cost_estimate=pl.CostEstimate(flops=micros * 1000000000, transcendentals=0, bytes_accessed=micros * 3000000),
        name=name,
    )


def prep(scal, tokens, cotangent, norm_params, talk):
    tok, dim = tokens.shape[1], tokens.shape[2]
    pad = SIDE * PITCH
    heads = talk.shape[1]
    n = heads * PITCH
    full = lambda *s: pl.BlockSpec(s, lambda i, sc: (0,) * len(s))
    return pl.pallas_call(
        prep_kernel,
        grid_spec=pltpu.PrefetchScalarGridSpec(
            num_scalar_prefetch=1,
            grid=(1,),
            in_specs=[
                pl.BlockSpec((1, tok, dim), lambda i, sc: (sc[0], 0, 0)),
                pl.BlockSpec((1, tok, dim), lambda i, sc: (sc[0], 0, 0)),
                full(*norm_params.shape),
                full(*talk.shape),
            ],
            out_specs=[full(pad, dim), full(pad, dim), full(pad, dim), full(4, n, n), full(n, 256), full(pad, n)],
            scratch_shapes=[pltpu.VMEM((tok, dim), f32)],
        ),
        out_shape=[SDS((pad, dim), f32), SDS((pad, dim), bf16), SDS((pad, dim), f32), SDS((4, n, n), bf16),
                   SDS((n, 256), bf16), SDS((pad, n), f32)],
        compiler_params=pltpu.CompilerParams(vmem_limit_bytes=16 << 20),
        cost_estimate=pl.CostEstimate(flops=1000000000, transcendentals=0, bytes_accessed=3000000),
        name="prep",
    )(scal, tokens, cotangent, norm_params, talk)


def attn_fwd(scal, x, a, kron, mask, bias, w, unroll=7):
    pad, dim = x.shape
    n = kron.shape[1]
    return call(
        attn_fwd_kernel, "attn_fwd", 1, 5 + len(w),
        [SDS((pad, dim), f32)] + [SDS((pad, 256), bf16)] * 4 + [SDS((SIDE, pad, n), bf16), SDS((SIDE, pad, n), f32)],
        [pltpu.VMEM((4, 256, dim), bf16), pltpu.VMEM((n, 256), f32)],
        mb=24, micros=10, parts=len(w), unroll=unroll,
    )(scal, x, a, kron, mask, bias, *w)


def ffn(scal, mid, dy, norm_params, w):
    pad, dim = mid.shape
    lanes = len(w) * 256
    return call(
        ffn_kernel, "ffn", 1, 3 + len(w),
        [SDS((SIDE * SIDE, dim), bf16), SDS((pad, dim), f32), SDS((8, dim), f32)] + [SDS((9, 54, dim), bf16)] * len(w),
        [
            pltpu.VMEM((lanes, dim), bf16), pltpu.VMEM((lanes, dim), bf16),
            pltpu.VMEM((pad + 2 * MARGIN, lanes), f32), pltpu.VMEM((pad + 2 * MARGIN, lanes), f32),
            pltpu.VMEM((pad, lanes), bf16), pltpu.VMEM((pad, lanes), bf16),
            pltpu.VMEM((9, lanes), f32), pltpu.VMEM((9, lanes), f32), pltpu.VMEM((pad, dim), f32),
        ],
        mb=24, micros=6, parts=len(w),
    )(scal, mid, dy, norm_params, *w)


def attn_bwd(scal, x, a, dmid, norm_params, gn2, kron, mask, q, k, v, o, s, p, w, unroll=7):
    pad, dim = x.shape
    n = kron.shape[1]
    return call(
        attn_bwd_kernel, "attn_bwd", 1, 13 + len(w),
        [SDS((SIDE * SIDE, dim), bf16)] + [SDS((5, 54, dim), bf16)] * len(w),
        [
            pltpu.VMEM((4, 256, dim), bf16), pltpu.VMEM((pad, 256), bf16), pltpu.VMEM((pad, 256), bf16),
            pltpu.VMEM((pad, 256), f32), pltpu.VMEM((pad, 256), f32),
            pltpu.VMEM((n, n), f32), pltpu.VMEM((n, n), f32), pltpu.VMEM((pad, dim), f32), pltpu.VMEM((n, 256), f32),
            pltpu.VMEM((24, dim), f32),
        ],
        mb=24, micros=14, parts=len(w), unroll=unroll,
    )(scal, x, a, dmid, norm_params, gn2, kron, mask, q, k, v, o, s, p, *w)


def from_peers(x, axis):
    n = lax.axis_size(axis)
    return [lax.ppermute(x, axis, [(i, i ^ k) for i in range(n)]) for k in range(1, n)]


def exchange(messages, axis):
    n = lax.axis_size(axis)
    return [messages[0]] + [
        lax.ppermute(messages[k], axis, [(i, i ^ k) for i in range(n)]) for k in range(1, n)
    ]


def local(
    tokens, cotangent, image_count, subnet_heads, subnet_width, block_slot,
    master, master_m1, master_m2, norm_params, norm_m1, norm_m2, talk, talk_m1, talk_m2, conv, conv_m1, conv_m2,
):
    slots, rows, dim = master.shape
    parts = lax.axis_size("head")
    ranks = lax.axis_size("dp")
    place_id = lax.axis_index("head").astype(jnp.int32)
    scal = jnp.concatenate([place_id[None], image_count, subnet_heads, subnet_width])
    (mine,) = call(cast_kernel, "cast", 0, 1, [SDS((ranks, slots, rows, dim), bf16)])(master)
    every = lax.all_to_all(mine, "dp", split_axis=0, concat_axis=0, tiled=True)
    x, a, dy, kron, mask, bias = prep(scal, tokens, cotangent, norm_params, talk)
    attn_w, ffn_w = call(
        select_kernel, "select", 1, 2, [SDS((4, rows, dim), bf16), SDS((9, rows, dim), bf16)]
    )(block_slot, every, conv)
    attn_w = [attn_w] + from_peers(attn_w, "head")
    ffn_w, attn_w[1:] = lax.optimization_barrier((ffn_w, attn_w[1:]))
    ffn_w = [ffn_w] + from_peers(ffn_w, "head")
    mid, q, k, v, o, s, p = attn_fwd(scal, x, a, kron, mask, bias, attn_w)
    out, dmid, gn2, *ffn_g = ffn(scal, mid, dy, norm_params, ffn_w)
    tg, *attn_g = attn_bwd(scal, x, a, dmid, norm_params, gn2, kron, mask, q, k, v, o, s, p, attn_w)
    ffn_g = exchange(ffn_g, "head")
    outs = [out] + from_peers(out, "head")
    attn_g = exchange(attn_g, "head")
    tg, attn_g[1:] = lax.optimization_barrier((tg, attn_g[1:]))
    tgs = [tg] + from_peers(tg, "head")
    (message,) = call(
        spread_kernel, "spread", 1, 2 * parts, [SDS((ranks, slots + 1, rows, dim), bf16)], parts=parts
    )(block_slot, *attn_g, *ffn_g)
    got = lax.all_to_all(message, "dp", split_axis=0, concat_axis=0, tiled=True)
    images = SDS((parts,) + tokens.shape[1:], f32)
    output, token_grad = call(assemble_kernel, "assemble", 1, 2 * parts, [images, images], parts=parts)(
        scal, *outs, *tgs
    )
    state = (master, master_m1, master_m2, norm_params, norm_m1, norm_m2, talk, talk_m1, talk_m2, conv, conv_m1, conv_m2)
    shapes = [SDS(t.shape, f32) for t in state]
    shapes.insert(3, SDS(master.shape, bf16))
    new = call(update_kernel, "update", 0, 13, shapes)(got, *state)
    return (output, token_grad, *new)


def solution(mesh):
    in_specs = (
        P("dp", None, None),
        P("dp", None, None),
        P("dp"),
        P(),
        P(),
        P(),
        P("dp", None, "head"),
        P("dp", None, "head"),
        P("dp", None, "head"),
        P(),
        P(),
        P(),
        P(),
        P(),
        P(),
        P(None, "head"),
        P(None, "head"),
        P(None, "head"),
    )
    out_specs = (
        P("dp", None, None),
        P("dp", None, None),
        P("dp", None, "head"),
        P("dp", None, "head"),
        P("dp", None, "head"),
        P("dp", None, "head"),
        P(),
        P(),
        P(),
        P(),
        P(),
        P(),
        P(None, "head"),
        P(None, "head"),
        P(None, "head"),
    )
    return jax.shard_map(local, mesh=mesh, in_specs=in_specs, out_specs=out_specs, check_vma=False)
```

```python
import functools
import jax
import jax.numpy as jnp
from jax import lax
from jax.experimental import pallas as pl
from jax.experimental.pallas import tpu as pltpu
from jax.sharding import PartitionSpec as P

HD = 18
SIDE = 14
PITCH = 16
MARGIN = 24
norm_eps = 1e-05
bf16 = jnp.bfloat16
f32 = jnp.float32


def nn(a, b):
    return lax.dot_general(a, b, (((1,), (0,)), ((), ())), preferred_element_type=f32)


def nt(a, b):
    return lax.dot_general(a, b, (((1,), (1,)), ((), ())), preferred_element_type=f32)


def tn(a, b):
    return lax.dot_general(a, b, (((0,), (0,)), ((), ())), preferred_element_type=f32)


def iota(shape, dim):
    return lax.broadcasted_iota(jnp.int32, shape, dim)


def split2(v):
    hi = v.astype(bf16)
    return hi, (v - hi.astype(f32)).astype(bf16)


def real_rows(shape):
    return (iota(shape, 0) & (PITCH - 1)) < SIDE


def head_mask(rows_heads, keep_heads=None):
    shape = (rows_heads * PITCH, 256)
    row_head = iota(shape, 0) >> 4
    lane = iota(shape, 1)
    rest = lane & 63
    lane_head = (lane >> 6) * 3 + (rest >= 18).astype(jnp.int32) + (rest >= 36).astype(jnp.int32)
    on = (row_head == lane_head) & (rest < 54)
    if keep_heads is not None:
        on = on & (row_head < keep_heads)
    return on


def true_head(rows, place):
    return ((rows // (3 * PITCH)) ^ place) * 3 + (rows // PITCH) % 3


def prep_kernel(scal, tok_ref, cot_ref, norm_ref, talk_ref, x_ref, a_ref, dy_ref, kron_ref, mask_ref, bias_ref, tmp_ref):
    x_ref[...] = jnp.zeros_like(x_ref)
    dy_ref[...] = jnp.zeros_like(dy_ref)
    valid = (scal[0] < scal[1]).astype(f32)
    tmp_ref[...] = tok_ref[0].astype(f32)
    for y in range(SIDE):
        x_ref[PITCH * y : PITCH * y + SIDE, :] = tmp_ref[SIDE * y : SIDE * (y + 1), :]
        dy_ref[PITCH * y : PITCH * y + SIDE, :] = cot_ref[0, SIDE * y : SIDE * (y + 1), :] * valid
    x = x_ref[...]
    centred = x - jnp.mean(x, axis=-1, keepdims=True)
    inv = lax.rsqrt(jnp.mean(centred * centred, axis=-1, keepdims=True) + norm_eps)
    a = centred * inv * norm_ref[0:1, :] + norm_ref[1:2, :]
    a_ref[...] = jnp.where(real_rows(a.shape), a, 0.0).astype(bf16)
    heads = talk_ref.shape[1]
    n = heads * PITCH
    ex = (true_head(iota((n, heads), 0), scal[0]) == iota((n, heads), 1)).astype(bf16)
    same = ((iota((n, n), 0) & (PITCH - 1)) == (iota((n, n), 1) & (PITCH - 1)))
    for i in range(2):
        for j, part in enumerate(split2(talk_ref[i])):
            if i == 0:
                half = nt(ex, part).astype(bf16)
            else:
                half = nn(ex, part).astype(bf16)
            kron_ref[2 * i + j] = jnp.where(same, nt(half, ex), 0.0).astype(bf16)
    mask_ref[...] = head_mask(heads).astype(bf16)
    bias_ref[...] = jnp.where(real_rows(bias_ref.shape), 0.0, -1e30)


def load_weight(dst_ref, w_refs, b):
    for k, w_ref in enumerate(w_refs):
        dst_ref[64 * k : 64 * k + 54, :] = w_ref[b]


def attn_fwd_kernel(
    scal, x_ref, a_ref, kron_ref, mask_ref, bias_ref, *refs, parts, unroll
):
    w_refs, refs = refs[:parts], refs[parts:]
    mid_ref, q_ref, k_ref, v_ref, o_ref, s_ref, p_ref, ws_ref, keep_ref = refs
    heads = kron_ref.shape[1] // PITCH
    n = heads * PITCH
    a = a_ref[...]
    ws_ref[...] = jnp.zeros_like(ws_ref)
    for b, dst in enumerate((q_ref, k_ref, v_ref)):
        load_weight(ws_ref.at[b], w_refs, b)
        dst[...] = nt(a, ws_ref[b]).astype(bf16)
    load_weight(ws_ref.at[3], w_refs, 3)
    scale = HD ** (-0.5)
    keep_rows = (true_head(iota((n, 1), 0), scal[0]) < scal[2]).astype(f32)
    keep_ref[...] = mask_ref[...].astype(f32) * keep_rows

    def group(y, _):
        rows = pl.ds(pl.multiple_of(y * PITCH, PITCH), PITCH)
        mask = mask_ref[...]
        qx = jnp.concatenate([q_ref[rows, :]] * heads, axis=0) * mask
        s = (nt(k_ref[...], qx) * scale).astype(bf16)
        s_ref[y] = s
        t = nn(s, kron_ref[0]) + nn(s, kron_ref[1])
        t = t + bias_ref[...]
        e = jnp.exp(t - jnp.max(t, axis=0, keepdims=True))
        p = e * (1.0 / jnp.sum(e, axis=0, keepdims=True))
        p_ref[y] = p
        ph, plo = split2(p)
        r = nt(kron_ref[2], ph).astype(bf16)
        o = nn(r, v_ref[...]) * keep_ref[...]
        o_ref[rows, :] = jnp.sum(o.reshape(heads, PITCH, 256), axis=0).astype(bf16)
        return 0

    lax.fori_loop(0, SIDE, group, 0, unroll=unroll)
    mid_ref[...] = x_ref[...] + nn(o_ref[...], ws_ref[3])


def ln_stats(v):
    centred = v - jnp.mean(v, axis=-1, keepdims=True)
    inv = lax.rsqrt(jnp.mean(centred * centred, axis=-1, keepdims=True) + norm_eps)
    return centred * inv, inv


def ln_back(grad, scaled, inv, gain):
    gs = grad * gain
    return inv * (
        gs - jnp.mean(gs, axis=-1, keepdims=True) - scaled * jnp.mean(gs * scaled, axis=-1, keepdims=True)
    )


def place(rows=216):
    shape = (rows, 256)
    lane = iota(shape, 1)
    rest = lane & 63
    return ((iota(shape, 0) == (lane >> 6) * 54 + rest) & (rest < 54)).astype(bf16)


def ffn_kernel(
    scal, mid_ref, dy_ref, norm_ref, *refs, parts
):
    w_refs, refs = refs[:parts], refs[parts:]
    out_ref, dmid_ref, gn_ref = refs[:3]
    gw_refs, refs = refs[3 : 3 + parts], refs[3 + parts :]
    win_ref, wdn_ref, h_ref, d_ref, gate_ref, dh_ref, cv_ref, gcv_ref, tmp_ref = refs
    hd = parts
    lanes = hd * 256
    win_ref[...] = jnp.zeros_like(win_ref)
    wdn_ref[...] = jnp.zeros_like(wdn_ref)
    pm = place()
    for h in range(hd):
        for j in range(4):
            at = 256 * h + 64 * j
            win_ref[at : at + 54, :] = w_refs[h][j]
            wdn_ref[at : at + 54, :] = w_refs[h][4 + j]
        both = nn(w_refs[h][8], pm)
        cv_ref[:, 256 * h : 256 * (h + 1)] = both[0:9] + both[16:25]
    mid = mid_ref[...]
    z, inv = ln_stats(mid)
    rows = real_rows(mid.shape)
    w = jnp.where(rows, z * norm_ref[2:3, :] + norm_ref[3:4, :], 0.0).astype(bf16)
    dy = dy_ref[...]
    e = dy.astype(bf16)
    tokens = mid.shape[0]
    pad = MARGIN
    zero = jnp.zeros((pad, lanes), f32)
    h_ref[0:pad, :] = zero
    h_ref[pad + tokens :, :] = zero
    d_ref[0:pad, :] = zero
    d_ref[pad + tokens :, :] = zero
    h_ref[pad : pad + tokens, :] = nt(w, win_ref[...])
    d_ref[pad : pad + tokens, :] = nt(e, wdn_ref[...])
    lane = iota((1, 128), 1)
    rmask = real_rows((tokens, 128))
    for c in range(lanes // 128):
        cols = slice(128 * c, 128 * (c + 1))
        glane = lane + 128 * c
        rest = glane & 63
        unit = (((glane >> 8) ^ scal[0]) * 4 + ((glane >> 6) & 3)) * 54 + rest
        keep = ((rest < 54) & (unit < scal[3])).astype(f32)
        act = jnp.zeros((tokens, 128), f32)
        for t in range(9):
            off = PITCH * (t // 3 - 1) + t % 3 - 1
            act = act + cv_ref[t : t + 1, cols] * h_ref[pad + off : pad + off + tokens, cols]
        sig = 1.0 / (1.0 + jnp.exp(-act))
        gate_ref[:, cols] = (act * sig * keep).astype(bf16)
        dact = d_ref[pad : pad + tokens, cols] * keep * sig * (1.0 + act * (1.0 - sig))
        d_ref[pad : pad + tokens, cols] = dact
        dh = jnp.zeros((tokens, 128), f32)
        for t in range(9):
            off = PITCH * (t // 3 - 1) + t % 3 - 1
            gcv_ref[t : t + 1, cols] = jnp.sum(
                dact * h_ref[pad + off : pad + off + tokens, cols], axis=0, keepdims=True
            )
            dh = dh + cv_ref[t : t + 1, cols] * d_ref[pad - off : pad - off + tokens, cols]
        dh_ref[:, cols] = jnp.where(rmask, dh, 0.0).astype(bf16)
    valid = (scal[0] < scal[1]).astype(f32)
    down = nn(gate_ref[...], wdn_ref[...])
    tmp_ref[...] = (mid + down) * valid
    for y in range(SIDE):
        out_ref[SIDE * y : SIDE * (y + 1), :] = tmp_ref[PITCH * y : PITCH * y + SIDE, :].astype(bf16)
    dw = nn(dh_ref[...], win_ref[...])
    gn_ref[...] = jnp.zeros_like(gn_ref)
    gn_ref[0:1, :] = jnp.sum(dw * z, axis=0, keepdims=True)
    gn_ref[1:2, :] = jnp.sum(dw, axis=0, keepdims=True)
    dmid_ref[...] = dy + ln_back(dw, z, inv, norm_ref[2:3, :])
    for h in range(hd):
        cols = slice(256 * h, 256 * (h + 1))
        gi = tn(dh_ref[:, cols], w).astype(bf16)
        gd = tn(gate_ref[:, cols], e).astype(bf16)
        for j in range(4):
            gw_refs[h][j] = gi[64 * j : 64 * j + 54]
            gw_refs[h][4 + j] = gd[64 * j : 64 * j + 54]
        hi, lo = split2(gcv_ref[:, cols])
        gw_refs[h][8] = jnp.zeros_like(gw_refs[h][8])
        gw_refs[h][8, 0:9] = nt(hi, pm).astype(bf16)
        gw_refs[h][8, 16:25] = nt(lo, pm).astype(bf16)


def scores_back_kernel(
    scal, dmid_ref, kron_ref, mask_ref, q_ref, k_ref, v_ref, s_ref, p_ref, *refs, parts, unroll
):
    w_refs, refs = refs[:parts], refs[parts:]
    gq_ref, gkb_ref, gvb_ref, mix_ref, wo_ref, do_ref, gk_ref, gv_ref, g0_ref, g1_ref, fm_ref = refs
    heads = kron_ref.shape[1] // PITCH
    n = heads * PITCH
    scale = HD ** (-0.5)
    wo_ref[...] = jnp.zeros_like(wo_ref)
    load_weight(wo_ref, w_refs, 3)
    f = dmid_ref[...].astype(bf16)
    lane = iota((1, 256), 1)
    rest = lane & 63
    lane_head = ((lane >> 6) ^ scal[0]) * 3 + (rest >= 18).astype(jnp.int32) + (rest >= 36).astype(jnp.int32)
    lane_keep = ((lane_head < scal[2]) & (rest < 54)).astype(f32)
    do_ref[...] = (nt(f, wo_ref[...]) * lane_keep).astype(bf16)
    g0_ref[...] = jnp.zeros_like(g0_ref)
    g1_ref[...] = jnp.zeros_like(g1_ref)
    gk_ref[...] = jnp.zeros_like(gk_ref)
    gv_ref[...] = jnp.zeros_like(gv_ref)
    fm_ref[...] = mask_ref[...].astype(f32)

    def group(y, _):
        rows = pl.ds(pl.multiple_of(y * PITCH, PITCH), PITCH)
        mask = mask_ref[...]
        qx = jnp.concatenate([q_ref[rows, :]] * heads, axis=0) * mask
        dx = jnp.concatenate([do_ref[rows, :]] * heads, axis=0) * mask
        v = v_ref[...]
        k = k_ref[...]
        p = p_ref[y]
        ph = p.astype(bf16)
        dr = nt(dx, v).astype(bf16)
        drt = nt(v, dx).astype(bf16)
        dp = nn(drt, kron_ref[2])
        dt = p * (dp - jnp.sum(dp * p, axis=0, keepdims=True))
        dth = dt.astype(bf16)
        g1_ref[...] += nn(dr, ph)
        srow = (nt(qx, k) * scale).astype(bf16)
        g0_ref[...] += nn(srow, dth)
        dst = nt(dth, kron_ref[0]).astype(bf16)
        dsr = nt(kron_ref[0], dth).astype(bf16)
        gk_ref[...] += nn(dst, qx)
        gq = nn(dsr, k) * fm_ref[...]
        gq_ref[rows, :] = (jnp.sum(gq.reshape(heads, PITCH, 256), axis=0) * scale).astype(bf16)
        rt = nt(ph, kron_ref[2]).astype(bf16)
        gv_ref[...] += nn(rt, dx)
        return 0

    lax.fori_loop(0, SIDE, group, 0, unroll=unroll)
    gkb_ref[...] = (gk_ref[...] * scale).astype(bf16)
    gvb_ref[...] = gv_ref[...].astype(bf16)
    same = (iota((n, n), 0) & (PITCH - 1)) == (iota((n, n), 1) & (PITCH - 1))
    ex = (true_head(iota((n, heads), 0), scal[0]) == iota((n, heads), 1)).astype(bf16)
    for i, ref in enumerate((g0_ref, g1_ref)):
        g = jnp.where(same, ref[...], 0.0)
        hi, lo = split2(g)
        cols = nn(hi, ex) + nn(lo, ex)
        hi, lo = split2(cols)
        if i == 0:
            mix_ref[i] = tn(hi, ex) + tn(lo, ex)
        else:
            mix_ref[i] = tn(ex, hi) + tn(ex, lo)


def weights_back_kernel(
    scal, x_ref, a_ref, dmid_ref, norm_ref, gn2_ref, o_ref, gq_ref, gk_ref, gv_ref, mix_ref, *refs, parts
):
    w_refs, refs = refs[:parts], refs[parts:]
    tg_ref, gw_refs, refs = refs[0], refs[1 : 1 + parts], refs[1 + parts :]
    ws_ref, tmp_ref, small_ref = refs
    heads = mix_ref.shape[1]
    ws_ref[...] = jnp.zeros_like(ws_ref)
    for b in range(3):
        load_weight(ws_ref.at[b], w_refs, b)
    gq, gk, gv = gq_ref[...], gk_ref[...], gv_ref[...]
    a = a_ref[...]
    f = dmid_ref[...].astype(bf16)
    for b, (g, t) in enumerate(((gq, a), (gk, a), (gv, a), (o_ref[...], f))):
        gw = tn(g, t).astype(bf16)
        for h in range(parts):
            gw_refs[h][b] = gw[64 * h : 64 * h + 54]
    da = nn(gq, ws_ref[0]) + nn(gk, ws_ref[1]) + nn(gv, ws_ref[2])
    z, inv = ln_stats(x_ref[...])
    small_ref[...] = jnp.zeros_like(small_ref)
    small_ref[0:1, :] = jnp.sum(da * z, axis=0, keepdims=True)
    small_ref[1:2, :] = jnp.sum(da, axis=0, keepdims=True)
    small_ref[2:4, :] = gn2_ref[0:2, :]
    for i in range(2):
        small_ref[8 : 8 + heads, 128 * i : 128 * i + heads] = mix_ref[i]
    tmp_ref[...] = dmid_ref[...] + ln_back(da, z, inv, norm_ref[0:1, :])
    for y in range(SIDE):
        tg_ref[SIDE * y : SIDE * (y + 1), :] = tmp_ref[PITCH * y : PITCH * y + SIDE, :].astype(bf16)
    hi, lo = split2(small_ref[...])
    for h in range(parts):
        gw_refs[h][4, 0:24] = hi
        gw_refs[h][4, 24:48] = lo
        gw_refs[h][4, 48:54] = jnp.zeros((6, hi.shape[1]), bf16)


def cast_kernel(m_ref, out_ref):
    low = m_ref[...].astype(bf16)
    for i in range(out_ref.shape[0]):
        out_ref[i] = low


def select_kernel(slot_ref, every_ref, conv_ref, attn_ref, ffn_ref):
    per = every_ref.shape[1]
    for b in range(12):
        slot = slot_ref[b]
        block = every_ref[slot // per, slot % per]
        if b < 4:
            attn_ref[b] = block
        else:
            ffn_ref[b - 4] = block
    hi, lo = split2(conv_ref[...])
    ffn_ref[8] = jnp.zeros_like(ffn_ref[8])
    ffn_ref[8, 0:9] = hi
    ffn_ref[8, 16:25] = lo


def total(refs, at):
    acc = refs[0][at].astype(f32)
    for ref in refs[1:]:
        acc = acc + ref[at].astype(f32)
    return acc


WIDE = 40
SMALL = 13


def spread_kernel(slot_ref, *refs, parts):
    attn, ffn_refs, out_ref, acc_ref, sm_ref = refs[:parts], refs[parts : 2 * parts], *refs[2 * parts :]
    ranks, per = out_ref.shape[:2]
    dim = attn[0].shape[2]
    for i in range(ranks * per):
        acc_ref[i] = jnp.zeros_like(acc_ref[i])
    for b in range(12):
        block = total(attn, b) if b < 4 else total(ffn_refs, b - 4)
        acc_ref[slot_ref[b], :, 0:dim] = block.astype(bf16)
    norm = total(attn, 4)
    norm = norm[0:24] + norm[24:48]
    conv = total(ffn_refs, 8)
    conv = conv[0:9] + conv[16:25]
    sm_ref[...] = jnp.zeros_like(sm_ref)
    flat_ref = sm_ref.at[per]
    flat_ref[0:4, 0:dim] = norm[0:4]
    flat_ref[4:SMALL, 0:dim] = conv
    flat = flat_ref[0:16, :]
    for j in range(6):
        at = SMALL * (j if j < 4 else j - 4)
        moved = pltpu.roll(flat, (dim - WIDE * j) % 256, 1)
        sm_ref[j // 4, at : at + SMALL, :] = moved[0:SMALL]
    mix = norm[8:20]
    heads = mix.shape[0]
    flat_ref[16:28, 0:128] = mix[:, 0:128]
    flat_ref[16:28, 128:dim] = mix[:, 128:dim]
    mix = flat_ref[16:28, :]
    lane = iota(mix.shape, 1)
    mix = jnp.where(lane < heads, mix, 0.0) + pltpu.roll(jnp.where(lane >= 128, mix, 0.0), 128 + heads, 1)
    sm_ref[1, 2 * SMALL : 2 * SMALL + heads, :] = pltpu.roll(mix, dim, 1)
    free = iota((acc_ref.shape[1], 256), 1) >= dim
    small = [jnp.where(free, sm_ref[i, 0 : acc_ref.shape[1], :], 0.0).astype(bf16) for i in range(per)]
    for r in range(ranks):
        for i in range(per):
            out_ref[r, i] = acc_ref[r * per + i] + small[i]


def adam(w, g, one, two, rate, decay):
    one_new = 0.5 * one + 0.5 * g
    two_new = 0.5 * two + 0.5 * g * g
    hat_one = one_new / (1.0 - 0.5**3)
    hat_two = two_new / (1.0 - 0.5**3)
    return w - rate * (hat_one / (jnp.sqrt(hat_two) + 1e-08) + decay * w), one_new, two_new


def update_kernel(got_ref, *refs):
    ins, outs, (g_ref, sm_ref, flat_ref) = refs[0:12], refs[12:25], refs[25:]
    ranks, per = got_ref.shape[:2]
    dim = ins[0].shape[2]
    rows = got_ref.shape[2]
    for i in range(per):
        g = got_ref[0, i].astype(f32)
        for r in range(1, ranks):
            g = g + got_ref[r, i].astype(f32)
        g_ref[:, i, :] = g[:, 0:dim]
        sm_ref[i, 0:rows, :] = g
    w, one, two = adam(ins[0][...], g_ref[...], ins[1][...], ins[2][...], 0.06, 0.05)
    outs[0][...], outs[1][...], outs[2][...], outs[3][...] = w, one, two, w.astype(bf16)
    flat = jnp.zeros((SMALL, 256), f32)
    lane = iota(flat.shape, 1)
    for j in range(6):
        at = SMALL * (j if j < 4 else j - 4)
        moved = pltpu.roll(sm_ref[j // 4, at : at + SMALL, :], (WIDE * j - dim) % 256, 1)
        flat = flat + jnp.where((lane >= WIDE * j) & (lane < WIDE * (j + 1)), moved, 0.0)
    flat_ref[0:SMALL, :] = flat
    heads = ins[6].shape[0]
    mix = pltpu.roll(sm_ref[1, 2 * SMALL : 2 * SMALL + heads, :], 256 - dim, 1)
    flat_ref[16 : 16 + heads, :] = mix
    flat_ref[32 : 32 + heads, :] = pltpu.roll(mix, 256 - heads, 1)
    outs[4][...], outs[5][...], outs[6][...] = adam(
        ins[3][...], flat_ref[0:4, 0:dim], ins[4][...], ins[5][...], 0.2, 0.0
    )
    for i in range(2):
        w, one, two = adam(
            ins[6][:, i, :], flat_ref[16 * (i + 1) : 16 * (i + 1) + heads, 0:heads], ins[7][:, i, :], ins[8][:, i, :],
            0.2, 0.0,
        )
        outs[7][:, i, :], outs[8][:, i, :], outs[9][:, i, :] = w, one, two
    outs[10][...], outs[11][...], outs[12][...] = adam(
        ins[9][...], flat_ref[4:SMALL, 0:dim], ins[10][...], ins[11][...], 0.2, 0.05
    )


def assemble_kernel(scal, *refs, parts):
    for i, out_ref in enumerate(refs[2 * parts :]):
        for k in range(parts):
            out_ref[scal[0] ^ k] = refs[parts * i + k][...].astype(f32)


VM = pl.BlockSpec(memory_space=pltpu.VMEM)
SM = pl.BlockSpec(memory_space=pltpu.SMEM)
SDS = jax.ShapeDtypeStruct


def call(body, name, n_scalar, n_in, out_shape, scratch=(), mb=16, micros=1, **kw):
    return pl.pallas_call(
        functools.partial(body, **kw) if kw else body,
        in_specs=[SM] * n_scalar + [VM] * n_in,
        out_specs=[VM] * len(out_shape),
        out_shape=out_shape,
        scratch_shapes=scratch,
        compiler_params=pltpu.CompilerParams(vmem_limit_bytes=mb << 20),
        cost_estimate=pl.CostEstimate(flops=micros * 1000000000, transcendentals=0, bytes_accessed=micros * 3000000),
        name=name,
    )


def prep(scal, tokens, cotangent, norm_params, talk):
    tok, dim = tokens.shape[1], tokens.shape[2]
    pad = SIDE * PITCH
    heads = talk.shape[1]
    n = heads * PITCH
    full = lambda *s: pl.BlockSpec(s, lambda i, sc: (0,) * len(s))
    return pl.pallas_call(
        prep_kernel,
        grid_spec=pltpu.PrefetchScalarGridSpec(
            num_scalar_prefetch=1,
            grid=(1,),
            in_specs=[
                pl.BlockSpec((1, tok, dim), lambda i, sc: (sc[0], 0, 0)),
                pl.BlockSpec((1, tok, dim), lambda i, sc: (sc[0], 0, 0)),
                full(*norm_params.shape),
                full(*talk.shape),
            ],
            out_specs=[full(pad, dim), full(pad, dim), full(pad, dim), full(4, n, n), full(n, 256), full(pad, n)],
            scratch_shapes=[pltpu.VMEM((tok, dim), f32)],
        ),
        out_shape=[SDS((pad, dim), f32), SDS((pad, dim), bf16), SDS((pad, dim), f32), SDS((4, n, n), bf16),
                   SDS((n, 256), bf16), SDS((pad, n), f32)],
        compiler_params=pltpu.CompilerParams(vmem_limit_bytes=16 << 20),
        cost_estimate=pl.CostEstimate(flops=1000000000, transcendentals=0, bytes_accessed=3000000),
        name="prep",
    )(scal, tokens, cotangent, norm_params, talk)


def attn_fwd(scal, x, a, kron, mask, bias, w, unroll=7):
    pad, dim = x.shape
    n = kron.shape[1]
    return call(
        attn_fwd_kernel, "attn_fwd", 1, 5 + len(w),
        [SDS((pad, dim), f32)] + [SDS((pad, 256), bf16)] * 4 + [SDS((SIDE, pad, n), bf16), SDS((SIDE, pad, n), f32)],
        [pltpu.VMEM((4, 256, dim), bf16), pltpu.VMEM((n, 256), f32)],
        mb=24, micros=10, parts=len(w), unroll=unroll,
    )(scal, x, a, kron, mask, bias, *w)


def ffn(scal, mid, dy, norm_params, w):
    pad, dim = mid.shape
    lanes = len(w) * 256
    return call(
        ffn_kernel, "ffn", 1, 3 + len(w),
        [SDS((SIDE * SIDE, dim), bf16), SDS((pad, dim), f32), SDS((8, dim), f32)] + [SDS((9, 54, dim), bf16)] * len(w),
        [
            pltpu.VMEM((lanes, dim), bf16), pltpu.VMEM((lanes, dim), bf16),
            pltpu.VMEM((pad + 2 * MARGIN, lanes), f32), pltpu.VMEM((pad + 2 * MARGIN, lanes), f32),
            pltpu.VMEM((pad, lanes), bf16), pltpu.VMEM((pad, lanes), bf16),
            pltpu.VMEM((9, lanes), f32), pltpu.VMEM((9, lanes), f32), pltpu.VMEM((pad, dim), f32),
        ],
        mb=24, micros=6, parts=len(w),
    )(scal, mid, dy, norm_params, *w)


def scores_back(scal, dmid, kron, mask, q, k, v, s, p, w, unroll=7):
    pad, dim = dmid.shape
    n = kron.shape[1]
    heads = n // PITCH
    return call(
        scores_back_kernel, "scores_back", 1, 8 + len(w),
        [SDS((pad, 256), bf16)] * 3 + [SDS((2, heads, heads), f32)],
        [
            pltpu.VMEM((256, dim), bf16), pltpu.VMEM((pad, 256), bf16),
            pltpu.VMEM((pad, 256), f32), pltpu.VMEM((pad, 256), f32),
            pltpu.VMEM((n, n), f32), pltpu.VMEM((n, n), f32), pltpu.VMEM((n, 256), f32),
        ],
        mb=24, micros=12, parts=len(w), unroll=unroll,
    )(scal, dmid, kron, mask, q, k, v, s, p, *w)


def weights_back(scal, x, a, dmid, norm_params, gn2, o, gq, gk, gv, mix, w):
    pad, dim = x.shape
    return call(
        weights_back_kernel, "weights_back", 1, 10 + len(w),
        [SDS((SIDE * SIDE, dim), bf16)] + [SDS((5, 54, dim), bf16)] * len(w),
        [pltpu.VMEM((3, 256, dim), bf16), pltpu.VMEM((pad, dim), f32), pltpu.VMEM((24, dim), f32)],
        mb=24, micros=3, parts=len(w),
    )(scal, x, a, dmid, norm_params, gn2, o, gq, gk, gv, mix, *w)


def from_peers(x, axis):
    n = lax.axis_size(axis)
    return [lax.ppermute(x, axis, [(i, i ^ k) for i in range(n)]) for k in range(1, n)]


def exchange(messages, axis):
    n = lax.axis_size(axis)
    return [messages[0]] + [
        lax.ppermute(messages[k], axis, [(i, i ^ k) for i in range(n)]) for k in range(1, n)
    ]


def swap(t):
    return jnp.swapaxes(t, 0, 1)


def whole(*shape):
    return pl.BlockSpec(shape, lambda i: (0,) * len(shape))


def staged(body, name, ins, outs, scratch=(), micros=1):
    return pl.pallas_call(
        body,
        grid=(1,),
        in_specs=[whole(*t.shape) for t in ins],
        out_specs=[whole(*t.shape) for t in outs],
        out_shape=outs,
        scratch_shapes=scratch,
        compiler_params=pltpu.CompilerParams(vmem_limit_bytes=16 << 20),
        cost_estimate=pl.CostEstimate(flops=micros * 1000000000, transcendentals=0, bytes_accessed=micros * 3000000),
        name=name,
    )(*ins)


def local(
    tokens, cotangent, image_count, subnet_heads, subnet_width, block_slot,
    master, master_m1, master_m2, norm_params, norm_m1, norm_m2, talk, talk_m1, talk_m2, conv, conv_m1, conv_m2,
):
    slots, rows, dim = master.shape
    parts = lax.axis_size("head")
    ranks = lax.axis_size("dp")
    place_id = lax.axis_index("head").astype(jnp.int32)
    scal = jnp.concatenate([place_id[None], image_count, subnet_heads, subnet_width])
    (mine,) = staged(cast_kernel, "cast", [swap(master)], [SDS((ranks, rows, slots, dim), bf16)])
    every = lax.all_to_all(jnp.swapaxes(mine, 1, 2), "dp", split_axis=0, concat_axis=0, tiled=True)
    x, a, dy, kron, mask, bias = prep(scal, tokens, cotangent, norm_params, talk)
    attn_w, ffn_w = call(
        select_kernel, "select", 1, 2, [SDS((4, rows, dim), bf16), SDS((9, rows, dim), bf16)]
    )(block_slot, every, conv)
    attn_w = [attn_w] + from_peers(attn_w, "head")
    ffn_w, attn_w[1:] = lax.optimization_barrier((ffn_w, attn_w[1:]))
    ffn_w = [ffn_w] + from_peers(ffn_w, "head")
    mid, q, k, v, o, s, p = attn_fwd(scal, x, a, kron, mask, bias, attn_w)
    out, dmid, gn2, *ffn_g = ffn(scal, mid, dy, norm_params, ffn_w)
    gq, gk, gv, mix = scores_back(scal, dmid, kron, mask, q, k, v, s, p, attn_w)
    ffn_g = exchange(ffn_g, "head")
    outs = [out] + from_peers(out, "head")
    gq, ffn_g[1:], outs[1:] = lax.optimization_barrier((gq, ffn_g[1:], outs[1:]))
    tg, *attn_g = weights_back(scal, x, a, dmid, norm_params, gn2, o, gq, gk, gv, mix, attn_w)
    attn_g = exchange(attn_g, "head")
    tg, attn_g[1:] = lax.optimization_barrier((tg, attn_g[1:]))
    tgs = [tg] + from_peers(tg, "head")
    (message,) = call(
        spread_kernel, "spread", 1, 2 * parts, [SDS((ranks, slots, rows, 256), bf16)],
        [pltpu.VMEM((ranks * slots, rows, 256), bf16), pltpu.VMEM((slots + 1, 64, 256), f32)], parts=parts,
    )(block_slot, *attn_g, *ffn_g)
    got = lax.all_to_all(message, "dp", split_axis=0, concat_axis=0, tiled=True)
    images = SDS((parts,) + tokens.shape[1:], f32)
    output, token_grad = call(assemble_kernel, "assemble", 1, 2 * parts, [images, images], parts=parts)(
        scal, *outs, *tgs
    )
    state = [
        swap(master), swap(master_m1), swap(master_m2), norm_params, norm_m1, norm_m2,
        swap(talk), swap(talk_m1), swap(talk_m2), conv, conv_m1, conv_m2,
    ]
    shapes = [SDS(t.shape, f32) for t in state]
    shapes.insert(3, SDS(state[0].shape, bf16))
    new = staged(
        update_kernel, "update", [got, *state], shapes,
        [pltpu.VMEM((rows, slots, dim), f32), pltpu.VMEM((slots, 64, 256), f32), pltpu.VMEM((48, 256), f32)],
    )
    new = [swap(t) if t.ndim == 3 else t for t in new]
    return (output, token_grad, *new)


def solution(mesh):
    in_specs = (
        P("dp", None, None),
        P("dp", None, None),
        P("dp"),
        P(),
        P(),
        P(),
        P("dp", None, "head"),
        P("dp", None, "head"),
        P("dp", None, "head"),
        P(),
        P(),
        P(),
        P(),
        P(),
        P(),
        P(None, "head"),
        P(None, "head"),
        P(None, "head"),
    )
    out_specs = (
        P("dp", None, None),
        P("dp", None, None),
        P("dp", None, "head"),
        P("dp", None, "head"),
        P("dp", None, "head"),
        P("dp", None, "head"),
        P(),
        P(),
        P(),
        P(),
        P(),
        P(),
        P(None, "head"),
        P(None, "head"),
        P(None, "head"),
    )
    return jax.shard_map(local, mesh=mesh, in_specs=in_specs, out_specs=out_specs, check_vma=False)
```

```python
import functools
import jax
import jax.numpy as jnp
from jax import lax
from jax.experimental import pallas as pl
from jax.experimental.pallas import tpu as pltpu
from jax.sharding import PartitionSpec as P

HD = 18
SIDE = 14
PITCH = 16
MARGIN = 24
FREE = 216
WIDE = 40
norm_eps = 1e-05
bf16 = jnp.bfloat16
f32 = jnp.float32


def nn(a, b):
    return lax.dot_general(a, b, (((1,), (0,)), ((), ())), preferred_element_type=f32)


def nt(a, b):
    return lax.dot_general(a, b, (((1,), (1,)), ((), ())), preferred_element_type=f32)


def tn(a, b):
    return lax.dot_general(a, b, (((0,), (0,)), ((), ())), preferred_element_type=f32)


def iota(shape, dim):
    return lax.broadcasted_iota(jnp.int32, shape, dim)


def split2(v):
    hi = v.astype(bf16)
    return hi, (v - hi.astype(f32)).astype(bf16)


def real_rows(shape):
    return (iota(shape, 0) & (PITCH - 1)) < SIDE


def lane_head(shape, dim, place):
    lane = iota(shape, dim)
    rest = lane & 63
    head = ((lane >> 6) ^ place) * 3 + (rest >= 18).astype(jnp.int32) + (rest >= 36).astype(jnp.int32)
    return jnp.where(rest < 54, head, -1)


def true_head(rows, place):
    return ((rows // (3 * PITCH)) ^ place) * 3 + (rows // PITCH) % 3


def prep_kernel(scal, tok_ref, cot_ref, norm_ref, talk_ref, x_ref, a_ref, dy_ref, mix_ref, bias_ref, tmp_ref):
    x_ref[...] = jnp.zeros_like(x_ref)
    dy_ref[...] = jnp.zeros_like(dy_ref)
    valid = (scal[0] < scal[1]).astype(f32)
    tmp_ref[...] = tok_ref[0].astype(f32)
    for y in range(SIDE):
        x_ref[PITCH * y : PITCH * y + SIDE, :] = tmp_ref[SIDE * y : SIDE * (y + 1), :]
        dy_ref[PITCH * y : PITCH * y + SIDE, :] = cot_ref[0, SIDE * y : SIDE * (y + 1), :] * valid
    x = x_ref[...]
    centred = x - jnp.mean(x, axis=-1, keepdims=True)
    inv = lax.rsqrt(jnp.mean(centred * centred, axis=-1, keepdims=True) + norm_eps)
    a = centred * inv * norm_ref[0:1, :] + norm_ref[1:2, :]
    a_ref[...] = jnp.where(real_rows(a.shape), a, 0.0).astype(bf16)
    heads = talk_ref.shape[1]
    n = heads * PITCH
    ex = (true_head(iota((n, heads), 0), scal[0]) == iota((n, heads), 1)).astype(bf16)
    el = (lane_head((256, heads), 0, scal[0]) == iota((256, heads), 1)).astype(bf16)
    for i in range(2):
        both = []
        for part in split2(talk_ref[i]):
            if i == 0:
                both.append(nt(nn(ex, part).astype(bf16), el))
            else:
                both.append(nt(nt(ex, part).astype(bf16), el))
        mix_ref[i] = (both[0] + both[1]) * (HD**-0.5 if i == 0 else 1.0)
    bias_ref[...] = jnp.where(real_rows(bias_ref.shape), 0.0, -1e30)


def load_weight(dst_ref, w_refs, b):
    for k, w_ref in enumerate(w_refs):
        dst_ref[64 * k : 64 * k + 54, :] = w_ref[b]


def tiled(rows, heads):
    return jnp.concatenate([rows] * heads, axis=0)


def over_heads(rows, heads):
    return jnp.sum(rows.reshape(heads, PITCH, rows.shape[1]), axis=0)


def attn_fwd_kernel(scal, x_ref, a_ref, mix_ref, bias_ref, *refs, parts, unroll):
    w_refs, refs = refs[:parts], refs[parts:]
    mid_ref, q_ref, k_ref, v_ref, o_ref, qw_ref, p_ref, pv_ref, ws_ref = refs
    heads = mix_ref.shape[1] // PITCH
    a = a_ref[...]
    ws_ref[...] = jnp.zeros_like(ws_ref)
    for b, dst in enumerate((q_ref, k_ref, v_ref)):
        load_weight(ws_ref.at[b], w_refs, b)
        dst[...] = nt(a, ws_ref[b]).astype(bf16)
    load_weight(ws_ref.at[3], w_refs, 3)
    head = lane_head((1, 256), 1, scal[0])
    keep = ((head >= 0) & (head < scal[2])).astype(f32)

    def group(y, _):
        rows = pl.ds(pl.multiple_of(y * PITCH, PITCH), PITCH)
        qw = (tiled(q_ref[rows, :].astype(f32), heads) * mix_ref[0]).astype(bf16)
        qw_ref[y] = qw
        t = nt(k_ref[...], qw) + bias_ref[...]
        e = jnp.exp(t - jnp.max(t, axis=0, keepdims=True))
        p = (e * (1.0 / jnp.sum(e, axis=0, keepdims=True))).astype(bf16)
        p_ref[y] = p
        pv = tn(p, v_ref[...])
        pv_ref[y] = pv.astype(bf16)
        o_ref[rows, :] = (over_heads(pv * mix_ref[1], heads) * keep).astype(bf16)
        return 0

    lax.fori_loop(0, SIDE, group, 0, unroll=unroll)
    mid_ref[...] = x_ref[...] + nn(o_ref[...], ws_ref[3])


def ln_stats(v):
    centred = v - jnp.mean(v, axis=-1, keepdims=True)
    inv = lax.rsqrt(jnp.mean(centred * centred, axis=-1, keepdims=True) + norm_eps)
    return centred * inv, inv


def ln_back(grad, scaled, inv, gain):
    gs = grad * gain
    return inv * (
        gs - jnp.mean(gs, axis=-1, keepdims=True) - scaled * jnp.mean(gs * scaled, axis=-1, keepdims=True)
    )


def in_free_lanes(flat, dst_ref, first_row):
    rows = flat.shape[0]
    for j in range(6):
        dst_ref[first_row + rows * j : first_row + rows * (j + 1), :] = pltpu.roll(flat, (FREE - WIDE * j) % 256, 1)


def from_free_lanes(src_ref, first_row, rows):
    lane = iota((rows, 256), 1)
    flat = jnp.zeros((rows, 256), f32)
    for j in range(6):
        moved = pltpu.roll(src_ref[first_row + rows * j : first_row + rows * (j + 1), :], (WIDE * j - FREE) % 256, 1)
        flat = flat + jnp.where((lane >= WIDE * j) & (lane < WIDE * (j + 1)), moved, 0.0)
    return flat


def place(rows=216):
    shape = (rows, 256)
    lane = iota(shape, 1)
    rest = lane & 63
    return ((iota(shape, 0) == (lane >> 6) * 54 + rest) & (rest < 54)).astype(bf16)


def ffn_kernel(
    scal, mid_ref, dy_ref, norm_ref, o_ref, *refs, parts
):
    w_refs, refs = refs[:parts], refs[parts:]
    out_ref, dmid_ref, gn_ref = refs[:3]
    gw_refs, refs = refs[3 : 3 + parts], refs[3 + parts :]
    win_ref, wdn_ref, h_ref, d_ref, gate_ref, dh_ref, cv_ref, gcv_ref, tmp_ref, sm_ref = refs
    hd = parts
    lanes = hd * 256
    win_ref[...] = jnp.zeros_like(win_ref)
    wdn_ref[...] = jnp.zeros_like(wdn_ref)
    pm = place()
    for h in range(hd):
        for j in range(4):
            at = 256 * h + 64 * j
            win_ref[at : at + 54, :] = w_refs[h][j]
            wdn_ref[at : at + 54, :] = w_refs[h][4 + j]
        both = nn(w_refs[h][8], pm)
        cv_ref[:, 256 * h : 256 * (h + 1)] = both[0:9] + both[16:25]
    mid = mid_ref[...]
    z, inv = ln_stats(mid)
    rows = real_rows(mid.shape)
    w = jnp.where(rows, z * norm_ref[2:3, :] + norm_ref[3:4, :], 0.0).astype(bf16)
    dy = dy_ref[...]
    e = dy.astype(bf16)
    tokens = mid.shape[0]
    pad = MARGIN
    zero = jnp.zeros((pad, lanes), f32)
    h_ref[0:pad, :] = zero
    h_ref[pad + tokens :, :] = zero
    d_ref[0:pad, :] = zero
    d_ref[pad + tokens :, :] = zero
    h_ref[pad : pad + tokens, :] = nt(w, win_ref[...])
    d_ref[pad : pad + tokens, :] = nt(e, wdn_ref[...])
    lane = iota((1, 128), 1)
    rmask = real_rows((tokens, 128))
    for c in range(lanes // 128):
        cols = slice(128 * c, 128 * (c + 1))
        glane = lane + 128 * c
        rest = glane & 63
        unit = (((glane >> 8) ^ scal[0]) * 4 + ((glane >> 6) & 3)) * 54 + rest
        keep = ((rest < 54) & (unit < scal[3])).astype(f32)
        act = jnp.zeros((tokens, 128), f32)
        for t in range(9):
            off = PITCH * (t // 3 - 1) + t % 3 - 1
            act = act + cv_ref[t : t + 1, cols] * h_ref[pad + off : pad + off + tokens, cols]
        sig = 1.0 / (1.0 + jnp.exp(-act))
        gate_ref[:, cols] = (act * sig * keep).astype(bf16)
        dact = d_ref[pad : pad + tokens, cols] * keep * sig * (1.0 + act * (1.0 - sig))
        d_ref[pad : pad + tokens, cols] = dact
        dh = jnp.zeros((tokens, 128), f32)
        for t in range(9):
            off = PITCH * (t // 3 - 1) + t % 3 - 1
            gcv_ref[t : t + 1, cols] = jnp.sum(
                dact * h_ref[pad + off : pad + off + tokens, cols], axis=0, keepdims=True
            )
            dh = dh + cv_ref[t : t + 1, cols] * d_ref[pad - off : pad - off + tokens, cols]
        dh_ref[:, cols] = jnp.where(rmask, dh, 0.0).astype(bf16)
    valid = (scal[0] < scal[1]).astype(f32)
    down = nn(gate_ref[...], wdn_ref[...])
    tmp_ref[...] = (mid + down) * valid
    for y in range(SIDE):
        out_ref[SIDE * y : SIDE * (y + 1), :] = tmp_ref[PITCH * y : PITCH * y + SIDE, :].astype(bf16)
    dw = nn(dh_ref[...], win_ref[...])
    gn_ref[...] = jnp.zeros_like(gn_ref)
    gn_ref[0:1, :] = jnp.sum(dw * z, axis=0, keepdims=True)
    gn_ref[1:2, :] = jnp.sum(dw, axis=0, keepdims=True)
    dmid = dy + ln_back(dw, z, inv, norm_ref[2:3, :])
    dmid_ref[...] = dmid
    go = tn(o_ref[...], dmid.astype(bf16)).astype(bf16)
    dim = mid.shape[1]
    free = iota((54, 256), 1) >= FREE
    pm = place(256)
    for h in range(hd):
        cols = slice(256 * h, 256 * (h + 1))
        gi = tn(dh_ref[:, cols], w).astype(bf16)
        gd = tn(gate_ref[:, cols], e).astype(bf16)
        for j in range(4):
            gw_refs[h][1 + j, :, 0:dim] = gi[64 * j : 64 * j + 54]
            gw_refs[h][5 + j, :, 0:dim] = gd[64 * j : 64 * j + 54]
        in_free_lanes(nt(gcv_ref[:, cols].astype(bf16), pm), sm_ref, 0)
        gw_refs[h][0] = jnp.where(free, sm_ref[0:54, :], 0.0).astype(bf16)
        gw_refs[h][0, :, 0:dim] = go[64 * h : 64 * h + 54]


def scores_back_kernel(
    scal, dmid_ref, mix_ref, q_ref, k_ref, v_ref, qw_ref, p_ref, pv_ref, *refs, parts, unroll, part
):
    heads = mix_ref.shape[1] // PITCH
    n = heads * PITCH
    if part == 0:
        w_refs, refs = refs[:parts], refs[parts:]
        do_ref, gq_ref, gk_ref, gv_ref, g0_ref, g1_ref, wo_ref = refs
        wo_ref[...] = jnp.zeros_like(wo_ref)
        load_weight(wo_ref, w_refs, 3)
        f = dmid_ref[...].astype(bf16)
        head = lane_head((1, 256), 1, scal[0])
        keep = ((head >= 0) & (head < scal[2])).astype(f32)
        do_ref[...] = (nt(f, wo_ref[...]) * keep).astype(bf16)
        for ref in (gk_ref, gv_ref, g0_ref, g1_ref):
            ref[...] = jnp.zeros_like(ref)
    else:
        do_ref, *sums, gq_ref, gkb_ref, gvb_ref, gt_ref, gk_ref, gv_ref, g0_ref, g1_ref = refs
        for ref, old in zip((gk_ref, gv_ref, g0_ref, g1_ref), sums):
            ref[...] = old[...]
    first = SIDE // 2 * part

    def group(y, _):
        out_rows = pl.ds(pl.multiple_of(y * PITCH, PITCH), PITCH)
        y = y + first
        rows = pl.ds(pl.multiple_of(y * PITCH, PITCH), PITCH)
        dot = tiled(do_ref[rows, :].astype(f32), heads)
        dw = (dot * mix_ref[1]).astype(bf16)
        dp = nt(v_ref[...], dw)
        p = p_ref[y]
        pf = p.astype(f32)
        dt = (pf * (dp - jnp.sum(dp * pf, axis=0, keepdims=True))).astype(bf16)
        gv_ref[...] += nn(p, dw)
        gk_ref[...] += nn(dt, qw_ref[y])
        dk = tn(dt, k_ref[...])
        gq_ref[out_rows, :] = over_heads(dk * mix_ref[0], heads).astype(bf16)
        g0_ref[...] += dk * tiled(q_ref[rows, :].astype(f32), heads)
        g1_ref[...] += pv_ref[y].astype(f32) * dot
        return 0

    lax.fori_loop(0, SIDE // 2, group, 0, unroll=unroll)
    if part == 0:
        return
    gkb_ref[...] = gk_ref[...].astype(bf16)
    gvb_ref[...] = gv_ref[...].astype(bf16)
    ex = (true_head(iota((n, heads), 0), scal[0]) == iota((n, heads), 1)).astype(bf16)
    el = (lane_head((256, heads), 0, scal[0]) == iota((256, heads), 1)).astype(bf16)
    for i, ref in enumerate((g0_ref, g1_ref)):
        hi, lo = split2(ref[...])
        hi, lo = split2(nn(hi, el) + nn(lo, el))
        if i == 0:
            gt_ref[i] = (tn(ex, hi) + tn(ex, lo)) * HD**-0.5
        else:
            gt_ref[i] = tn(hi, ex) + tn(lo, ex)


def weights_back_kernel(
    scal, x_ref, a_ref, dmid_ref, norm_ref, gn2_ref, gqa_ref, gqb_ref, gk_ref, gv_ref, gt_ref, *refs, parts
):
    w_refs, refs = refs[:parts], refs[parts:]
    tg_ref, gw_refs, refs = refs[0], refs[1 : 1 + parts], refs[1 + parts :]
    ws_ref, tmp_ref, flat_ref, sm_ref = refs
    heads = gt_ref.shape[1]
    dim = x_ref.shape[1]
    ws_ref[...] = jnp.zeros_like(ws_ref)
    for b in range(3):
        load_weight(ws_ref.at[b], w_refs, b)
    gq = jnp.concatenate([gqa_ref[...], gqb_ref[...]], axis=0)
    gk, gv = gk_ref[...], gv_ref[...]
    a = a_ref[...]
    da = nn(gq, ws_ref[0]) + nn(gk, ws_ref[1]) + nn(gv, ws_ref[2])
    z, inv = ln_stats(x_ref[...])
    flat_ref[...] = jnp.zeros_like(flat_ref)
    flat_ref[0:1, 0:dim] = jnp.sum(da * z, axis=0, keepdims=True)
    flat_ref[1:2, 0:dim] = jnp.sum(da, axis=0, keepdims=True)
    flat_ref[2:4, 0:dim] = gn2_ref[0:2, :]
    for i in range(2):
        flat_ref[8 : 8 + heads, 128 * i : 128 * i + heads] = gt_ref[i]
    sm_ref[...] = jnp.zeros_like(sm_ref)
    in_free_lanes(flat_ref[0:4, :], sm_ref, 0)
    mix = flat_ref[8 : 8 + heads, :]
    first = iota(mix.shape, 1) < 128
    mix = jnp.where(first, mix, 0.0) + pltpu.roll(jnp.where(first, 0.0, mix), 128 + heads, 1)
    sm_ref[24 : 24 + heads, :] = pltpu.roll(mix, FREE, 1)
    small = jnp.where(iota((54, 256), 1) >= FREE, sm_ref[0:54, :], 0.0).astype(bf16)
    for h in range(parts):
        gw_refs[h][0] = small
    for b, g in enumerate((gq, gk, gv)):
        gw = tn(g, a).astype(bf16)
        for h in range(parts):
            gw_refs[h][b, :, 0:dim] = gw[64 * h : 64 * h + 54]
    tmp_ref[...] = dmid_ref[...] + ln_back(da, z, inv, norm_ref[0:1, :])
    for y in range(SIDE):
        tg_ref[SIDE * y : SIDE * (y + 1), :] = tmp_ref[PITCH * y : PITCH * y + SIDE, :].astype(bf16)


def cast_kernel(m_hbm, out_ref, m_ref, sem):
    copy = pltpu.make_async_copy(m_hbm, m_ref, sem)
    copy.start()
    copy.wait()
    low = m_ref[...].astype(bf16)
    for i in range(out_ref.shape[0]):
        out_ref[i] = low


def select_kernel(slot_ref, every_ref, conv_ref, attn_ref, ffn_ref):
    per = every_ref.shape[1]
    for b in range(12):
        slot = slot_ref[b]
        block = every_ref[slot // per, slot % per]
        if b < 4:
            attn_ref[b] = block
        else:
            ffn_ref[b - 4] = block
    hi, lo = split2(conv_ref[...])
    ffn_ref[8] = jnp.zeros_like(ffn_ref[8])
    ffn_ref[8, 0:9] = hi
    ffn_ref[8, 16:25] = lo


def total(refs, at):
    acc = refs[0][at].astype(f32)
    for ref in refs[1:]:
        acc = acc + ref[at].astype(f32)
    return acc


def half_sum_kernel(a_ref, b_ref, out_ref):
    out_ref[...] = (a_ref[...].astype(f32) + b_ref[...].astype(f32)).astype(bf16)


def spread_ffn_kernel(slot_ref, *refs, ranks):
    ffn_refs, out_ref = refs[:-1], refs[-1]
    per = out_ref.shape[0] // ranks
    out_ref[...] = jnp.zeros_like(out_ref)
    for b in range(9):
        block = total(ffn_refs, b)
        out_ref[slot_ref[3 + b], :, 0:FREE] = block[:, 0:FREE].astype(bf16)
        if b == 0:
            wide = block[:, FREE:].astype(bf16)
    for r in range(ranks):
        out_ref[r * per, :, FREE:] = wide


def spread_attn_kernel(slot_ref, old_ref, *refs, ranks):
    attn, out_ref = refs[:-1], refs[-1]
    per = out_ref.shape[0] // ranks
    out_ref[...] = old_ref[...]
    for b in range(3):
        block = total(attn, b)
        out_ref[slot_ref[b], :, 0:FREE] = block[:, 0:FREE].astype(bf16)
        if b == 0:
            wide = block[:, FREE:].astype(bf16)
    for r in range(ranks):
        out_ref[r * per + 1, :, FREE:] = wide


def adam(w, g, one, two, rate, decay):
    one_new = 0.5 * one + 0.5 * g
    two_new = 0.5 * two + 0.5 * g * g
    hat_one = one_new / (1.0 - 0.5**3)
    hat_two = two_new / (1.0 - 0.5**3)
    return w - rate * (hat_one / (jnp.sqrt(hat_two) + 1e-08) + decay * w), one_new, two_new


def update_kernel(got_ref, *refs, ranks):
    ins, outs, (g_ref, sm_ref, flat_ref) = refs[0:12], refs[12:25], refs[25:]
    per = got_ref.shape[0] // ranks
    dim = ins[0].shape[2]
    rows = got_ref.shape[1]
    for i in range(per):
        g = got_ref[i].astype(f32)
        for r in range(1, ranks):
            g = g + got_ref[r * per + i].astype(f32)
        g_ref[:, i, :] = g[:, 0:dim]
        sm_ref[i, 0:rows, :] = g
    w, one, two = adam(ins[0][...], g_ref[...], ins[1][...], ins[2][...], 0.06, 0.05)
    outs[0][...], outs[1][...], outs[2][...], outs[3][...] = w, one, two, w.astype(bf16)
    heads = ins[6].shape[0]
    flat_ref[0:9, :] = from_free_lanes(sm_ref.at[0], 0, 9)
    flat_ref[16:20, :] = from_free_lanes(sm_ref.at[1], 0, 4)
    mix = pltpu.roll(sm_ref[1, 24 : 24 + heads, :], 256 - FREE, 1)
    flat_ref[32 : 32 + heads, :] = mix
    flat_ref[48 : 48 + heads, :] = pltpu.roll(mix, 256 - heads, 1)
    outs[4][...], outs[5][...], outs[6][...] = adam(
        ins[3][...], flat_ref[16:20, 0:dim], ins[4][...], ins[5][...], 0.2, 0.0
    )
    for i in range(2):
        w, one, two = adam(
            ins[6][:, i, :], flat_ref[16 * (i + 2) : 16 * (i + 2) + heads, 0:heads], ins[7][:, i, :], ins[8][:, i, :],
            0.2, 0.0,
        )
        outs[7][:, i, :], outs[8][:, i, :], outs[9][:, i, :] = w, one, two
    outs[10][...], outs[11][...], outs[12][...] = adam(
        ins[9][...], flat_ref[0:9, 0:dim], ins[10][...], ins[11][...], 0.2, 0.05
    )


def assemble_kernel(scal, *refs):
    for k, ref in enumerate(refs[:-1]):
        refs[-1][scal[0] ^ k] = ref[...].astype(f32)


VM = pl.BlockSpec(memory_space=pltpu.VMEM)
SM = pl.BlockSpec(memory_space=pltpu.SMEM)
SDS = jax.ShapeDtypeStruct


def call(body, name, n_scalar, n_in, out_shape, scratch=(), mb=16, micros=1, **kw):
    return pl.pallas_call(
        functools.partial(body, **kw) if kw else body,
        in_specs=[SM] * n_scalar + [VM] * n_in,
        out_specs=[VM] * len(out_shape),
        out_shape=out_shape,
        scratch_shapes=scratch,
        compiler_params=pltpu.CompilerParams(vmem_limit_bytes=mb << 20),
        cost_estimate=pl.CostEstimate(flops=micros * 1000000000, transcendentals=0, bytes_accessed=micros * 3000000),
        name=name,
    )


def prep(scal, tokens, cotangent, norm_params, talk):
    tok, dim = tokens.shape[1], tokens.shape[2]
    pad = SIDE * PITCH
    heads = talk.shape[1]
    n = heads * PITCH
    full = lambda *s: pl.BlockSpec(s, lambda i, sc: (0,) * len(s))
    return pl.pallas_call(
        prep_kernel,
        grid_spec=pltpu.PrefetchScalarGridSpec(
            num_scalar_prefetch=1,
            grid=(1,),
            in_specs=[
                pl.BlockSpec((1, tok, dim), lambda i, sc: (sc[0], 0, 0)),
                pl.BlockSpec((1, tok, dim), lambda i, sc: (sc[0], 0, 0)),
                full(*norm_params.shape),
                full(*talk.shape),
            ],
            out_specs=[full(pad, dim), full(pad, dim), full(pad, dim), full(2, n, 256), full(pad, n)],
            scratch_shapes=[pltpu.VMEM((tok, dim), f32)],
        ),
        out_shape=[SDS((pad, dim), f32), SDS((pad, dim), bf16), SDS((pad, dim), f32), SDS((2, n, 256), f32),
                   SDS((pad, n), f32)],
        compiler_params=pltpu.CompilerParams(vmem_limit_bytes=16 << 20),
        cost_estimate=pl.CostEstimate(flops=1000000000, transcendentals=0, bytes_accessed=3000000),
        name="prep",
    )(scal, tokens, cotangent, norm_params, talk)


def attn_fwd(scal, x, a, mix, bias, w, unroll=7):
    pad, dim = x.shape
    n = mix.shape[1]
    return call(
        attn_fwd_kernel, "attn_fwd", 1, 4 + len(w),
        [SDS((pad, dim), f32)] + [SDS((pad, 256), bf16)] * 4
        + [SDS((SIDE, n, 256), bf16), SDS((SIDE, pad, n), bf16), SDS((SIDE, n, 256), bf16)],
        [pltpu.VMEM((4, 256, dim), bf16)],
        mb=24, micros=10, parts=len(w), unroll=unroll,
    )(scal, x, a, mix, bias, *w)


def ffn(scal, mid, dy, norm_params, o, w):
    pad, dim = mid.shape
    lanes = len(w) * 256
    return call(
        ffn_kernel, "ffn", 1, 4 + len(w),
        [SDS((SIDE * SIDE, dim), bf16), SDS((pad, dim), f32), SDS((8, dim), f32)] + [SDS((9, 54, 256), bf16)] * len(w),
        [
            pltpu.VMEM((lanes, dim), bf16), pltpu.VMEM((lanes, dim), bf16),
            pltpu.VMEM((pad + 2 * MARGIN, lanes), f32), pltpu.VMEM((pad + 2 * MARGIN, lanes), f32),
            pltpu.VMEM((pad, lanes), bf16), pltpu.VMEM((pad, lanes), bf16),
            pltpu.VMEM((9, lanes), f32), pltpu.VMEM((9, lanes), f32), pltpu.VMEM((pad, dim), f32),
            pltpu.VMEM((56, 256), f32),
        ],
        mb=24, micros=6, parts=len(w),
    )(scal, mid, dy, norm_params, o, *w)


def scores_back(scal, dmid, mix, q, k, v, qw, p, pv, more, part, unroll=7):
    pad, dim = dmid.shape
    n = mix.shape[1]
    heads = n // PITCH
    sums = [SDS((pad, 256), f32)] * 2 + [SDS((n, 256), f32)] * 2
    half = SDS((pad // 2, 256), bf16)
    if part == 0:
        outs = [SDS((pad, 256), bf16), half] + sums
        scratch = [pltpu.VMEM((256, dim), bf16)]
    else:
        outs = [half] + [SDS((pad, 256), bf16)] * 2 + [SDS((2, heads, heads), f32)]
        scratch = [pltpu.VMEM(t.shape, f32) for t in sums]
    return call(
        scores_back_kernel, "scores_back", 1, 8 + len(more), outs, scratch,
        mb=24, micros=4, parts=len(more), unroll=unroll, part=part,
    )(scal, dmid, mix, q, k, v, qw, p, pv, *more)


def weights_back(scal, x, a, dmid, norm_params, gn2, gqa, gqb, gk, gv, gt, w):
    pad, dim = x.shape
    return call(
        weights_back_kernel, "weights_back", 1, 10 + len(w),
        [SDS((SIDE * SIDE, dim), bf16)] + [SDS((3, 54, 256), bf16)] * len(w),
        [pltpu.VMEM((3, 256, dim), bf16), pltpu.VMEM((pad, dim), f32), pltpu.VMEM((24, 256), f32),
         pltpu.VMEM((56, 256), f32)],
        mb=24, micros=3, parts=len(w),
    )(scal, x, a, dmid, norm_params, gn2, gqa, gqb, gk, gv, gt, *w)


def permute(x, axis, k):
    return lax.ppermute(x, axis, [(i, i ^ k) for i in range(lax.axis_size(axis))])


def swap(t):
    return jnp.swapaxes(t, 0, 1)


def whole(*shape):
    return pl.BlockSpec(shape, lambda i: (0,) * len(shape))


def staged(body, name, ins, outs, scratch=(), micros=1):
    return pl.pallas_call(
        body,
        grid=(1,),
        in_specs=[whole(*t.shape) for t in ins],
        out_specs=[whole(*t.shape) for t in outs],
        out_shape=outs,
        scratch_shapes=scratch,
        compiler_params=pltpu.CompilerParams(vmem_limit_bytes=16 << 20),
        cost_estimate=pl.CostEstimate(flops=micros * 1000000000, transcendentals=0, bytes_accessed=micros * 3000000),
        name=name,
    )(*ins)


def local(
    tokens, cotangent, image_count, subnet_heads, subnet_width, block_slot,
    master, master_m1, master_m2, norm_params, norm_m1, norm_m2, talk, talk_m1, talk_m2, conv, conv_m1, conv_m2,
):
    slots, rows, dim = master.shape
    parts = lax.axis_size("head")
    ranks = lax.axis_size("dp")
    place_id = lax.axis_index("head").astype(jnp.int32)
    scal = jnp.concatenate([place_id[None], image_count, subnet_heads, subnet_width])
    mine = pl.pallas_call(
        cast_kernel,
        grid=(1,),
        in_specs=[pl.BlockSpec(memory_space=pltpu.HBM)],
        out_specs=whole(ranks, rows, slots, dim),
        out_shape=SDS((ranks, rows, slots, dim), bf16),
        scratch_shapes=[pltpu.VMEM((rows, slots, dim), f32), pltpu.SemaphoreType.DMA],
        compiler_params=pltpu.CompilerParams(vmem_limit_bytes=16 << 20),
        name="cast",
    )(swap(master))
    every = lax.all_to_all(jnp.swapaxes(mine, 1, 2), "dp", split_axis=0, concat_axis=0, tiled=True)
    x, a, dy, mix, bias = prep(scal, tokens, cotangent, norm_params, talk)
    every, x = lax.optimization_barrier((every, x))
    attn_w, ffn_w = call(
        select_kernel, "select", 1, 2, [SDS((4, rows, dim), bf16), SDS((9, rows, dim), bf16)]
    )(block_slot, every, conv)
    attn_2, attn_1 = permute(attn_w, "head", 2), permute(attn_w, "head", 1)
    attn_3 = permute(attn_2, "head", 1)
    attn_w = [attn_w, attn_1, attn_2, attn_3]
    ffn_2, ffn_1 = permute(ffn_w, "head", 2), permute(ffn_w, "head", 1)
    mid, q, k, v, o, qw, p, pv = attn_fwd(scal, x, a, mix, bias, attn_w)
    mid, ffn_2 = lax.optimization_barrier((mid, ffn_2))
    ffn_w = [ffn_w, ffn_1, ffn_2, permute(ffn_2, "head", 1)]
    out, dmid, gn2, *ffn_g = ffn(scal, mid, dy, norm_params, o, ffn_w)
    ffn_1, ffn_3 = permute(ffn_g[1], "head", 1), permute(ffn_g[3], "head", 1)
    out_2, out_1 = permute(out, "head", 2), permute(out, "head", 1)
    do, gqa, *sums = scores_back(scal, dmid, mix, q, k, v, qw, p, pv, attn_w, 0)
    do, ffn_1, ffn_3, out_1, out_2 = lax.optimization_barrier((do, ffn_1, ffn_3, out_1, out_2))
    (half,) = call(half_sum_kernel, "half_sum", 0, 2, [SDS(ffn_3.shape, bf16)])(ffn_g[2], ffn_3)
    ffn_2, out_3 = permute(half, "head", 2), permute(out_2, "head", 1)
    gqb, gk, gv, gt = scores_back(scal, dmid, mix, q, k, v, qw, p, pv, [do, *sums], 1)
    tg, *attn_g = weights_back(scal, x, a, dmid, norm_params, gn2, gqa, gqb, gk, gv, gt, attn_w)
    attn_1, attn_3 = permute(attn_g[1], "head", 1), permute(attn_g[3], "head", 1)
    (half,) = call(half_sum_kernel, "half_sum", 0, 2, [SDS(attn_3.shape, bf16)])(attn_g[2], attn_3)
    attn_2 = permute(half, "head", 2)
    (message,) = call(
        spread_ffn_kernel, "spread_ffn", 1, 3, [SDS((ranks * slots, rows, 256), bf16)], ranks=ranks
    )(block_slot, ffn_g[0], ffn_1, ffn_2)
    tg, attn_2, message, out_3 = lax.optimization_barrier((tg, attn_2, message, out_3))
    tg_2, tg_1 = permute(tg, "head", 2), permute(tg, "head", 1)
    tg_3 = permute(tg_2, "head", 1)
    (message,) = call(
        spread_attn_kernel, "spread_attn", 1, 4, [SDS(message.shape, bf16)], ranks=ranks
    )(block_slot, message, attn_g[0], attn_1, attn_2)
    got = lax.all_to_all(message, "dp", split_axis=0, concat_axis=0, tiled=True)
    shape = SDS((parts,) + tokens.shape[1:], f32)
    (output,) = call(assemble_kernel, "assemble", 1, parts, [shape])(scal, out, out_1, out_2, out_3)
    (token_grad,) = call(assemble_kernel, "assemble", 1, parts, [shape])(scal, tg, tg_1, tg_2, tg_3)
    state = [
        swap(master), swap(master_m1), swap(master_m2), norm_params, norm_m1, norm_m2,
        swap(talk), swap(talk_m1), swap(talk_m2), conv, conv_m1, conv_m2,
    ]
    shapes = [SDS(t.shape, f32) for t in state]
    shapes.insert(3, SDS(state[0].shape, bf16))
    new = staged(
        functools.partial(update_kernel, ranks=ranks), "update", [got, *state], shapes,
        [pltpu.VMEM((rows, slots, dim), f32), pltpu.VMEM((slots, 64, 256), f32), pltpu.VMEM((64, 256), f32)],
    )
    new = [swap(t) if t.ndim == 3 else t for t in new]
    return (output, token_grad, *new)


def solution(mesh):
    in_specs = (
        P("dp", None, None),
        P("dp", None, None),
        P("dp"),
        P(),
        P(),
        P(),
        P("dp", None, "head"),
        P("dp", None, "head"),
        P("dp", None, "head"),
        P(),
        P(),
        P(),
        P(),
        P(),
        P(),
        P(None, "head"),
        P(None, "head"),
        P(None, "head"),
    )
    out_specs = (
        P("dp", None, None),
        P("dp", None, None),
        P("dp", None, "head"),
        P("dp", None, "head"),
        P("dp", None, "head"),
        P("dp", None, "head"),
        P(),
        P(),
        P(),
        P(),
        P(),
        P(),
        P(None, "head"),
        P(None, "head"),
        P(None, "head"),
    )
    return jax.shard_map(local, mesh=mesh, in_specs=in_specs, out_specs=out_specs, check_vma=False)
```

```python
import functools
import jax
import jax.numpy as jnp
from jax import lax
from jax.experimental import pallas as pl
from jax.experimental.pallas import tpu as pltpu
from jax.sharding import PartitionSpec as P

HD = 18
SIDE = 14
PITCH = 16
MARGIN = 24
FREE = 216
WIDE = 40
norm_eps = 1e-05
bf16 = jnp.bfloat16
f32 = jnp.float32


def nn(a, b):
    return lax.dot_general(a, b, (((1,), (0,)), ((), ())), preferred_element_type=f32)


def nt(a, b):
    return lax.dot_general(a, b, (((1,), (1,)), ((), ())), preferred_element_type=f32)


def tn(a, b):
    return lax.dot_general(a, b, (((0,), (0,)), ((), ())), preferred_element_type=f32)


def iota(shape, dim):
    return lax.broadcasted_iota(jnp.int32, shape, dim)


def split2(v):
    hi = v.astype(bf16)
    return hi, (v - hi.astype(f32)).astype(bf16)


def real_rows(shape):
    return (iota(shape, 0) & (PITCH - 1)) < SIDE


def lane_head(shape, dim, place):
    lane = iota(shape, dim)
    rest = lane & 63
    head = ((lane >> 6) ^ place) * 3 + (rest >= 18).astype(jnp.int32) + (rest >= 36).astype(jnp.int32)
    return jnp.where(rest < 54, head, -1)


def true_head(rows, place):
    return ((rows // (3 * PITCH)) ^ place) * 3 + (rows // PITCH) % 3


def prep_kernel(scal, tok_ref, cot_ref, norm_ref, talk_ref, x_ref, a_ref, dy_ref, mix_ref, bias_ref, tmp_ref):
    x_ref[...] = jnp.zeros_like(x_ref)
    dy_ref[...] = jnp.zeros_like(dy_ref)
    valid = (scal[0] < scal[1]).astype(f32)
    tmp_ref[...] = tok_ref[0].astype(f32)
    for y in range(SIDE):
        x_ref[PITCH * y : PITCH * y + SIDE, :] = tmp_ref[SIDE * y : SIDE * (y + 1), :]
        dy_ref[PITCH * y : PITCH * y + SIDE, :] = cot_ref[0, SIDE * y : SIDE * (y + 1), :] * valid
    x = x_ref[...]
    centred = x - jnp.mean(x, axis=-1, keepdims=True)
    inv = lax.rsqrt(jnp.mean(centred * centred, axis=-1, keepdims=True) + norm_eps)
    a = centred * inv * norm_ref[0:1, :] + norm_ref[1:2, :]
    a_ref[...] = jnp.where(real_rows(a.shape), a, 0.0).astype(bf16)
    heads = talk_ref.shape[1]
    n = heads * PITCH
    ex = (true_head(iota((n, heads), 0), scal[0]) == iota((n, heads), 1)).astype(bf16)
    el = (lane_head((256, heads), 0, scal[0]) == iota((256, heads), 1)).astype(bf16)
    for i in range(2):
        both = []
        for part in split2(talk_ref[i]):
            if i == 0:
                both.append(nt(nn(ex, part).astype(bf16), el))
            else:
                both.append(nt(nt(ex, part).astype(bf16), el))
        mix_ref[i] = (both[0] + both[1]) * (HD**-0.5 if i == 0 else 1.0)
    bias_ref[...] = jnp.where(real_rows(bias_ref.shape), 0.0, -1e30)


def load_weight(dst_ref, w_refs, b):
    for k, w_ref in enumerate(w_refs):
        dst_ref[64 * k : 64 * k + 54, :] = w_ref[b]


def tiled(rows, heads):
    return jnp.concatenate([rows] * heads, axis=0)


def over_heads(rows, heads):
    return jnp.sum(rows.reshape(heads, PITCH, rows.shape[1]), axis=0)


def attn_fwd_kernel(scal, x_ref, a_ref, mix_ref, bias_ref, *refs, parts, unroll):
    w_refs, refs = refs[:parts], refs[parts:]
    mid_ref, q_ref, k_ref, v_ref, o_ref, qw_ref, p_ref, pv_ref, ws_ref = refs
    heads = mix_ref.shape[1] // PITCH
    a = a_ref[...]
    ws_ref[...] = jnp.zeros_like(ws_ref)
    for b, dst in enumerate((q_ref, k_ref, v_ref)):
        load_weight(ws_ref.at[b], w_refs, b)
        dst[...] = nt(a, ws_ref[b]).astype(bf16)
    load_weight(ws_ref.at[3], w_refs, 3)
    head = lane_head((1, 256), 1, scal[0])
    keep = ((head >= 0) & (head < scal[2])).astype(f32)

    def group(y, _):
        rows = pl.ds(pl.multiple_of(y * PITCH, PITCH), PITCH)
        qw = (tiled(q_ref[rows, :].astype(f32), heads) * mix_ref[0]).astype(bf16)
        qw_ref[y] = qw
        t = nt(k_ref[...], qw) + bias_ref[...]
        e = jnp.exp(t - jnp.max(t, axis=0, keepdims=True))
        p = (e * (1.0 / jnp.sum(e, axis=0, keepdims=True))).astype(bf16)
        p_ref[y] = p
        pv = tn(p, v_ref[...])
        pv_ref[y] = pv.astype(bf16)
        o_ref[rows, :] = (over_heads(pv * mix_ref[1], heads) * keep).astype(bf16)
        return 0

    lax.fori_loop(0, SIDE, group, 0, unroll=unroll)
    mid_ref[...] = x_ref[...] + nn(o_ref[...], ws_ref[3])


def ln_stats(v):
    centred = v - jnp.mean(v, axis=-1, keepdims=True)
    inv = lax.rsqrt(jnp.mean(centred * centred, axis=-1, keepdims=True) + norm_eps)
    return centred * inv, inv


def ln_back(grad, scaled, inv, gain):
    gs = grad * gain
    return inv * (
        gs - jnp.mean(gs, axis=-1, keepdims=True) - scaled * jnp.mean(gs * scaled, axis=-1, keepdims=True)
    )


def in_free_lanes(flat, dst_ref, first_row):
    rows = flat.shape[0]
    for j in range(6):
        dst_ref[first_row + rows * j : first_row + rows * (j + 1), :] = pltpu.roll(flat, (FREE - WIDE * j) % 256, 1)


def from_free_lanes(src_ref, first_row, rows):
    lane = iota((rows, 256), 1)
    flat = jnp.zeros((rows, 256), f32)
    for j in range(6):
        moved = pltpu.roll(src_ref[first_row + rows * j : first_row + rows * (j + 1), :], (WIDE * j - FREE) % 256, 1)
        flat = flat + jnp.where((lane >= WIDE * j) & (lane < WIDE * (j + 1)), moved, 0.0)
    return flat


def place(rows=216):
    shape = (rows, 256)
    lane = iota(shape, 1)
    rest = lane & 63
    return ((iota(shape, 0) == (lane >> 6) * 54 + rest) & (rest < 54)).astype(bf16)


def ffn_kernel(
    scal, mid_ref, dy_ref, norm_ref, o_ref, *refs, parts
):
    w_refs, refs = refs[:parts], refs[parts:]
    out_ref, dmid_ref, gn_ref = refs[:3]
    gw_refs, refs = refs[3 : 3 + parts], refs[3 + parts :]
    win_ref, wdn_ref, h_ref, d_ref, gate_ref, dh_ref, cv_ref, gcv_ref, tmp_ref, sm_ref = refs
    hd = parts
    lanes = hd * 256
    win_ref[...] = jnp.zeros_like(win_ref)
    wdn_ref[...] = jnp.zeros_like(wdn_ref)
    pm = place()
    for h in range(hd):
        for j in range(4):
            at = 256 * h + 64 * j
            win_ref[at : at + 54, :] = w_refs[h][j]
            wdn_ref[at : at + 54, :] = w_refs[h][4 + j]
        both = nn(w_refs[h][8], pm)
        cv_ref[:, 256 * h : 256 * (h + 1)] = both[0:9] + both[16:25]
    mid = mid_ref[...]
    z, inv = ln_stats(mid)
    rows = real_rows(mid.shape)
    w = jnp.where(rows, z * norm_ref[2:3, :] + norm_ref[3:4, :], 0.0).astype(bf16)
    dy = dy_ref[...]
    e = dy.astype(bf16)
    tokens = mid.shape[0]
    pad = MARGIN
    zero = jnp.zeros((pad, lanes), f32)
    h_ref[0:pad, :] = zero
    h_ref[pad + tokens :, :] = zero
    d_ref[0:pad, :] = zero
    d_ref[pad + tokens :, :] = zero
    h_ref[pad : pad + tokens, :] = nt(w, win_ref[...])
    d_ref[pad : pad + tokens, :] = nt(e, wdn_ref[...])
    lane = iota((1, 128), 1)
    rmask = real_rows((tokens, 128))
    for c in range(lanes // 128):
        cols = slice(128 * c, 128 * (c + 1))
        glane = lane + 128 * c
        rest = glane & 63
        unit = (((glane >> 8) ^ scal[0]) * 4 + ((glane >> 6) & 3)) * 54 + rest
        keep = ((rest < 54) & (unit < scal[3])).astype(f32)
        act = jnp.zeros((tokens, 128), f32)
        for t in range(9):
            off = PITCH * (t // 3 - 1) + t % 3 - 1
            act = act + cv_ref[t : t + 1, cols] * h_ref[pad + off : pad + off + tokens, cols]
        sig = 1.0 / (1.0 + jnp.exp(-act))
        gate_ref[:, cols] = (act * sig * keep).astype(bf16)
        dact = d_ref[pad : pad + tokens, cols] * keep * sig * (1.0 + act * (1.0 - sig))
        d_ref[pad : pad + tokens, cols] = dact
        dh = jnp.zeros((tokens, 128), f32)
        for t in range(9):
            off = PITCH * (t // 3 - 1) + t % 3 - 1
            gcv_ref[t : t + 1, cols] = jnp.sum(
                dact * h_ref[pad + off : pad + off + tokens, cols], axis=0, keepdims=True
            )
            dh = dh + cv_ref[t : t + 1, cols] * d_ref[pad - off : pad - off + tokens, cols]
        dh_ref[:, cols] = jnp.where(rmask, dh, 0.0).astype(bf16)
    valid = (scal[0] < scal[1]).astype(f32)
    down = nn(gate_ref[...], wdn_ref[...])
    tmp_ref[...] = (mid + down) * valid
    for y in range(SIDE):
        out_ref[SIDE * y : SIDE * (y + 1), :] = tmp_ref[PITCH * y : PITCH * y + SIDE, :].astype(bf16)
    dw = nn(dh_ref[...], win_ref[...])
    gn_ref[...] = jnp.zeros_like(gn_ref)
    gn_ref[0:1, :] = jnp.sum(dw * z, axis=0, keepdims=True)
    gn_ref[1:2, :] = jnp.sum(dw, axis=0, keepdims=True)
    dmid = dy + ln_back(dw, z, inv, norm_ref[2:3, :])
    dmid_ref[...] = dmid
    go = tn(o_ref[...], dmid.astype(bf16)).astype(bf16)
    dim = mid.shape[1]
    free = iota((54, 256), 1) >= FREE
    pm = place(256)
    for h in range(hd):
        cols = slice(256 * h, 256 * (h + 1))
        gi = tn(dh_ref[:, cols], w).astype(bf16)
        gd = tn(gate_ref[:, cols], e).astype(bf16)
        for j in range(4):
            gw_refs[h][1 + j, :, 0:dim] = gi[64 * j : 64 * j + 54]
            gw_refs[h][5 + j, :, 0:dim] = gd[64 * j : 64 * j + 54]
        in_free_lanes(nt(gcv_ref[:, cols].astype(bf16), pm), sm_ref, 0)
        gw_refs[h][0] = jnp.where(free, sm_ref[0:54, :], 0.0).astype(bf16)
        gw_refs[h][0, :, 0:dim] = go[64 * h : 64 * h + 54]


def scores_back_kernel(
    scal, dmid_ref, mix_ref, q_ref, k_ref, v_ref, qw_ref, p_ref, pv_ref, *refs, parts, unroll, part
):
    heads = mix_ref.shape[1] // PITCH
    n = heads * PITCH
    if part == 0:
        w_refs, refs = refs[:parts], refs[parts:]
        do_ref, gq_ref, gk_ref, gv_ref, g0_ref, g1_ref, wo_ref = refs
        wo_ref[...] = jnp.zeros_like(wo_ref)
        load_weight(wo_ref, w_refs, 3)
        f = dmid_ref[...].astype(bf16)
        head = lane_head((1, 256), 1, scal[0])
        keep = ((head >= 0) & (head < scal[2])).astype(f32)
        do_ref[...] = (nt(f, wo_ref[...]) * keep).astype(bf16)
        for ref in (gk_ref, gv_ref, g0_ref, g1_ref):
            ref[...] = jnp.zeros_like(ref)
    else:
        do_ref, *sums, gq_ref, gkb_ref, gvb_ref, gt_ref, gk_ref, gv_ref, g0_ref, g1_ref = refs
        for ref, old in zip((gk_ref, gv_ref, g0_ref, g1_ref), sums):
            ref[...] = old[...]
    first = SIDE // 2 * part

    def group(y, _):
        out_rows = pl.ds(pl.multiple_of(y * PITCH, PITCH), PITCH)
        y = y + first
        rows = pl.ds(pl.multiple_of(y * PITCH, PITCH), PITCH)
        dot = tiled(do_ref[rows, :].astype(f32), heads)
        dw = (dot * mix_ref[1]).astype(bf16)
        dp = nt(v_ref[...], dw)
        p = p_ref[y]
        pf = p.astype(f32)
        dt = (pf * (dp - jnp.sum(dp * pf, axis=0, keepdims=True))).astype(bf16)
        gv_ref[...] += nn(p, dw)
        gk_ref[...] += nn(dt, qw_ref[y])
        dk = tn(dt, k_ref[...])
        gq_ref[out_rows, :] = over_heads(dk * mix_ref[0], heads).astype(bf16)
        g0_ref[...] += dk * tiled(q_ref[rows, :].astype(f32), heads)
        g1_ref[...] += pv_ref[y].astype(f32) * dot
        return 0

    lax.fori_loop(0, SIDE // 2, group, 0, unroll=unroll)
    if part == 0:
        return
    gkb_ref[...] = gk_ref[...].astype(bf16)
    gvb_ref[...] = gv_ref[...].astype(bf16)
    ex = (true_head(iota((n, heads), 0), scal[0]) == iota((n, heads), 1)).astype(bf16)
    el = (lane_head((256, heads), 0, scal[0]) == iota((256, heads), 1)).astype(bf16)
    for i, ref in enumerate((g0_ref, g1_ref)):
        hi, lo = split2(ref[...])
        hi, lo = split2(nn(hi, el) + nn(lo, el))
        if i == 0:
            gt_ref[i] = (tn(ex, hi) + tn(ex, lo)) * HD**-0.5
        else:
            gt_ref[i] = tn(hi, ex) + tn(lo, ex)


def weights_back_kernel(
    scal, x_ref, a_ref, dmid_ref, norm_ref, gn2_ref, gqa_ref, gqb_ref, gk_ref, gv_ref, gt_ref, y_ref, *refs, parts
):
    w_refs, refs = refs[:parts], refs[parts:]
    both_ref, gw_refs, refs = refs[0], refs[1 : 1 + parts], refs[1 + parts :]
    ws_ref, tmp_ref, flat_ref, sm_ref = refs
    heads = gt_ref.shape[1]
    dim = x_ref.shape[1]
    ws_ref[...] = jnp.zeros_like(ws_ref)
    for b in range(3):
        load_weight(ws_ref.at[b], w_refs, b)
    gq = jnp.concatenate([gqa_ref[...], gqb_ref[...]], axis=0)
    gk, gv = gk_ref[...], gv_ref[...]
    a = a_ref[...]
    da = nn(gq, ws_ref[0]) + nn(gk, ws_ref[1]) + nn(gv, ws_ref[2])
    z, inv = ln_stats(x_ref[...])
    flat_ref[...] = jnp.zeros_like(flat_ref)
    flat_ref[0:1, 0:dim] = jnp.sum(da * z, axis=0, keepdims=True)
    flat_ref[1:2, 0:dim] = jnp.sum(da, axis=0, keepdims=True)
    flat_ref[2:4, 0:dim] = gn2_ref[0:2, :]
    for i in range(2):
        flat_ref[8 : 8 + heads, 128 * i : 128 * i + heads] = gt_ref[i]
    sm_ref[...] = jnp.zeros_like(sm_ref)
    in_free_lanes(flat_ref[0:4, :], sm_ref, 0)
    mix = flat_ref[8 : 8 + heads, :]
    first = iota(mix.shape, 1) < 128
    mix = jnp.where(first, mix, 0.0) + pltpu.roll(jnp.where(first, 0.0, mix), 128 + heads, 1)
    sm_ref[24 : 24 + heads, :] = pltpu.roll(mix, FREE, 1)
    small = jnp.where(iota((54, 256), 1) >= FREE, sm_ref[0:54, :], 0.0).astype(bf16)
    for h in range(parts):
        gw_refs[h][0] = small
    for b, g in enumerate((gq, gk, gv)):
        gw = tn(g, a).astype(bf16)
        for h in range(parts):
            gw_refs[h][b, :, 0:dim] = gw[64 * h : 64 * h + 54]
    tmp_ref[...] = dmid_ref[...] + ln_back(da, z, inv, norm_ref[0:1, :])
    for y in range(SIDE):
        both_ref[1, SIDE * y : SIDE * (y + 1), :] = tmp_ref[PITCH * y : PITCH * y + SIDE, :].astype(bf16)
    both_ref[0] = y_ref[...]


def cast_kernel(m_hbm, out_ref, m_ref, sem):
    copy = pltpu.make_async_copy(m_hbm, m_ref, sem)
    copy.start()
    copy.wait()
    for i in range(out_ref.shape[0]):
        out_ref[i] = m_ref[:, i, :].astype(bf16)


def pair_kernel(own_ref, other_ref, out_ref):
    out_ref[0] = own_ref[...]
    out_ref[1] = other_ref[...]


def select_kernel(slot_ref, scal, conv_ref, *refs):
    pairs, (attn_ref, ffn_ref, every_ref) = refs[:-3], refs[-3:]
    for k, ref in enumerate(pairs):
        every_ref[scal[5] ^ k] = ref[...]
    per = every_ref.shape[2]
    for b in range(12):
        slot = slot_ref[b]
        rank = slot // per
        block = every_ref[rank // 2, (rank % 2) ^ scal[4], slot % per]
        if b < 4:
            attn_ref[b] = block
        else:
            ffn_ref[b - 4] = block
    hi, lo = split2(conv_ref[...])
    ffn_ref[8] = jnp.zeros_like(ffn_ref[8])
    ffn_ref[8, 0:9] = hi
    ffn_ref[8, 16:25] = lo


def total(refs, at):
    acc = refs[0][at].astype(f32)
    for ref in refs[1:]:
        acc = acc + ref[at].astype(f32)
    return acc


def half_sum_kernel(a_ref, b_ref, out_ref):
    out_ref[...] = (a_ref[...].astype(f32) + b_ref[...].astype(f32)).astype(bf16)


def spot(slot, scal, per):
    rank = slot // per
    return (rank // 2) ^ scal[5], (rank % 2) ^ scal[4], slot % per


def spread_ffn_kernel(slot_ref, scal, *refs):
    ffn_refs, out_ref = refs[:-1], refs[-1]
    pairs, _, per = out_ref.shape[:3]
    out_ref[...] = jnp.zeros_like(out_ref)
    for b in range(9):
        block = total(ffn_refs, b)
        k, j, i = spot(slot_ref[3 + b], scal, per)
        out_ref[k, j, i, :, 0:FREE] = block[:, 0:FREE].astype(bf16)
        if b == 0:
            wide = block[:, FREE:].astype(bf16)
    for k in range(pairs):
        for j in range(2):
            out_ref[k, j, 0, :, FREE:] = wide


def spread_attn_kernel(slot_ref, scal, old_ref, *refs, parts):
    attn, outs, all_ref = refs[:parts], refs[parts:-1], refs[-1]
    pairs, _, per = all_ref.shape[:3]
    all_ref[...] = old_ref[...]
    for b in range(3):
        block = total(attn, b)
        k, j, i = spot(slot_ref[b], scal, per)
        all_ref[k, j, i, :, 0:FREE] = block[:, 0:FREE].astype(bf16)
        if b == 0:
            wide = block[:, FREE:].astype(bf16)
    for k in range(pairs):
        outs[k][...] = all_ref[k]
        for j in range(2):
            outs[k][j, 1, :, FREE:] = wide


def pair_sum_kernel(*refs):
    own_ref, other_ref = refs[-2:]
    own_ref[...] = total(refs[:-2], 0)
    other_ref[...] = total(refs[:-2], 1).astype(bf16)


def adam(w, g, one, two, rate, decay):
    one_new = 0.5 * one + 0.5 * g
    two_new = 0.5 * two + 0.5 * g * g
    hat_one = one_new / (1.0 - 0.5**3)
    hat_two = two_new / (1.0 - 0.5**3)
    return w - rate * (hat_one / (jnp.sqrt(hat_two) + 1e-08) + decay * w), one_new, two_new


def update_kernel(own_ref, other_ref, *refs):
    ins, outs, (g_ref, sm_ref, flat_ref) = refs[0:12], refs[12:25], refs[25:]
    per, rows = own_ref.shape[:2]
    dim = ins[0].shape[2]
    for i in range(per):
        g = own_ref[i] + other_ref[i].astype(f32)
        g_ref[:, i, :] = g[:, 0:dim]
        sm_ref[i, 0:rows, :] = g
    w, one, two = adam(ins[0][...], g_ref[...], ins[1][...], ins[2][...], 0.06, 0.05)
    outs[0][...], outs[1][...], outs[2][...], outs[3][...] = w, one, two, w.astype(bf16)
    heads = ins[6].shape[0]
    flat_ref[0:9, :] = from_free_lanes(sm_ref.at[0], 0, 9)
    flat_ref[16:20, :] = from_free_lanes(sm_ref.at[1], 0, 4)
    mix = pltpu.roll(sm_ref[1, 24 : 24 + heads, :], 256 - FREE, 1)
    flat_ref[32 : 32 + heads, :] = mix
    flat_ref[48 : 48 + heads, :] = pltpu.roll(mix, 256 - heads, 1)
    outs[4][...], outs[5][...], outs[6][...] = adam(
        ins[3][...], flat_ref[16:20, 0:dim], ins[4][...], ins[5][...], 0.2, 0.0
    )
    for i in range(2):
        w, one, two = adam(
            ins[6][:, i, :], flat_ref[16 * (i + 2) : 16 * (i + 2) + heads, 0:heads], ins[7][:, i, :], ins[8][:, i, :],
            0.2, 0.0,
        )
        outs[7][:, i, :], outs[8][:, i, :], outs[9][:, i, :] = w, one, two
    outs[10][...], outs[11][...], outs[12][...] = adam(
        ins[9][...], flat_ref[0:9, 0:dim], ins[10][...], ins[11][...], 0.2, 0.05
    )


def assemble_kernel(scal, *refs):
    ins, outs, (all_ref,) = refs[:-3], refs[-3:-1], refs[-1:]
    parts, tokens = len(ins), ins[0].shape[1]
    step = 32
    shape = (parts * step, parts * step)
    row, col = iota(shape, 0), iota(shape, 1)
    pick = ((row // parts == col % step) & (row % parts == col // step)).astype(bf16)
    full = all_ref.shape[1]
    for k in range(parts):
        all_ref[k, tokens // step * step : full, :] = jnp.zeros((full - tokens // step * step, all_ref.shape[2]), bf16)
    for i, out_ref in enumerate(outs):
        for k, ref in enumerate(ins):
            all_ref[scal[0] ^ k, 0:tokens, :] = ref[i]
        for at in range(0, tokens, step):
            mixed = nn(pick, jnp.concatenate([all_ref[k, at : at + step, :] for k in range(parts)], axis=0))
            for t in range(min(step, tokens - at)):
                out_ref[at + t] = mixed[parts * t : parts * (t + 1)]


VM = pl.BlockSpec(memory_space=pltpu.VMEM)
SM = pl.BlockSpec(memory_space=pltpu.SMEM)
SDS = jax.ShapeDtypeStruct


def call(body, name, n_scalar, n_in, out_shape, scratch=(), mb=16, micros=1, **kw):
    return pl.pallas_call(
        functools.partial(body, **kw) if kw else body,
        in_specs=[SM] * n_scalar + [VM] * n_in,
        out_specs=[VM] * len(out_shape),
        out_shape=out_shape,
        scratch_shapes=scratch,
        compiler_params=pltpu.CompilerParams(vmem_limit_bytes=mb << 20),
        cost_estimate=pl.CostEstimate(flops=micros * 1000000000, transcendentals=0, bytes_accessed=micros * 3000000),
        name=name,
    )


def prep(scal, tokens, cotangent, norm_params, talk):
    tok, dim = tokens.shape[1], tokens.shape[2]
    pad = SIDE * PITCH
    heads = talk.shape[1]
    n = heads * PITCH
    full = lambda *s: pl.BlockSpec(s, lambda i, sc: (0,) * len(s))
    return pl.pallas_call(
        prep_kernel,
        grid_spec=pltpu.PrefetchScalarGridSpec(
            num_scalar_prefetch=1,
            grid=(1,),
            in_specs=[
                pl.BlockSpec((1, tok, dim), lambda i, sc: (sc[0], 0, 0)),
                pl.BlockSpec((1, tok, dim), lambda i, sc: (sc[0], 0, 0)),
                full(*norm_params.shape),
                full(*talk.shape),
            ],
            out_specs=[full(pad, dim), full(pad, dim), full(pad, dim), full(2, n, 256), full(pad, n)],
            scratch_shapes=[pltpu.VMEM((tok, dim), f32)],
        ),
        out_shape=[SDS((pad, dim), f32), SDS((pad, dim), bf16), SDS((pad, dim), f32), SDS((2, n, 256), f32),
                   SDS((pad, n), f32)],
        compiler_params=pltpu.CompilerParams(vmem_limit_bytes=16 << 20),
        cost_estimate=pl.CostEstimate(flops=1000000000, transcendentals=0, bytes_accessed=3000000),
        name="prep",
    )(scal, tokens, cotangent, norm_params, talk)


def attn_fwd(scal, x, a, mix, bias, w, unroll=7):
    pad, dim = x.shape
    n = mix.shape[1]
    return call(
        attn_fwd_kernel, "attn_fwd", 1, 4 + len(w),
        [SDS((pad, dim), f32)] + [SDS((pad, 256), bf16)] * 4
        + [SDS((SIDE, n, 256), bf16), SDS((SIDE, pad, n), bf16), SDS((SIDE, n, 256), bf16)],
        [pltpu.VMEM((4, 256, dim), bf16)],
        mb=24, micros=1, parts=len(w), unroll=unroll,
    )(scal, x, a, mix, bias, *w)


def ffn(scal, mid, dy, norm_params, o, w):
    pad, dim = mid.shape
    lanes = len(w) * 256
    return call(
        ffn_kernel, "ffn", 1, 4 + len(w),
        [SDS((SIDE * SIDE, dim), bf16), SDS((pad, dim), f32), SDS((8, dim), f32)] + [SDS((9, 54, 256), bf16)] * len(w),
        [
            pltpu.VMEM((lanes, dim), bf16), pltpu.VMEM((lanes, dim), bf16),
            pltpu.VMEM((pad + 2 * MARGIN, lanes), f32), pltpu.VMEM((pad + 2 * MARGIN, lanes), f32),
            pltpu.VMEM((pad, lanes), bf16), pltpu.VMEM((pad, lanes), bf16),
            pltpu.VMEM((9, lanes), f32), pltpu.VMEM((9, lanes), f32), pltpu.VMEM((pad, dim), f32),
            pltpu.VMEM((56, 256), f32),
        ],
        mb=24, micros=6, parts=len(w),
    )(scal, mid, dy, norm_params, o, *w)


def scores_back(scal, dmid, mix, q, k, v, qw, p, pv, more, part, unroll=7):
    pad, dim = dmid.shape
    n = mix.shape[1]
    heads = n // PITCH
    sums = [SDS((pad, 256), f32)] * 2 + [SDS((n, 256), f32)] * 2
    half = SDS((pad // 2, 256), bf16)
    if part == 0:
        outs = [SDS((pad, 256), bf16), half] + sums
        scratch = [pltpu.VMEM((256, dim), bf16)]
    else:
        outs = [half] + [SDS((pad, 256), bf16)] * 2 + [SDS((2, heads, heads), f32)]
        scratch = [pltpu.VMEM(t.shape, f32) for t in sums]
    return call(
        scores_back_kernel, "scores_back", 1, 8 + len(more), outs, scratch,
        mb=24, micros=4, parts=len(more), unroll=unroll, part=part,
    )(scal, dmid, mix, q, k, v, qw, p, pv, *more)


def weights_back(scal, x, a, dmid, norm_params, gn2, gqa, gqb, gk, gv, gt, out, w):
    pad, dim = x.shape
    return call(
        weights_back_kernel, "weights_back", 1, 11 + len(w),
        [SDS((2, SIDE * SIDE, dim), bf16)] + [SDS((3, 54, 256), bf16)] * len(w),
        [pltpu.VMEM((3, 256, dim), bf16), pltpu.VMEM((pad, dim), f32), pltpu.VMEM((24, 256), f32),
         pltpu.VMEM((56, 256), f32)],
        mb=24, micros=3, parts=len(w),
    )(scal, x, a, dmid, norm_params, gn2, gqa, gqb, gk, gv, gt, out, *w)


def permute(x, axis, k):
    return lax.ppermute(x, axis, [(i, i ^ k) for i in range(lax.axis_size(axis))])


def swap(t):
    return jnp.swapaxes(t, 0, 1)


def whole(*shape):
    return pl.BlockSpec(shape, lambda i: (0,) * len(shape))


def staged(body, name, ins, outs, scratch=(), micros=1):
    return pl.pallas_call(
        body,
        grid=(1,),
        in_specs=[whole(*t.shape) for t in ins],
        out_specs=[whole(*t.shape) for t in outs],
        out_shape=outs,
        scratch_shapes=scratch,
        compiler_params=pltpu.CompilerParams(vmem_limit_bytes=16 << 20),
        cost_estimate=pl.CostEstimate(flops=micros * 1000000000, transcendentals=0, bytes_accessed=micros * 3000000),
        name=name,
    )(*ins)


def local(
    tokens, cotangent, image_count, subnet_heads, subnet_width, block_slot,
    master, master_m1, master_m2, norm_params, norm_m1, norm_m2, talk, talk_m1, talk_m2, conv, conv_m1, conv_m2,
):
    slots, rows, dim = master.shape
    parts = lax.axis_size("head")
    ranks = lax.axis_size("dp")
    place_id = lax.axis_index("head").astype(jnp.int32)
    rank = lax.axis_index("dp").astype(jnp.int32)
    scal = jnp.concatenate(
        [place_id[None], image_count, subnet_heads, subnet_width, (rank % 2)[None], (rank // 2)[None]]
    )
    mine = pl.pallas_call(
        cast_kernel,
        grid=(1,),
        in_specs=[pl.BlockSpec(memory_space=pltpu.HBM)],
        out_specs=whole(slots, rows, dim),
        out_shape=SDS((slots, rows, dim), bf16),
        scratch_shapes=[pltpu.VMEM((rows, slots, dim), f32), pltpu.SemaphoreType.DMA],
        compiler_params=pltpu.CompilerParams(vmem_limit_bytes=16 << 20),
        name="cast",
    )(swap(master))
    (pair,) = call(pair_kernel, "pair", 0, 2, [SDS((2, slots, rows, dim), bf16)])(mine, permute(mine, "dp", 1))
    pair, tokens, cotangent, talk_in = lax.optimization_barrier((pair, tokens, cotangent, talk))
    pairs = [pair] + [permute(pair, "dp", 2 * k) for k in range(1, ranks // 2)]
    x, a, dy, mix, bias = prep(scal, tokens, cotangent, norm_params, talk_in)
    pairs[1], x = lax.optimization_barrier((pairs[1], x))
    attn_w, ffn_w = call(
        select_kernel, "select", 2, 1 + len(pairs), [SDS((4, rows, dim), bf16), SDS((9, rows, dim), bf16)],
        [pltpu.VMEM((ranks // 2, 2, slots, rows, dim), bf16)],
    )(block_slot, scal, conv, *pairs)
    attn_2, attn_1 = permute(attn_w, "head", 2), permute(attn_w, "head", 1)
    attn_3 = permute(attn_2, "head", 1)
    attn_w = [attn_w, attn_1, attn_2, attn_3]
    ffn_2, ffn_1 = permute(ffn_w, "head", 2), permute(ffn_w, "head", 1)
    mid, q, k, v, o, qw, p, pv = attn_fwd(scal, x, a, mix, bias, attn_w)
    mid, ffn_2 = lax.optimization_barrier((mid, ffn_2))
    ffn_w = [ffn_w, ffn_1, ffn_2, permute(ffn_2, "head", 1)]
    out, dmid, gn2, *ffn_g = ffn(scal, mid, dy, norm_params, o, ffn_w)
    ffn_1, ffn_3 = permute(ffn_g[1], "head", 1), permute(ffn_g[3], "head", 1)
    do, gqa, *sums = scores_back(scal, dmid, mix, q, k, v, qw, p, pv, attn_w, 0)
    do, ffn_1, ffn_3 = lax.optimization_barrier((do, ffn_1, ffn_3))
    (half,) = call(half_sum_kernel, "half_sum", 0, 2, [SDS(ffn_3.shape, bf16)])(ffn_g[2], ffn_3)
    ffn_2 = permute(half, "head", 2)
    gqb, gk, gv, gt = scores_back(scal, dmid, mix, q, k, v, qw, p, pv, [do, *sums], 1)
    both, *attn_g = weights_back(scal, x, a, dmid, norm_params, gn2, gqa, gqb, gk, gv, gt, out, attn_w)
    attn_1, attn_3 = permute(attn_g[1], "head", 1), permute(attn_g[3], "head", 1)
    (half,) = call(half_sum_kernel, "half_sum", 0, 2, [SDS(attn_3.shape, bf16)])(attn_g[2], attn_3)
    attn_2 = permute(half, "head", 2)
    (message,) = call(
        spread_ffn_kernel, "spread_ffn", 2, 3, [SDS((ranks // 2, 2, slots, rows, 256), bf16)]
    )(block_slot, scal, ffn_g[0], ffn_1, ffn_2)
    messages = list(call(
        spread_attn_kernel, "spread_attn", 2, 4, [SDS(message.shape[1:], bf16)] * (ranks // 2),
        [pltpu.VMEM(message.shape, bf16)], parts=3,
    )(block_slot, scal, message, attn_g[0], attn_1, attn_2))
    both, messages[1] = lax.optimization_barrier((both, messages[1]))
    both_2, both_1 = permute(both, "head", 2), permute(both, "head", 1)
    both_3 = permute(both_2, "head", 1)
    messages = [messages[0]] + [permute(messages[k], "dp", 2 * k) for k in range(1, ranks // 2)]
    own, other = call(
        pair_sum_kernel, "pair_sum", 0, ranks // 2, [SDS((slots, rows, 256), f32), SDS((slots, rows, 256), bf16)]
    )(*messages)
    other = permute(other, "dp", 1)
    shape = SDS((tokens.shape[1], parts, dim), f32)
    output, token_grad = pl.pallas_call(
        assemble_kernel,
        grid=(1,),
        in_specs=[SM] + [whole(*both.shape)] * parts,
        out_specs=[whole(*shape.shape)] * 2,
        out_shape=[shape, shape],
        scratch_shapes=[pltpu.VMEM((parts, 224, dim), bf16)],
        compiler_params=pltpu.CompilerParams(vmem_limit_bytes=16 << 20),
        cost_estimate=pl.CostEstimate(flops=1000000000, transcendentals=0, bytes_accessed=3000000),
        name="assemble",
    )(scal, both, both_1, both_2, both_3)
    other, output, token_grad = lax.optimization_barrier((other, output, token_grad))
    state = [
        swap(master), swap(master_m1), swap(master_m2), norm_params, norm_m1, norm_m2,
        swap(talk), swap(talk_m1), swap(talk_m2), conv, conv_m1, conv_m2,
    ]
    shapes = [SDS(t.shape, f32) for t in state]
    shapes.insert(3, SDS(state[0].shape, bf16))
    new = staged(
        update_kernel, "update", [own, other, *state], shapes,
        [pltpu.VMEM((rows, slots, dim), f32), pltpu.VMEM((slots, 64, 256), f32), pltpu.VMEM((64, 256), f32)],
    )
    new = [swap(t) if t.ndim == 3 else t for t in new]
    return (swap(output), swap(token_grad), *new)


def solution(mesh):
    in_specs = (
        P("dp", None, None),
        P("dp", None, None),
        P("dp"),
        P(),
        P(),
        P(),
        P("dp", None, "head"),
        P("dp", None, "head"),
        P("dp", None, "head"),
        P(),
        P(),
        P(),
        P(),
        P(),
        P(),
        P(None, "head"),
        P(None, "head"),
        P(None, "head"),
    )
    out_specs = (
        P("dp", None, None),
        P("dp", None, None),
        P("dp", None, "head"),
        P("dp", None, "head"),
        P("dp", None, "head"),
        P("dp", None, "head"),
        P(),
        P(),
        P(),
        P(),
        P(),
        P(),
        P(None, "head"),
        P(None, "head"),
        P(None, "head"),
    )
    return jax.shard_map(local, mesh=mesh, in_specs=in_specs, out_specs=out_specs, check_vma=False)
```

```python
import functools
import jax
import jax.numpy as jnp
from jax import lax
from jax.experimental import pallas as pl
from jax.experimental.pallas import tpu as pltpu
from jax.sharding import PartitionSpec as P

HD = 18
SIDE = 14
PITCH = 16
MARGIN = 24
FREE = 216
WIDE = 40
norm_eps = 1e-05
bf16 = jnp.bfloat16
f32 = jnp.float32


def nn(a, b):
    return lax.dot_general(a, b, (((1,), (0,)), ((), ())), preferred_element_type=f32)


def nt(a, b):
    return lax.dot_general(a, b, (((1,), (1,)), ((), ())), preferred_element_type=f32)


def tn(a, b):
    return lax.dot_general(a, b, (((0,), (0,)), ((), ())), preferred_element_type=f32)


def iota(shape, dim):
    return lax.broadcasted_iota(jnp.int32, shape, dim)


def split2(v):
    hi = v.astype(bf16)
    return hi, (v - hi.astype(f32)).astype(bf16)


def real_rows(shape):
    return (iota(shape, 0) & (PITCH - 1)) < SIDE


def lane_head(shape, dim, place):
    lane = iota(shape, dim)
    rest = lane & 63
    head = ((lane >> 6) ^ place) * 3 + (rest >= 18).astype(jnp.int32) + (rest >= 36).astype(jnp.int32)
    return jnp.where(rest < 54, head, -1)


def true_head(rows, place):
    return ((rows // (3 * PITCH)) ^ place) * 3 + (rows // PITCH) % 3


def prep_kernel(scal, tok_ref, cot_ref, norm_ref, talk_ref, x_ref, a_ref, dy_ref, mix_ref, bias_ref, tmp_ref):
    x_ref[...] = jnp.zeros_like(x_ref)
    dy_ref[...] = jnp.zeros_like(dy_ref)
    valid = (scal[0] < scal[1]).astype(f32)
    tmp_ref[...] = tok_ref[0].astype(f32)
    for y in range(SIDE):
        x_ref[PITCH * y : PITCH * y + SIDE, :] = tmp_ref[SIDE * y : SIDE * (y + 1), :]
        dy_ref[PITCH * y : PITCH * y + SIDE, :] = cot_ref[0, SIDE * y : SIDE * (y + 1), :] * valid
    x = x_ref[...]
    centred = x - jnp.mean(x, axis=-1, keepdims=True)
    inv = lax.rsqrt(jnp.mean(centred * centred, axis=-1, keepdims=True) + norm_eps)
    a = centred * inv * norm_ref[0:1, :] + norm_ref[1:2, :]
    a_ref[...] = jnp.where(real_rows(a.shape), a, 0.0).astype(bf16)
    heads = talk_ref.shape[1]
    n = heads * PITCH
    ex = (true_head(iota((n, heads), 0), scal[0]) == iota((n, heads), 1)).astype(bf16)
    el = (lane_head((256, heads), 0, scal[0]) == iota((256, heads), 1)).astype(bf16)
    for i in range(2):
        both = []
        for part in split2(talk_ref[i]):
            if i == 0:
                both.append(nt(nn(ex, part).astype(bf16), el))
            else:
                both.append(nt(nt(ex, part).astype(bf16), el))
        mix_ref[i] = (both[0] + both[1]) * (HD**-0.5 if i == 0 else 1.0)
    bias_ref[...] = jnp.where(real_rows(bias_ref.shape), 0.0, -1e30)


def load_weight(dst_ref, w_refs, b):
    for k, w_ref in enumerate(w_refs):
        dst_ref[64 * k : 64 * k + 54, :] = w_ref[b]


def tiled(rows, heads):
    return jnp.concatenate([rows] * heads, axis=0)


def over_heads(rows, heads):
    return jnp.sum(rows.reshape(heads, PITCH, rows.shape[1]), axis=0)


def attn_fwd_kernel(scal, x_ref, a_ref, mix_ref, bias_ref, *refs, parts, unroll):
    w_refs, refs = refs[:parts], refs[parts:]
    mid_ref, q_ref, k_ref, v_ref, o_ref, qw_ref, p_ref, pv_ref, ws_ref, t_ref = refs
    heads = mix_ref.shape[1] // PITCH
    a = a_ref[...]
    ws_ref[...] = jnp.zeros_like(ws_ref)
    for b, dst in enumerate((q_ref, k_ref, v_ref)):
        load_weight(ws_ref.at[b], w_refs, b)
        dst[...] = nt(a, ws_ref[b]).astype(bf16)
    load_weight(ws_ref.at[3], w_refs, 3)
    head = lane_head((1, 256), 1, scal[0])
    keep = ((head >= 0) & (head < scal[2])).astype(f32)

    def groups(b, _):
        ys = [b * unroll + u for u in range(unroll)]
        rows = [pl.ds(pl.multiple_of(y * PITCH, PITCH), PITCH) for y in ys]
        for u, y in enumerate(ys):
            qw_ref[y] = (tiled(q_ref[rows[u], :].astype(f32), heads) * mix_ref[0]).astype(bf16)
        for u, y in enumerate(ys):
            t_ref[u] = nt(k_ref[...], qw_ref[y]) + bias_ref[...]
        for u, y in enumerate(ys):
            t = t_ref[u]
            e = jnp.exp(t - jnp.max(t, axis=0, keepdims=True))
            p_ref[y] = (e * (1.0 / jnp.sum(e, axis=0, keepdims=True))).astype(bf16)
        for u, y in enumerate(ys):
            pv = tn(p_ref[y], v_ref[...])
            pv_ref[y] = pv.astype(bf16)
            o_ref[rows[u], :] = (over_heads(pv * mix_ref[1], heads) * keep).astype(bf16)
        return 0

    lax.fori_loop(0, SIDE // unroll, groups, 0)
    mid_ref[...] = x_ref[...] + nn(o_ref[...], ws_ref[3])


def ln_stats(v):
    centred = v - jnp.mean(v, axis=-1, keepdims=True)
    inv = lax.rsqrt(jnp.mean(centred * centred, axis=-1, keepdims=True) + norm_eps)
    return centred * inv, inv


def ln_back(grad, scaled, inv, gain):
    gs = grad * gain
    return inv * (
        gs - jnp.mean(gs, axis=-1, keepdims=True) - scaled * jnp.mean(gs * scaled, axis=-1, keepdims=True)
    )


def in_free_lanes(flat, dst_ref, first_row):
    rows = flat.shape[0]
    for j in range(6):
        dst_ref[first_row + rows * j : first_row + rows * (j + 1), :] = pltpu.roll(flat, (FREE - WIDE * j) % 256, 1)


def from_free_lanes(src_ref, first_row, rows):
    lane = iota((rows, 256), 1)
    flat = jnp.zeros((rows, 256), f32)
    for j in range(6):
        moved = pltpu.roll(src_ref[first_row + rows * j : first_row + rows * (j + 1), :], (WIDE * j - FREE) % 256, 1)
        flat = flat + jnp.where((lane >= WIDE * j) & (lane < WIDE * (j + 1)), moved, 0.0)
    return flat


def place(rows=216):
    shape = (rows, 256)
    lane = iota(shape, 1)
    rest = lane & 63
    return ((iota(shape, 0) == (lane >> 6) * 54 + rest) & (rest < 54)).astype(bf16)


def ffn_kernel(scal, mid_ref, dy_ref, norm_ref, o_ref, *refs, parts):
    w_refs, refs = refs[:parts], refs[parts:]
    out_ref, dmid_ref, gn_ref = refs[:3]
    gw_refs, refs = refs[3 : 3 + parts], refs[3 + parts :]
    win_ref, wdn_ref, h_ref, d_ref, gate_ref, dh_ref, cv_ref, gcv_ref, tmp_ref, sm_ref, down_ref, dw_ref = refs
    pm = place(256)
    mid = mid_ref[...]
    tokens, dim = mid.shape
    z, inv = ln_stats(mid)
    rows = real_rows(mid.shape)
    w = jnp.where(rows, z * norm_ref[2:3, :] + norm_ref[3:4, :], 0.0).astype(bf16)
    dy = dy_ref[...]
    e = dy.astype(bf16)
    pad = MARGIN
    zero = jnp.zeros((pad, 128), f32)
    lane = iota((1, 128), 1)
    free = iota((54, 256), 1) >= FREE
    for h in range(parts):
        for j in range(4):
            at = 64 * j
            win_ref[h, at : at + 54, :] = w_refs[h][j]
            wdn_ref[h, at : at + 54, :] = w_refs[h][4 + j]
            win_ref[h, at + 54 : at + 64, :] = jnp.zeros((10, dim), bf16)
            wdn_ref[h, at + 54 : at + 64, :] = jnp.zeros((10, dim), bf16)
        both = nn(w_refs[h][8], pm[0:dim])
        cv_ref[:, 256 * h : 256 * (h + 1)] = both[0:9] + both[16:25]
    def up(h):
        hidden = nt(w, win_ref[h])
        dgate = nt(e, wdn_ref[h])
        for half in range(2):
            c = 2 * h + half
            mine = slice(128 * half, 128 * (half + 1))
            for ref, value in ((h_ref, hidden), (d_ref, dgate)):
                ref[c, 0:pad, :] = zero
                ref[c, pad + tokens :, :] = zero
                ref[c, pad : pad + tokens, :] = value[:, mine]

    def middle(h):
        for half in range(2):
            c = 2 * h + half
            cols = slice(128 * c, 128 * (c + 1))
            mine = slice(128 * half, 128 * (half + 1))
            glane = lane + 128 * c
            unit = (((glane >> 8) ^ scal[0]) * 4 + ((glane >> 6) & 3)) * 54 + (glane & 63)
            keep = (unit < scal[3]).astype(f32)
            act = None
            for t in range(9):
                off = pad + PITCH * (t // 3 - 1) + t % 3 - 1
                term = cv_ref[t : t + 1, cols] * h_ref[c, off : off + tokens, :]
                act = term if act is None else act + term
            sig = 0.5 * jnp.tanh(0.5 * act) + 0.5
            silu = act * sig
            gate_ref[h, :, mine] = (silu * keep).astype(bf16)
            dact = d_ref[c, pad : pad + tokens, :] * keep * (silu + sig * (1.0 - silu))
            d_ref[c, pad : pad + tokens, :] = dact
            dh = None
            for t in range(9):
                shift = PITCH * (t // 3 - 1) + t % 3 - 1
                gcv_ref[t : t + 1, cols] = jnp.sum(
                    dact * h_ref[c, pad + shift : pad + shift + tokens, :], axis=0, keepdims=True
                )
                term = cv_ref[t : t + 1, cols] * d_ref[c, pad - shift : pad - shift + tokens, :]
                dh = term if dh is None else dh + term
            dh_ref[h, :, mine] = dh.astype(bf16)

    def back(h):
        gi = tn(dh_ref[h], w).astype(bf16)
        gd = tn(gate_ref[h], e).astype(bf16)
        for j in range(4):
            gw_refs[h][1 + j, :, 0:dim] = gi[64 * j : 64 * j + 54]
            gw_refs[h][5 + j, :, 0:dim] = gd[64 * j : 64 * j + 54]
        in_free_lanes(nt(gcv_ref[:, 256 * h : 256 * (h + 1)].astype(bf16), pm), sm_ref.at[h], 0)
        gw_refs[h][0] = jnp.where(free, sm_ref[h, 0:54, :], 0.0).astype(bf16)

    for h in range(parts):
        up(h)
    for h in range(parts):
        middle(h)
    down_ref[...] = sum(nn(gate_ref[h], wdn_ref[h]) for h in range(parts))
    dw_ref[...] = sum(nn(dh_ref[h], win_ref[h]) for h in range(parts))
    for h in range(parts):
        back(h)
    valid = (scal[0] < scal[1]).astype(f32)
    tmp_ref[...] = (mid + down_ref[...]) * valid
    for y in range(SIDE):
        out_ref[SIDE * y : SIDE * (y + 1), :] = tmp_ref[PITCH * y : PITCH * y + SIDE, :].astype(bf16)
    dw = jnp.where(rows, dw_ref[...], 0.0)
    gn_ref[...] = jnp.zeros_like(gn_ref)
    gn_ref[0:1, :] = jnp.sum(dw * z, axis=0, keepdims=True)
    gn_ref[1:2, :] = jnp.sum(dw, axis=0, keepdims=True)
    dmid = dy + ln_back(dw, z, inv, norm_ref[2:3, :])
    dmid_ref[...] = dmid
    go = tn(o_ref[...], dmid.astype(bf16)).astype(bf16)
    for h in range(parts):
        gw_refs[h][0, :, 0:dim] = go[64 * h : 64 * h + 54]


def scores_back_kernel(
    scal, dmid_ref, mix_ref, q_ref, k_ref, v_ref, qw_ref, p_ref, pv_ref, *refs, parts, part
):
    heads = mix_ref.shape[1] // PITCH
    n = heads * PITCH
    if part == 0:
        w_refs, refs = refs[:parts], refs[parts:]
        do_ref, gq_ref, gk_ref, gv_ref, g0_ref, g1_ref, wo_ref, dw_ref, dp_ref, dt_ref = refs
        wo_ref[...] = jnp.zeros_like(wo_ref)
        load_weight(wo_ref, w_refs, 3)
        f = dmid_ref[...].astype(bf16)
        head = lane_head((1, 256), 1, scal[0])
        keep = ((head >= 0) & (head < scal[2])).astype(f32)
        do_ref[...] = (nt(f, wo_ref[...]) * keep).astype(bf16)
        for ref in (gk_ref, gv_ref, g0_ref, g1_ref):
            ref[...] = jnp.zeros_like(ref)
    else:
        do_ref, *sums, gq_ref, gkb_ref, gvb_ref, gt_ref, gk_ref, gv_ref, g0_ref, g1_ref, dw_ref, dp_ref, dt_ref = refs
        for ref, old in zip((gk_ref, gv_ref, g0_ref, g1_ref), sums):
            ref[...] = old[...]
    first = SIDE // 2 * part

    ys = [first + u for u in range(SIDE // 2)]
    rows = [slice(PITCH * y, PITCH * (y + 1)) for y in ys]
    for u, y in enumerate(ys):
        dw_ref[u] = (tiled(do_ref[rows[u], :].astype(f32), heads) * mix_ref[1]).astype(bf16)
    for u, y in enumerate(ys):
        dp_ref[u] = nt(v_ref[...], dw_ref[u])
    for u, y in enumerate(ys):
        dp = dp_ref[u]
        p = p_ref[y].astype(f32)
        dt_ref[u] = (p * (dp - jnp.sum(dp * p, axis=0, keepdims=True))).astype(bf16)
    gv_ref[...] += sum(nn(p_ref[y], dw_ref[u]) for u, y in enumerate(ys))
    gk_ref[...] += sum(nn(dt_ref[u], qw_ref[y]) for u, y in enumerate(ys))
    for u, y in enumerate(ys):
        dk = tn(dt_ref[u], k_ref[...])
        gq_ref[PITCH * u : PITCH * (u + 1), :] = over_heads(dk * mix_ref[0], heads).astype(bf16)
        g0_ref[...] += dk * tiled(q_ref[rows[u], :].astype(f32), heads)
    for u, y in enumerate(ys):
        g1_ref[...] += pv_ref[y].astype(f32) * tiled(do_ref[rows[u], :].astype(f32), heads)
    if part == 0:
        return
    gkb_ref[...] = gk_ref[...].astype(bf16)
    gvb_ref[...] = gv_ref[...].astype(bf16)
    ex = (true_head(iota((n, heads), 0), scal[0]) == iota((n, heads), 1)).astype(bf16)
    el = (lane_head((256, heads), 0, scal[0]) == iota((256, heads), 1)).astype(bf16)
    for i, ref in enumerate((g0_ref, g1_ref)):
        hi, lo = split2(ref[...])
        hi, lo = split2(nn(hi, el) + nn(lo, el))
        if i == 0:
            gt_ref[i] = (tn(ex, hi) + tn(ex, lo)) * HD**-0.5
        else:
            gt_ref[i] = tn(hi, ex) + tn(lo, ex)


def weights_back_kernel(
    scal, x_ref, a_ref, dmid_ref, norm_ref, gn2_ref, gqa_ref, gqb_ref, gk_ref, gv_ref, gt_ref, y_ref, *refs, parts
):
    w_refs, refs = refs[:parts], refs[parts:]
    both_ref, gw_refs, refs = refs[0], refs[1 : 1 + parts], refs[1 + parts :]
    ws_ref, tmp_ref, flat_ref, sm_ref = refs
    heads = gt_ref.shape[1]
    dim = x_ref.shape[1]
    ws_ref[...] = jnp.zeros_like(ws_ref)
    for b in range(3):
        load_weight(ws_ref.at[b], w_refs, b)
    gq = jnp.concatenate([gqa_ref[...], gqb_ref[...]], axis=0)
    gk, gv = gk_ref[...], gv_ref[...]
    a = a_ref[...]
    da = nn(gq, ws_ref[0]) + nn(gk, ws_ref[1]) + nn(gv, ws_ref[2])
    z, inv = ln_stats(x_ref[...])
    flat_ref[...] = jnp.zeros_like(flat_ref)
    flat_ref[0:1, 0:dim] = jnp.sum(da * z, axis=0, keepdims=True)
    flat_ref[1:2, 0:dim] = jnp.sum(da, axis=0, keepdims=True)
    flat_ref[2:4, 0:dim] = gn2_ref[0:2, :]
    for i in range(2):
        flat_ref[8 : 8 + heads, 128 * i : 128 * i + heads] = gt_ref[i]
    sm_ref[...] = jnp.zeros_like(sm_ref)
    in_free_lanes(flat_ref[0:4, :], sm_ref, 0)
    mix = flat_ref[8 : 8 + heads, :]
    first = iota(mix.shape, 1) < 128
    mix = jnp.where(first, mix, 0.0) + pltpu.roll(jnp.where(first, 0.0, mix), 128 + heads, 1)
    sm_ref[24 : 24 + heads, :] = pltpu.roll(mix, FREE, 1)
    small = jnp.where(iota((54, 256), 1) >= FREE, sm_ref[0:54, :], 0.0).astype(bf16)
    for h in range(parts):
        gw_refs[h][0] = small
    for b, g in enumerate((gq, gk, gv)):
        gw = tn(g, a).astype(bf16)
        for h in range(parts):
            gw_refs[h][b, :, 0:dim] = gw[64 * h : 64 * h + 54]
    tmp_ref[...] = dmid_ref[...] + ln_back(da, z, inv, norm_ref[0:1, :])
    for y in range(SIDE):
        both_ref[1, SIDE * y : SIDE * (y + 1), :] = tmp_ref[PITCH * y : PITCH * y + SIDE, :].astype(bf16)
    both_ref[0] = y_ref[...]


def cast_kernel(m_hbm, out_ref, m_ref, sem):
    copy = pltpu.make_async_copy(m_hbm, m_ref, sem)
    copy.start()
    copy.wait()
    for i in range(out_ref.shape[0]):
        out_ref[i] = m_ref[:, i, :].astype(bf16)


def pair_kernel(own_ref, other_ref, out_ref):
    out_ref[0] = own_ref[...]
    out_ref[1] = other_ref[...]


def select_kernel(slot_ref, scal, conv_ref, *refs):
    pairs, (attn_ref, ffn_ref, every_ref) = refs[:-3], refs[-3:]
    for k, ref in enumerate(pairs):
        every_ref[scal[5] ^ k] = ref[...]
    per = every_ref.shape[2]
    for b in range(12):
        slot = slot_ref[b]
        rank = slot // per
        block = every_ref[rank // 2, (rank % 2) ^ scal[4], slot % per]
        if b < 4:
            attn_ref[b] = block
        else:
            ffn_ref[b - 4] = block
    hi, lo = split2(conv_ref[...])
    ffn_ref[8] = jnp.zeros_like(ffn_ref[8])
    ffn_ref[8, 0:9] = hi
    ffn_ref[8, 16:25] = lo


def total(refs, at):
    acc = refs[0][at].astype(f32)
    for ref in refs[1:]:
        acc = acc + ref[at].astype(f32)
    return acc


def half_sum_kernel(a_ref, b_ref, out_ref):
    out_ref[...] = (a_ref[...].astype(f32) + b_ref[...].astype(f32)).astype(bf16)


def spot(slot, scal, per):
    rank = slot // per
    return (rank // 2) ^ scal[5], (rank % 2) ^ scal[4], slot % per


def spread_ffn_kernel(slot_ref, scal, *refs):
    ffn_refs, out_ref = refs[:-1], refs[-1]
    pairs, _, per = out_ref.shape[:3]
    out_ref[...] = jnp.zeros_like(out_ref)
    for b in range(9):
        block = total(ffn_refs, b)
        k, j, i = spot(slot_ref[3 + b], scal, per)
        out_ref[k, j, i, :, 0:FREE] = block[:, 0:FREE].astype(bf16)
        if b == 0:
            wide = block[:, FREE:].astype(bf16)
    for k in range(pairs):
        for j in range(2):
            out_ref[k, j, 0, :, FREE:] = wide


def spread_attn_kernel(slot_ref, scal, old_ref, *refs, parts):
    attn, outs, all_ref = refs[:parts], refs[parts:-1], refs[-1]
    pairs, _, per = all_ref.shape[:3]
    all_ref[...] = old_ref[...]
    for b in range(3):
        block = total(attn, b)
        k, j, i = spot(slot_ref[b], scal, per)
        all_ref[k, j, i, :, 0:FREE] = block[:, 0:FREE].astype(bf16)
        if b == 0:
            wide = block[:, FREE:].astype(bf16)
    for k in range(pairs):
        outs[k][...] = all_ref[k]
        for j in range(2):
            outs[k][j, 1, :, FREE:] = wide


def pair_sum_kernel(*refs):
    own_ref, other_ref = refs[-2:]
    own_ref[...] = total(refs[:-2], 0)
    other_ref[...] = total(refs[:-2], 1).astype(bf16)


def adam(w, g, one, two, rate, decay):
    one_new = 0.5 * one + 0.5 * g
    two_new = 0.5 * two + 0.5 * g * g
    hat_one = one_new / (1.0 - 0.5**3)
    hat_two = two_new / (1.0 - 0.5**3)
    return w - rate * (hat_one / (jnp.sqrt(hat_two) + 1e-08) + decay * w), one_new, two_new


def update_kernel(own_ref, other_ref, *refs):
    ins, outs, (g_ref, sm_ref, flat_ref) = refs[0:12], refs[12:25], refs[25:]
    per, rows = own_ref.shape[:2]
    dim = ins[0].shape[2]
    for i in range(per):
        g = own_ref[i] + other_ref[i].astype(f32)
        g_ref[:, i, :] = g[:, 0:dim]
        sm_ref[i, 0:rows, :] = g
    w, one, two = adam(ins[0][...], g_ref[...], ins[1][...], ins[2][...], 0.06, 0.05)
    outs[0][...], outs[1][...], outs[2][...], outs[3][...] = w, one, two, w.astype(bf16)
    heads = ins[6].shape[0]
    flat_ref[0:9, :] = from_free_lanes(sm_ref.at[0], 0, 9)
    flat_ref[16:20, :] = from_free_lanes(sm_ref.at[1], 0, 4)
    mix = pltpu.roll(sm_ref[1, 24 : 24 + heads, :], 256 - FREE, 1)
    flat_ref[32 : 32 + heads, :] = mix
    flat_ref[48 : 48 + heads, :] = pltpu.roll(mix, 256 - heads, 1)
    outs[4][...], outs[5][...], outs[6][...] = adam(
        ins[3][...], flat_ref[16:20, 0:dim], ins[4][...], ins[5][...], 0.2, 0.0
    )
    for i in range(2):
        w, one, two = adam(
            ins[6][:, i, :], flat_ref[16 * (i + 2) : 16 * (i + 2) + heads, 0:heads], ins[7][:, i, :], ins[8][:, i, :],
            0.2, 0.0,
        )
        outs[7][:, i, :], outs[8][:, i, :], outs[9][:, i, :] = w, one, two
    outs[10][...], outs[11][...], outs[12][...] = adam(
        ins[9][...], flat_ref[0:9, 0:dim], ins[10][...], ins[11][...], 0.2, 0.05
    )


def assemble_kernel(scal, *refs):
    ins, outs, (all_ref,) = refs[:-3], refs[-3:-1], refs[-1:]
    parts, tokens = len(ins), ins[0].shape[1]
    step = 32
    shape = (parts * step, parts * step)
    row, col = iota(shape, 0), iota(shape, 1)
    pick = ((row // parts == col % step) & (row % parts == col // step)).astype(bf16)
    full = all_ref.shape[1]
    for k in range(parts):
        all_ref[k, tokens // step * step : full, :] = jnp.zeros((full - tokens // step * step, all_ref.shape[2]), bf16)
    for i, out_ref in enumerate(outs):
        for k, ref in enumerate(ins):
            all_ref[scal[0] ^ k, 0:tokens, :] = ref[i]
        for at in range(0, tokens, step):
            mixed = nn(pick, jnp.concatenate([all_ref[k, at : at + step, :] for k in range(parts)], axis=0))
            for t in range(min(step, tokens - at)):
                out_ref[at + t] = mixed[parts * t : parts * (t + 1)]


VM = pl.BlockSpec(memory_space=pltpu.VMEM)
SM = pl.BlockSpec(memory_space=pltpu.SMEM)
SDS = jax.ShapeDtypeStruct


def call(body, name, n_scalar, n_in, out_shape, scratch=(), mb=16, micros=1, **kw):
    return pl.pallas_call(
        functools.partial(body, **kw) if kw else body,
        in_specs=[SM] * n_scalar + [VM] * n_in,
        out_specs=[VM] * len(out_shape),
        out_shape=out_shape,
        scratch_shapes=scratch,
        compiler_params=pltpu.CompilerParams(vmem_limit_bytes=mb << 20),
        cost_estimate=pl.CostEstimate(flops=micros * 1000000000, transcendentals=0, bytes_accessed=micros * 3000000),
        name=name,
    )


def prep(scal, tokens, cotangent, norm_params, talk):
    tok, dim = tokens.shape[1], tokens.shape[2]
    pad = SIDE * PITCH
    heads = talk.shape[1]
    n = heads * PITCH
    full = lambda *s: pl.BlockSpec(s, lambda i, sc: (0,) * len(s))
    return pl.pallas_call(
        prep_kernel,
        grid_spec=pltpu.PrefetchScalarGridSpec(
            num_scalar_prefetch=1,
            grid=(1,),
            in_specs=[
                pl.BlockSpec((1, tok, dim), lambda i, sc: (sc[0], 0, 0)),
                pl.BlockSpec((1, tok, dim), lambda i, sc: (sc[0], 0, 0)),
                full(*norm_params.shape),
                full(*talk.shape),
            ],
            out_specs=[full(pad, dim), full(pad, dim), full(pad, dim), full(2, n, 256), full(pad, n)],
            scratch_shapes=[pltpu.VMEM((tok, dim), f32)],
        ),
        out_shape=[SDS((pad, dim), f32), SDS((pad, dim), bf16), SDS((pad, dim), f32), SDS((2, n, 256), f32),
                   SDS((pad, n), f32)],
        compiler_params=pltpu.CompilerParams(vmem_limit_bytes=16 << 20),
        cost_estimate=pl.CostEstimate(flops=1000000000, transcendentals=0, bytes_accessed=3000000),
        name="prep",
    )(scal, tokens, cotangent, norm_params, talk)


def attn_fwd(scal, x, a, mix, bias, w, unroll=14):
    pad, dim = x.shape
    n = mix.shape[1]
    return call(
        attn_fwd_kernel, "attn_fwd", 1, 4 + len(w),
        [SDS((pad, dim), f32)] + [SDS((pad, 256), bf16)] * 4
        + [SDS((SIDE, n, 256), bf16), SDS((SIDE, pad, n), bf16), SDS((SIDE, n, 256), bf16)],
        [pltpu.VMEM((4, 256, dim), bf16), pltpu.VMEM((unroll, pad, n), f32)],
        mb=24, micros=1, parts=len(w), unroll=unroll,
    )(scal, x, a, mix, bias, *w)


def ffn(scal, mid, dy, norm_params, o, w):
    pad, dim = mid.shape
    lanes = len(w) * 256
    return call(
        ffn_kernel, "ffn", 1, 4 + len(w),
        [SDS((SIDE * SIDE, dim), bf16), SDS((pad, dim), f32), SDS((8, dim), f32)] + [SDS((9, 54, 256), bf16)] * len(w),
        [
            pltpu.VMEM((len(w), 256, dim), bf16), pltpu.VMEM((len(w), 256, dim), bf16),
            pltpu.VMEM((lanes // 128, pad + 2 * MARGIN, 128), f32), pltpu.VMEM((lanes // 128, pad + 2 * MARGIN, 128), f32),
            pltpu.VMEM((len(w), pad, 256), bf16), pltpu.VMEM((len(w), pad, 256), bf16),
            pltpu.VMEM((9, lanes), f32), pltpu.VMEM((9, lanes), f32), pltpu.VMEM((pad, dim), f32),
            pltpu.VMEM((len(w), 56, 256), f32), pltpu.VMEM((pad, dim), f32), pltpu.VMEM((pad, dim), f32),
        ],
        mb=24, micros=6, parts=len(w),
    )(scal, mid, dy, norm_params, o, *w)


def scores_back(scal, dmid, mix, q, k, v, qw, p, pv, more, part):
    pad, dim = dmid.shape
    n = mix.shape[1]
    heads = n // PITCH
    sums = [SDS((pad, 256), f32)] * 2 + [SDS((n, 256), f32)] * 2
    half = SDS((pad // 2, 256), bf16)
    if part == 0:
        outs = [SDS((pad, 256), bf16), half] + sums
        scratch = [pltpu.VMEM((256, dim), bf16)]
    else:
        outs = [half] + [SDS((pad, 256), bf16)] * 2 + [SDS((2, heads, heads), f32)]
        scratch = [pltpu.VMEM(t.shape, f32) for t in sums]
    scratch += [
        pltpu.VMEM((SIDE // 2, n, 256), bf16), pltpu.VMEM((SIDE // 2, pad, n), f32), pltpu.VMEM((SIDE // 2, pad, n), bf16)
    ]
    return call(
        scores_back_kernel, "scores_back", 1, 8 + len(more), outs, scratch,
        mb=24, micros=4, parts=len(more), part=part,
    )(scal, dmid, mix, q, k, v, qw, p, pv, *more)


def weights_back(scal, x, a, dmid, norm_params, gn2, gqa, gqb, gk, gv, gt, out, w):
    pad, dim = x.shape
    return call(
        weights_back_kernel, "weights_back", 1, 11 + len(w),
        [SDS((2, SIDE * SIDE, dim), bf16)] + [SDS((3, 54, 256), bf16)] * len(w),
        [pltpu.VMEM((3, 256, dim), bf16), pltpu.VMEM((pad, dim), f32), pltpu.VMEM((24, 256), f32),
         pltpu.VMEM((56, 256), f32)],
        mb=24, micros=3, parts=len(w),
    )(scal, x, a, dmid, norm_params, gn2, gqa, gqb, gk, gv, gt, out, *w)


def permute(x, axis, k):
    return lax.ppermute(x, axis, [(i, i ^ k) for i in range(lax.axis_size(axis))])


def swap(t):
    return jnp.swapaxes(t, 0, 1)


def whole(*shape):
    return pl.BlockSpec(shape, lambda i: (0,) * len(shape))


def staged(body, name, ins, outs, scratch=(), micros=1):
    return pl.pallas_call(
        body,
        grid=(1,),
        in_specs=[whole(*t.shape) for t in ins],
        out_specs=[whole(*t.shape) for t in outs],
        out_shape=outs,
        scratch_shapes=scratch,
        compiler_params=pltpu.CompilerParams(vmem_limit_bytes=16 << 20),
        cost_estimate=pl.CostEstimate(flops=micros * 1000000000, transcendentals=0, bytes_accessed=micros * 3000000),
        name=name,
    )(*ins)


def local(
    tokens, cotangent, image_count, subnet_heads, subnet_width, block_slot,
    master, master_m1, master_m2, norm_params, norm_m1, norm_m2, talk, talk_m1, talk_m2, conv, conv_m1, conv_m2,
):
    slots, rows, dim = master.shape
    parts = lax.axis_size("head")
    ranks = lax.axis_size("dp")
    place_id = lax.axis_index("head").astype(jnp.int32)
    rank = lax.axis_index("dp").astype(jnp.int32)
    scal = jnp.concatenate(
        [place_id[None], image_count, subnet_heads, subnet_width, (rank % 2)[None], (rank // 2)[None]]
    )
    mine = pl.pallas_call(
        cast_kernel,
        grid=(1,),
        in_specs=[pl.BlockSpec(memory_space=pltpu.HBM)],
        out_specs=whole(slots, rows, dim),
        out_shape=SDS((slots, rows, dim), bf16),
        scratch_shapes=[pltpu.VMEM((rows, slots, dim), f32), pltpu.SemaphoreType.DMA],
        compiler_params=pltpu.CompilerParams(vmem_limit_bytes=16 << 20),
        name="cast",
    )(swap(master))
    (pair,) = call(pair_kernel, "pair", 0, 2, [SDS((2, slots, rows, dim), bf16)])(mine, permute(mine, "dp", 1))
    pair, tokens, cotangent, talk_in = lax.optimization_barrier((pair, tokens, cotangent, talk))
    pairs = [pair] + [permute(pair, "dp", 2 * k) for k in range(1, ranks // 2)]
    x, a, dy, mix, bias = prep(scal, tokens, cotangent, norm_params, talk_in)
    pairs[1], x = lax.optimization_barrier((pairs[1], x))
    attn_w, ffn_w = call(
        select_kernel, "select", 2, 1 + len(pairs), [SDS((4, rows, dim), bf16), SDS((9, rows, dim), bf16)],
        [pltpu.VMEM((ranks // 2, 2, slots, rows, dim), bf16)],
    )(block_slot, scal, conv, *pairs)
    attn_2, attn_1 = permute(attn_w, "head", 2), permute(attn_w, "head", 1)
    attn_3 = permute(attn_2, "head", 1)
    attn_w = [attn_w, attn_1, attn_2, attn_3]
    ffn_2, ffn_1 = permute(ffn_w, "head", 2), permute(ffn_w, "head", 1)
    mid, q, k, v, o, qw, p, pv = attn_fwd(scal, x, a, mix, bias, attn_w)
    mid, ffn_2 = lax.optimization_barrier((mid, ffn_2))
    ffn_w = [ffn_w, ffn_1, ffn_2, permute(ffn_2, "head", 1)]
    out, dmid, gn2, *ffn_g = ffn(scal, mid, dy, norm_params, o, ffn_w)
    ffn_1, ffn_3 = permute(ffn_g[1], "head", 1), permute(ffn_g[3], "head", 1)
    do, gqa, *sums = scores_back(scal, dmid, mix, q, k, v, qw, p, pv, attn_w, 0)
    do, ffn_1, ffn_3 = lax.optimization_barrier((do, ffn_1, ffn_3))
    (half,) = call(half_sum_kernel, "half_sum", 0, 2, [SDS(ffn_3.shape, bf16)])(ffn_g[2], ffn_3)
    ffn_2 = permute(half, "head", 2)
    gqb, gk, gv, gt = scores_back(scal, dmid, mix, q, k, v, qw, p, pv, [do, *sums], 1)
    both, *attn_g = weights_back(scal, x, a, dmid, norm_params, gn2, gqa, gqb, gk, gv, gt, out, attn_w)
    attn_1, attn_3 = permute(attn_g[1], "head", 1), permute(attn_g[3], "head", 1)
    (half,) = call(half_sum_kernel, "half_sum", 0, 2, [SDS(attn_3.shape, bf16)])(attn_g[2], attn_3)
    attn_2 = permute(half, "head", 2)
    (message,) = call(
        spread_ffn_kernel, "spread_ffn", 2, 3, [SDS((ranks // 2, 2, slots, rows, 256), bf16)]
    )(block_slot, scal, ffn_g[0], ffn_1, ffn_2)
    messages = list(call(
        spread_attn_kernel, "spread_attn", 2, 4, [SDS(message.shape[1:], bf16)] * (ranks // 2),
        [pltpu.VMEM(message.shape, bf16)], parts=3,
    )(block_slot, scal, message, attn_g[0], attn_1, attn_2))
    both, messages[1] = lax.optimization_barrier((both, messages[1]))
    both_2, both_1 = permute(both, "head", 2), permute(both, "head", 1)
    both_3 = permute(both_2, "head", 1)
    messages = [messages[0]] + [permute(messages[k], "dp", 2 * k) for k in range(1, ranks // 2)]
    own, other = call(
        pair_sum_kernel, "pair_sum", 0, ranks // 2, [SDS((slots, rows, 256), f32), SDS((slots, rows, 256), bf16)]
    )(*messages)
    other = permute(other, "dp", 1)
    shape = SDS((tokens.shape[1], parts, dim), f32)
    output, token_grad = pl.pallas_call(
        assemble_kernel,
        grid=(1,),
        in_specs=[SM] + [whole(*both.shape)] * parts,
        out_specs=[whole(*shape.shape)] * 2,
        out_shape=[shape, shape],
        scratch_shapes=[pltpu.VMEM((parts, 224, dim), bf16)],
        compiler_params=pltpu.CompilerParams(vmem_limit_bytes=16 << 20),
        cost_estimate=pl.CostEstimate(flops=1000000000, transcendentals=0, bytes_accessed=3000000),
        name="assemble",
    )(scal, both, both_1, both_2, both_3)
    other, output, token_grad = lax.optimization_barrier((other, output, token_grad))
    state = [
        swap(master), swap(master_m1), swap(master_m2), norm_params, norm_m1, norm_m2,
        swap(talk), swap(talk_m1), swap(talk_m2), conv, conv_m1, conv_m2,
    ]
    shapes = [SDS(t.shape, f32) for t in state]
    shapes.insert(3, SDS(state[0].shape, bf16))
    new = staged(
        update_kernel, "update", [own, other, *state], shapes,
        [pltpu.VMEM((rows, slots, dim), f32), pltpu.VMEM((slots, 64, 256), f32), pltpu.VMEM((64, 256), f32)],
    )
    new = [swap(t) if t.ndim == 3 else t for t in new]
    return (swap(output), swap(token_grad), *new)


def solution(mesh):
    in_specs = (
        P("dp", None, None),
        P("dp", None, None),
        P("dp"),
        P(),
        P(),
        P(),
        P("dp", None, "head"),
        P("dp", None, "head"),
        P("dp", None, "head"),
        P(),
        P(),
        P(),
        P(),
        P(),
        P(),
        P(None, "head"),
        P(None, "head"),
        P(None, "head"),
    )
    out_specs = (
        P("dp", None, None),
        P("dp", None, None),
        P("dp", None, "head"),
        P("dp", None, "head"),
        P("dp", None, "head"),
        P("dp", None, "head"),
        P(),
        P(),
        P(),
        P(),
        P(),
        P(),
        P(None, "head"),
        P(None, "head"),
        P(None, "head"),
    )
    return jax.shard_map(local, mesh=mesh, in_specs=in_specs, out_specs=out_specs, check_vma=False)
```

```python
import functools
import jax
import jax.numpy as jnp
from jax import lax
from jax.experimental import pallas as pl
from jax.experimental.pallas import tpu as pltpu
from jax.sharding import PartitionSpec as P

HD = 18
SIDE = 14
PITCH = 16
MARGIN = 24
BUNCH = 4
EARLY = 4


def bunches(first, last):
    return [(y, min(BUNCH, last - y)) for y in range(first, last, BUNCH)]

FREE = 216
WIDE = 40
norm_eps = 1e-05
bf16 = jnp.bfloat16
f32 = jnp.float32


def nn(a, b):
    return lax.dot_general(a, b, (((1,), (0,)), ((), ())), preferred_element_type=f32)


def nt(a, b):
    return lax.dot_general(a, b, (((1,), (1,)), ((), ())), preferred_element_type=f32)


def tn(a, b):
    return lax.dot_general(a, b, (((0,), (0,)), ((), ())), preferred_element_type=f32)


def iota(shape, dim):
    return lax.broadcasted_iota(jnp.int32, shape, dim)


def split2(v):
    hi = v.astype(bf16)
    return hi, (v - hi.astype(f32)).astype(bf16)


def real_rows(shape):
    return (iota(shape, 0) & (PITCH - 1)) < SIDE


def lane_head(shape, dim, place):
    lane = iota(shape, dim)
    rest = lane & 63
    head = ((lane >> 6) ^ place) * 3 + (rest >= 18).astype(jnp.int32) + (rest >= 36).astype(jnp.int32)
    return jnp.where(rest < 54, head, -1)


def true_head(rows, place):
    head = rows >> 4
    part = (head >= 3).astype(jnp.int32) + (head >= 6).astype(jnp.int32) + (head >= 9).astype(jnp.int32)
    return (part ^ place) * 3 + (head - 3 * part)


def prep_kernel(scal, tok_ref, cot_ref, norm_ref, talk_ref, x_ref, a_ref, dy_ref, mix_ref, bias_ref, tmp_ref):
    x_ref[...] = jnp.zeros_like(x_ref)
    dy_ref[...] = jnp.zeros_like(dy_ref)
    valid = (scal[0] < scal[1]).astype(f32)
    tmp_ref[...] = tok_ref[0].astype(f32)
    for y in range(SIDE):
        x_ref[PITCH * y : PITCH * y + SIDE, :] = tmp_ref[SIDE * y : SIDE * (y + 1), :]
        dy_ref[PITCH * y : PITCH * y + SIDE, :] = cot_ref[0, SIDE * y : SIDE * (y + 1), :] * valid
    x = x_ref[...]
    centred = x - jnp.mean(x, axis=-1, keepdims=True)
    inv = lax.rsqrt(jnp.mean(centred * centred, axis=-1, keepdims=True) + norm_eps)
    a = centred * inv * norm_ref[0:1, :] + norm_ref[1:2, :]
    a_ref[...] = jnp.where(real_rows(a.shape), a, 0.0).astype(bf16)
    heads = talk_ref.shape[1]
    n = heads * PITCH
    ex = (true_head(iota((n, heads), 0), scal[0]) == iota((n, heads), 1)).astype(bf16)
    el = (lane_head((256, heads), 0, scal[0]) == iota((256, heads), 1)).astype(bf16)
    for i in range(2):
        both = []
        for part in split2(talk_ref[i]):
            if i == 0:
                both.append(nt(nn(ex, part).astype(bf16), el))
            else:
                both.append(nt(nt(ex, part).astype(bf16), el))
        mix_ref[i] = (both[0] + both[1]) * (HD**-0.5 if i == 0 else 1.0)
    bias_ref[...] = jnp.where(real_rows(bias_ref.shape), 0.0, -1e30)


def load_weight(dst_ref, w_refs, b):
    for k, w_ref in enumerate(w_refs):
        dst_ref[64 * k : 64 * k + 54, :] = w_ref[b]


def tiled(rows, heads):
    return jnp.concatenate([rows] * heads, axis=0)


def over_heads(rows, heads):
    return jnp.sum(rows.reshape(heads, PITCH, rows.shape[1]), axis=0)


def attn_fwd_kernel(scal, x_ref, a_ref, mix_ref, bias_ref, *refs, parts):
    w_refs, refs = refs[:parts], refs[parts:]
    mid_ref, q_ref, k_ref, v_ref, o_ref, qw_ref, p_ref, pv_ref, ws_ref, t_ref = refs
    heads = mix_ref.shape[1] // PITCH
    a = a_ref[...]
    ws_ref[...] = jnp.zeros_like(ws_ref)
    for b, dst in enumerate((q_ref, k_ref, v_ref)):
        load_weight(ws_ref.at[b], w_refs, b)
        dst[...] = nt(a, ws_ref[b]).astype(bf16)
    load_weight(ws_ref.at[3], w_refs, 3)
    head = lane_head((1, 256), 1, scal[0])
    keep = ((head >= 0) & (head < scal[2])).astype(f32)

    n = heads * PITCH
    for y in range(SIDE):
        q = q_ref[PITCH * y : PITCH * (y + 1), :].astype(f32)
        qw_ref[n * y : n * (y + 1), :] = (tiled(q, heads) * mix_ref[0]).astype(bf16)
    for b, (y, count) in enumerate(bunches(0, SIDE)):
        t_ref[b, :, 0 : n * count] = nt(k_ref[...], qw_ref[n * y : n * (y + count), :])
    for b, (y, count) in enumerate(bunches(0, SIDE)):
        for at in range(0, n * count, 128):
            t = t_ref[b, :, at : at + 128] + bias_ref[...]
            e = jnp.exp(t - jnp.max(t, axis=0, keepdims=True))
            p_ref[b, :, at : at + 128] = (e * (1.0 / jnp.sum(e, axis=0, keepdims=True))).astype(bf16)
    for b, (first, count) in enumerate(bunches(0, SIDE)):
        pv = tn(p_ref[b, :, 0 : n * count], v_ref[...])
        pv_ref[n * first : n * (first + count), :] = pv.astype(bf16)
        for u in range(count):
            o = over_heads(pv[n * u : n * (u + 1)] * mix_ref[1], heads)
            o_ref[PITCH * (first + u) : PITCH * (first + u + 1), :] = (o * keep).astype(bf16)
    mid_ref[...] = x_ref[...] + nn(o_ref[...], ws_ref[3])


def ln_stats(v):
    centred = v - jnp.mean(v, axis=-1, keepdims=True)
    inv = lax.rsqrt(jnp.mean(centred * centred, axis=-1, keepdims=True) + norm_eps)
    return centred * inv, inv


def ln_back(grad, scaled, inv, gain):
    gs = grad * gain
    return inv * (
        gs - jnp.mean(gs, axis=-1, keepdims=True) - scaled * jnp.mean(gs * scaled, axis=-1, keepdims=True)
    )


def in_free_lanes(flat, dst_ref, first_row):
    rows = flat.shape[0]
    for j in range(6):
        dst_ref[first_row + rows * j : first_row + rows * (j + 1), :] = pltpu.roll(flat, (FREE - WIDE * j) % 256, 1)


def from_free_lanes(src_ref, first_row, rows):
    lane = iota((rows, 256), 1)
    flat = jnp.zeros((rows, 256), f32)
    for j in range(6):
        moved = pltpu.roll(src_ref[first_row + rows * j : first_row + rows * (j + 1), :], (WIDE * j - FREE) % 256, 1)
        flat = flat + jnp.where((lane >= WIDE * j) & (lane < WIDE * (j + 1)), moved, 0.0)
    return flat


def place(rows=216):
    shape = (rows, 256)
    lane = iota(shape, 1)
    rest = lane & 63
    return ((iota(shape, 0) == (lane >> 6) * 54 + rest) & (rest < 54)).astype(bf16)


def up(w_ref, w, e, win_ref, wdn_ref, h_ref, d_ref, cv_ref):
    tokens, dim = w.shape
    pad = MARGIN
    for j in range(4):
        at = 64 * j
        win_ref[at : at + 54, :] = w_ref[j]
        wdn_ref[at : at + 54, :] = w_ref[4 + j]
        win_ref[at + 54 : at + 64, :] = jnp.zeros((10, dim), bf16)
        wdn_ref[at + 54 : at + 64, :] = jnp.zeros((10, dim), bf16)
    both = nn(w_ref[8], place(dim))
    cv_ref[...] = both[0:9] + both[16:25]
    hidden = nt(w, win_ref[...])
    dgate = nt(e, wdn_ref[...])
    zero = jnp.zeros((pad, 128), f32)
    for half in range(2):
        mine = slice(128 * half, 128 * (half + 1))
        for ref, value in ((h_ref, hidden), (d_ref, dgate)):
            ref[half, 0:pad, :] = zero
            ref[half, pad + tokens :, :] = zero
            ref[half, pad : pad + tokens, :] = value[:, mine]


def middle(scal, k, h_ref, d_ref, gate_ref, dh_ref, cv_ref, gcv_ref):
    tokens = gate_ref.shape[0]
    pad = MARGIN
    for half in range(2):
        cols = slice(128 * half, 128 * (half + 1))
        lane = iota((1, 128), 1) + 128 * half
        unit = ((k ^ scal[0]) * 4 + (lane >> 6)) * 54 + (lane & 63)
        keep = (unit < scal[3]).astype(f32)
        act = None
        for t in range(9):
            off = pad + PITCH * (t // 3 - 1) + t % 3 - 1
            term = cv_ref[t : t + 1, cols] * h_ref[half, off : off + tokens, :]
            act = term if act is None else act + term
        sig = 0.5 * jnp.tanh(0.5 * act) + 0.5
        silu = act * sig
        gate_ref[:, cols] = (silu * keep).astype(bf16)
        dact = d_ref[half, pad : pad + tokens, :] * keep * (silu + sig * (1.0 - silu))
        d_ref[half, pad : pad + tokens, :] = dact
        dh = None
        for t in range(9):
            shift = PITCH * (t // 3 - 1) + t % 3 - 1
            gcv_ref[t : t + 1, cols] = jnp.sum(
                dact * h_ref[half, pad + shift : pad + shift + tokens, :], axis=0, keepdims=True
            )
            term = cv_ref[t : t + 1, cols] * d_ref[half, pad - shift : pad - shift + tokens, :]
            dh = term if dh is None else dh + term
        dh_ref[:, cols] = dh.astype(bf16)


def ffn_first_kernel(scal, mid_ref, dy_ref, norm_ref, *refs, parts):
    w_refs, refs = refs[:parts], refs[parts:]
    z_ref, inv_ref, w_ref, e_ref, win_ref, wdn_ref, gate_ref, dh_ref, gcv_ref, h_ref, d_ref, cv_ref = refs
    z, inv = ln_stats(mid_ref[...])
    z_ref[...] = z
    inv_ref[...] = jnp.broadcast_to(inv, inv_ref.shape)
    w = jnp.where(real_rows(z.shape), z * norm_ref[2:3, :] + norm_ref[3:4, :], 0.0).astype(bf16)
    e = dy_ref[...].astype(bf16)
    w_ref[...] = w
    e_ref[...] = e
    for k in range(parts):
        up(w_refs[k], w, e, win_ref.at[k], wdn_ref.at[k], h_ref.at[k], d_ref.at[k], cv_ref.at[k])
    for k in range(parts):
        middle(
            scal, k, h_ref.at[k], d_ref.at[k], gate_ref.at[k], dh_ref.at[k], cv_ref.at[k], gcv_ref.at[k]
        )


def ffn_last_kernel(
    scal, mid_ref, dy_ref, norm_ref, o_ref, z_ref, inv_ref, w_ref, e_ref, *refs, parts
):
    wins, wdns, gates, dhs, gcvs, last_ref = refs[:6]
    out_ref, dmid_ref, gn_ref = refs[6:9]
    gw_refs, refs = refs[9 : 9 + parts], refs[9 + parts :]
    win_ref, wdn_ref, gate_ref, dh_ref, gcv_ref, h_ref, d_ref, cv_ref, tmp_ref, sm_ref, dw_ref = refs
    w, e = w_ref[...], e_ref[...]
    dim = w.shape[1]
    k = parts - 1
    up(last_ref, w, e, win_ref, wdn_ref, h_ref, d_ref, cv_ref)
    for h in range(k):
        gi = tn(dhs[h], w).astype(bf16)
        gd = tn(gates[h], e).astype(bf16)
        for j in range(4):
            gw_refs[h][1 + j, :, 0:dim] = gi[64 * j : 64 * j + 54]
            gw_refs[h][5 + j, :, 0:dim] = gd[64 * j : 64 * j + 54]
    middle(scal, k, h_ref, d_ref, gate_ref, dh_ref, cv_ref, gcv_ref)
    wins, wdns, gates, dhs, gcvs = [
        [ref.at[i] for i in range(k)] + [own]
        for ref, own in ((wins, win_ref), (wdns, wdn_ref), (gates, gate_ref), (dhs, dh_ref), (gcvs, gcv_ref))
    ]
    dw_ref[...] = sum(nn(dhs[h][...], wins[h][...]) for h in range(parts))
    valid = (scal[0] < scal[1]).astype(f32)
    tmp_ref[...] = (mid_ref[...] + sum(nn(gates[h][...], wdns[h][...]) for h in range(parts))) * valid
    free = iota((54, 256), 1) >= FREE
    pm = place(256)
    for h in range(parts):
        if h == k:
            gi = tn(dhs[h][...], w).astype(bf16)
            gd = tn(gates[h][...], e).astype(bf16)
            for j in range(4):
                gw_refs[h][1 + j, :, 0:dim] = gi[64 * j : 64 * j + 54]
                gw_refs[h][5 + j, :, 0:dim] = gd[64 * j : 64 * j + 54]
        in_free_lanes(nt(gcvs[h][...].astype(bf16), pm), sm_ref.at[h], 0)
        gw_refs[h][0] = jnp.where(free, sm_ref[h, 0:54, :], 0.0).astype(bf16)
    for y in range(SIDE):
        out_ref[SIDE * y : SIDE * (y + 1), :] = tmp_ref[PITCH * y : PITCH * y + SIDE, :].astype(bf16)
    z, inv = z_ref[...], inv_ref[:, 0:1]
    dw = jnp.where(real_rows(z.shape), dw_ref[...], 0.0)
    gn_ref[...] = jnp.zeros_like(gn_ref)
    gn_ref[0:1, :] = jnp.sum(dw * z, axis=0, keepdims=True)
    gn_ref[1:2, :] = jnp.sum(dw, axis=0, keepdims=True)
    dmid = dy_ref[...] + ln_back(dw, z, inv, norm_ref[2:3, :])
    dmid_ref[...] = dmid
    go = tn(o_ref[...], dmid.astype(bf16)).astype(bf16)
    for h in range(parts):
        gw_refs[h][0, :, 0:dim] = go[64 * h : 64 * h + 54]


def scores_back_kernel(
    scal, dmid_ref, mix_ref, q_ref, k_ref, v_ref, qw_ref, p_ref, pv_ref, *refs, parts, part
):
    heads = mix_ref.shape[1] // PITCH
    n = heads * PITCH
    if part == 0:
        w_refs, refs = refs[:parts], refs[parts:]
        do_ref, gq_ref, gk_ref, gv_ref, g0_ref, g1_ref, wo_ref, dw_ref, dp_ref, dt_ref = refs
        wo_ref[...] = jnp.zeros_like(wo_ref)
        load_weight(wo_ref, w_refs, 3)
        f = dmid_ref[...].astype(bf16)
        head = lane_head((1, 256), 1, scal[0])
        keep = ((head >= 0) & (head < scal[2])).astype(f32)
        do_ref[...] = (nt(f, wo_ref[...]) * keep).astype(bf16)
        for ref in (gk_ref, gv_ref, g0_ref, g1_ref):
            ref[...] = jnp.zeros_like(ref)
    else:
        do_ref, *sums, gq_ref, gkb_ref, gvb_ref, gt_ref, gk_ref, gv_ref, g0_ref, g1_ref, dw_ref, dp_ref, dt_ref = refs
        for ref, old in zip((gk_ref, gv_ref, g0_ref, g1_ref), sums):
            ref[...] = old[...]
    first, last = (0, EARLY) if part == 0 else (EARLY, SIDE)
    for y in range(first, last):
        do = do_ref[PITCH * y : PITCH * (y + 1), :].astype(f32)
        at = n * (y - first)
        dw_ref[at : at + n, :] = (tiled(do, heads) * mix_ref[1]).astype(bf16)
    groups = [(b, b + first // BUNCH, y, count) for b, (y, count) in enumerate(bunches(first, last))]
    for b, _, y, count in groups:
        at = n * (y - first)
        dp_ref[b, :, 0 : n * count] = nt(v_ref[...], dw_ref[at : at + n * count, :])
    for b, whole_b, y, count in groups:
        for at in range(0, n * count, 128):
            dp = dp_ref[b, :, at : at + 128]
            p = p_ref[whole_b, :, at : at + 128].astype(f32)
            dt_ref[b, :, at : at + 128] = (p * (dp - jnp.sum(dp * p, axis=0, keepdims=True))).astype(bf16)
    gv, gk = gv_ref[...], gk_ref[...]
    for b, whole_b, y, count in groups:
        at = n * (y - first)
        gv = gv + nn(p_ref[whole_b, :, 0 : n * count], dw_ref[at : at + n * count, :])
        gk = gk + nn(dt_ref[b, :, 0 : n * count], qw_ref[n * y : n * (y + count), :])
    gv_ref[...] = gv
    gk_ref[...] = gk
    for b, _, y, count in groups:
        dk = tn(dt_ref[b, :, 0 : n * count], k_ref[...])
        for u in range(count):
            mine = dk[n * u : n * (u + 1)]
            at = PITCH * (y + u)
            gq_ref[at - PITCH * first : at - PITCH * first + PITCH, :] = over_heads(mine * mix_ref[0], heads).astype(bf16)
            g0_ref[...] += mine * tiled(q_ref[at : at + PITCH, :].astype(f32), heads)
    for y in range(first, last):
        do = do_ref[PITCH * y : PITCH * (y + 1), :].astype(f32)
        g1_ref[...] += pv_ref[n * y : n * (y + 1), :].astype(f32) * tiled(do, heads)
    if part == 0:
        return
    gkb_ref[...] = gk_ref[...].astype(bf16)
    gvb_ref[...] = gv_ref[...].astype(bf16)
    ex = (true_head(iota((n, heads), 0), scal[0]) == iota((n, heads), 1)).astype(bf16)
    el = (lane_head((256, heads), 0, scal[0]) == iota((256, heads), 1)).astype(bf16)
    for i, ref in enumerate((g0_ref, g1_ref)):
        hi, lo = split2(ref[...])
        hi, lo = split2(nn(hi, el) + nn(lo, el))
        if i == 0:
            gt_ref[i] = (tn(ex, hi) + tn(ex, lo)) * HD**-0.5
        else:
            gt_ref[i] = tn(hi, ex) + tn(lo, ex)


def weights_back_kernel(
    scal, x_ref, a_ref, dmid_ref, norm_ref, gn2_ref, gqa_ref, gqb_ref, gk_ref, gv_ref, gt_ref, y_ref, *refs, parts
):
    w_refs, refs = refs[:parts], refs[parts:]
    both_ref, gw_refs, refs = refs[0], refs[1 : 1 + parts], refs[1 + parts :]
    ws_ref, tmp_ref, flat_ref, sm_ref = refs
    heads = gt_ref.shape[1]
    dim = x_ref.shape[1]
    ws_ref[...] = jnp.zeros_like(ws_ref)
    for b in range(3):
        load_weight(ws_ref.at[b], w_refs, b)
    gq = jnp.concatenate([gqa_ref[...], gqb_ref[...]], axis=0)
    gk, gv = gk_ref[...], gv_ref[...]
    a = a_ref[...]
    da = nn(gq, ws_ref[0]) + nn(gk, ws_ref[1]) + nn(gv, ws_ref[2])
    z, inv = ln_stats(x_ref[...])
    flat_ref[...] = jnp.zeros_like(flat_ref)
    flat_ref[0:1, 0:dim] = jnp.sum(da * z, axis=0, keepdims=True)
    flat_ref[1:2, 0:dim] = jnp.sum(da, axis=0, keepdims=True)
    flat_ref[2:4, 0:dim] = gn2_ref[0:2, :]
    for i in range(2):
        flat_ref[8 : 8 + heads, 128 * i : 128 * i + heads] = gt_ref[i]
    sm_ref[...] = jnp.zeros_like(sm_ref)
    in_free_lanes(flat_ref[0:4, :], sm_ref, 0)
    mix = flat_ref[8 : 8 + heads, :]
    first = iota(mix.shape, 1) < 128
    mix = jnp.where(first, mix, 0.0) + pltpu.roll(jnp.where(first, 0.0, mix), 128 + heads, 1)
    sm_ref[24 : 24 + heads, :] = pltpu.roll(mix, FREE, 1)
    small = jnp.where(iota((54, 256), 1) >= FREE, sm_ref[0:54, :], 0.0).astype(bf16)
    for h in range(parts):
        gw_refs[h][0] = small
    for b, g in enumerate((gq, gk, gv)):
        gw = tn(g, a).astype(bf16)
        for h in range(parts):
            gw_refs[h][b, :, 0:dim] = gw[64 * h : 64 * h + 54]
    tmp_ref[...] = dmid_ref[...] + ln_back(da, z, inv, norm_ref[0:1, :])
    for y in range(SIDE):
        both_ref[1, SIDE * y : SIDE * (y + 1), :] = tmp_ref[PITCH * y : PITCH * y + SIDE, :].astype(bf16)
    both_ref[0] = y_ref[...]


def cast_kernel(m_hbm, out_ref, m_ref, sem):
    copy = pltpu.make_async_copy(m_hbm, m_ref, sem)
    copy.start()
    copy.wait()
    for i in range(out_ref.shape[0]):
        out_ref[i] = m_ref[:, i, :].astype(bf16)


def spot(slot, per):
    bits = per.bit_length() - 1
    return slot >> (bits + 1), (slot >> bits) & 1, slot & (per - 1)


def stack_kernel(*refs):
    for k, ref in enumerate(refs[:-1]):
        refs[-1][k] = ref[...]


def select_kernel(slot_ref, scal, conv_ref, own_ref, other_ref, attn_ref, ffn_ref, every_ref):
    every_ref[0] = own_ref[...]
    every_ref[1] = other_ref[...]
    per = own_ref.shape[1]
    for b in range(12):
        pair, place, own = spot(slot_ref[b], per)
        block = every_ref[place ^ scal[4], pair ^ scal[5], own]
        if b < 4:
            attn_ref[b] = block
        else:
            ffn_ref[b - 4] = block
    hi, lo = split2(conv_ref[...])
    ffn_ref[8] = jnp.zeros_like(ffn_ref[8])
    ffn_ref[8, 0:9] = hi
    ffn_ref[8, 16:25] = lo


def total(refs, at):
    acc = refs[0][at].astype(f32)
    for ref in refs[1:]:
        acc = acc + ref[at].astype(f32)
    return acc


def half_sum_kernel(a_ref, b_ref, out_ref):
    out_ref[...] = (a_ref[...].astype(f32) + b_ref[...].astype(f32)).astype(bf16)


def spread_ffn_kernel(slot_ref, scal, *refs):
    ffn_refs, out_ref = refs[:-1], refs[-1]
    pairs, _, per = out_ref.shape[:3]
    out_ref[...] = jnp.zeros_like(out_ref)
    for b in range(9):
        block = total(ffn_refs, b)
        k, j, i = spot(slot_ref[3 + b], per)
        out_ref[k ^ scal[5], j ^ scal[4], i, :, 0:FREE] = block[:, 0:FREE].astype(bf16)
        if b == 0:
            wide = block[:, FREE:].astype(bf16)
    for k in range(pairs):
        for j in range(2):
            out_ref[k, j, 0, :, FREE:] = wide


def spread_attn_kernel(slot_ref, scal, old_ref, *refs, parts):
    attn, outs, all_ref = refs[:parts], refs[parts:-1], refs[-1]
    pairs, _, per = all_ref.shape[:3]
    all_ref[...] = old_ref[...]
    for b in range(3):
        block = total(attn, b)
        k, j, i = spot(slot_ref[b], per)
        all_ref[k ^ scal[5], j ^ scal[4], i, :, 0:FREE] = block[:, 0:FREE].astype(bf16)
        if b == 0:
            wide = block[:, FREE:].astype(bf16)
    for j in range(2):
        outs[j][...] = all_ref[:, j]
        for k in range(pairs):
            outs[j][k, 1, :, FREE:] = wide


def place_sum_kernel(own_ref, other_ref, *outs):
    for k, out_ref in enumerate(outs):
        out_ref[...] = (own_ref[k].astype(f32) + other_ref[k].astype(f32)).astype(out_ref.dtype)


def adam(w, g, one, two, rate, decay):
    one_new = 0.5 * one + 0.5 * g
    two_new = 0.5 * two + 0.5 * g * g
    hat_one = one_new / (1.0 - 0.5**3)
    hat_two = two_new / (1.0 - 0.5**3)
    return w - rate * (hat_one / (jnp.sqrt(hat_two) + 1e-08) + decay * w), one_new, two_new


def update_kernel(*refs):
    got, refs = refs[:-28], refs[-28:]
    ins, outs, (g_ref, sm_ref, flat_ref) = refs[0:12], refs[12:25], refs[25:]
    per, rows = got[0].shape[:2]
    dim = ins[0].shape[2]
    for i in range(per):
        g = total(got, i)
        g_ref[:, i, :] = g[:, 0:dim]
        sm_ref[i, 0:rows, :] = g
    w, one, two = adam(ins[0][...], g_ref[...], ins[1][...], ins[2][...], 0.06, 0.05)
    outs[0][...], outs[1][...], outs[2][...], outs[3][...] = w, one, two, w.astype(bf16)
    heads = ins[6].shape[0]
    flat_ref[0:9, :] = from_free_lanes(sm_ref.at[0], 0, 9)
    flat_ref[16:20, :] = from_free_lanes(sm_ref.at[1], 0, 4)
    mix = pltpu.roll(sm_ref[1, 24 : 24 + heads, :], 256 - FREE, 1)
    flat_ref[32 : 32 + heads, :] = mix
    flat_ref[48 : 48 + heads, :] = pltpu.roll(mix, 256 - heads, 1)
    outs[4][...], outs[5][...], outs[6][...] = adam(
        ins[3][...], flat_ref[16:20, 0:dim], ins[4][...], ins[5][...], 0.2, 0.0
    )
    for i in range(2):
        w, one, two = adam(
            ins[6][:, i, :], flat_ref[16 * (i + 2) : 16 * (i + 2) + heads, 0:heads], ins[7][:, i, :], ins[8][:, i, :],
            0.2, 0.0,
        )
        outs[7][:, i, :], outs[8][:, i, :], outs[9][:, i, :] = w, one, two
    outs[10][...], outs[11][...], outs[12][...] = adam(
        ins[9][...], flat_ref[0:9, 0:dim], ins[10][...], ins[11][...], 0.2, 0.05
    )


def assemble_kernel(scal, *refs):
    ins, outs, (all_ref,) = refs[:-3], refs[-3:-1], refs[-1:]
    parts, tokens = len(ins), ins[0].shape[1]
    step = 32
    shape = (parts * step, parts * step)
    row, col = iota(shape, 0), iota(shape, 1)
    bits = parts.bit_length() - 1
    pick = ((row >> bits == col & (step - 1)) & (row & (parts - 1) == col >> 5)).astype(bf16)
    full = all_ref.shape[1]
    for k in range(parts):
        all_ref[k, tokens // step * step : full, :] = jnp.zeros((full - tokens // step * step, all_ref.shape[2]), bf16)
    for i, out_ref in enumerate(outs):
        for k, ref in enumerate(ins):
            all_ref[scal[0] ^ k, 0:tokens, :] = ref[i]
        for at in range(0, tokens, step):
            mixed = nn(pick, jnp.concatenate([all_ref[k, at : at + step, :] for k in range(parts)], axis=0))
            for t in range(min(step, tokens - at)):
                out_ref[at + t] = mixed[parts * t : parts * (t + 1)]


VM = pl.BlockSpec(memory_space=pltpu.VMEM)
SM = pl.BlockSpec(memory_space=pltpu.SMEM)
SDS = jax.ShapeDtypeStruct


def call(body, name, n_scalar, n_in, out_shape, scratch=(), mb=16, micros=1, **kw):
    return pl.pallas_call(
        functools.partial(body, **kw) if kw else body,
        in_specs=[SM] * n_scalar + [VM] * n_in,
        out_specs=[VM] * len(out_shape),
        out_shape=out_shape,
        scratch_shapes=scratch,
        compiler_params=pltpu.CompilerParams(vmem_limit_bytes=mb << 20),
        cost_estimate=pl.CostEstimate(flops=micros * 1000000000, transcendentals=0, bytes_accessed=micros * 3000000),
        name=name,
    )


def prep(scal, tokens, cotangent, norm_params, talk):
    tok, dim = tokens.shape[1], tokens.shape[2]
    pad = SIDE * PITCH
    heads = talk.shape[1]
    n = heads * PITCH
    full = lambda *s: pl.BlockSpec(s, lambda i, sc: (0,) * len(s))
    return pl.pallas_call(
        prep_kernel,
        grid_spec=pltpu.PrefetchScalarGridSpec(
            num_scalar_prefetch=1,
            grid=(1,),
            in_specs=[
                pl.BlockSpec((1, tok, dim), lambda i, sc: (sc[0], 0, 0)),
                pl.BlockSpec((1, tok, dim), lambda i, sc: (sc[0], 0, 0)),
                full(*norm_params.shape),
                full(*talk.shape),
            ],
            out_specs=[full(pad, dim), full(pad, dim), full(pad, dim), full(2, n, 256), full(pad, 128)],
            scratch_shapes=[pltpu.VMEM((tok, dim), f32)],
        ),
        out_shape=[SDS((pad, dim), f32), SDS((pad, dim), bf16), SDS((pad, dim), f32), SDS((2, n, 256), f32),
                   SDS((pad, 128), f32)],
        compiler_params=pltpu.CompilerParams(vmem_limit_bytes=16 << 20),
        cost_estimate=pl.CostEstimate(flops=1000000000, transcendentals=0, bytes_accessed=3000000),
        name="prep",
    )(scal, tokens, cotangent, norm_params, talk)


def attn_fwd(scal, x, a, mix, bias, w):
    pad, dim = x.shape
    n = mix.shape[1]
    grid = (len(bunches(0, SIDE)), pad, n * BUNCH)
    return call(
        attn_fwd_kernel, "attn_fwd", 1, 4 + len(w),
        [SDS((pad, dim), f32)] + [SDS((pad, 256), bf16)] * 4
        + [SDS((SIDE * n, 256), bf16), SDS(grid, bf16), SDS((SIDE * n, 256), bf16)],
        [pltpu.VMEM((4, 256, dim), bf16), pltpu.VMEM(grid, f32)],
        mb=24, micros=1, parts=len(w),
    )(scal, x, a, mix, bias, *w)


def ffn_first(scal, mid, dy, norm_params, w):
    pad, dim = mid.shape
    count = len(w)
    lanes = [(count, 256, dim)] * 2 + [(count, pad, 256)] * 2
    grids = [pltpu.VMEM((count, 2, pad + 2 * MARGIN, 128), f32)] * 2
    return call(
        ffn_first_kernel, "ffn_first", 1, 3 + count,
        [SDS((pad, dim), f32), SDS((pad, 128), f32), SDS((pad, dim), bf16), SDS((pad, dim), bf16)]
        + [SDS(t, bf16) for t in lanes] + [SDS((count, 9, 256), f32)],
        grids + [pltpu.VMEM((count, 9, 256), f32)],
        mb=24, micros=3, parts=count,
    )(scal, mid, dy, norm_params, *w)


def ffn_last(scal, mid, dy, norm_params, o, first, w):
    pad, dim = mid.shape
    parts = first[4].shape[0] + 1
    grids = [pltpu.VMEM((2, pad + 2 * MARGIN, 128), f32)] * 2
    return call(
        ffn_last_kernel, "ffn_last", 1, 14,
        [SDS((SIDE * SIDE, dim), bf16), SDS((pad, dim), f32), SDS((8, dim), f32)] + [SDS((9, 54, 256), bf16)] * parts,
        [pltpu.VMEM((256, dim), bf16)] * 2 + [pltpu.VMEM((pad, 256), bf16)] * 2 + [pltpu.VMEM((9, 256), f32)] + grids
        + [
            pltpu.VMEM((9, 256), f32), pltpu.VMEM((pad, dim), f32), pltpu.VMEM((parts, 56, 256), f32),
            pltpu.VMEM((pad, dim), f32),
        ],
        mb=24, micros=4, parts=parts,
    )(scal, mid, dy, norm_params, o, *first, w)


def scores_back(scal, dmid, mix, q, k, v, qw, p, pv, more, part):
    pad, dim = dmid.shape
    n = mix.shape[1]
    heads = n // PITCH
    sums = [SDS((pad, 256), f32)] * 2 + [SDS((n, 256), f32)] * 2
    count = EARLY if part == 0 else SIDE - EARLY
    half = SDS((PITCH * count, 256), bf16)
    if part == 0:
        outs = [SDS((pad, 256), bf16), half] + sums
        scratch = [pltpu.VMEM((256, dim), bf16)]
    else:
        outs = [half] + [SDS((pad, 256), bf16)] * 2 + [SDS((2, heads, heads), f32)]
        scratch = [pltpu.VMEM(t.shape, f32) for t in sums]
    scratch += [
        pltpu.VMEM((n * count, 256), bf16), pltpu.VMEM((-(-count // BUNCH), pad, n * BUNCH), f32),
        pltpu.VMEM((-(-count // BUNCH), pad, n * BUNCH), bf16),
    ]
    return call(
        scores_back_kernel, "scores_back", 1, 8 + len(more), outs, scratch,
        mb=24, micros=4, parts=len(more), part=part,
    )(scal, dmid, mix, q, k, v, qw, p, pv, *more)


def weights_back(scal, x, a, dmid, norm_params, gn2, gqa, gqb, gk, gv, gt, out, w):
    pad, dim = x.shape
    return call(
        weights_back_kernel, "weights_back", 1, 11 + len(w),
        [SDS((2, SIDE * SIDE, dim), bf16)] + [SDS((3, 54, 256), bf16)] * len(w),
        [pltpu.VMEM((3, 256, dim), bf16), pltpu.VMEM((pad, dim), f32), pltpu.VMEM((24, 256), f32),
         pltpu.VMEM((56, 256), f32)],
        mb=24, micros=3, parts=len(w),
    )(scal, x, a, dmid, norm_params, gn2, gqa, gqb, gk, gv, gt, out, *w)


def permute(x, axis, k):
    return lax.ppermute(x, axis, [(i, i ^ k) for i in range(lax.axis_size(axis))])


def swap(t):
    return jnp.swapaxes(t, 0, 1)


def whole(*shape):
    return pl.BlockSpec(shape, lambda i: (0,) * len(shape))


def staged(body, name, ins, outs, scratch=(), micros=1):
    return pl.pallas_call(
        body,
        grid=(1,),
        in_specs=[VM] * len(ins),
        out_specs=[whole(*t.shape) for t in outs],
        out_shape=outs,
        scratch_shapes=scratch,
        compiler_params=pltpu.CompilerParams(vmem_limit_bytes=16 << 20),
        cost_estimate=pl.CostEstimate(flops=micros * 1000000000, transcendentals=0, bytes_accessed=micros * 3000000),
        name=name,
    )(*ins)


def local(
    tokens, cotangent, image_count, subnet_heads, subnet_width, block_slot,
    master, master_m1, master_m2, norm_params, norm_m1, norm_m2, talk, talk_m1, talk_m2, conv, conv_m1, conv_m2,
):
    slots, rows, dim = master.shape
    parts = lax.axis_size("head")
    ranks = lax.axis_size("dp")
    place_id = lax.axis_index("head").astype(jnp.int32)
    rank = lax.axis_index("dp").astype(jnp.int32)
    scal = jnp.concatenate(
        [place_id[None], image_count, subnet_heads, subnet_width, (rank % 2)[None], (rank // 2)[None]]
    )
    mine = pl.pallas_call(
        cast_kernel,
        grid=(1,),
        in_specs=[pl.BlockSpec(memory_space=pltpu.HBM)],
        out_specs=whole(slots, rows, dim),
        out_shape=SDS((slots, rows, dim), bf16),
        scratch_shapes=[pltpu.VMEM((rows, slots, dim), f32), pltpu.SemaphoreType.DMA],
        compiler_params=pltpu.CompilerParams(vmem_limit_bytes=16 << 20),
        name="cast",
    )(swap(master))
    pairs = ranks // 2
    far = {k: permute(mine, "dp", 2 * k) for k in (*range(2, pairs), 1)}
    (own,) = call(stack_kernel, "stack", 0, pairs, [SDS((pairs, slots, rows, dim), bf16)])(
        mine, *[far[k] for k in range(1, pairs)]
    )
    own, tokens, cotangent, talk_in = lax.optimization_barrier((own, tokens, cotangent, talk))
    other = permute(own, "dp", 1)
    x, a, dy, mix, bias = prep(scal, tokens, cotangent, norm_params, talk_in)
    other, x = lax.optimization_barrier((other, x))
    attn_w, ffn_w = call(
        select_kernel, "select", 2, 3, [SDS((4, rows, dim), bf16), SDS((9, rows, dim), bf16)],
        [pltpu.VMEM((2, pairs, slots, rows, dim), bf16)],
    )(block_slot, scal, conv, own, other)
    attn_2, attn_1 = permute(attn_w, "head", 2), permute(attn_w, "head", 1)
    attn_3 = permute(attn_2, "head", 1)
    attn_w = [attn_w, attn_1, attn_2, attn_3]
    ffn_2, ffn_1 = permute(ffn_w, "head", 2), permute(ffn_w, "head", 1)
    mid, q, k, v, o, qw, p, pv = attn_fwd(scal, x, a, mix, bias, attn_w)
    mid, ffn_2 = lax.optimization_barrier((mid, ffn_2))
    ffn_3 = permute(ffn_2, "head", 1)
    first = list(ffn_first(scal, mid, dy, norm_params, [ffn_w, ffn_1, ffn_2]))
    first[0], ffn_3 = lax.optimization_barrier((first[0], ffn_3))
    out, dmid, gn2, *ffn_g = ffn_last(scal, mid, dy, norm_params, o, first, ffn_3)
    ffn_1, ffn_3 = permute(ffn_g[1], "head", 1), permute(ffn_g[3], "head", 1)
    do, gqa, *sums = scores_back(scal, dmid, mix, q, k, v, qw, p, pv, attn_w, 0)
    do, ffn_1, ffn_3 = lax.optimization_barrier((do, ffn_1, ffn_3))
    (half,) = call(half_sum_kernel, "half_sum", 0, 2, [SDS(ffn_3.shape, bf16)])(ffn_g[2], ffn_3)
    ffn_2 = permute(half, "head", 2)
    gqb, gk, gv, gt = scores_back(scal, dmid, mix, q, k, v, qw, p, pv, [do, *sums], 1)
    both, *attn_g = weights_back(scal, x, a, dmid, norm_params, gn2, gqa, gqb, gk, gv, gt, out, attn_w)
    attn_1, attn_3 = permute(attn_g[1], "head", 1), permute(attn_g[3], "head", 1)
    (half,) = call(half_sum_kernel, "half_sum", 0, 2, [SDS(attn_3.shape, bf16)])(attn_g[2], attn_3)
    attn_2 = permute(half, "head", 2)
    (message,) = call(
        spread_ffn_kernel, "spread_ffn", 2, 3, [SDS((ranks // 2, 2, slots, rows, 256), bf16)]
    )(block_slot, scal, ffn_g[0], ffn_1, ffn_2)
    both, message = lax.optimization_barrier((both, message))
    both_2, both_1 = permute(both, "head", 2), permute(both, "head", 1)
    both_3 = permute(both_2, "head", 1)
    own, other = call(
        spread_attn_kernel, "spread_attn", 2, 4, [SDS((pairs,) + message.shape[2:], bf16)] * 2,
        [pltpu.VMEM(message.shape, bf16)], parts=3,
    )(block_slot, scal, message, attn_g[0], attn_1, attn_2)
    slot_shape = (slots, rows, 256)
    got = list(call(
        place_sum_kernel, "place_sum", 0, 2, [SDS(slot_shape, f32)] + [SDS(slot_shape, bf16)] * (pairs - 1)
    )(own, permute(other, "dp", 1)))
    far = {k: permute(got[k], "dp", 2 * k) for k in (*range(2, pairs), 1)}
    got[1:] = [far[k] for k in range(1, pairs)]
    shape = SDS((tokens.shape[1], parts, dim), f32)
    output, token_grad = pl.pallas_call(
        assemble_kernel,
        grid=(1,),
        in_specs=[SM] + [whole(*both.shape)] * parts,
        out_specs=[whole(*shape.shape)] * 2,
        out_shape=[shape, shape],
        scratch_shapes=[pltpu.VMEM((parts, 224, dim), bf16)],
        compiler_params=pltpu.CompilerParams(vmem_limit_bytes=16 << 20),
        cost_estimate=pl.CostEstimate(flops=1000000000, transcendentals=0, bytes_accessed=3000000),
        name="assemble",
    )(scal, both, both_1, both_2, both_3)
    got[-1], output, token_grad = lax.optimization_barrier((got[-1], output, token_grad))
    state = [
        swap(master), swap(master_m1), swap(master_m2), norm_params, norm_m1, norm_m2,
        swap(talk), swap(talk_m1), swap(talk_m2), conv, conv_m1, conv_m2,
    ]
    shapes = [SDS(t.shape, f32) for t in state]
    shapes.insert(3, SDS(state[0].shape, bf16))
    new = staged(
        update_kernel, "update", [*got, *state], shapes,
        [pltpu.VMEM((rows, slots, dim), f32), pltpu.VMEM((slots, 64, 256), f32), pltpu.VMEM((64, 256), f32)],
    )
    new = [swap(t) if t.ndim == 3 else t for t in new]
    return (swap(output), swap(token_grad), *new)


def solution(mesh):
    in_specs = (
        P("dp", None, None),
        P("dp", None, None),
        P("dp"),
        P(),
        P(),
        P(),
        P("dp", None, "head"),
        P("dp", None, "head"),
        P("dp", None, "head"),
        P(),
        P(),
        P(),
        P(),
        P(),
        P(),
        P(None, "head"),
        P(None, "head"),
        P(None, "head"),
    )
    out_specs = (
        P("dp", None, None),
        P("dp", None, None),
        P("dp", None, "head"),
        P("dp", None, "head"),
        P("dp", None, "head"),
        P("dp", None, "head"),
        P(),
        P(),
        P(),
        P(),
        P(),
        P(),
        P(None, "head"),
        P(None, "head"),
        P(None, "head"),
    )
    return jax.shard_map(local, mesh=mesh, in_specs=in_specs, out_specs=out_specs, check_vma=False)
```

```python
import functools
import jax
import jax.numpy as jnp
from jax import lax
from jax.experimental import pallas as pl
from jax.experimental.pallas import tpu as pltpu
from jax.sharding import PartitionSpec as P

HD = 18
SIDE = 14
PITCH = 16
MARGIN = 24
BUNCH = 4
EARLY = 4


def bunches(first, last):
    return [(y, min(BUNCH, last - y)) for y in range(first, last, BUNCH)]

FREE = 216
WIDE = 40
norm_eps = 1e-05
bf16 = jnp.bfloat16
f32 = jnp.float32


def nn(a, b):
    return lax.dot_general(a, b, (((1,), (0,)), ((), ())), preferred_element_type=f32)


def nt(a, b):
    return lax.dot_general(a, b, (((1,), (1,)), ((), ())), preferred_element_type=f32)


def tn(a, b):
    return lax.dot_general(a, b, (((0,), (0,)), ((), ())), preferred_element_type=f32)


def iota(shape, dim):
    return lax.broadcasted_iota(jnp.int32, shape, dim)


def split2(v):
    hi = v.astype(bf16)
    return hi, (v - hi.astype(f32)).astype(bf16)


def real_rows(shape):
    return (iota(shape, 0) & (PITCH - 1)) < SIDE


def lane_head(shape, dim, place):
    lane = iota(shape, dim)
    rest = lane & 63
    head = ((lane >> 6) ^ place) * 3 + (rest >= 18).astype(jnp.int32) + (rest >= 36).astype(jnp.int32)
    return jnp.where(rest < 54, head, -1)


def true_head(rows, place):
    head = rows >> 4
    part = (head >= 3).astype(jnp.int32) + (head >= 6).astype(jnp.int32) + (head >= 9).astype(jnp.int32)
    return (part ^ place) * 3 + (head - 3 * part)


def prep_kernel(scal, tok_ref, cot_ref, norm_ref, talk_ref, x_ref, a_ref, dy_ref, mix_ref, bias_ref, tmp_ref):
    x_ref[...] = jnp.zeros_like(x_ref)
    dy_ref[...] = jnp.zeros_like(dy_ref)
    valid = (scal[0] < scal[1]).astype(f32)
    tmp_ref[...] = tok_ref[0].astype(f32)
    for y in range(SIDE):
        x_ref[PITCH * y : PITCH * y + SIDE, :] = tmp_ref[SIDE * y : SIDE * (y + 1), :]
        dy_ref[PITCH * y : PITCH * y + SIDE, :] = cot_ref[0, SIDE * y : SIDE * (y + 1), :] * valid
    x = x_ref[...]
    centred = x - jnp.mean(x, axis=-1, keepdims=True)
    inv = lax.rsqrt(jnp.mean(centred * centred, axis=-1, keepdims=True) + norm_eps)
    a = centred * inv * norm_ref[0:1, :] + norm_ref[1:2, :]
    a_ref[...] = jnp.where(real_rows(a.shape), a, 0.0).astype(bf16)
    heads = talk_ref.shape[1]
    n = heads * PITCH
    ex = (true_head(iota((n, heads), 0), scal[0]) == iota((n, heads), 1)).astype(bf16)
    el = (lane_head((256, heads), 0, scal[0]) == iota((256, heads), 1)).astype(bf16)
    for i in range(2):
        both = []
        for part in split2(talk_ref[i]):
            if i == 0:
                both.append(nt(nn(ex, part).astype(bf16), el))
            else:
                both.append(nt(nt(ex, part).astype(bf16), el))
        mix_ref[i] = (both[0] + both[1]) * (HD**-0.5 if i == 0 else 1.0)
    bias_ref[...] = jnp.where(real_rows(bias_ref.shape), 0.0, -1e30)


def load_weight(dst_ref, w_refs, b):
    for k, w_ref in enumerate(w_refs):
        dst_ref[64 * k : 64 * k + 54, :] = w_ref[b]


def tiled(rows, heads):
    return jnp.concatenate([rows] * heads, axis=0)


def over_heads(rows, heads):
    return jnp.sum(rows.reshape(heads, PITCH, rows.shape[1]), axis=0)


def attn_fwd_kernel(scal, x_ref, a_ref, mix_ref, bias_ref, *refs, parts):
    w_refs, refs = refs[:parts], refs[parts:]
    mid_ref, q_ref, k_ref, v_ref, o_ref, qw_ref, p_ref, pv_ref, ws_ref, t_ref = refs
    heads = mix_ref.shape[1] // PITCH
    a = a_ref[...]
    ws_ref[...] = jnp.zeros_like(ws_ref)
    for b, dst in enumerate((q_ref, k_ref, v_ref)):
        load_weight(ws_ref.at[b], w_refs, b)
        dst[...] = nt(a, ws_ref[b]).astype(bf16)
    load_weight(ws_ref.at[3], w_refs, 3)
    head = lane_head((1, 256), 1, scal[0])
    keep = ((head >= 0) & (head < scal[2])).astype(f32)

    n = heads * PITCH
    for y in range(SIDE):
        q = q_ref[PITCH * y : PITCH * (y + 1), :].astype(f32)
        qw_ref[n * y : n * (y + 1), :] = (tiled(q, heads) * mix_ref[0]).astype(bf16)
    for b, (y, count) in enumerate(bunches(0, SIDE)):
        t_ref[b, :, 0 : n * count] = nt(k_ref[...], qw_ref[n * y : n * (y + count), :])
    for b, (y, count) in enumerate(bunches(0, SIDE)):
        for at in range(0, n * count, 128):
            t = t_ref[b, :, at : at + 128] + bias_ref[...]
            e = jnp.exp(t - jnp.max(t, axis=0, keepdims=True))
            p_ref[b, :, at : at + 128] = (e * (1.0 / jnp.sum(e, axis=0, keepdims=True))).astype(bf16)
    for b, (first, count) in enumerate(bunches(0, SIDE)):
        pv = tn(p_ref[b, :, 0 : n * count], v_ref[...])
        pv_ref[n * first : n * (first + count), :] = pv.astype(bf16)
        for u in range(count):
            o = over_heads(pv[n * u : n * (u + 1)] * mix_ref[1], heads)
            o_ref[PITCH * (first + u) : PITCH * (first + u + 1), :] = (o * keep).astype(bf16)
    mid_ref[...] = x_ref[...] + nn(o_ref[...], ws_ref[3])


def ln_stats(v):
    centred = v - jnp.mean(v, axis=-1, keepdims=True)
    inv = lax.rsqrt(jnp.mean(centred * centred, axis=-1, keepdims=True) + norm_eps)
    return centred * inv, inv


def ln_back(grad, scaled, inv, gain):
    gs = grad * gain
    return inv * (
        gs - jnp.mean(gs, axis=-1, keepdims=True) - scaled * jnp.mean(gs * scaled, axis=-1, keepdims=True)
    )


def in_free_lanes(flat, dst_ref, first_row):
    rows = flat.shape[0]
    for j in range(6):
        dst_ref[first_row + rows * j : first_row + rows * (j + 1), :] = pltpu.roll(flat, (FREE - WIDE * j) % 256, 1)


def from_free_lanes(src_ref, first_row, rows):
    lane = iota((rows, 256), 1)
    flat = jnp.zeros((rows, 256), f32)
    for j in range(6):
        moved = pltpu.roll(src_ref[first_row + rows * j : first_row + rows * (j + 1), :], (WIDE * j - FREE) % 256, 1)
        flat = flat + jnp.where((lane >= WIDE * j) & (lane < WIDE * (j + 1)), moved, 0.0)
    return flat


def place(rows=216):
    shape = (rows, 256)
    lane = iota(shape, 1)
    rest = lane & 63
    return ((iota(shape, 0) == (lane >> 6) * 54 + rest) & (rest < 54)).astype(bf16)


def up(w_ref, w, e, win_ref, wdn_ref, h_ref, d_ref, cv_ref):
    tokens, dim = w.shape
    pad = MARGIN
    for j in range(4):
        at = 64 * j
        win_ref[at : at + 54, :] = w_ref[j]
        wdn_ref[at : at + 54, :] = w_ref[4 + j]
        win_ref[at + 54 : at + 64, :] = jnp.zeros((10, dim), bf16)
        wdn_ref[at + 54 : at + 64, :] = jnp.zeros((10, dim), bf16)
    both = nn(w_ref[8], place(dim))
    cv_ref[...] = both[0:9] + both[16:25]
    hidden = nt(w, win_ref[...])
    dgate = nt(e, wdn_ref[...])
    zero = jnp.zeros((pad, 128), f32)
    for half in range(2):
        mine = slice(128 * half, 128 * (half + 1))
        for ref, value in ((h_ref, hidden), (d_ref, dgate)):
            ref[half, 0:pad, :] = zero
            ref[half, pad + tokens :, :] = zero
            ref[half, pad : pad + tokens, :] = value[:, mine]


def middle(scal, k, h_ref, d_ref, gate_ref, dh_ref, cv_ref, gcv_ref):
    tokens = gate_ref.shape[0]
    pad = MARGIN
    for half in range(2):
        cols = slice(128 * half, 128 * (half + 1))
        lane = iota((1, 128), 1) + 128 * half
        unit = ((k ^ scal[0]) * 4 + (lane >> 6)) * 54 + (lane & 63)
        keep = (unit < scal[3]).astype(f32)
        act = None
        for t in range(9):
            off = pad + PITCH * (t // 3 - 1) + t % 3 - 1
            term = cv_ref[t : t + 1, cols] * h_ref[half, off : off + tokens, :]
            act = term if act is None else act + term
        sig = 0.5 * jnp.tanh(0.5 * act) + 0.5
        silu = act * sig
        gate_ref[:, cols] = (silu * keep).astype(bf16)
        dact = d_ref[half, pad : pad + tokens, :] * keep * (silu + sig * (1.0 - silu))
        d_ref[half, pad : pad + tokens, :] = dact
        dh = None
        for t in range(9):
            shift = PITCH * (t // 3 - 1) + t % 3 - 1
            gcv_ref[t : t + 1, cols] = jnp.sum(
                dact * h_ref[half, pad + shift : pad + shift + tokens, :], axis=0, keepdims=True
            )
            term = cv_ref[t : t + 1, cols] * d_ref[half, pad - shift : pad - shift + tokens, :]
            dh = term if dh is None else dh + term
        dh_ref[:, cols] = dh.astype(bf16)


def ffn_first_kernel(scal, mid_ref, dy_ref, norm_ref, *refs, parts):
    w_refs, refs = refs[:parts], refs[parts:]
    z_ref, inv_ref, w_ref, e_ref, win_ref, wdn_ref, gate_ref, dh_ref, gcv_ref, h_ref, d_ref, cv_ref = refs
    z, inv = ln_stats(mid_ref[...])
    z_ref[...] = z
    inv_ref[...] = jnp.broadcast_to(inv, inv_ref.shape)
    w = jnp.where(real_rows(z.shape), z * norm_ref[2:3, :] + norm_ref[3:4, :], 0.0).astype(bf16)
    e = dy_ref[...].astype(bf16)
    w_ref[...] = w
    e_ref[...] = e
    for k in range(parts):
        up(w_refs[k], w, e, win_ref.at[k], wdn_ref.at[k], h_ref.at[k], d_ref.at[k], cv_ref.at[k])
    for k in range(parts):
        middle(
            scal, k, h_ref.at[k], d_ref.at[k], gate_ref.at[k], dh_ref.at[k], cv_ref.at[k], gcv_ref.at[k]
        )


def ffn_last_kernel(
    scal, mid_ref, dy_ref, norm_ref, o_ref, z_ref, inv_ref, w_ref, e_ref, *refs, parts, late
):
    early = parts - late
    wins, wdns, gates, dhs, gcvs = refs[:5]
    last_refs, refs = refs[5 : 5 + late], refs[5 + late :]
    out_ref, dmid_ref, gn_ref = refs[:3]
    gw_refs, refs = refs[3 : 3 + parts], refs[3 + parts :]
    win_ref, wdn_ref, gate_ref, dh_ref, gcv_ref, h_ref, d_ref, cv_ref, tmp_ref, sm_ref, dw_ref = refs
    w, e = w_ref[...], e_ref[...]
    dim = w.shape[1]
    wins, wdns, gates, dhs, gcvs = [
        [ref.at[i] for i in range(early)] + [own.at[i] for i in range(late)]
        for ref, own in ((wins, win_ref), (wdns, wdn_ref), (gates, gate_ref), (dhs, dh_ref), (gcvs, gcv_ref))
    ]

    def back(h):
        gi = tn(dhs[h][...], w).astype(bf16)
        gd = tn(gates[h][...], e).astype(bf16)
        for j in range(4):
            gw_refs[h][1 + j, :, 0:dim] = gi[64 * j : 64 * j + 54]
            gw_refs[h][5 + j, :, 0:dim] = gd[64 * j : 64 * j + 54]

    for i in range(late):
        up(last_refs[i], w, e, win_ref.at[i], wdn_ref.at[i], h_ref.at[i], d_ref.at[i], cv_ref.at[i])
    for h in range(early):
        back(h)
    for i in range(late):
        middle(
            scal, early + i, h_ref.at[i], d_ref.at[i], gate_ref.at[i], dh_ref.at[i], cv_ref.at[i], gcv_ref.at[i]
        )
    dw_ref[...] = sum(nn(dhs[h][...], wins[h][...]) for h in range(parts))
    valid = (scal[0] < scal[1]).astype(f32)
    tmp_ref[...] = (mid_ref[...] + sum(nn(gates[h][...], wdns[h][...]) for h in range(parts))) * valid
    free = iota((54, 256), 1) >= FREE
    pm = place(256)
    for h in range(parts):
        if h >= early:
            back(h)
        in_free_lanes(nt(gcvs[h][...].astype(bf16), pm), sm_ref.at[h], 0)
        gw_refs[h][0] = jnp.where(free, sm_ref[h, 0:54, :], 0.0).astype(bf16)
    for y in range(SIDE):
        out_ref[SIDE * y : SIDE * (y + 1), :] = tmp_ref[PITCH * y : PITCH * y + SIDE, :].astype(bf16)
    z, inv = z_ref[...], inv_ref[:, 0:1]
    dw = jnp.where(real_rows(z.shape), dw_ref[...], 0.0)
    gn_ref[...] = jnp.zeros_like(gn_ref)
    gn_ref[0:1, :] = jnp.sum(dw * z, axis=0, keepdims=True)
    gn_ref[1:2, :] = jnp.sum(dw, axis=0, keepdims=True)
    dmid = dy_ref[...] + ln_back(dw, z, inv, norm_ref[2:3, :])
    dmid_ref[...] = dmid
    go = tn(o_ref[...], dmid.astype(bf16)).astype(bf16)
    for h in range(parts):
        gw_refs[h][0, :, 0:dim] = go[64 * h : 64 * h + 54]


def scores_back_kernel(
    scal, dmid_ref, mix_ref, q_ref, k_ref, v_ref, qw_ref, p_ref, pv_ref, *refs, parts, part
):
    heads = mix_ref.shape[1] // PITCH
    n = heads * PITCH
    if part == 0:
        w_refs, refs = refs[:parts], refs[parts:]
        do_ref, gq_ref, gk_ref, gv_ref, g0_ref, g1_ref, wo_ref, dw_ref, dp_ref, dt_ref = refs
        wo_ref[...] = jnp.zeros_like(wo_ref)
        load_weight(wo_ref, w_refs, 3)
        f = dmid_ref[...].astype(bf16)
        head = lane_head((1, 256), 1, scal[0])
        keep = ((head >= 0) & (head < scal[2])).astype(f32)
        do_ref[...] = (nt(f, wo_ref[...]) * keep).astype(bf16)
        for ref in (gk_ref, gv_ref, g0_ref, g1_ref):
            ref[...] = jnp.zeros_like(ref)
    else:
        do_ref, *sums, gq_ref, gkb_ref, gvb_ref, gt_ref, gk_ref, gv_ref, g0_ref, g1_ref, dw_ref, dp_ref, dt_ref = refs
        for ref, old in zip((gk_ref, gv_ref, g0_ref, g1_ref), sums):
            ref[...] = old[...]
    first, last = (0, EARLY) if part == 0 else (EARLY, SIDE)
    for y in range(first, last):
        do = do_ref[PITCH * y : PITCH * (y + 1), :].astype(f32)
        at = n * (y - first)
        dw_ref[at : at + n, :] = (tiled(do, heads) * mix_ref[1]).astype(bf16)
    groups = [(b, b + first // BUNCH, y, count) for b, (y, count) in enumerate(bunches(first, last))]
    for b, _, y, count in groups:
        at = n * (y - first)
        dp_ref[b, :, 0 : n * count] = nt(v_ref[...], dw_ref[at : at + n * count, :])
    for b, whole_b, y, count in groups:
        for at in range(0, n * count, 128):
            dp = dp_ref[b, :, at : at + 128]
            p = p_ref[whole_b, :, at : at + 128].astype(f32)
            dt_ref[b, :, at : at + 128] = (p * (dp - jnp.sum(dp * p, axis=0, keepdims=True))).astype(bf16)
    gv, gk = gv_ref[...], gk_ref[...]
    for b, whole_b, y, count in groups:
        at = n * (y - first)
        gv = gv + nn(p_ref[whole_b, :, 0 : n * count], dw_ref[at : at + n * count, :])
        gk = gk + nn(dt_ref[b, :, 0 : n * count], qw_ref[n * y : n * (y + count), :])
    gv_ref[...] = gv
    gk_ref[...] = gk
    for b, _, y, count in groups:
        dk = tn(dt_ref[b, :, 0 : n * count], k_ref[...])
        for u in range(count):
            mine = dk[n * u : n * (u + 1)]
            at = PITCH * (y + u)
            gq_ref[at - PITCH * first : at - PITCH * first + PITCH, :] = over_heads(mine * mix_ref[0], heads).astype(bf16)
            g0_ref[...] += mine * tiled(q_ref[at : at + PITCH, :].astype(f32), heads)
    for y in range(first, last):
        do = do_ref[PITCH * y : PITCH * (y + 1), :].astype(f32)
        g1_ref[...] += pv_ref[n * y : n * (y + 1), :].astype(f32) * tiled(do, heads)
    if part == 0:
        return
    gkb_ref[...] = gk_ref[...].astype(bf16)
    gvb_ref[...] = gv_ref[...].astype(bf16)
    ex = (true_head(iota((n, heads), 0), scal[0]) == iota((n, heads), 1)).astype(bf16)
    el = (lane_head((256, heads), 0, scal[0]) == iota((256, heads), 1)).astype(bf16)
    for i, ref in enumerate((g0_ref, g1_ref)):
        hi, lo = split2(ref[...])
        hi, lo = split2(nn(hi, el) + nn(lo, el))
        if i == 0:
            gt_ref[i] = (tn(ex, hi) + tn(ex, lo)) * HD**-0.5
        else:
            gt_ref[i] = tn(hi, ex) + tn(lo, ex)


def weights_back_kernel(
    scal, x_ref, a_ref, dmid_ref, norm_ref, gn2_ref, gqa_ref, gqb_ref, gk_ref, gv_ref, gt_ref, y_ref, *refs, parts
):
    w_refs, refs = refs[:parts], refs[parts:]
    both_ref, gw_refs, refs = refs[0], refs[1 : 1 + parts], refs[1 + parts :]
    ws_ref, tmp_ref, flat_ref, sm_ref = refs
    heads = gt_ref.shape[1]
    dim = x_ref.shape[1]
    ws_ref[...] = jnp.zeros_like(ws_ref)
    for b in range(3):
        load_weight(ws_ref.at[b], w_refs, b)
    gq = jnp.concatenate([gqa_ref[...], gqb_ref[...]], axis=0)
    gk, gv = gk_ref[...], gv_ref[...]
    a = a_ref[...]
    da = nn(gq, ws_ref[0]) + nn(gk, ws_ref[1]) + nn(gv, ws_ref[2])
    z, inv = ln_stats(x_ref[...])
    flat_ref[...] = jnp.zeros_like(flat_ref)
    flat_ref[0:1, 0:dim] = jnp.sum(da * z, axis=0, keepdims=True)
    flat_ref[1:2, 0:dim] = jnp.sum(da, axis=0, keepdims=True)
    flat_ref[2:4, 0:dim] = gn2_ref[0:2, :]
    for i in range(2):
        flat_ref[8 : 8 + heads, 128 * i : 128 * i + heads] = gt_ref[i]
    sm_ref[...] = jnp.zeros_like(sm_ref)
    in_free_lanes(flat_ref[0:4, :], sm_ref, 0)
    mix = flat_ref[8 : 8 + heads, :]
    first = iota(mix.shape, 1) < 128
    mix = jnp.where(first, mix, 0.0) + pltpu.roll(jnp.where(first, 0.0, mix), 128 + heads, 1)
    sm_ref[24 : 24 + heads, :] = pltpu.roll(mix, FREE, 1)
    small = jnp.where(iota((54, 256), 1) >= FREE, sm_ref[0:54, :], 0.0).astype(bf16)
    for h in range(parts):
        gw_refs[h][0] = small
    for b, g in enumerate((gq, gk, gv)):
        gw = tn(g, a).astype(bf16)
        for h in range(parts):
            gw_refs[h][b, :, 0:dim] = gw[64 * h : 64 * h + 54]
    tmp_ref[...] = dmid_ref[...] + ln_back(da, z, inv, norm_ref[0:1, :])
    for y in range(SIDE):
        both_ref[1, SIDE * y : SIDE * (y + 1), :] = tmp_ref[PITCH * y : PITCH * y + SIDE, :].astype(bf16)
    both_ref[0] = y_ref[...]


def cast_kernel(m_hbm, out_ref, m_ref, sem):
    copy = pltpu.make_async_copy(m_hbm, m_ref, sem)
    copy.start()
    copy.wait()
    for i in range(out_ref.shape[0]):
        out_ref[i] = m_ref[:, i, :].astype(bf16)


def spot(slot, per):
    bits = per.bit_length() - 1
    return slot >> (bits + 1), (slot >> bits) & 1, slot & (per - 1)


def stack_kernel(*refs):
    for k, ref in enumerate(refs[:-1]):
        refs[-1][k] = ref[...]


def select_kernel(slot_ref, scal, conv_ref, *refs):
    sources, (attn_ref, ffn_ref, every_ref) = refs[:4], refs[4:]
    per = sources[0].shape[0]
    for i in range(2):
        every_ref[i, 0] = sources[2 * i][...]
        every_ref[i, 1:] = sources[2 * i + 1][...]
    for b in range(12):
        pair, place, own = spot(slot_ref[b], per)
        block = every_ref[place ^ scal[4], pair ^ scal[5], own]
        if b < 4:
            attn_ref[b] = block
        else:
            ffn_ref[b - 4] = block
    hi, lo = split2(conv_ref[...])
    ffn_ref[8] = jnp.zeros_like(ffn_ref[8])
    ffn_ref[8, 0:9] = hi
    ffn_ref[8, 16:25] = lo


def total(refs, at):
    acc = refs[0][at].astype(f32)
    for ref in refs[1:]:
        acc = acc + ref[at].astype(f32)
    return acc


def half_sum_kernel(a_ref, b_ref, out_ref):
    out_ref[...] = (a_ref[...].astype(f32) + b_ref[...].astype(f32)).astype(bf16)


def spread_ffn_kernel(slot_ref, scal, *refs):
    ffn_refs, out_ref = refs[:-1], refs[-1]
    pairs, _, per = out_ref.shape[:3]
    out_ref[...] = jnp.zeros_like(out_ref)
    for b in range(9):
        block = total(ffn_refs, b)
        k, j, i = spot(slot_ref[3 + b], per)
        out_ref[k ^ scal[5], j ^ scal[4], i, :, 0:FREE] = block[:, 0:FREE].astype(bf16)
        if b == 0:
            wide = block[:, FREE:].astype(bf16)
    for k in range(pairs):
        for j in range(2):
            out_ref[k, j, 0, :, FREE:] = wide


def spread_attn_kernel(slot_ref, scal, old_ref, *refs, parts):
    attn, outs = refs[:parts], refs[parts:]
    half, per = outs[0].shape[:2]
    for i, ref in enumerate(outs):
        ref[...] = old_ref[half * (i % 2) : half * (i % 2 + 1), i // 2]
    for b in range(3):
        block = total(attn, b)
        low = block[:, 0:FREE].astype(bf16)
        if b == 0:
            wide = block[:, FREE:].astype(bf16)
        pair, place, own = spot(slot_ref[b], per)
        pair, place = pair ^ scal[5], place ^ scal[4]
        for i, ref in enumerate(outs):

            @pl.when((place == i // 2) & ((pair >= half) == (i % 2 == 1)))
            def _():
                ref[pair & (half - 1), own, :, 0:FREE] = low

    for ref in outs:
        for k in range(half):
            ref[k, 1, :, FREE:] = wide


def place_sum_kernel(own_ref, other_ref, *outs):
    for k, out_ref in enumerate(outs):
        out_ref[...] = (own_ref[k].astype(f32) + other_ref[k].astype(f32)).astype(out_ref.dtype)


def adam(w, g, one, two, rate, decay):
    one_new = 0.5 * one + 0.5 * g
    two_new = 0.5 * two + 0.5 * g * g
    hat_one = one_new / (1.0 - 0.5**3)
    hat_two = two_new / (1.0 - 0.5**3)
    return w - rate * (hat_one / (jnp.sqrt(hat_two) + 1e-08) + decay * w), one_new, two_new


def update_kernel(*refs):
    got, refs = refs[:-28], refs[-28:]
    ins, outs, (g_ref, sm_ref, flat_ref) = refs[0:12], refs[12:25], refs[25:]
    per, rows = got[0].shape[:2]
    dim = ins[0].shape[2]
    for i in range(per):
        g = total(got, i)
        g_ref[:, i, :] = g[:, 0:dim]
        sm_ref[i, 0:rows, :] = g
    w, one, two = adam(ins[0][...], g_ref[...], ins[1][...], ins[2][...], 0.06, 0.05)
    outs[0][...], outs[1][...], outs[2][...], outs[3][...] = w, one, two, w.astype(bf16)
    heads = ins[6].shape[0]
    flat_ref[0:9, :] = from_free_lanes(sm_ref.at[0], 0, 9)
    flat_ref[16:20, :] = from_free_lanes(sm_ref.at[1], 0, 4)
    mix = pltpu.roll(sm_ref[1, 24 : 24 + heads, :], 256 - FREE, 1)
    flat_ref[32 : 32 + heads, :] = mix
    flat_ref[48 : 48 + heads, :] = pltpu.roll(mix, 256 - heads, 1)
    outs[4][...], outs[5][...], outs[6][...] = adam(
        ins[3][...], flat_ref[16:20, 0:dim], ins[4][...], ins[5][...], 0.2, 0.0
    )
    for i in range(2):
        w, one, two = adam(
            ins[6][:, i, :], flat_ref[16 * (i + 2) : 16 * (i + 2) + heads, 0:heads], ins[7][:, i, :], ins[8][:, i, :],
            0.2, 0.0,
        )
        outs[7][:, i, :], outs[8][:, i, :], outs[9][:, i, :] = w, one, two
    outs[10][...], outs[11][...], outs[12][...] = adam(
        ins[9][...], flat_ref[0:9, 0:dim], ins[10][...], ins[11][...], 0.2, 0.05
    )


def assemble_kernel(scal, *refs):
    ins, outs, (all_ref,) = refs[:-3], refs[-3:-1], refs[-1:]
    parts, tokens = len(ins), ins[0].shape[1]
    step = 32
    shape = (parts * step, parts * step)
    row, col = iota(shape, 0), iota(shape, 1)
    bits = parts.bit_length() - 1
    pick = ((row >> bits == col & (step - 1)) & (row & (parts - 1) == col >> 5)).astype(bf16)
    full = all_ref.shape[1]
    for k in range(parts):
        all_ref[k, tokens // step * step : full, :] = jnp.zeros((full - tokens // step * step, all_ref.shape[2]), bf16)
    for i, out_ref in enumerate(outs):
        for k, ref in enumerate(ins):
            all_ref[scal[0] ^ k, 0:tokens, :] = ref[i]
        for at in range(0, tokens, step):
            mixed = nn(pick, jnp.concatenate([all_ref[k, at : at + step, :] for k in range(parts)], axis=0))
            for t in range(min(step, tokens - at)):
                out_ref[at + t] = mixed[parts * t : parts * (t + 1)]


VM = pl.BlockSpec(memory_space=pltpu.VMEM)
SM = pl.BlockSpec(memory_space=pltpu.SMEM)
SDS = jax.ShapeDtypeStruct


def call(body, name, n_scalar, n_in, out_shape, scratch=(), mb=16, micros=1, **kw):
    return pl.pallas_call(
        functools.partial(body, **kw) if kw else body,
        in_specs=[SM] * n_scalar + [VM] * n_in,
        out_specs=[VM] * len(out_shape),
        out_shape=out_shape,
        scratch_shapes=scratch,
        compiler_params=pltpu.CompilerParams(vmem_limit_bytes=mb << 20),
        cost_estimate=pl.CostEstimate(flops=micros * 1000000000, transcendentals=0, bytes_accessed=micros * 3000000),
        name=name,
    )


def prep(scal, tokens, cotangent, norm_params, talk):
    tok, dim = tokens.shape[1], tokens.shape[2]
    pad = SIDE * PITCH
    heads = talk.shape[1]
    n = heads * PITCH
    full = lambda *s: pl.BlockSpec(s, lambda i, sc: (0,) * len(s))
    return pl.pallas_call(
        prep_kernel,
        grid_spec=pltpu.PrefetchScalarGridSpec(
            num_scalar_prefetch=1,
            grid=(1,),
            in_specs=[
                pl.BlockSpec((1, tok, dim), lambda i, sc: (sc[0], 0, 0)),
                pl.BlockSpec((1, tok, dim), lambda i, sc: (sc[0], 0, 0)),
                full(*norm_params.shape),
                full(*talk.shape),
            ],
            out_specs=[full(pad, dim), full(pad, dim), full(pad, dim), full(2, n, 256), full(pad, 128)],
            scratch_shapes=[pltpu.VMEM((tok, dim), f32)],
        ),
        out_shape=[SDS((pad, dim), f32), SDS((pad, dim), bf16), SDS((pad, dim), f32), SDS((2, n, 256), f32),
                   SDS((pad, 128), f32)],
        compiler_params=pltpu.CompilerParams(vmem_limit_bytes=16 << 20),
        cost_estimate=pl.CostEstimate(flops=1000000000, transcendentals=0, bytes_accessed=3000000),
        name="prep",
    )(scal, tokens, cotangent, norm_params, talk)


def attn_fwd(scal, x, a, mix, bias, w):
    pad, dim = x.shape
    n = mix.shape[1]
    grid = (len(bunches(0, SIDE)), pad, n * BUNCH)
    return call(
        attn_fwd_kernel, "attn_fwd", 1, 4 + len(w),
        [SDS((pad, dim), f32)] + [SDS((pad, 256), bf16)] * 4
        + [SDS((SIDE * n, 256), bf16), SDS(grid, bf16), SDS((SIDE * n, 256), bf16)],
        [pltpu.VMEM((4, 256, dim), bf16), pltpu.VMEM(grid, f32)],
        mb=24, micros=1, parts=len(w),
    )(scal, x, a, mix, bias, *w)


def ffn_first(scal, mid, dy, norm_params, w):
    pad, dim = mid.shape
    count = len(w)
    lanes = [(count, 256, dim)] * 2 + [(count, pad, 256)] * 2
    grids = [pltpu.VMEM((count, 2, pad + 2 * MARGIN, 128), f32)] * 2
    return call(
        ffn_first_kernel, "ffn_first", 1, 3 + count,
        [SDS((pad, dim), f32), SDS((pad, 128), f32), SDS((pad, dim), bf16), SDS((pad, dim), bf16)]
        + [SDS(t, bf16) for t in lanes] + [SDS((count, 9, 256), f32)],
        grids + [pltpu.VMEM((count, 9, 256), f32)],
        mb=24, micros=3, parts=count,
    )(scal, mid, dy, norm_params, *w)


def ffn_last(scal, mid, dy, norm_params, o, first, w):
    pad, dim = mid.shape
    late = len(w)
    parts = first[4].shape[0] + late
    grids = [pltpu.VMEM((late, 2, pad + 2 * MARGIN, 128), f32)] * 2
    return call(
        ffn_last_kernel, "ffn_last", 1, 13 + late,
        [SDS((SIDE * SIDE, dim), bf16), SDS((pad, dim), f32), SDS((8, dim), f32)] + [SDS((9, 54, 256), bf16)] * parts,
        [pltpu.VMEM((late, 256, dim), bf16)] * 2 + [pltpu.VMEM((late, pad, 256), bf16)] * 2
        + [pltpu.VMEM((late, 9, 256), f32)] + grids
        + [
            pltpu.VMEM((late, 9, 256), f32), pltpu.VMEM((pad, dim), f32), pltpu.VMEM((parts, 56, 256), f32),
            pltpu.VMEM((pad, dim), f32),
        ],
        mb=24, micros=4, parts=parts, late=late,
    )(scal, mid, dy, norm_params, o, *first, *w)


def scores_back(scal, dmid, mix, q, k, v, qw, p, pv, more, part):
    pad, dim = dmid.shape
    n = mix.shape[1]
    heads = n // PITCH
    sums = [SDS((pad, 256), f32)] * 2 + [SDS((n, 256), f32)] * 2
    count = EARLY if part == 0 else SIDE - EARLY
    half = SDS((PITCH * count, 256), bf16)
    if part == 0:
        outs = [SDS((pad, 256), bf16), half] + sums
        scratch = [pltpu.VMEM((256, dim), bf16)]
    else:
        outs = [half] + [SDS((pad, 256), bf16)] * 2 + [SDS((2, heads, heads), f32)]
        scratch = [pltpu.VMEM(t.shape, f32) for t in sums]
    scratch += [
        pltpu.VMEM((n * count, 256), bf16), pltpu.VMEM((-(-count // BUNCH), pad, n * BUNCH), f32),
        pltpu.VMEM((-(-count // BUNCH), pad, n * BUNCH), bf16),
    ]
    return call(
        scores_back_kernel, "scores_back", 1, 8 + len(more), outs, scratch,
        mb=24, micros=4, parts=len(more), part=part,
    )(scal, dmid, mix, q, k, v, qw, p, pv, *more)


def weights_back(scal, x, a, dmid, norm_params, gn2, gqa, gqb, gk, gv, gt, out, w):
    pad, dim = x.shape
    return call(
        weights_back_kernel, "weights_back", 1, 11 + len(w),
        [SDS((2, SIDE * SIDE, dim), bf16)] + [SDS((3, 54, 256), bf16)] * len(w),
        [pltpu.VMEM((3, 256, dim), bf16), pltpu.VMEM((pad, dim), f32), pltpu.VMEM((24, 256), f32),
         pltpu.VMEM((56, 256), f32)],
        mb=24, micros=3, parts=len(w),
    )(scal, x, a, dmid, norm_params, gn2, gqa, gqb, gk, gv, gt, out, *w)


def permute(x, axis, k):
    return lax.ppermute(x, axis, [(i, i ^ k) for i in range(lax.axis_size(axis))])


def swap(t):
    return jnp.swapaxes(t, 0, 1)


def whole(*shape):
    return pl.BlockSpec(shape, lambda i: (0,) * len(shape))


def staged(body, name, ins, outs, scratch=(), micros=1):
    return pl.pallas_call(
        body,
        grid=(1,),
        in_specs=[VM] * len(ins),
        out_specs=[whole(*t.shape) for t in outs],
        out_shape=outs,
        scratch_shapes=scratch,
        compiler_params=pltpu.CompilerParams(vmem_limit_bytes=16 << 20),
        cost_estimate=pl.CostEstimate(flops=micros * 1000000000, transcendentals=0, bytes_accessed=micros * 3000000),
        name=name,
    )(*ins)


def local(
    tokens, cotangent, image_count, subnet_heads, subnet_width, block_slot,
    master, master_m1, master_m2, norm_params, norm_m1, norm_m2, talk, talk_m1, talk_m2, conv, conv_m1, conv_m2,
):
    slots, rows, dim = master.shape
    parts = lax.axis_size("head")
    ranks = lax.axis_size("dp")
    place_id = lax.axis_index("head").astype(jnp.int32)
    rank = lax.axis_index("dp").astype(jnp.int32)
    scal = jnp.concatenate(
        [place_id[None], image_count, subnet_heads, subnet_width, (rank % 2)[None], (rank // 2)[None]]
    )
    mine = pl.pallas_call(
        cast_kernel,
        grid=(1,),
        in_specs=[pl.BlockSpec(memory_space=pltpu.HBM)],
        out_specs=whole(slots, rows, dim),
        out_shape=SDS((slots, rows, dim), bf16),
        scratch_shapes=[pltpu.VMEM((rows, slots, dim), f32), pltpu.SemaphoreType.DMA],
        compiler_params=pltpu.CompilerParams(vmem_limit_bytes=16 << 20),
        name="cast",
    )(swap(master))
    pairs = ranks // 2
    half = pairs // 2
    near, far = range(1, half), range(half, pairs)
    apart = {k: permute(mine, "dp", 2 * k) for k in (*far, *near)}
    near_other = permute(mine, "dp", 1)
    apart[1], near_other = lax.optimization_barrier((apart[1], near_other))
    apart[half], tokens, cotangent, talk_in = lax.optimization_barrier((apart[half], tokens, cotangent, talk))
    (far_own,) = call(stack_kernel, "stack", 0, pairs - 1, [SDS((pairs - 1, slots, rows, dim), bf16)])(
        *[apart[k] for k in range(1, pairs)]
    )
    far_other = permute(far_own, "dp", 1)
    x, a, dy, mix, bias = prep(scal, tokens, cotangent, norm_params, talk_in)
    far_other, x = lax.optimization_barrier((far_other, x))
    attn_w, ffn_w = call(
        select_kernel, "select", 2, 5, [SDS((4, rows, dim), bf16), SDS((9, rows, dim), bf16)],
        [pltpu.VMEM((2, pairs, slots, rows, dim), bf16)],
    )(block_slot, scal, conv, mine, far_own, near_other, far_other)
    attn_2, attn_1 = permute(attn_w, "head", 2), permute(attn_w, "head", 1)
    attn_3 = permute(attn_2, "head", 1)
    attn_w = [attn_w, attn_1, attn_2, attn_3]
    ffn_2, ffn_1 = permute(ffn_w, "head", 2), permute(ffn_w, "head", 1)
    mid, q, k, v, o, qw, p, pv = attn_fwd(scal, x, a, mix, bias, attn_w)
    mid, ffn_2 = lax.optimization_barrier((mid, ffn_2))
    ffn_3 = permute(ffn_2, "head", 1)
    first = list(ffn_first(scal, mid, dy, norm_params, [ffn_w, ffn_1]))
    first[0], ffn_3 = lax.optimization_barrier((first[0], ffn_3))
    out, dmid, gn2, *ffn_g = ffn_last(scal, mid, dy, norm_params, o, first, [ffn_2, ffn_3])
    ffn_1, ffn_3 = permute(ffn_g[1], "head", 1), permute(ffn_g[3], "head", 1)
    do, gqa, *sums = scores_back(scal, dmid, mix, q, k, v, qw, p, pv, attn_w, 0)
    do, ffn_1, ffn_3 = lax.optimization_barrier((do, ffn_1, ffn_3))
    (summed,) = call(half_sum_kernel, "half_sum", 0, 2, [SDS(ffn_3.shape, bf16)])(ffn_g[2], ffn_3)
    ffn_2 = permute(summed, "head", 2)
    gqb, gk, gv, gt = scores_back(scal, dmid, mix, q, k, v, qw, p, pv, [do, *sums], 1)
    both, *attn_g = weights_back(scal, x, a, dmid, norm_params, gn2, gqa, gqb, gk, gv, gt, out, attn_w)
    attn_1, attn_3 = permute(attn_g[1], "head", 1), permute(attn_g[3], "head", 1)
    (summed,) = call(half_sum_kernel, "half_sum", 0, 2, [SDS(attn_3.shape, bf16)])(attn_g[2], attn_3)
    attn_2 = permute(summed, "head", 2)
    (message,) = call(
        spread_ffn_kernel, "spread_ffn", 2, 3, [SDS((ranks // 2, 2, slots, rows, 256), bf16)]
    )(block_slot, scal, ffn_g[0], ffn_1, ffn_2)
    both, message = lax.optimization_barrier((both, message))
    both_2, both_1 = permute(both, "head", 2), permute(both, "head", 1)
    both_3 = permute(both_2, "head", 1)
    near_own, far_own, near_other, far_other = call(
        spread_attn_kernel, "spread_attn", 2, 4, [SDS((half,) + message.shape[2:], bf16)] * 4, parts=3,
    )(block_slot, scal, message, attn_g[0], attn_1, attn_2)
    slot_shape = (slots, rows, 256)
    far_other = permute(far_other, "dp", 1)
    near_other = permute(near_other, "dp", 1)
    far_sum = call(place_sum_kernel, "place_sum", 0, 2, [SDS(slot_shape, bf16)] * half)(far_own, far_other)
    far_sum = [permute(far_sum[k - half], "dp", 2 * k) for k in far]
    own, *near_sum = call(
        place_sum_kernel, "place_sum", 0, 2, [SDS(slot_shape, f32)] + [SDS(slot_shape, bf16)] * (half - 1)
    )(near_own, near_other)
    got = [own] + [permute(near_sum[k - 1], "dp", 2 * k) for k in near] + far_sum
    shape = SDS((tokens.shape[1], parts, dim), f32)
    output, token_grad = pl.pallas_call(
        assemble_kernel,
        grid=(1,),
        in_specs=[SM] + [whole(*both.shape)] * parts,
        out_specs=[whole(*shape.shape)] * 2,
        out_shape=[shape, shape],
        scratch_shapes=[pltpu.VMEM((parts, 224, dim), bf16)],
        compiler_params=pltpu.CompilerParams(vmem_limit_bytes=16 << 20),
        cost_estimate=pl.CostEstimate(flops=1000000000, transcendentals=0, bytes_accessed=3000000),
        name="assemble",
    )(scal, both, both_1, both_2, both_3)
    got[-1], output, token_grad = lax.optimization_barrier((got[-1], output, token_grad))
    state = [
        swap(master), swap(master_m1), swap(master_m2), norm_params, norm_m1, norm_m2,
        swap(talk), swap(talk_m1), swap(talk_m2), conv, conv_m1, conv_m2,
    ]
    shapes = [SDS(t.shape, f32) for t in state]
    shapes.insert(3, SDS(state[0].shape, bf16))
    new = staged(
        update_kernel, "update", [*got, *state], shapes,
        [pltpu.VMEM((rows, slots, dim), f32), pltpu.VMEM((slots, 64, 256), f32), pltpu.VMEM((64, 256), f32)],
    )
    new = [swap(t) if t.ndim == 3 else t for t in new]
    return (swap(output), swap(token_grad), *new)


def solution(mesh):
    in_specs = (
        P("dp", None, None),
        P("dp", None, None),
        P("dp"),
        P(),
        P(),
        P(),
        P("dp", None, "head"),
        P("dp", None, "head"),
        P("dp", None, "head"),
        P(),
        P(),
        P(),
        P(),
        P(),
        P(),
        P(None, "head"),
        P(None, "head"),
        P(None, "head"),
    )
    out_specs = (
        P("dp", None, None),
        P("dp", None, None),
        P("dp", None, "head"),
        P("dp", None, "head"),
        P("dp", None, "head"),
        P("dp", None, "head"),
        P(),
        P(),
        P(),
        P(),
        P(),
        P(),
        P(None, "head"),
        P(None, "head"),
        P(None, "head"),
    )
    return jax.shard_map(local, mesh=mesh, in_specs=in_specs, out_specs=out_specs, check_vma=False)
```

```python
import functools
import jax
import jax.numpy as jnp
from jax import lax
from jax.experimental import pallas as pl
from jax.experimental.pallas import tpu as pltpu
from jax.sharding import PartitionSpec as P

HD = 18
SIDE = 14
PITCH = 16
MARGIN = 24
BUNCH = 4
EARLY = 4


def bunches(first, last):
    return [(y, min(BUNCH, last - y)) for y in range(first, last, BUNCH)]

FREE = 216
WIDE = 40
norm_eps = 1e-05
bf16 = jnp.bfloat16
f32 = jnp.float32


def nn(a, b):
    return lax.dot_general(a, b, (((1,), (0,)), ((), ())), preferred_element_type=f32)


def nt(a, b):
    return lax.dot_general(a, b, (((1,), (1,)), ((), ())), preferred_element_type=f32)


def tn(a, b):
    return lax.dot_general(a, b, (((0,), (0,)), ((), ())), preferred_element_type=f32)


def iota(shape, dim):
    return lax.broadcasted_iota(jnp.int32, shape, dim)


def split2(v):
    hi = v.astype(bf16)
    return hi, (v - hi.astype(f32)).astype(bf16)


def real_rows(shape):
    return (iota(shape, 0) & (PITCH - 1)) < SIDE


def lane_head(shape, dim, place):
    lane = iota(shape, dim)
    rest = lane & 63
    head = ((lane >> 6) ^ place) * 3 + (rest >= 18).astype(jnp.int32) + (rest >= 36).astype(jnp.int32)
    return jnp.where(rest < 54, head, -1)


def true_head(rows, place):
    head = rows >> 4
    part = (head >= 3).astype(jnp.int32) + (head >= 6).astype(jnp.int32) + (head >= 9).astype(jnp.int32)
    return (part ^ place) * 3 + (head - 3 * part)


def prep_kernel(
    scal, tok_ref, cot_ref, norm_ref, talk_ref, x_ref, a_ref, dy_ref, mix_ref, bias_ref, keep_ref, ex_ref, el_ref, tmp_ref
):
    x_ref[...] = jnp.zeros_like(x_ref)
    dy_ref[...] = jnp.zeros_like(dy_ref)
    valid = (scal[0] < scal[1]).astype(f32)
    tmp_ref[...] = tok_ref[0].astype(f32)
    for y in range(SIDE):
        x_ref[PITCH * y : PITCH * y + SIDE, :] = tmp_ref[SIDE * y : SIDE * (y + 1), :]
        dy_ref[PITCH * y : PITCH * y + SIDE, :] = cot_ref[0, SIDE * y : SIDE * (y + 1), :] * valid
    x = x_ref[...]
    centred = x - jnp.mean(x, axis=-1, keepdims=True)
    inv = lax.rsqrt(jnp.mean(centred * centred, axis=-1, keepdims=True) + norm_eps)
    a = centred * inv * norm_ref[0:1, :] + norm_ref[1:2, :]
    a_ref[...] = jnp.where(real_rows(a.shape), a, 0.0).astype(bf16)
    heads = talk_ref.shape[1]
    n = heads * PITCH
    ex = (true_head(iota((n, heads), 0), scal[0]) == iota((n, heads), 1)).astype(bf16)
    el = (lane_head((256, heads), 0, scal[0]) == iota((256, heads), 1)).astype(bf16)
    for i in range(2):
        both = []
        for part in split2(talk_ref[i]):
            if i == 0:
                both.append(nt(nn(ex, part).astype(bf16), el))
            else:
                both.append(nt(nt(ex, part).astype(bf16), el))
        mix_ref[i] = (both[0] + both[1]) * (HD**-0.5 if i == 0 else 1.0)
    bias_ref[...] = jnp.where(real_rows(bias_ref.shape), 0.0, -1e30)
    lanes = lane_head((1, 256), 1, scal[0])
    keep_ref[0:1, :] = ((lanes >= 0) & (lanes < scal[2])).astype(f32)
    lane = iota((1, 256), 1)
    for k in range(keep_ref.shape[0] - 2):
        unit = ((k ^ scal[0]) * 4 + (lane >> 6)) * 54 + (lane & 63)
        keep_ref[1 + k : 2 + k, :] = (unit < scal[3]).astype(f32)
    keep_ref[keep_ref.shape[0] - 1 :, :] = jnp.broadcast_to(valid, (1, 256))
    ex_ref[...] = ex
    el_ref[...] = el


def load_weight(dst_ref, w_refs, b):
    for k, w_ref in enumerate(w_refs):
        dst_ref[64 * k : 64 * k + 54, :] = w_ref[b]


def tiled(rows, heads):
    return jnp.concatenate([rows] * heads, axis=0)


def over_heads(rows, heads):
    return jnp.sum(rows.reshape(heads, PITCH, rows.shape[1]), axis=0)


def attn_fwd_kernel(x_ref, a_ref, mix_ref, bias_ref, keep_ref, *refs, parts):
    w_refs, refs = refs[:parts], refs[parts:]
    mid_ref, q_ref, k_ref, v_ref, o_ref, qw_ref, p_ref, pv_ref, ws_ref, t_ref = refs
    heads = mix_ref.shape[1] // PITCH
    a = a_ref[...]
    ws_ref[...] = jnp.zeros_like(ws_ref)
    for b, dst in enumerate((q_ref, k_ref, v_ref)):
        load_weight(ws_ref.at[b], w_refs, b)
        dst[...] = nt(a, ws_ref[b]).astype(bf16)
    load_weight(ws_ref.at[3], w_refs, 3)
    keep = keep_ref[0:1, :]

    n = heads * PITCH
    for y in range(SIDE):
        q = q_ref[PITCH * y : PITCH * (y + 1), :].astype(f32)
        qw_ref[n * y : n * (y + 1), :] = (tiled(q, heads) * mix_ref[0]).astype(bf16)
    for b, (y, count) in enumerate(bunches(0, SIDE)):
        t_ref[b, :, 0 : n * count] = nt(k_ref[...], qw_ref[n * y : n * (y + count), :])
    for b, (y, count) in enumerate(bunches(0, SIDE)):
        for at in range(0, n * count, 128):
            t = t_ref[b, :, at : at + 128] + bias_ref[...]
            e = jnp.exp(t - jnp.max(t, axis=0, keepdims=True))
            p_ref[b, :, at : at + 128] = (e * (1.0 / jnp.sum(e, axis=0, keepdims=True))).astype(bf16)
    for b, (first, count) in enumerate(bunches(0, SIDE)):
        pv = tn(p_ref[b, :, 0 : n * count], v_ref[...])
        pv_ref[n * first : n * (first + count), :] = pv.astype(bf16)
        for u in range(count):
            o = over_heads(pv[n * u : n * (u + 1)] * mix_ref[1], heads)
            o_ref[PITCH * (first + u) : PITCH * (first + u + 1), :] = (o * keep).astype(bf16)
    mid_ref[...] = x_ref[...] + nn(o_ref[...], ws_ref[3])


def ln_stats(v):
    centred = v - jnp.mean(v, axis=-1, keepdims=True)
    inv = lax.rsqrt(jnp.mean(centred * centred, axis=-1, keepdims=True) + norm_eps)
    return centred * inv, inv


def ln_back(grad, scaled, inv, gain):
    gs = grad * gain
    return inv * (
        gs - jnp.mean(gs, axis=-1, keepdims=True) - scaled * jnp.mean(gs * scaled, axis=-1, keepdims=True)
    )


def in_free_lanes(flat, dst_ref, first_row):
    rows = flat.shape[0]
    for j in range(6):
        dst_ref[first_row + rows * j : first_row + rows * (j + 1), :] = pltpu.roll(flat, (FREE - WIDE * j) % 256, 1)


def from_free_lanes(src_ref, first_row, rows):
    lane = iota((rows, 256), 1)
    flat = jnp.zeros((rows, 256), f32)
    for j in range(6):
        moved = pltpu.roll(src_ref[first_row + rows * j : first_row + rows * (j + 1), :], (WIDE * j - FREE) % 256, 1)
        flat = flat + jnp.where((lane >= WIDE * j) & (lane < WIDE * (j + 1)), moved, 0.0)
    return flat


def place(rows=216):
    shape = (rows, 256)
    lane = iota(shape, 1)
    rest = lane & 63
    return ((iota(shape, 0) == (lane >> 6) * 54 + rest) & (rest < 54)).astype(bf16)


def up(w_ref, w, e, win_ref, wdn_ref, h_ref, d_ref, cv_ref):
    tokens, dim = w.shape
    pad = MARGIN
    for j in range(4):
        at = 64 * j
        win_ref[at : at + 54, :] = w_ref[j]
        wdn_ref[at : at + 54, :] = w_ref[4 + j]
        win_ref[at + 54 : at + 64, :] = jnp.zeros((10, dim), bf16)
        wdn_ref[at + 54 : at + 64, :] = jnp.zeros((10, dim), bf16)
    both = nn(w_ref[8], place(dim))
    cv_ref[...] = both[0:9] + both[16:25]
    hidden = nt(w, win_ref[...])
    dgate = nt(e, wdn_ref[...])
    zero = jnp.zeros((pad, 128), f32)
    for half in range(2):
        mine = slice(128 * half, 128 * (half + 1))
        for ref, value in ((h_ref, hidden), (d_ref, dgate)):
            ref[half, 0:pad, :] = zero
            ref[half, pad + tokens :, :] = zero
            ref[half, pad : pad + tokens, :] = value[:, mine]


def middle(keep, h_ref, d_ref, gate_ref, dh_ref, cv_ref, gcv_ref):
    tokens = gate_ref.shape[0]
    pad = MARGIN
    for half in range(2):
        cols = slice(128 * half, 128 * (half + 1))
        on = keep[:, cols]
        act = None
        for t in range(9):
            off = pad + PITCH * (t // 3 - 1) + t % 3 - 1
            term = cv_ref[t : t + 1, cols] * h_ref[half, off : off + tokens, :]
            act = term if act is None else act + term
        sig = 0.5 * jnp.tanh(0.5 * act) + 0.5
        silu = act * sig
        gate_ref[:, cols] = (silu * on).astype(bf16)
        dact = d_ref[half, pad : pad + tokens, :] * on * (silu + sig * (1.0 - silu))
        d_ref[half, pad : pad + tokens, :] = dact
        dh = None
        for t in range(9):
            shift = PITCH * (t // 3 - 1) + t % 3 - 1
            gcv_ref[t : t + 1, cols] = jnp.sum(
                dact * h_ref[half, pad + shift : pad + shift + tokens, :], axis=0, keepdims=True
            )
            term = cv_ref[t : t + 1, cols] * d_ref[half, pad - shift : pad - shift + tokens, :]
            dh = term if dh is None else dh + term
        dh_ref[:, cols] = dh.astype(bf16)


def ffn_first_kernel(mid_ref, dy_ref, norm_ref, keep_ref, *refs, parts):
    w_refs, refs = refs[:parts], refs[parts:]
    z_ref, inv_ref, w_ref, e_ref, win_ref, wdn_ref, gate_ref, dh_ref, gcv_ref, h_ref, d_ref, cv_ref = refs
    z, inv = ln_stats(mid_ref[...])
    z_ref[...] = z
    inv_ref[...] = jnp.broadcast_to(inv, inv_ref.shape)
    w = jnp.where(real_rows(z.shape), z * norm_ref[2:3, :] + norm_ref[3:4, :], 0.0).astype(bf16)
    e = dy_ref[...].astype(bf16)
    w_ref[...] = w
    e_ref[...] = e
    for k in range(parts):
        up(w_refs[k], w, e, win_ref.at[k], wdn_ref.at[k], h_ref.at[k], d_ref.at[k], cv_ref.at[k])
    for k in range(parts):
        middle(
            keep_ref[1 + k : 2 + k, :], h_ref.at[k], d_ref.at[k], gate_ref.at[k], dh_ref.at[k], cv_ref.at[k], gcv_ref.at[k]
        )


def ffn_last_kernel(
    mid_ref, dy_ref, norm_ref, keep_ref, o_ref, z_ref, inv_ref, w_ref, e_ref, *refs, parts, late
):
    early = parts - late
    wins, wdns, gates, dhs, gcvs = refs[:5]
    last_refs, refs = refs[5 : 5 + late], refs[5 + late :]
    out_ref, dmid_ref, gn_ref = refs[:3]
    gw_refs, refs = refs[3 : 3 + parts], refs[3 + parts :]
    win_ref, wdn_ref, gate_ref, dh_ref, gcv_ref, h_ref, d_ref, cv_ref, tmp_ref, sm_ref, dw_ref = refs
    w, e = w_ref[...], e_ref[...]
    dim = w.shape[1]
    wins, wdns, gates, dhs, gcvs = [
        [ref.at[i] for i in range(early)] + [own.at[i] for i in range(late)]
        for ref, own in ((wins, win_ref), (wdns, wdn_ref), (gates, gate_ref), (dhs, dh_ref), (gcvs, gcv_ref))
    ]

    def back(h):
        gi = tn(dhs[h][...], w).astype(bf16)
        gd = tn(gates[h][...], e).astype(bf16)
        for j in range(4):
            gw_refs[h][1 + j, :, 0:dim] = gi[64 * j : 64 * j + 54]
            gw_refs[h][5 + j, :, 0:dim] = gd[64 * j : 64 * j + 54]

    for i in range(late):
        up(last_refs[i], w, e, win_ref.at[i], wdn_ref.at[i], h_ref.at[i], d_ref.at[i], cv_ref.at[i])
    for h in range(early):
        back(h)
    for i in range(late):
        middle(
            keep_ref[1 + early + i : 2 + early + i, :], h_ref.at[i], d_ref.at[i], gate_ref.at[i], dh_ref.at[i], cv_ref.at[i], gcv_ref.at[i]
        )
    dw_ref[...] = sum(nn(dhs[h][...], wins[h][...]) for h in range(parts))
    valid = keep_ref[parts + 1 : parts + 2, 0:1]
    tmp_ref[...] = (mid_ref[...] + sum(nn(gates[h][...], wdns[h][...]) for h in range(parts))) * valid
    free = iota((54, 256), 1) >= FREE
    pm = place(256)
    for h in range(parts):
        if h >= early:
            back(h)
        in_free_lanes(nt(gcvs[h][...].astype(bf16), pm), sm_ref.at[h], 0)
        gw_refs[h][0] = jnp.where(free, sm_ref[h, 0:54, :], 0.0).astype(bf16)
    for y in range(SIDE):
        out_ref[SIDE * y : SIDE * (y + 1), :] = tmp_ref[PITCH * y : PITCH * y + SIDE, :].astype(bf16)
    z, inv = z_ref[...], inv_ref[:, 0:1]
    dw = jnp.where(real_rows(z.shape), dw_ref[...], 0.0)
    gn_ref[...] = jnp.zeros_like(gn_ref)
    gn_ref[0:1, :] = jnp.sum(dw * z, axis=0, keepdims=True)
    gn_ref[1:2, :] = jnp.sum(dw, axis=0, keepdims=True)
    dmid = dy_ref[...] + ln_back(dw, z, inv, norm_ref[2:3, :])
    dmid_ref[...] = dmid
    go = tn(o_ref[...], dmid.astype(bf16)).astype(bf16)
    for h in range(parts):
        gw_refs[h][0, :, 0:dim] = go[64 * h : 64 * h + 54]


def scores_back_kernel(
    dmid_ref, mix_ref, keep_ref, ex_ref, el_ref, q_ref, k_ref, v_ref, qw_ref, p_ref, pv_ref, *refs, parts, part
):
    heads = mix_ref.shape[1] // PITCH
    n = heads * PITCH
    if part == 0:
        w_refs, refs = refs[:parts], refs[parts:]
        do_ref, gq_ref, gk_ref, gv_ref, g0_ref, g1_ref, wo_ref, dw_ref, dp_ref, dt_ref = refs
        wo_ref[...] = jnp.zeros_like(wo_ref)
        load_weight(wo_ref, w_refs, 3)
        f = dmid_ref[...].astype(bf16)
        keep = keep_ref[0:1, :]
        do_ref[...] = (nt(f, wo_ref[...]) * keep).astype(bf16)
        for ref in (gk_ref, gv_ref, g0_ref, g1_ref):
            ref[...] = jnp.zeros_like(ref)
    else:
        do_ref, *sums, gq_ref, gkb_ref, gvb_ref, gt_ref, gk_ref, gv_ref, g0_ref, g1_ref, dw_ref, dp_ref, dt_ref = refs
        for ref, old in zip((gk_ref, gv_ref, g0_ref, g1_ref), sums):
            ref[...] = old[...]
    first, last = (0, EARLY) if part == 0 else (EARLY, SIDE)
    for y in range(first, last):
        do = do_ref[PITCH * y : PITCH * (y + 1), :].astype(f32)
        at = n * (y - first)
        dw_ref[at : at + n, :] = (tiled(do, heads) * mix_ref[1]).astype(bf16)
    groups = [(b, b + first // BUNCH, y, count) for b, (y, count) in enumerate(bunches(first, last))]
    for b, _, y, count in groups:
        at = n * (y - first)
        dp_ref[b, :, 0 : n * count] = nt(v_ref[...], dw_ref[at : at + n * count, :])
    for b, whole_b, y, count in groups:
        for at in range(0, n * count, 128):
            dp = dp_ref[b, :, at : at + 128]
            p = p_ref[whole_b, :, at : at + 128].astype(f32)
            dt_ref[b, :, at : at + 128] = (p * (dp - jnp.sum(dp * p, axis=0, keepdims=True))).astype(bf16)
    gv, gk = gv_ref[...], gk_ref[...]
    for b, whole_b, y, count in groups:
        at = n * (y - first)
        gv = gv + nn(p_ref[whole_b, :, 0 : n * count], dw_ref[at : at + n * count, :])
        gk = gk + nn(dt_ref[b, :, 0 : n * count], qw_ref[n * y : n * (y + count), :])
    gv_ref[...] = gv
    gk_ref[...] = gk
    for b, _, y, count in groups:
        dk = tn(dt_ref[b, :, 0 : n * count], k_ref[...])
        for u in range(count):
            mine = dk[n * u : n * (u + 1)]
            at = PITCH * (y + u)
            gq_ref[at - PITCH * first : at - PITCH * first + PITCH, :] = over_heads(mine * mix_ref[0], heads).astype(bf16)
            g0_ref[...] += mine * tiled(q_ref[at : at + PITCH, :].astype(f32), heads)
    for y in range(first, last):
        do = do_ref[PITCH * y : PITCH * (y + 1), :].astype(f32)
        g1_ref[...] += pv_ref[n * y : n * (y + 1), :].astype(f32) * tiled(do, heads)
    if part == 0:
        return
    gkb_ref[...] = gk_ref[...].astype(bf16)
    gvb_ref[...] = gv_ref[...].astype(bf16)
    ex, el = ex_ref[...], el_ref[...]
    for i, ref in enumerate((g0_ref, g1_ref)):
        hi, lo = split2(ref[...])
        hi, lo = split2(nn(hi, el) + nn(lo, el))
        if i == 0:
            gt_ref[i] = (tn(ex, hi) + tn(ex, lo)) * HD**-0.5
        else:
            gt_ref[i] = tn(hi, ex) + tn(lo, ex)


def weights_back_kernel(
    x_ref, a_ref, dmid_ref, norm_ref, gn2_ref, gqa_ref, gqb_ref, gk_ref, gv_ref, gt_ref, y_ref, *refs, parts
):
    w_refs, refs = refs[:parts], refs[parts:]
    both_ref, gw_refs, refs = refs[0], refs[1 : 1 + parts], refs[1 + parts :]
    ws_ref, tmp_ref, flat_ref, sm_ref = refs
    heads = gt_ref.shape[1]
    dim = x_ref.shape[1]
    ws_ref[...] = jnp.zeros_like(ws_ref)
    for b in range(3):
        load_weight(ws_ref.at[b], w_refs, b)
    gq = jnp.concatenate([gqa_ref[...], gqb_ref[...]], axis=0)
    gk, gv = gk_ref[...], gv_ref[...]
    a = a_ref[...]
    da = nn(gq, ws_ref[0]) + nn(gk, ws_ref[1]) + nn(gv, ws_ref[2])
    z, inv = ln_stats(x_ref[...])
    flat_ref[...] = jnp.zeros_like(flat_ref)
    flat_ref[0:1, 0:dim] = jnp.sum(da * z, axis=0, keepdims=True)
    flat_ref[1:2, 0:dim] = jnp.sum(da, axis=0, keepdims=True)
    flat_ref[2:4, 0:dim] = gn2_ref[0:2, :]
    for i in range(2):
        flat_ref[8 : 8 + heads, 128 * i : 128 * i + heads] = gt_ref[i]
    sm_ref[...] = jnp.zeros_like(sm_ref)
    in_free_lanes(flat_ref[0:4, :], sm_ref, 0)
    mix = flat_ref[8 : 8 + heads, :]
    first = iota(mix.shape, 1) < 128
    mix = jnp.where(first, mix, 0.0) + pltpu.roll(jnp.where(first, 0.0, mix), 128 + heads, 1)
    sm_ref[24 : 24 + heads, :] = pltpu.roll(mix, FREE, 1)
    small = jnp.where(iota((54, 256), 1) >= FREE, sm_ref[0:54, :], 0.0).astype(bf16)
    for h in range(parts):
        gw_refs[h][0] = small
    for b, g in enumerate((gq, gk, gv)):
        gw = tn(g, a).astype(bf16)
        for h in range(parts):
            gw_refs[h][b, :, 0:dim] = gw[64 * h : 64 * h + 54]
    tmp_ref[...] = dmid_ref[...] + ln_back(da, z, inv, norm_ref[0:1, :])
    for y in range(SIDE):
        both_ref[1, SIDE * y : SIDE * (y + 1), :] = tmp_ref[PITCH * y : PITCH * y + SIDE, :].astype(bf16)
    both_ref[0] = y_ref[...]


def cast_kernel(m_hbm, out_ref, m_ref, sem):
    copy = pltpu.make_async_copy(m_hbm, m_ref, sem)
    copy.start()
    copy.wait()
    for i in range(out_ref.shape[0]):
        out_ref[i] = m_ref[:, i, :].astype(bf16)


def spot(slot, per):
    bits = per.bit_length() - 1
    return slot >> (bits + 1), (slot >> bits) & 1, slot & (per - 1)


def stack_kernel(*refs):
    for k, ref in enumerate(refs[:-1]):
        refs[-1][k] = ref[...]


def select_kernel(slot_ref, scal, conv_ref, *refs):
    sources, (attn_ref, ffn_ref, every_ref) = refs[:4], refs[4:]
    per = sources[0].shape[0]
    for i in range(2):
        every_ref[i, 0] = sources[2 * i][...]
        every_ref[i, 1:] = sources[2 * i + 1][...]
    for b in range(12):
        pair, place, own = spot(slot_ref[b], per)
        block = every_ref[place ^ scal[4], pair ^ scal[5], own]
        if b < 4:
            attn_ref[b] = block
        else:
            ffn_ref[b - 4] = block
    hi, lo = split2(conv_ref[...])
    ffn_ref[8] = jnp.zeros_like(ffn_ref[8])
    ffn_ref[8, 0:9] = hi
    ffn_ref[8, 16:25] = lo


def total(refs, at):
    acc = refs[0][at].astype(f32)
    for ref in refs[1:]:
        acc = acc + ref[at].astype(f32)
    return acc


def half_sum_kernel(a_ref, b_ref, out_ref):
    out_ref[...] = (a_ref[...].astype(f32) + b_ref[...].astype(f32)).astype(bf16)


def spread_ffn_kernel(slot_ref, scal, *refs):
    ffn_refs, out_ref = refs[:-1], refs[-1]
    pairs, _, per = out_ref.shape[:3]
    out_ref[...] = jnp.zeros_like(out_ref)
    for b in range(9):
        block = total(ffn_refs, b)
        k, j, i = spot(slot_ref[3 + b], per)
        out_ref[k ^ scal[5], j ^ scal[4], i, :, 0:FREE] = block[:, 0:FREE].astype(bf16)
        if b == 0:
            wide = block[:, FREE:].astype(bf16)
    for k in range(pairs):
        for j in range(2):
            out_ref[k, j, 0, :, FREE:] = wide


def spread_attn_kernel(slot_ref, scal, old_ref, *refs, parts):
    attn, outs = refs[:parts], refs[parts:]
    half, per = outs[0].shape[:2]
    for i, ref in enumerate(outs):
        ref[...] = old_ref[half * (i % 2) : half * (i % 2 + 1), i // 2]
    for b in range(3):
        block = total(attn, b)
        low = block[:, 0:FREE].astype(bf16)
        if b == 0:
            wide = block[:, FREE:].astype(bf16)
        pair, place, own = spot(slot_ref[b], per)
        pair, place = pair ^ scal[5], place ^ scal[4]
        for i, ref in enumerate(outs):

            @pl.when((place == i // 2) & ((pair >= half) == (i % 2 == 1)))
            def _():
                ref[pair & (half - 1), own, :, 0:FREE] = low

    for ref in outs:
        for k in range(half):
            ref[k, 1, :, FREE:] = wide


def place_sum_kernel(own_ref, other_ref, *outs):
    for k, out_ref in enumerate(outs):
        out_ref[...] = (own_ref[k].astype(f32) + other_ref[k].astype(f32)).astype(out_ref.dtype)


def adam(w, g, one, two, rate, decay):
    one_new = 0.5 * one + 0.5 * g
    two_new = 0.5 * two + 0.5 * g * g
    hat_one = one_new / (1.0 - 0.5**3)
    hat_two = two_new / (1.0 - 0.5**3)
    return w - rate * (hat_one / (jnp.sqrt(hat_two) + 1e-08) + decay * w), one_new, two_new


def update_kernel(*refs):
    got, refs = refs[:-28], refs[-28:]
    ins, outs, (g_ref, sm_ref, flat_ref) = refs[0:12], refs[12:25], refs[25:]
    per, rows = got[0].shape[:2]
    dim = ins[0].shape[2]
    for i in range(per):
        g = total(got, i)
        g_ref[:, i, :] = g[:, 0:dim]
        sm_ref[i, 0:rows, :] = g
    w, one, two = adam(ins[0][...], g_ref[...], ins[1][...], ins[2][...], 0.06, 0.05)
    outs[0][...], outs[1][...], outs[2][...], outs[3][...] = w, one, two, w.astype(bf16)
    heads = ins[6].shape[0]
    flat_ref[0:9, :] = from_free_lanes(sm_ref.at[0], 0, 9)
    flat_ref[16:20, :] = from_free_lanes(sm_ref.at[1], 0, 4)
    mix = pltpu.roll(sm_ref[1, 24 : 24 + heads, :], 256 - FREE, 1)
    flat_ref[32 : 32 + heads, :] = mix
    flat_ref[48 : 48 + heads, :] = pltpu.roll(mix, 256 - heads, 1)
    outs[4][...], outs[5][...], outs[6][...] = adam(
        ins[3][...], flat_ref[16:20, 0:dim], ins[4][...], ins[5][...], 0.2, 0.0
    )
    for i in range(2):
        w, one, two = adam(
            ins[6][:, i, :], flat_ref[16 * (i + 2) : 16 * (i + 2) + heads, 0:heads], ins[7][:, i, :], ins[8][:, i, :],
            0.2, 0.0,
        )
        outs[7][:, i, :], outs[8][:, i, :], outs[9][:, i, :] = w, one, two
    outs[10][...], outs[11][...], outs[12][...] = adam(
        ins[9][...], flat_ref[0:9, 0:dim], ins[10][...], ins[11][...], 0.2, 0.05
    )


def assemble_kernel(scal, *refs):
    ins, outs, (all_ref,) = refs[:-3], refs[-3:-1], refs[-1:]
    parts, tokens = len(ins), ins[0].shape[1]
    step = 32
    shape = (parts * step, parts * step)
    row, col = iota(shape, 0), iota(shape, 1)
    bits = parts.bit_length() - 1
    pick = ((row >> bits == col & (step - 1)) & (row & (parts - 1) == col >> 5)).astype(bf16)
    full = all_ref.shape[1]
    for k in range(parts):
        all_ref[k, tokens // step * step : full, :] = jnp.zeros((full - tokens // step * step, all_ref.shape[2]), bf16)
    for i, out_ref in enumerate(outs):
        for k, ref in enumerate(ins):
            all_ref[scal[0] ^ k, 0:tokens, :] = ref[i]
        for at in range(0, tokens, step):
            mixed = nn(pick, jnp.concatenate([all_ref[k, at : at + step, :] for k in range(parts)], axis=0))
            for t in range(min(step, tokens - at)):
                out_ref[at + t] = mixed[parts * t : parts * (t + 1)]


VM = pl.BlockSpec(memory_space=pltpu.VMEM)
SM = pl.BlockSpec(memory_space=pltpu.SMEM)
SDS = jax.ShapeDtypeStruct


def call(body, name, n_scalar, n_in, out_shape, scratch=(), mb=16, micros=1, **kw):
    return pl.pallas_call(
        functools.partial(body, **kw) if kw else body,
        in_specs=[SM] * n_scalar + [VM] * n_in,
        out_specs=[VM] * len(out_shape),
        out_shape=out_shape,
        scratch_shapes=scratch,
        compiler_params=pltpu.CompilerParams(vmem_limit_bytes=mb << 20),
        cost_estimate=pl.CostEstimate(flops=micros * 1000000000, transcendentals=0, bytes_accessed=micros * 3000000),
        name=name,
    )


def prep(scal, tokens, cotangent, norm_params, talk, parts):
    tok, dim = tokens.shape[1], tokens.shape[2]
    pad = SIDE * PITCH
    heads = talk.shape[1]
    n = heads * PITCH
    full = lambda *s: pl.BlockSpec(s, lambda i, sc: (0,) * len(s))
    return pl.pallas_call(
        prep_kernel,
        grid_spec=pltpu.PrefetchScalarGridSpec(
            num_scalar_prefetch=1,
            grid=(1,),
            in_specs=[
                pl.BlockSpec((1, tok, dim), lambda i, sc: (sc[0], 0, 0)),
                pl.BlockSpec((1, tok, dim), lambda i, sc: (sc[0], 0, 0)),
                full(*norm_params.shape),
                full(*talk.shape),
            ],
            out_specs=[full(pad, dim), full(pad, dim), full(pad, dim), full(2, n, 256), full(pad, 128),
                full(parts + 2, 256), full(n, heads), full(256, heads),
            ],
            scratch_shapes=[pltpu.VMEM((tok, dim), f32)],
        ),
        out_shape=[SDS((pad, dim), f32), SDS((pad, dim), bf16), SDS((pad, dim), f32), SDS((2, n, 256), f32),
                   SDS((pad, 128), f32), SDS((parts + 2, 256), f32), SDS((n, heads), bf16), SDS((256, heads), bf16)],
        compiler_params=pltpu.CompilerParams(vmem_limit_bytes=16 << 20),
        cost_estimate=pl.CostEstimate(flops=1000000000, transcendentals=0, bytes_accessed=3000000),
        name="prep",
    )(scal, tokens, cotangent, norm_params, talk)


def attn_fwd(x, a, mix, bias, keep, w):
    pad, dim = x.shape
    n = mix.shape[1]
    grid = (len(bunches(0, SIDE)), pad, n * BUNCH)
    return call(
        attn_fwd_kernel, "attn_fwd", 0, 5 + len(w),
        [SDS((pad, dim), f32)] + [SDS((pad, 256), bf16)] * 4
        + [SDS((SIDE * n, 256), bf16), SDS(grid, bf16), SDS((SIDE * n, 256), bf16)],
        [pltpu.VMEM((4, 256, dim), bf16), pltpu.VMEM(grid, f32)],
        mb=24, micros=1, parts=len(w),
    )(x, a, mix, bias, keep, *w)


def ffn_first(mid, dy, norm_params, keep, w):
    pad, dim = mid.shape
    count = len(w)
    lanes = [(count, 256, dim)] * 2 + [(count, pad, 256)] * 2
    grids = [pltpu.VMEM((count, 2, pad + 2 * MARGIN, 128), f32)] * 2
    return call(
        ffn_first_kernel, "ffn_first", 0, 4 + count,
        [SDS((pad, dim), f32), SDS((pad, 128), f32), SDS((pad, dim), bf16), SDS((pad, dim), bf16)]
        + [SDS(t, bf16) for t in lanes] + [SDS((count, 9, 256), f32)],
        grids + [pltpu.VMEM((count, 9, 256), f32)],
        mb=24, micros=3, parts=count,
    )(mid, dy, norm_params, keep, *w)


def ffn_last(mid, dy, norm_params, keep, o, first, w):
    pad, dim = mid.shape
    late = len(w)
    parts = first[4].shape[0] + late
    grids = [pltpu.VMEM((late, 2, pad + 2 * MARGIN, 128), f32)] * 2
    return call(
        ffn_last_kernel, "ffn_last", 0, 14 + late,
        [SDS((SIDE * SIDE, dim), bf16), SDS((pad, dim), f32), SDS((8, dim), f32)] + [SDS((9, 54, 256), bf16)] * parts,
        [pltpu.VMEM((late, 256, dim), bf16)] * 2 + [pltpu.VMEM((late, pad, 256), bf16)] * 2
        + [pltpu.VMEM((late, 9, 256), f32)] + grids
        + [
            pltpu.VMEM((late, 9, 256), f32), pltpu.VMEM((pad, dim), f32), pltpu.VMEM((parts, 56, 256), f32),
            pltpu.VMEM((pad, dim), f32),
        ],
        mb=24, micros=4, parts=parts, late=late,
    )(mid, dy, norm_params, keep, o, *first, *w)


def scores_back(dmid, mix, keep, ex, el, q, k, v, qw, p, pv, more, part):
    pad, dim = dmid.shape
    n = mix.shape[1]
    heads = n // PITCH
    sums = [SDS((pad, 256), f32)] * 2 + [SDS((n, 256), f32)] * 2
    count = EARLY if part == 0 else SIDE - EARLY
    half = SDS((PITCH * count, 256), bf16)
    if part == 0:
        outs = [SDS((pad, 256), bf16), half] + sums
        scratch = [pltpu.VMEM((256, dim), bf16)]
    else:
        outs = [half] + [SDS((pad, 256), bf16)] * 2 + [SDS((2, heads, heads), f32)]
        scratch = [pltpu.VMEM(t.shape, f32) for t in sums]
    scratch += [
        pltpu.VMEM((n * count, 256), bf16), pltpu.VMEM((-(-count // BUNCH), pad, n * BUNCH), f32),
        pltpu.VMEM((-(-count // BUNCH), pad, n * BUNCH), bf16),
    ]
    return call(
        scores_back_kernel, "scores_back", 0, 11 + len(more), outs, scratch,
        mb=24, micros=4, parts=len(more), part=part,
    )(dmid, mix, keep, ex, el, q, k, v, qw, p, pv, *more)


def weights_back(x, a, dmid, norm_params, gn2, gqa, gqb, gk, gv, gt, out, w):
    pad, dim = x.shape
    return call(
        weights_back_kernel, "weights_back", 0, 11 + len(w),
        [SDS((2, SIDE * SIDE, dim), bf16)] + [SDS((3, 54, 256), bf16)] * len(w),
        [pltpu.VMEM((3, 256, dim), bf16), pltpu.VMEM((pad, dim), f32), pltpu.VMEM((24, 256), f32),
         pltpu.VMEM((56, 256), f32)],
        mb=24, micros=3, parts=len(w),
    )(x, a, dmid, norm_params, gn2, gqa, gqb, gk, gv, gt, out, *w)


def permute(x, axis, k):
    return lax.ppermute(x, axis, [(i, i ^ k) for i in range(lax.axis_size(axis))])


def swap(t):
    return jnp.swapaxes(t, 0, 1)


def whole(*shape):
    return pl.BlockSpec(shape, lambda i: (0,) * len(shape))


def staged(body, name, ins, outs, scratch=(), micros=1):
    return pl.pallas_call(
        body,
        grid=(1,),
        in_specs=[VM] * len(ins),
        out_specs=[whole(*t.shape) for t in outs],
        out_shape=outs,
        scratch_shapes=scratch,
        compiler_params=pltpu.CompilerParams(vmem_limit_bytes=16 << 20),
        cost_estimate=pl.CostEstimate(flops=micros * 1000000000, transcendentals=0, bytes_accessed=micros * 3000000),
        name=name,
    )(*ins)


def local(
    tokens, cotangent, image_count, subnet_heads, subnet_width, block_slot,
    master, master_m1, master_m2, norm_params, norm_m1, norm_m2, talk, talk_m1, talk_m2, conv, conv_m1, conv_m2,
):
    slots, rows, dim = master.shape
    parts = lax.axis_size("head")
    ranks = lax.axis_size("dp")
    place_id = lax.axis_index("head").astype(jnp.int32)
    rank = lax.axis_index("dp").astype(jnp.int32)
    scal = jnp.concatenate(
        [place_id[None], image_count, subnet_heads, subnet_width, (rank % 2)[None], (rank // 2)[None]]
    )
    mine = pl.pallas_call(
        cast_kernel,
        grid=(1,),
        in_specs=[pl.BlockSpec(memory_space=pltpu.HBM)],
        out_specs=whole(slots, rows, dim),
        out_shape=SDS((slots, rows, dim), bf16),
        scratch_shapes=[pltpu.VMEM((rows, slots, dim), f32), pltpu.SemaphoreType.DMA],
        compiler_params=pltpu.CompilerParams(vmem_limit_bytes=16 << 20),
        name="cast",
    )(swap(master))
    pairs = ranks // 2
    half = pairs // 2
    near, far = range(1, half), range(half, pairs)
    apart = {k: permute(mine, "dp", 2 * k) for k in (*far, *near)}
    near_other = permute(mine, "dp", 1)
    apart[1], near_other = lax.optimization_barrier((apart[1], near_other))
    apart[half], tokens, cotangent, talk_in = lax.optimization_barrier((apart[half], tokens, cotangent, talk))
    (far_own,) = call(stack_kernel, "stack", 0, pairs - 1, [SDS((pairs - 1, slots, rows, dim), bf16)])(
        *[apart[k] for k in range(1, pairs)]
    )
    far_other = permute(far_own, "dp", 1)
    x, a, dy, mix, bias, keep, ex, el = prep(scal, tokens, cotangent, norm_params, talk_in, parts)
    far_other, x = lax.optimization_barrier((far_other, x))
    attn_w, ffn_w = call(
        select_kernel, "select", 2, 5, [SDS((4, rows, dim), bf16), SDS((9, rows, dim), bf16)],
        [pltpu.VMEM((2, pairs, slots, rows, dim), bf16)],
    )(block_slot, scal, conv, mine, far_own, near_other, far_other)
    attn_2, attn_1 = permute(attn_w, "head", 2), permute(attn_w, "head", 1)
    attn_3 = permute(attn_2, "head", 1)
    attn_w = [attn_w, attn_1, attn_2, attn_3]
    ffn_2, ffn_1 = permute(ffn_w, "head", 2), permute(ffn_w, "head", 1)
    mid, q, k, v, o, qw, p, pv = attn_fwd(x, a, mix, bias, keep, attn_w)
    mid, ffn_2 = lax.optimization_barrier((mid, ffn_2))
    ffn_3 = permute(ffn_2, "head", 1)
    first = list(ffn_first(mid, dy, norm_params, keep, [ffn_w, ffn_1]))
    first[0], ffn_3 = lax.optimization_barrier((first[0], ffn_3))
    out, dmid, gn2, *ffn_g = ffn_last(mid, dy, norm_params, keep, o, first, [ffn_2, ffn_3])
    ffn_1, ffn_3 = permute(ffn_g[1], "head", 1), permute(ffn_g[3], "head", 1)
    do, gqa, *sums = scores_back(dmid, mix, keep, ex, el, q, k, v, qw, p, pv, attn_w, 0)
    do, ffn_1, ffn_3 = lax.optimization_barrier((do, ffn_1, ffn_3))
    (summed,) = call(half_sum_kernel, "half_sum", 0, 2, [SDS(ffn_3.shape, bf16)])(ffn_g[2], ffn_3)
    ffn_2 = permute(summed, "head", 2)
    gqb, gk, gv, gt = scores_back(dmid, mix, keep, ex, el, q, k, v, qw, p, pv, [do, *sums], 1)
    both, *attn_g = weights_back(x, a, dmid, norm_params, gn2, gqa, gqb, gk, gv, gt, out, attn_w)
    attn_1, attn_3 = permute(attn_g[1], "head", 1), permute(attn_g[3], "head", 1)
    (summed,) = call(half_sum_kernel, "half_sum", 0, 2, [SDS(attn_3.shape, bf16)])(attn_g[2], attn_3)
    attn_2 = permute(summed, "head", 2)
    (message,) = call(
        spread_ffn_kernel, "spread_ffn", 2, 3, [SDS((ranks // 2, 2, slots, rows, 256), bf16)]
    )(block_slot, scal, ffn_g[0], ffn_1, ffn_2)
    both, message = lax.optimization_barrier((both, message))
    both_2, both_1 = permute(both, "head", 2), permute(both, "head", 1)
    both_3 = permute(both_2, "head", 1)
    near_own, far_own, near_other, far_other = call(
        spread_attn_kernel, "spread_attn", 2, 4, [SDS((half,) + message.shape[2:], bf16)] * 4, parts=3,
    )(block_slot, scal, message, attn_g[0], attn_1, attn_2)
    slot_shape = (slots, rows, 256)
    far_other = permute(far_other, "dp", 1)
    near_other = permute(near_other, "dp", 1)
    far_sum = call(place_sum_kernel, "place_sum", 0, 2, [SDS(slot_shape, bf16)] * half)(far_own, far_other)
    far_sum = [permute(far_sum[k - half], "dp", 2 * k) for k in far]
    own, *near_sum = call(
        place_sum_kernel, "place_sum", 0, 2, [SDS(slot_shape, f32)] + [SDS(slot_shape, bf16)] * (half - 1)
    )(near_own, near_other)
    got = [own] + [permute(near_sum[k - 1], "dp", 2 * k) for k in near] + far_sum
    shape = SDS((tokens.shape[1], parts, dim), f32)
    output, token_grad = pl.pallas_call(
        assemble_kernel,
        grid=(1,),
        in_specs=[SM] + [whole(*both.shape)] * parts,
        out_specs=[whole(*shape.shape)] * 2,
        out_shape=[shape, shape],
        scratch_shapes=[pltpu.VMEM((parts, 224, dim), bf16)],
        compiler_params=pltpu.CompilerParams(vmem_limit_bytes=16 << 20),
        cost_estimate=pl.CostEstimate(flops=1000000000, transcendentals=0, bytes_accessed=3000000),
        name="assemble",
    )(scal, both, both_1, both_2, both_3)
    got[-1], output, token_grad = lax.optimization_barrier((got[-1], output, token_grad))
    state = [
        swap(master), swap(master_m1), swap(master_m2), norm_params, norm_m1, norm_m2,
        swap(talk), swap(talk_m1), swap(talk_m2), conv, conv_m1, conv_m2,
    ]
    shapes = [SDS(t.shape, f32) for t in state]
    shapes.insert(3, SDS(state[0].shape, bf16))
    new = staged(
        update_kernel, "update", [*got, *state], shapes,
        [pltpu.VMEM((rows, slots, dim), f32), pltpu.VMEM((slots, 64, 256), f32), pltpu.VMEM((64, 256), f32)],
    )
    new = [swap(t) if t.ndim == 3 else t for t in new]
    return (swap(output), swap(token_grad), *new)


def solution(mesh):
    in_specs = (
        P("dp", None, None),
        P("dp", None, None),
        P("dp"),
        P(),
        P(),
        P(),
        P("dp", None, "head"),
        P("dp", None, "head"),
        P("dp", None, "head"),
        P(),
        P(),
        P(),
        P(),
        P(),
        P(),
        P(None, "head"),
        P(None, "head"),
        P(None, "head"),
    )
    out_specs = (
        P("dp", None, None),
        P("dp", None, None),
        P("dp", None, "head"),
        P("dp", None, "head"),
        P("dp", None, "head"),
        P("dp", None, "head"),
        P(),
        P(),
        P(),
        P(),
        P(),
        P(),
        P(None, "head"),
        P(None, "head"),
        P(None, "head"),
    )
    return jax.shard_map(local, mesh=mesh, in_specs=in_specs, out_specs=out_specs, check_vma=False)
```

```python
import functools
import jax
import jax.numpy as jnp
from jax import lax
from jax.experimental import pallas as pl
from jax.experimental.pallas import tpu as pltpu
from jax.sharding import PartitionSpec as P

HD = 18
SIDE = 14
PITCH = 16
MARGIN = 24
BUNCH = 4
EARLY = 4


def bunches(first, last):
    return [(y, min(BUNCH, last - y)) for y in range(first, last, BUNCH)]

FREE = 216
WIDE = 40
norm_eps = 1e-05
bf16 = jnp.bfloat16
f32 = jnp.float32


def nn(a, b):
    return lax.dot_general(a, b, (((1,), (0,)), ((), ())), preferred_element_type=f32)


def nt(a, b):
    return lax.dot_general(a, b, (((1,), (1,)), ((), ())), preferred_element_type=f32)


def tn(a, b):
    return lax.dot_general(a, b, (((0,), (0,)), ((), ())), preferred_element_type=f32)


def iota(shape, dim):
    return lax.broadcasted_iota(jnp.int32, shape, dim)


def split2(v):
    hi = v.astype(bf16)
    return hi, (v - hi.astype(f32)).astype(bf16)


def real_rows(shape):
    return (iota(shape, 0) & (PITCH - 1)) < SIDE


def lane_head(shape, dim, place):
    lane = iota(shape, dim)
    rest = lane & 63
    head = ((lane >> 6) ^ place) * 3 + (rest >= 18).astype(jnp.int32) + (rest >= 36).astype(jnp.int32)
    return jnp.where(rest < 54, head, -1)


def true_head(rows, place):
    head = rows >> 4
    part = (head >= 3).astype(jnp.int32) + (head >= 6).astype(jnp.int32) + (head >= 9).astype(jnp.int32)
    return (part ^ place) * 3 + (head - 3 * part)


def spot(slot, per):
    bits = per.bit_length() - 1
    return slot >> (bits + 1), (slot >> bits) & 1, slot & (per - 1)


def prep_kernel(
    scal, slot_ref, tok_ref, cot_ref, norm_ref, talk_ref, x_ref, a_ref, dy_ref, mix_ref, bias_ref, keep_ref, ex_ref, el_ref, sel_ref, tmp_ref, *, pairs
):
    x_ref[...] = jnp.zeros_like(x_ref)
    dy_ref[...] = jnp.zeros_like(dy_ref)
    valid = (scal[0] < scal[1]).astype(f32)
    tmp_ref[...] = tok_ref[0].astype(f32)
    for y in range(SIDE):
        x_ref[PITCH * y : PITCH * y + SIDE, :] = tmp_ref[SIDE * y : SIDE * (y + 1), :]
        dy_ref[PITCH * y : PITCH * y + SIDE, :] = cot_ref[0, SIDE * y : SIDE * (y + 1), :] * valid
    x = x_ref[...]
    centred = x - jnp.mean(x, axis=-1, keepdims=True)
    inv = lax.rsqrt(jnp.mean(centred * centred, axis=-1, keepdims=True) + norm_eps)
    a = centred * inv * norm_ref[0:1, :] + norm_ref[1:2, :]
    a_ref[...] = jnp.where(real_rows(a.shape), a, 0.0).astype(bf16)
    heads = talk_ref.shape[1]
    n = heads * PITCH
    ex = (true_head(iota((n, heads), 0), scal[0]) == iota((n, heads), 1)).astype(bf16)
    el = (lane_head((256, heads), 0, scal[0]) == iota((256, heads), 1)).astype(bf16)
    for i in range(2):
        both = []
        for part in split2(talk_ref[i]):
            if i == 0:
                both.append(nt(nn(ex, part).astype(bf16), el))
            else:
                both.append(nt(nt(ex, part).astype(bf16), el))
        mix_ref[i] = (both[0] + both[1]) * (HD**-0.5 if i == 0 else 1.0)
    bias_ref[...] = jnp.where(real_rows(bias_ref.shape), 0.0, -1e30)
    lanes = lane_head((1, 256), 1, scal[0])
    keep_ref[0:1, :] = ((lanes >= 0) & (lanes < scal[2])).astype(f32)
    lane = iota((1, 256), 1)
    for k in range(keep_ref.shape[0] - 2):
        unit = ((k ^ scal[0]) * 4 + (lane >> 6)) * 54 + (lane & 63)
        keep_ref[1 + k : 2 + k, :] = (unit < scal[3]).astype(f32)
    keep_ref[keep_ref.shape[0] - 1 :, :] = jnp.broadcast_to(valid, (1, 256))
    ex_ref[...] = ex
    el_ref[...] = el
    blocks, slots = sel_ref.shape[:2]
    per = slots // (2 * pairs)
    for b in range(blocks):
        pair, place, own = spot(slot_ref[b], per)
        at = ((place ^ scal[4]) * pairs + (pair ^ scal[5])) * per + own
        sel_ref[b] = (iota(sel_ref.shape[1:], 0) == at).astype(f32)


def load_weight(dst_ref, w_refs, b):
    for k, w_ref in enumerate(w_refs):
        dst_ref[64 * k : 64 * k + 54, :] = w_ref[b]


def tiled(rows, heads):
    return jnp.concatenate([rows] * heads, axis=0)


def over_heads(rows, heads):
    return jnp.sum(rows.reshape(heads, PITCH, rows.shape[1]), axis=0)


def attn_fwd_kernel(x_ref, a_ref, mix_ref, bias_ref, keep_ref, *refs, parts):
    w_refs, refs = refs[:parts], refs[parts:]
    mid_ref, q_ref, k_ref, v_ref, o_ref, qw_ref, p_ref, pv_ref, ws_ref, t_ref = refs
    heads = mix_ref.shape[1] // PITCH
    a = a_ref[...]
    ws_ref[...] = jnp.zeros_like(ws_ref)
    for b, dst in enumerate((q_ref, k_ref, v_ref)):
        load_weight(ws_ref.at[b], w_refs, b)
        dst[...] = nt(a, ws_ref[b]).astype(bf16)
    load_weight(ws_ref.at[3], w_refs, 3)
    keep = keep_ref[0:1, :]

    n = heads * PITCH
    for y in range(SIDE):
        q = q_ref[PITCH * y : PITCH * (y + 1), :].astype(f32)
        qw_ref[n * y : n * (y + 1), :] = (tiled(q, heads) * mix_ref[0]).astype(bf16)
    for b, (y, count) in enumerate(bunches(0, SIDE)):
        t_ref[b, :, 0 : n * count] = nt(k_ref[...], qw_ref[n * y : n * (y + count), :])
    for b, (y, count) in enumerate(bunches(0, SIDE)):
        for at in range(0, n * count, 128):
            t = t_ref[b, :, at : at + 128] + bias_ref[...]
            e = jnp.exp(t - jnp.max(t, axis=0, keepdims=True))
            p_ref[b, :, at : at + 128] = (e * (1.0 / jnp.sum(e, axis=0, keepdims=True))).astype(bf16)
    for b, (first, count) in enumerate(bunches(0, SIDE)):
        pv = tn(p_ref[b, :, 0 : n * count], v_ref[...])
        pv_ref[n * first : n * (first + count), :] = pv.astype(bf16)
        for u in range(count):
            o = over_heads(pv[n * u : n * (u + 1)] * mix_ref[1], heads)
            o_ref[PITCH * (first + u) : PITCH * (first + u + 1), :] = (o * keep).astype(bf16)
    mid_ref[...] = x_ref[...] + nn(o_ref[...], ws_ref[3])


def ln_stats(v):
    centred = v - jnp.mean(v, axis=-1, keepdims=True)
    inv = lax.rsqrt(jnp.mean(centred * centred, axis=-1, keepdims=True) + norm_eps)
    return centred * inv, inv


def ln_back(grad, scaled, inv, gain):
    gs = grad * gain
    return inv * (
        gs - jnp.mean(gs, axis=-1, keepdims=True) - scaled * jnp.mean(gs * scaled, axis=-1, keepdims=True)
    )


def in_free_lanes(flat, dst_ref, first_row):
    rows = flat.shape[0]
    for j in range(6):
        dst_ref[first_row + rows * j : first_row + rows * (j + 1), :] = pltpu.roll(flat, (FREE - WIDE * j) % 256, 1)


def from_free_lanes(src_ref, first_row, rows):
    lane = iota((rows, 256), 1)
    flat = jnp.zeros((rows, 256), f32)
    for j in range(6):
        moved = pltpu.roll(src_ref[first_row + rows * j : first_row + rows * (j + 1), :], (WIDE * j - FREE) % 256, 1)
        flat = flat + jnp.where((lane >= WIDE * j) & (lane < WIDE * (j + 1)), moved, 0.0)
    return flat


def place(rows=216):
    shape = (rows, 256)
    lane = iota(shape, 1)
    rest = lane & 63
    return ((iota(shape, 0) == (lane >> 6) * 54 + rest) & (rest < 54)).astype(bf16)


def up(w_ref, w, e, win_ref, wdn_ref, h_ref, d_ref, cv_ref):
    tokens, dim = w.shape
    pad = MARGIN
    for j in range(4):
        at = 64 * j
        win_ref[at : at + 54, :] = w_ref[j]
        wdn_ref[at : at + 54, :] = w_ref[4 + j]
        win_ref[at + 54 : at + 64, :] = jnp.zeros((10, dim), bf16)
        wdn_ref[at + 54 : at + 64, :] = jnp.zeros((10, dim), bf16)
    both = nn(w_ref[8], place(dim))
    cv_ref[...] = both[0:9] + both[16:25]
    hidden = nt(w, win_ref[...])
    dgate = nt(e, wdn_ref[...])
    zero = jnp.zeros((pad, 128), f32)
    for half in range(2):
        mine = slice(128 * half, 128 * (half + 1))
        for ref, value in ((h_ref, hidden), (d_ref, dgate)):
            ref[half, 0:pad, :] = zero
            ref[half, pad + tokens :, :] = zero
            ref[half, pad : pad + tokens, :] = value[:, mine]


def middle(keep, h_ref, d_ref, gate_ref, dh_ref, cv_ref, gcv_ref):
    tokens = gate_ref.shape[0]
    pad = MARGIN
    for half in range(2):
        cols = slice(128 * half, 128 * (half + 1))
        on = keep[:, cols]
        act = None
        for t in range(9):
            off = pad + PITCH * (t // 3 - 1) + t % 3 - 1
            term = cv_ref[t : t + 1, cols] * h_ref[half, off : off + tokens, :]
            act = term if act is None else act + term
        sig = 0.5 * jnp.tanh(0.5 * act) + 0.5
        silu = act * sig
        gate_ref[:, cols] = (silu * on).astype(bf16)
        dact = d_ref[half, pad : pad + tokens, :] * on * (silu + sig * (1.0 - silu))
        d_ref[half, pad : pad + tokens, :] = dact
        dh = None
        for t in range(9):
            shift = PITCH * (t // 3 - 1) + t % 3 - 1
            gcv_ref[t : t + 1, cols] = jnp.sum(
                dact * h_ref[half, pad + shift : pad + shift + tokens, :], axis=0, keepdims=True
            )
            term = cv_ref[t : t + 1, cols] * d_ref[half, pad - shift : pad - shift + tokens, :]
            dh = term if dh is None else dh + term
        dh_ref[:, cols] = dh.astype(bf16)


def ffn_first_kernel(mid_ref, dy_ref, norm_ref, keep_ref, *refs, parts):
    w_refs, refs = refs[:parts], refs[parts:]
    z_ref, inv_ref, w_ref, e_ref, win_ref, wdn_ref, gate_ref, dh_ref, gcv_ref, h_ref, d_ref, cv_ref = refs
    z, inv = ln_stats(mid_ref[...])
    z_ref[...] = z
    inv_ref[...] = jnp.broadcast_to(inv, inv_ref.shape)
    w = jnp.where(real_rows(z.shape), z * norm_ref[2:3, :] + norm_ref[3:4, :], 0.0).astype(bf16)
    e = dy_ref[...].astype(bf16)
    w_ref[...] = w
    e_ref[...] = e
    for k in range(parts):
        up(w_refs[k], w, e, win_ref.at[k], wdn_ref.at[k], h_ref.at[k], d_ref.at[k], cv_ref.at[k])
    for k in range(parts):
        middle(
            keep_ref[1 + k : 2 + k, :], h_ref.at[k], d_ref.at[k], gate_ref.at[k], dh_ref.at[k], cv_ref.at[k], gcv_ref.at[k]
        )


def ffn_last_kernel(
    mid_ref, dy_ref, norm_ref, keep_ref, o_ref, z_ref, inv_ref, w_ref, e_ref, *refs, parts, late
):
    early = parts - late
    wins, wdns, gates, dhs, gcvs = refs[:5]
    last_refs, refs = refs[5 : 5 + late], refs[5 + late :]
    out_ref, dmid_ref, gn_ref = refs[:3]
    gw_refs, refs = refs[3 : 3 + parts], refs[3 + parts :]
    win_ref, wdn_ref, gate_ref, dh_ref, gcv_ref, h_ref, d_ref, cv_ref, tmp_ref, sm_ref, dw_ref = refs
    w, e = w_ref[...], e_ref[...]
    dim = w.shape[1]
    wins, wdns, gates, dhs, gcvs = [
        [ref.at[i] for i in range(early)] + [own.at[i] for i in range(late)]
        for ref, own in ((wins, win_ref), (wdns, wdn_ref), (gates, gate_ref), (dhs, dh_ref), (gcvs, gcv_ref))
    ]

    def back(h):
        gi = tn(dhs[h][...], w).astype(bf16)
        gd = tn(gates[h][...], e).astype(bf16)
        for j in range(4):
            gw_refs[h][1 + j, :, 0:dim] = gi[64 * j : 64 * j + 54]
            gw_refs[h][5 + j, :, 0:dim] = gd[64 * j : 64 * j + 54]

    for i in range(late):
        up(last_refs[i], w, e, win_ref.at[i], wdn_ref.at[i], h_ref.at[i], d_ref.at[i], cv_ref.at[i])
    for h in range(early):
        back(h)
    for i in range(late):
        middle(
            keep_ref[1 + early + i : 2 + early + i, :], h_ref.at[i], d_ref.at[i], gate_ref.at[i], dh_ref.at[i], cv_ref.at[i], gcv_ref.at[i]
        )
    dw_ref[...] = sum(nn(dhs[h][...], wins[h][...]) for h in range(parts))
    valid = keep_ref[parts + 1 : parts + 2, 0:1]
    tmp_ref[...] = (mid_ref[...] + sum(nn(gates[h][...], wdns[h][...]) for h in range(parts))) * valid
    free = iota((54, 256), 1) >= FREE
    pm = place(256)
    for h in range(parts):
        if h >= early:
            back(h)
        in_free_lanes(nt(gcvs[h][...].astype(bf16), pm), sm_ref.at[h], 0)
        gw_refs[h][0] = jnp.where(free, sm_ref[h, 0:54, :], 0.0).astype(bf16)
    for y in range(SIDE):
        out_ref[SIDE * y : SIDE * (y + 1), :] = tmp_ref[PITCH * y : PITCH * y + SIDE, :].astype(bf16)
    z, inv = z_ref[...], inv_ref[:, 0:1]
    dw = jnp.where(real_rows(z.shape), dw_ref[...], 0.0)
    gn_ref[...] = jnp.zeros_like(gn_ref)
    gn_ref[0:1, :] = jnp.sum(dw * z, axis=0, keepdims=True)
    gn_ref[1:2, :] = jnp.sum(dw, axis=0, keepdims=True)
    dmid = dy_ref[...] + ln_back(dw, z, inv, norm_ref[2:3, :])
    dmid_ref[...] = dmid
    go = tn(o_ref[...], dmid.astype(bf16)).astype(bf16)
    for h in range(parts):
        gw_refs[h][0, :, 0:dim] = go[64 * h : 64 * h + 54]


def scores_back_kernel(
    dmid_ref, mix_ref, keep_ref, ex_ref, el_ref, q_ref, k_ref, v_ref, qw_ref, p_ref, pv_ref, *refs, parts, part
):
    heads = mix_ref.shape[1] // PITCH
    n = heads * PITCH
    if part == 0:
        w_refs, refs = refs[:parts], refs[parts:]
        do_ref, gq_ref, gk_ref, gv_ref, g0_ref, g1_ref, wo_ref, dw_ref, dp_ref, dt_ref = refs
        wo_ref[...] = jnp.zeros_like(wo_ref)
        load_weight(wo_ref, w_refs, 3)
        f = dmid_ref[...].astype(bf16)
        keep = keep_ref[0:1, :]
        do_ref[...] = (nt(f, wo_ref[...]) * keep).astype(bf16)
        for ref in (gk_ref, gv_ref, g0_ref, g1_ref):
            ref[...] = jnp.zeros_like(ref)
    else:
        do_ref, *sums, gq_ref, gkb_ref, gvb_ref, gt_ref, gk_ref, gv_ref, g0_ref, g1_ref, dw_ref, dp_ref, dt_ref = refs
        for ref, old in zip((gk_ref, gv_ref, g0_ref, g1_ref), sums):
            ref[...] = old[...]
    first, last = (0, EARLY) if part == 0 else (EARLY, SIDE)
    for y in range(first, last):
        do = do_ref[PITCH * y : PITCH * (y + 1), :].astype(f32)
        at = n * (y - first)
        dw_ref[at : at + n, :] = (tiled(do, heads) * mix_ref[1]).astype(bf16)
    groups = [(b, b + first // BUNCH, y, count) for b, (y, count) in enumerate(bunches(first, last))]
    for b, _, y, count in groups:
        at = n * (y - first)
        dp_ref[b, :, 0 : n * count] = nt(v_ref[...], dw_ref[at : at + n * count, :])
    for b, whole_b, y, count in groups:
        for at in range(0, n * count, 128):
            dp = dp_ref[b, :, at : at + 128]
            p = p_ref[whole_b, :, at : at + 128].astype(f32)
            dt_ref[b, :, at : at + 128] = (p * (dp - jnp.sum(dp * p, axis=0, keepdims=True))).astype(bf16)
    gv, gk = gv_ref[...], gk_ref[...]
    for b, whole_b, y, count in groups:
        at = n * (y - first)
        gv = gv + nn(p_ref[whole_b, :, 0 : n * count], dw_ref[at : at + n * count, :])
        gk = gk + nn(dt_ref[b, :, 0 : n * count], qw_ref[n * y : n * (y + count), :])
    gv_ref[...] = gv
    gk_ref[...] = gk
    for b, _, y, count in groups:
        dk = tn(dt_ref[b, :, 0 : n * count], k_ref[...])
        for u in range(count):
            mine = dk[n * u : n * (u + 1)]
            at = PITCH * (y + u)
            gq_ref[at - PITCH * first : at - PITCH * first + PITCH, :] = over_heads(mine * mix_ref[0], heads).astype(bf16)
            g0_ref[...] += mine * tiled(q_ref[at : at + PITCH, :].astype(f32), heads)
    for y in range(first, last):
        do = do_ref[PITCH * y : PITCH * (y + 1), :].astype(f32)
        g1_ref[...] += pv_ref[n * y : n * (y + 1), :].astype(f32) * tiled(do, heads)
    if part == 0:
        return
    gkb_ref[...] = gk_ref[...].astype(bf16)
    gvb_ref[...] = gv_ref[...].astype(bf16)
    ex, el = ex_ref[...], el_ref[...]
    for i, ref in enumerate((g0_ref, g1_ref)):
        hi, lo = split2(ref[...])
        hi, lo = split2(nn(hi, el) + nn(lo, el))
        if i == 0:
            gt_ref[i] = (tn(ex, hi) + tn(ex, lo)) * HD**-0.5
        else:
            gt_ref[i] = tn(hi, ex) + tn(lo, ex)


def weights_back_kernel(
    x_ref, a_ref, dmid_ref, norm_ref, gn2_ref, gqa_ref, gqb_ref, gk_ref, gv_ref, gt_ref, y_ref, *refs, parts
):
    w_refs, refs = refs[:parts], refs[parts:]
    both_ref, gw_refs, refs = refs[0], refs[1 : 1 + parts], refs[1 + parts :]
    ws_ref, tmp_ref, flat_ref, sm_ref = refs
    heads = gt_ref.shape[1]
    dim = x_ref.shape[1]
    ws_ref[...] = jnp.zeros_like(ws_ref)
    for b in range(3):
        load_weight(ws_ref.at[b], w_refs, b)
    gq = jnp.concatenate([gqa_ref[...], gqb_ref[...]], axis=0)
    gk, gv = gk_ref[...], gv_ref[...]
    a = a_ref[...]
    da = nn(gq, ws_ref[0]) + nn(gk, ws_ref[1]) + nn(gv, ws_ref[2])
    z, inv = ln_stats(x_ref[...])
    flat_ref[...] = jnp.zeros_like(flat_ref)
    flat_ref[0:1, 0:dim] = jnp.sum(da * z, axis=0, keepdims=True)
    flat_ref[1:2, 0:dim] = jnp.sum(da, axis=0, keepdims=True)
    flat_ref[2:4, 0:dim] = gn2_ref[0:2, :]
    for i in range(2):
        flat_ref[8 : 8 + heads, 128 * i : 128 * i + heads] = gt_ref[i]
    sm_ref[...] = jnp.zeros_like(sm_ref)
    in_free_lanes(flat_ref[0:4, :], sm_ref, 0)
    mix = flat_ref[8 : 8 + heads, :]
    first = iota(mix.shape, 1) < 128
    mix = jnp.where(first, mix, 0.0) + pltpu.roll(jnp.where(first, 0.0, mix), 128 + heads, 1)
    sm_ref[24 : 24 + heads, :] = pltpu.roll(mix, FREE, 1)
    small = jnp.where(iota((54, 256), 1) >= FREE, sm_ref[0:54, :], 0.0).astype(bf16)
    for h in range(parts):
        gw_refs[h][0] = small
    for b, g in enumerate((gq, gk, gv)):
        gw = tn(g, a).astype(bf16)
        for h in range(parts):
            gw_refs[h][b, :, 0:dim] = gw[64 * h : 64 * h + 54]
    tmp_ref[...] = dmid_ref[...] + ln_back(da, z, inv, norm_ref[0:1, :])
    for y in range(SIDE):
        both_ref[1, SIDE * y : SIDE * (y + 1), :] = tmp_ref[PITCH * y : PITCH * y + SIDE, :].astype(bf16)
    both_ref[0] = y_ref[...]


def cast_kernel(m_hbm, out_ref, m_ref, sem):
    copy = pltpu.make_async_copy(m_hbm, m_ref, sem)
    copy.start()
    copy.wait()
    for i in range(out_ref.shape[0]):
        out_ref[i] = m_ref[:, i, :].astype(bf16)


def stack_kernel(*refs):
    for k, ref in enumerate(refs[:-1]):
        refs[-1][k] = ref[...]


def slots_of(sources):
    found = []
    for i, ref in enumerate(sources):
        ranks = [ref] if i % 2 == 0 else [ref.at[k] for k in range(ref.shape[0])]
        found += [rank[own] for rank in ranks for own in range(rank.shape[0])]
    return found


def pick(sel_ref, b, slots):
    dim = slots[0].shape[1]
    block = None
    for i, slot in enumerate(slots):
        term = sel_ref[b, i : i + 1, 0:dim] * slot.astype(f32)
        block = term if block is None else block + term
    return block.astype(bf16)


def select_attn_kernel(sel_ref, *refs):
    slots = slots_of(refs[:-1])
    for b in range(4):
        refs[-1][b] = pick(sel_ref, b, slots)


def select_ffn_kernel(sel_ref, conv_ref, *refs):
    slots, ffn_ref = slots_of(refs[:-1]), refs[-1]
    for b in range(8):
        ffn_ref[b] = pick(sel_ref, 4 + b, slots)
    hi, lo = split2(conv_ref[...])
    ffn_ref[8] = jnp.zeros_like(ffn_ref[8])
    ffn_ref[8, 0:9] = hi
    ffn_ref[8, 16:25] = lo


def total(refs, at):
    acc = refs[0][at].astype(f32)
    for ref in refs[1:]:
        acc = acc + ref[at].astype(f32)
    return acc


def half_sum_kernel(a_ref, b_ref, out_ref):
    out_ref[...] = (a_ref[...].astype(f32) + b_ref[...].astype(f32)).astype(bf16)


def spread_ffn_kernel(slot_ref, scal, *refs):
    ffn_refs, out_ref = refs[:-1], refs[-1]
    pairs, _, per = out_ref.shape[:3]
    out_ref[...] = jnp.zeros_like(out_ref)
    for b in range(9):
        block = total(ffn_refs, b)
        k, j, i = spot(slot_ref[3 + b], per)
        out_ref[k ^ scal[5], j ^ scal[4], i, :, 0:FREE] = block[:, 0:FREE].astype(bf16)
        if b == 0:
            wide = block[:, FREE:].astype(bf16)
    for k in range(pairs):
        for j in range(2):
            out_ref[k, j, 0, :, FREE:] = wide


def spread_attn_kernel(sel_ref, old_ref, *refs, parts):
    attn, outs = refs[:parts], refs[parts:]
    half, per = outs[0].shape[:2]
    blocks = [total(attn, b) for b in range(3)]
    wide = blocks[0][:, FREE:].astype(bf16)
    blocks = [block[:, 0:FREE] for block in blocks]
    for i, ref in enumerate(outs):
        for k in range(half):
            pair = half * (i % 2) + k
            for own in range(per):
                old = old_ref[pair, i // 2, own]
                at = (i // 2 * 2 * half + pair) * per + own
                low = old[:, 0:FREE].astype(f32)
                for b in range(3):
                    low = low + sel_ref[b, at : at + 1, 0:FREE] * blocks[b]
                ref[k, own] = old
                ref[k, own, :, 0:FREE] = low.astype(bf16)
            ref[k, 1, :, FREE:] = wide


def place_sum_kernel(own_ref, other_ref, *outs):
    for k, out_ref in enumerate(outs):
        out_ref[...] = (own_ref[k].astype(f32) + other_ref[k].astype(f32)).astype(out_ref.dtype)


def adam(w, g, one, two, rate, decay):
    one_new = 0.5 * one + 0.5 * g
    two_new = 0.5 * two + 0.5 * g * g
    hat_one = one_new / (1.0 - 0.5**3)
    hat_two = two_new / (1.0 - 0.5**3)
    return w - rate * (hat_one / (jnp.sqrt(hat_two) + 1e-08) + decay * w), one_new, two_new


def update_kernel(*refs):
    got, refs = refs[:-28], refs[-28:]
    ins, outs, (g_ref, sm_ref, flat_ref) = refs[0:12], refs[12:25], refs[25:]
    per, rows = got[0].shape[:2]
    dim = ins[0].shape[2]
    for i in range(per):
        g = total(got, i)
        g_ref[:, i, :] = g[:, 0:dim]
        sm_ref[i, 0:rows, :] = g
    w, one, two = adam(ins[0][...], g_ref[...], ins[1][...], ins[2][...], 0.06, 0.05)
    outs[0][...], outs[1][...], outs[2][...], outs[3][...] = w, one, two, w.astype(bf16)
    heads = ins[6].shape[0]
    flat_ref[0:9, :] = from_free_lanes(sm_ref.at[0], 0, 9)
    flat_ref[16:20, :] = from_free_lanes(sm_ref.at[1], 0, 4)
    mix = pltpu.roll(sm_ref[1, 24 : 24 + heads, :], 256 - FREE, 1)
    flat_ref[32 : 32 + heads, :] = mix
    flat_ref[48 : 48 + heads, :] = pltpu.roll(mix, 256 - heads, 1)
    outs[4][...], outs[5][...], outs[6][...] = adam(
        ins[3][...], flat_ref[16:20, 0:dim], ins[4][...], ins[5][...], 0.2, 0.0
    )
    for i in range(2):
        w, one, two = adam(
            ins[6][:, i, :], flat_ref[16 * (i + 2) : 16 * (i + 2) + heads, 0:heads], ins[7][:, i, :], ins[8][:, i, :],
            0.2, 0.0,
        )
        outs[7][:, i, :], outs[8][:, i, :], outs[9][:, i, :] = w, one, two
    outs[10][...], outs[11][...], outs[12][...] = adam(
        ins[9][...], flat_ref[0:9, 0:dim], ins[10][...], ins[11][...], 0.2, 0.05
    )


def assemble_kernel(scal, *refs):
    ins, outs, (all_ref,) = refs[:-3], refs[-3:-1], refs[-1:]
    parts, tokens = len(ins), ins[0].shape[1]
    step = 32
    shape = (parts * step, parts * step)
    row, col = iota(shape, 0), iota(shape, 1)
    bits = parts.bit_length() - 1
    pick = ((row >> bits == col & (step - 1)) & (row & (parts - 1) == col >> 5)).astype(bf16)
    full = all_ref.shape[1]
    for k in range(parts):
        all_ref[k, tokens // step * step : full, :] = jnp.zeros((full - tokens // step * step, all_ref.shape[2]), bf16)
    for i, out_ref in enumerate(outs):
        for k, ref in enumerate(ins):
            all_ref[scal[0] ^ k, 0:tokens, :] = ref[i]
        for at in range(0, tokens, step):
            mixed = nn(pick, jnp.concatenate([all_ref[k, at : at + step, :] for k in range(parts)], axis=0))
            for t in range(min(step, tokens - at)):
                out_ref[at + t] = mixed[parts * t : parts * (t + 1)]


VM = pl.BlockSpec(memory_space=pltpu.VMEM)
SM = pl.BlockSpec(memory_space=pltpu.SMEM)
SDS = jax.ShapeDtypeStruct


def call(body, name, n_scalar, n_in, out_shape, scratch=(), mb=16, micros=1, **kw):
    return pl.pallas_call(
        functools.partial(body, **kw) if kw else body,
        in_specs=[SM] * n_scalar + [VM] * n_in,
        out_specs=[VM] * len(out_shape),
        out_shape=out_shape,
        scratch_shapes=scratch,
        compiler_params=pltpu.CompilerParams(vmem_limit_bytes=mb << 20),
        cost_estimate=pl.CostEstimate(flops=micros * 1000000000, transcendentals=0, bytes_accessed=micros * 3000000),
        name=name,
    )


def prep(scal, block_slot, tokens, cotangent, norm_params, talk, parts, pairs, slots):
    tok, dim = tokens.shape[1], tokens.shape[2]
    pad = SIDE * PITCH
    heads = talk.shape[1]
    n = heads * PITCH
    full = lambda *s: pl.BlockSpec(s, lambda i, sc, bs: (0,) * len(s))
    return pl.pallas_call(
        functools.partial(prep_kernel, pairs=pairs),
        grid_spec=pltpu.PrefetchScalarGridSpec(
            num_scalar_prefetch=2,
            grid=(1,),
            in_specs=[
                pl.BlockSpec((1, tok, dim), lambda i, sc, bs: (sc[0], 0, 0)),
                pl.BlockSpec((1, tok, dim), lambda i, sc, bs: (sc[0], 0, 0)),
                full(*norm_params.shape),
                full(*talk.shape),
            ],
            out_specs=[full(pad, dim), full(pad, dim), full(pad, dim), full(2, n, 256), full(pad, 128),
                full(parts + 2, 256), full(n, heads), full(256, heads),
                full(12, slots, 256),
            ],
            scratch_shapes=[pltpu.VMEM((tok, dim), f32)],
        ),
        out_shape=[SDS((pad, dim), f32), SDS((pad, dim), bf16), SDS((pad, dim), f32), SDS((2, n, 256), f32),
                   SDS((pad, 128), f32), SDS((parts + 2, 256), f32), SDS((n, heads), bf16), SDS((256, heads), bf16),
                   SDS((12, slots, 256), f32)],
        compiler_params=pltpu.CompilerParams(vmem_limit_bytes=16 << 20),
        cost_estimate=pl.CostEstimate(flops=1000000000, transcendentals=0, bytes_accessed=3000000),
        name="prep",
    )(scal, block_slot, tokens, cotangent, norm_params, talk)


def attn_fwd(x, a, mix, bias, keep, w):
    pad, dim = x.shape
    n = mix.shape[1]
    grid = (len(bunches(0, SIDE)), pad, n * BUNCH)
    return call(
        attn_fwd_kernel, "attn_fwd", 0, 5 + len(w),
        [SDS((pad, dim), f32)] + [SDS((pad, 256), bf16)] * 4
        + [SDS((SIDE * n, 256), bf16), SDS(grid, bf16), SDS((SIDE * n, 256), bf16)],
        [pltpu.VMEM((4, 256, dim), bf16), pltpu.VMEM(grid, f32)],
        mb=24, micros=1, parts=len(w),
    )(x, a, mix, bias, keep, *w)


def ffn_first(mid, dy, norm_params, keep, w):
    pad, dim = mid.shape
    count = len(w)
    lanes = [(count, 256, dim)] * 2 + [(count, pad, 256)] * 2
    grids = [pltpu.VMEM((count, 2, pad + 2 * MARGIN, 128), f32)] * 2
    return call(
        ffn_first_kernel, "ffn_first", 0, 4 + count,
        [SDS((pad, dim), f32), SDS((pad, 128), f32), SDS((pad, dim), bf16), SDS((pad, dim), bf16)]
        + [SDS(t, bf16) for t in lanes] + [SDS((count, 9, 256), f32)],
        grids + [pltpu.VMEM((count, 9, 256), f32)],
        mb=24, micros=3, parts=count,
    )(mid, dy, norm_params, keep, *w)


def ffn_last(mid, dy, norm_params, keep, o, first, w):
    pad, dim = mid.shape
    late = len(w)
    parts = first[4].shape[0] + late
    grids = [pltpu.VMEM((late, 2, pad + 2 * MARGIN, 128), f32)] * 2
    return call(
        ffn_last_kernel, "ffn_last", 0, 14 + late,
        [SDS((SIDE * SIDE, dim), bf16), SDS((pad, dim), f32), SDS((8, dim), f32)] + [SDS((9, 54, 256), bf16)] * parts,
        [pltpu.VMEM((late, 256, dim), bf16)] * 2 + [pltpu.VMEM((late, pad, 256), bf16)] * 2
        + [pltpu.VMEM((late, 9, 256), f32)] + grids
        + [
            pltpu.VMEM((late, 9, 256), f32), pltpu.VMEM((pad, dim), f32), pltpu.VMEM((parts, 56, 256), f32),
            pltpu.VMEM((pad, dim), f32),
        ],
        mb=24, micros=4, parts=parts, late=late,
    )(mid, dy, norm_params, keep, o, *first, *w)


def scores_back(dmid, mix, keep, ex, el, q, k, v, qw, p, pv, more, part):
    pad, dim = dmid.shape
    n = mix.shape[1]
    heads = n // PITCH
    sums = [SDS((pad, 256), f32)] * 2 + [SDS((n, 256), f32)] * 2
    count = EARLY if part == 0 else SIDE - EARLY
    half = SDS((PITCH * count, 256), bf16)
    if part == 0:
        outs = [SDS((pad, 256), bf16), half] + sums
        scratch = [pltpu.VMEM((256, dim), bf16)]
    else:
        outs = [half] + [SDS((pad, 256), bf16)] * 2 + [SDS((2, heads, heads), f32)]
        scratch = [pltpu.VMEM(t.shape, f32) for t in sums]
    scratch += [
        pltpu.VMEM((n * count, 256), bf16), pltpu.VMEM((-(-count // BUNCH), pad, n * BUNCH), f32),
        pltpu.VMEM((-(-count // BUNCH), pad, n * BUNCH), bf16),
    ]
    return call(
        scores_back_kernel, "scores_back", 0, 11 + len(more), outs, scratch,
        mb=24, micros=4, parts=len(more), part=part,
    )(dmid, mix, keep, ex, el, q, k, v, qw, p, pv, *more)


def weights_back(x, a, dmid, norm_params, gn2, gqa, gqb, gk, gv, gt, out, w):
    pad, dim = x.shape
    return call(
        weights_back_kernel, "weights_back", 0, 11 + len(w),
        [SDS((2, SIDE * SIDE, dim), bf16)] + [SDS((3, 54, 256), bf16)] * len(w),
        [pltpu.VMEM((3, 256, dim), bf16), pltpu.VMEM((pad, dim), f32), pltpu.VMEM((24, 256), f32),
         pltpu.VMEM((56, 256), f32)],
        mb=24, micros=3, parts=len(w),
    )(x, a, dmid, norm_params, gn2, gqa, gqb, gk, gv, gt, out, *w)


def permute(x, axis, k):
    return lax.ppermute(x, axis, [(i, i ^ k) for i in range(lax.axis_size(axis))])


def swap(t):
    return jnp.swapaxes(t, 0, 1)


def whole(*shape):
    return pl.BlockSpec(shape, lambda i: (0,) * len(shape))


def staged(body, name, ins, outs, scratch=(), micros=1):
    return pl.pallas_call(
        body,
        grid=(1,),
        in_specs=[VM] * len(ins),
        out_specs=[whole(*t.shape) for t in outs],
        out_shape=outs,
        scratch_shapes=scratch,
        compiler_params=pltpu.CompilerParams(vmem_limit_bytes=16 << 20),
        cost_estimate=pl.CostEstimate(flops=micros * 1000000000, transcendentals=0, bytes_accessed=micros * 3000000),
        name=name,
    )(*ins)


def local(
    tokens, cotangent, image_count, subnet_heads, subnet_width, block_slot,
    master, master_m1, master_m2, norm_params, norm_m1, norm_m2, talk, talk_m1, talk_m2, conv, conv_m1, conv_m2,
):
    slots, rows, dim = master.shape
    parts = lax.axis_size("head")
    ranks = lax.axis_size("dp")
    place_id = lax.axis_index("head").astype(jnp.int32)
    rank = lax.axis_index("dp").astype(jnp.int32)
    scal = jnp.concatenate(
        [place_id[None], image_count, subnet_heads, subnet_width, (rank % 2)[None], (rank // 2)[None]]
    )
    mine = pl.pallas_call(
        cast_kernel,
        grid=(1,),
        in_specs=[pl.BlockSpec(memory_space=pltpu.HBM)],
        out_specs=whole(slots, rows, dim),
        out_shape=SDS((slots, rows, dim), bf16),
        scratch_shapes=[pltpu.VMEM((rows, slots, dim), f32), pltpu.SemaphoreType.DMA],
        compiler_params=pltpu.CompilerParams(vmem_limit_bytes=16 << 20),
        name="cast",
    )(swap(master))
    pairs = ranks // 2
    half = pairs // 2
    near, far = range(1, half), range(half, pairs)
    apart = {k: permute(mine, "dp", 2 * k) for k in (*far, *near)}
    near_other = permute(mine, "dp", 1)
    apart[1], near_other = lax.optimization_barrier((apart[1], near_other))
    apart[half], tokens, cotangent, talk_in = lax.optimization_barrier((apart[half], tokens, cotangent, talk))
    (far_own,) = call(stack_kernel, "stack", 0, pairs - 1, [SDS((pairs - 1, slots, rows, dim), bf16)])(
        *[apart[k] for k in range(1, pairs)]
    )
    far_other = permute(far_own, "dp", 1)
    x, a, dy, mix, bias, keep, ex, el, sel = prep(
        scal, block_slot, tokens, cotangent, norm_params, talk_in, parts, pairs, ranks * slots
    )
    far_other, x = lax.optimization_barrier((far_other, x))
    sources = (mine, far_own, near_other, far_other)
    (attn_w,) = call(select_attn_kernel, "select_attn", 0, 5, [SDS((4, rows, dim), bf16)])(sel, *sources)
    (ffn_w,) = call(select_ffn_kernel, "select_ffn", 0, 6, [SDS((9, rows, dim), bf16)])(sel, conv, *sources)
    attn_2, attn_1 = permute(attn_w, "head", 2), permute(attn_w, "head", 1)
    attn_3 = permute(attn_2, "head", 1)
    attn_w = [attn_w, attn_1, attn_2, attn_3]
    ffn_2, ffn_1 = permute(ffn_w, "head", 2), permute(ffn_w, "head", 1)
    mid, q, k, v, o, qw, p, pv = attn_fwd(x, a, mix, bias, keep, attn_w)
    mid, ffn_2 = lax.optimization_barrier((mid, ffn_2))
    ffn_3 = permute(ffn_2, "head", 1)
    first = list(ffn_first(mid, dy, norm_params, keep, [ffn_w, ffn_1]))
    first[0], ffn_3 = lax.optimization_barrier((first[0], ffn_3))
    out, dmid, gn2, *ffn_g = ffn_last(mid, dy, norm_params, keep, o, first, [ffn_2, ffn_3])
    ffn_3 = permute(ffn_g[3], "head", 1)
    do, gqa, *sums = scores_back(dmid, mix, keep, ex, el, q, k, v, qw, p, pv, attn_w, 0)
    do, ffn_3 = lax.optimization_barrier((do, ffn_3))
    (summed,) = call(half_sum_kernel, "half_sum", 0, 2, [SDS(ffn_3.shape, bf16)])(ffn_g[2], ffn_3)
    ffn_g[1], summed = lax.optimization_barrier((ffn_g[1], summed))
    ffn_2, ffn_1 = permute(summed, "head", 2), permute(ffn_g[1], "head", 1)
    gqb, gk, gv, gt = scores_back(dmid, mix, keep, ex, el, q, k, v, qw, p, pv, [do, *sums], 1)
    both, *attn_g = weights_back(x, a, dmid, norm_params, gn2, gqa, gqb, gk, gv, gt, out, attn_w)
    attn_1, attn_3 = permute(attn_g[1], "head", 1), permute(attn_g[3], "head", 1)
    (summed,) = call(half_sum_kernel, "half_sum", 0, 2, [SDS(attn_3.shape, bf16)])(attn_g[2], attn_3)
    both, summed = lax.optimization_barrier((both, summed))
    attn_2 = permute(summed, "head", 2)
    both_2, both_1 = permute(both, "head", 2), permute(both, "head", 1)
    both_3 = permute(both_2, "head", 1)
    (message,) = call(
        spread_ffn_kernel, "spread_ffn", 2, 3, [SDS((ranks // 2, 2, slots, rows, 256), bf16)]
    )(block_slot, scal, ffn_g[0], ffn_1, ffn_2)
    near_own, far_own, near_other, far_other = call(
        spread_attn_kernel, "spread_attn", 0, 5, [SDS((half,) + message.shape[2:], bf16)] * 4, parts=3,
    )(sel, message, attn_g[0], attn_1, attn_2)
    slot_shape = (slots, rows, 256)
    far_other = permute(far_other, "dp", 1)
    near_other = permute(near_other, "dp", 1)
    far_sum = call(place_sum_kernel, "place_sum", 0, 2, [SDS(slot_shape, bf16)] * half)(far_own, far_other)
    far_sum = [permute(far_sum[k - half], "dp", 2 * k) for k in far]
    own, *near_sum = call(
        place_sum_kernel, "place_sum", 0, 2, [SDS(slot_shape, f32)] + [SDS(slot_shape, bf16)] * (half - 1)
    )(near_own, near_other)
    got = [own] + [permute(near_sum[k - 1], "dp", 2 * k) for k in near] + far_sum
    shape = SDS((tokens.shape[1], parts, dim), f32)
    output, token_grad = pl.pallas_call(
        assemble_kernel,
        grid=(1,),
        in_specs=[SM] + [whole(*both.shape)] * parts,
        out_specs=[whole(*shape.shape)] * 2,
        out_shape=[shape, shape],
        scratch_shapes=[pltpu.VMEM((parts, 224, dim), bf16)],
        compiler_params=pltpu.CompilerParams(vmem_limit_bytes=16 << 20),
        cost_estimate=pl.CostEstimate(flops=1000000000, transcendentals=0, bytes_accessed=3000000),
        name="assemble",
    )(scal, both, both_1, both_2, both_3)
    got[-1], output, token_grad = lax.optimization_barrier((got[-1], output, token_grad))
    state = [
        swap(master), swap(master_m1), swap(master_m2), norm_params, norm_m1, norm_m2,
        swap(talk), swap(talk_m1), swap(talk_m2), conv, conv_m1, conv_m2,
    ]
    shapes = [SDS(t.shape, f32) for t in state]
    shapes.insert(3, SDS(state[0].shape, bf16))
    new = staged(
        update_kernel, "update", [*got, *state], shapes,
        [pltpu.VMEM((rows, slots, dim), f32), pltpu.VMEM((slots, 64, 256), f32), pltpu.VMEM((64, 256), f32)],
    )
    new = [swap(t) if t.ndim == 3 else t for t in new]
    return (swap(output), swap(token_grad), *new)


def solution(mesh):
    in_specs = (
        P("dp", None, None),
        P("dp", None, None),
        P("dp"),
        P(),
        P(),
        P(),
        P("dp", None, "head"),
        P("dp", None, "head"),
        P("dp", None, "head"),
        P(),
        P(),
        P(),
        P(),
        P(),
        P(),
        P(None, "head"),
        P(None, "head"),
        P(None, "head"),
    )
    out_specs = (
        P("dp", None, None),
        P("dp", None, None),
        P("dp", None, "head"),
        P("dp", None, "head"),
        P("dp", None, "head"),
        P("dp", None, "head"),
        P(),
        P(),
        P(),
        P(),
        P(),
        P(),
        P(None, "head"),
        P(None, "head"),
        P(None, "head"),
    )
    return jax.shard_map(local, mesh=mesh, in_specs=in_specs, out_specs=out_specs, check_vma=False)
```

```python
import functools
import jax
import jax.numpy as jnp
from jax import lax
from jax.experimental import pallas as pl
from jax.experimental.pallas import tpu as pltpu
from jax.sharding import PartitionSpec as P

HD = 18
SIDE = 14
PITCH = 16
MARGIN = 24
BUNCH = 4
EARLY = 4


def bunches(first, last):
    return [(y, min(BUNCH, last - y)) for y in range(first, last, BUNCH)]

FREE = 216
WIDE = 40
norm_eps = 1e-05
bf16 = jnp.bfloat16
f32 = jnp.float32


def nn(a, b):
    return lax.dot_general(a, b, (((1,), (0,)), ((), ())), preferred_element_type=f32)


def nt(a, b):
    return lax.dot_general(a, b, (((1,), (1,)), ((), ())), preferred_element_type=f32)


def tn(a, b):
    return lax.dot_general(a, b, (((0,), (0,)), ((), ())), preferred_element_type=f32)


def iota(shape, dim):
    return lax.broadcasted_iota(jnp.int32, shape, dim)


def split2(v):
    hi = v.astype(bf16)
    return hi, (v - hi.astype(f32)).astype(bf16)


def real_rows(shape):
    return (iota(shape, 0) & (PITCH - 1)) < SIDE


def lane_head(shape, dim, place):
    lane = iota(shape, dim)
    rest = lane & 63
    head = ((lane >> 6) ^ place) * 3 + (rest >= 18).astype(jnp.int32) + (rest >= 36).astype(jnp.int32)
    return jnp.where(rest < 54, head, -1)


def true_head(rows, place):
    head = rows >> 4
    part = (head >= 3).astype(jnp.int32) + (head >= 6).astype(jnp.int32) + (head >= 9).astype(jnp.int32)
    return (part ^ place) * 3 + (head - 3 * part)


def spot(slot, per):
    bits = per.bit_length() - 1
    return slot >> (bits + 1), (slot >> bits) & 1, slot & (per - 1)


def prep_kernel(
    scal, slot_ref, tok_ref, cot_ref, norm_ref, talk_ref, x_ref, a_ref, dy_ref, mix_ref, bias_ref, keep_ref, ex_ref, el_ref, sel_ref, tmp_ref, *, pairs
):
    x_ref[...] = jnp.zeros_like(x_ref)
    dy_ref[...] = jnp.zeros_like(dy_ref)
    valid = (scal[0] < scal[1]).astype(f32)
    tmp_ref[...] = tok_ref[0].astype(f32)
    for y in range(SIDE):
        x_ref[PITCH * y : PITCH * y + SIDE, :] = tmp_ref[SIDE * y : SIDE * (y + 1), :]
        dy_ref[PITCH * y : PITCH * y + SIDE, :] = cot_ref[0, SIDE * y : SIDE * (y + 1), :] * valid
    x = x_ref[...]
    centred = x - jnp.mean(x, axis=-1, keepdims=True)
    inv = lax.rsqrt(jnp.mean(centred * centred, axis=-1, keepdims=True) + norm_eps)
    a = centred * inv * norm_ref[0:1, :] + norm_ref[1:2, :]
    a_ref[...] = jnp.where(real_rows(a.shape), a, 0.0).astype(bf16)
    heads = talk_ref.shape[1]
    n = heads * PITCH
    ex = (true_head(iota((n, heads), 0), scal[0]) == iota((n, heads), 1)).astype(bf16)
    el = (lane_head((256, heads), 0, scal[0]) == iota((256, heads), 1)).astype(bf16)
    for i in range(2):
        both = []
        for part in split2(talk_ref[i]):
            if i == 0:
                both.append(nt(nn(ex, part).astype(bf16), el))
            else:
                both.append(nt(nt(ex, part).astype(bf16), el))
        mix_ref[i] = (both[0] + both[1]) * (HD**-0.5 if i == 0 else 1.0)
    bias_ref[...] = jnp.where(real_rows(bias_ref.shape), 0.0, -1e30)
    lanes = lane_head((1, 256), 1, scal[0])
    keep_ref[0:1, :] = ((lanes >= 0) & (lanes < scal[2])).astype(f32)
    lane = iota((1, 256), 1)
    for k in range(keep_ref.shape[0] - 2):
        unit = ((k ^ scal[0]) * 4 + (lane >> 6)) * 54 + (lane & 63)
        keep_ref[1 + k : 2 + k, :] = (unit < scal[3]).astype(f32)
    keep_ref[keep_ref.shape[0] - 1 :, :] = jnp.broadcast_to(valid, (1, 256))
    ex_ref[...] = ex
    el_ref[...] = el
    blocks, slots = sel_ref.shape[:2]
    per = slots // (2 * pairs)
    for b in range(blocks):
        pair, place, own = spot(slot_ref[b], per)
        at = ((place ^ scal[4]) * pairs + (pair ^ scal[5])) * per + own
        sel_ref[b] = (iota(sel_ref.shape[1:], 0) == at).astype(f32)


def load_weight(dst_ref, w_refs, b):
    for k, w_ref in enumerate(w_refs):
        dst_ref[64 * k : 64 * k + 54, :] = w_ref[b]


def tiled(rows, heads):
    return jnp.concatenate([rows] * heads, axis=0)


def over_heads(rows, heads):
    return jnp.sum(rows.reshape(heads, PITCH, rows.shape[1]), axis=0)


def attn_fwd_kernel(x_ref, a_ref, mix_ref, bias_ref, keep_ref, *refs, parts):
    w_refs, refs = refs[:parts], refs[parts:]
    mid_ref, q_ref, k_ref, v_ref, o_ref, qw_ref, p_ref, pv_ref, ws_ref, t_ref = refs
    heads = mix_ref.shape[1] // PITCH
    a = a_ref[...]
    ws_ref[...] = jnp.zeros_like(ws_ref)
    for b, dst in enumerate((q_ref, k_ref, v_ref)):
        load_weight(ws_ref.at[b], w_refs, b)
        dst[...] = nt(a, ws_ref[b]).astype(bf16)
    load_weight(ws_ref.at[3], w_refs, 3)
    keep = keep_ref[0:1, :]

    n = heads * PITCH
    for y in range(SIDE):
        q = q_ref[PITCH * y : PITCH * (y + 1), :].astype(f32)
        qw_ref[n * y : n * (y + 1), :] = (tiled(q, heads) * mix_ref[0]).astype(bf16)
    for b, (y, count) in enumerate(bunches(0, SIDE)):
        t_ref[b, :, 0 : n * count] = nt(k_ref[...], qw_ref[n * y : n * (y + count), :])
    for b, (y, count) in enumerate(bunches(0, SIDE)):
        for at in range(0, n * count, 128):
            t = t_ref[b, :, at : at + 128] + bias_ref[...]
            e = jnp.exp(t - jnp.max(t, axis=0, keepdims=True))
            p_ref[b, :, at : at + 128] = (e * (1.0 / jnp.sum(e, axis=0, keepdims=True))).astype(bf16)
    for b, (first, count) in enumerate(bunches(0, SIDE)):
        pv = tn(p_ref[b, :, 0 : n * count], v_ref[...])
        pv_ref[n * first : n * (first + count), :] = pv.astype(bf16)
        for u in range(count):
            o = over_heads(pv[n * u : n * (u + 1)] * mix_ref[1], heads)
            o_ref[PITCH * (first + u) : PITCH * (first + u + 1), :] = (o * keep).astype(bf16)
    mid_ref[...] = x_ref[...] + nn(o_ref[...], ws_ref[3])


def ln_stats(v):
    centred = v - jnp.mean(v, axis=-1, keepdims=True)
    inv = lax.rsqrt(jnp.mean(centred * centred, axis=-1, keepdims=True) + norm_eps)
    return centred * inv, inv


def ln_back(grad, scaled, inv, gain):
    gs = grad * gain
    return inv * (
        gs - jnp.mean(gs, axis=-1, keepdims=True) - scaled * jnp.mean(gs * scaled, axis=-1, keepdims=True)
    )


def in_free_lanes(flat, dst_ref, first_row):
    rows = flat.shape[0]
    for j in range(6):
        dst_ref[first_row + rows * j : first_row + rows * (j + 1), :] = pltpu.roll(flat, (FREE - WIDE * j) % 256, 1)


def from_free_lanes(src_ref, first_row, rows):
    lane = iota((rows, 256), 1)
    flat = jnp.zeros((rows, 256), f32)
    for j in range(6):
        moved = pltpu.roll(src_ref[first_row + rows * j : first_row + rows * (j + 1), :], (WIDE * j - FREE) % 256, 1)
        flat = flat + jnp.where((lane >= WIDE * j) & (lane < WIDE * (j + 1)), moved, 0.0)
    return flat


def place(rows=216):
    shape = (rows, 256)
    lane = iota(shape, 1)
    rest = lane & 63
    return ((iota(shape, 0) == (lane >> 6) * 54 + rest) & (rest < 54)).astype(bf16)


def up(w_ref, w, e, win_ref, wdn_ref, h_ref, d_ref, cv_ref):
    tokens, dim = w.shape
    pad = MARGIN
    for j in range(4):
        at = 64 * j
        win_ref[at : at + 54, :] = w_ref[j]
        wdn_ref[at : at + 54, :] = w_ref[4 + j]
        win_ref[at + 54 : at + 64, :] = jnp.zeros((10, dim), bf16)
        wdn_ref[at + 54 : at + 64, :] = jnp.zeros((10, dim), bf16)
    both = nn(w_ref[8], place(dim))
    cv_ref[...] = both[0:9] + both[16:25]
    hidden = nt(w, win_ref[...])
    dgate = nt(e, wdn_ref[...])
    zero = jnp.zeros((pad, 128), f32)
    for half in range(2):
        mine = slice(128 * half, 128 * (half + 1))
        for ref, value in ((h_ref, hidden), (d_ref, dgate)):
            ref[half, 0:pad, :] = zero
            ref[half, pad + tokens :, :] = zero
            ref[half, pad : pad + tokens, :] = value[:, mine]


def middle(keep, h_ref, d_ref, gate_ref, dh_ref, cv_ref, gcv_ref):
    tokens = gate_ref.shape[0]
    pad = MARGIN
    for half in range(2):
        cols = slice(128 * half, 128 * (half + 1))
        on = keep[:, cols]
        act = None
        for t in range(9):
            off = pad + PITCH * (t // 3 - 1) + t % 3 - 1
            term = cv_ref[t : t + 1, cols] * h_ref[half, off : off + tokens, :]
            act = term if act is None else act + term
        sig = 0.5 * jnp.tanh(0.5 * act) + 0.5
        silu = act * sig
        gate_ref[:, cols] = (silu * on).astype(bf16)
        dact = d_ref[half, pad : pad + tokens, :] * on * (silu + sig * (1.0 - silu))
        d_ref[half, pad : pad + tokens, :] = dact
        dh = None
        for t in range(9):
            shift = PITCH * (t // 3 - 1) + t % 3 - 1
            gcv_ref[t : t + 1, cols] = jnp.sum(
                dact * h_ref[half, pad + shift : pad + shift + tokens, :], axis=0, keepdims=True
            )
            term = cv_ref[t : t + 1, cols] * d_ref[half, pad - shift : pad - shift + tokens, :]
            dh = term if dh is None else dh + term
        dh_ref[:, cols] = dh.astype(bf16)


def ffn_first_kernel(mid_ref, dy_ref, norm_ref, keep_ref, *refs, parts):
    w_refs, refs = refs[:parts], refs[parts:]
    z_ref, inv_ref, w_ref, e_ref, win_ref, wdn_ref, gate_ref, dh_ref, gcv_ref, h_ref, d_ref, cv_ref = refs
    z, inv = ln_stats(mid_ref[...])
    z_ref[...] = z
    inv_ref[...] = jnp.broadcast_to(inv, inv_ref.shape)
    w = jnp.where(real_rows(z.shape), z * norm_ref[2:3, :] + norm_ref[3:4, :], 0.0).astype(bf16)
    e = dy_ref[...].astype(bf16)
    w_ref[...] = w
    e_ref[...] = e
    for k in range(parts):
        up(w_refs[k], w, e, win_ref.at[k], wdn_ref.at[k], h_ref.at[k], d_ref.at[k], cv_ref.at[k])
    for k in range(parts):
        middle(
            keep_ref[1 + k : 2 + k, :], h_ref.at[k], d_ref.at[k], gate_ref.at[k], dh_ref.at[k], cv_ref.at[k], gcv_ref.at[k]
        )


def ffn_last_kernel(
    mid_ref, dy_ref, norm_ref, keep_ref, o_ref, z_ref, inv_ref, w_ref, e_ref, *refs, parts, late
):
    early = parts - late
    wins, wdns, gates, dhs, gcvs = refs[:5]
    last_refs, refs = refs[5 : 5 + late], refs[5 + late :]
    out_ref, dmid_ref, gn_ref = refs[:3]
    gw_refs, refs = refs[3 : 3 + parts], refs[3 + parts :]
    win_ref, wdn_ref, gate_ref, dh_ref, gcv_ref, h_ref, d_ref, cv_ref, tmp_ref, sm_ref, dw_ref = refs
    w, e = w_ref[...], e_ref[...]
    dim = w.shape[1]
    wins, wdns, gates, dhs, gcvs = [
        [ref.at[i] for i in range(early)] + [own.at[i] for i in range(late)]
        for ref, own in ((wins, win_ref), (wdns, wdn_ref), (gates, gate_ref), (dhs, dh_ref), (gcvs, gcv_ref))
    ]

    def back(h):
        gi = tn(dhs[h][...], w).astype(bf16)
        gd = tn(gates[h][...], e).astype(bf16)
        for j in range(4):
            gw_refs[h][1 + j, :, 0:dim] = gi[64 * j : 64 * j + 54]
            gw_refs[h][5 + j, :, 0:dim] = gd[64 * j : 64 * j + 54]

    for i in range(late):
        up(last_refs[i], w, e, win_ref.at[i], wdn_ref.at[i], h_ref.at[i], d_ref.at[i], cv_ref.at[i])
    for h in range(early):
        back(h)
    for i in range(late):
        middle(
            keep_ref[1 + early + i : 2 + early + i, :], h_ref.at[i], d_ref.at[i], gate_ref.at[i], dh_ref.at[i], cv_ref.at[i], gcv_ref.at[i]
        )
    dw_ref[...] = sum(nn(dhs[h][...], wins[h][...]) for h in range(parts))
    valid = keep_ref[parts + 1 : parts + 2, 0:1]
    tmp_ref[...] = (mid_ref[...] + sum(nn(gates[h][...], wdns[h][...]) for h in range(parts))) * valid
    free = iota((54, 256), 1) >= FREE
    pm = place(256)
    for h in range(parts):
        if h >= early:
            back(h)
        in_free_lanes(nt(gcvs[h][...].astype(bf16), pm), sm_ref.at[h], 0)
        gw_refs[h][0] = jnp.where(free, sm_ref[h, 0:54, :], 0.0).astype(bf16)
    for y in range(SIDE):
        out_ref[SIDE * y : SIDE * (y + 1), :] = tmp_ref[PITCH * y : PITCH * y + SIDE, :].astype(bf16)
    z, inv = z_ref[...], inv_ref[:, 0:1]
    dw = jnp.where(real_rows(z.shape), dw_ref[...], 0.0)
    gn_ref[...] = jnp.zeros_like(gn_ref)
    gn_ref[0:1, :] = jnp.sum(dw * z, axis=0, keepdims=True)
    gn_ref[1:2, :] = jnp.sum(dw, axis=0, keepdims=True)
    dmid = dy_ref[...] + ln_back(dw, z, inv, norm_ref[2:3, :])
    dmid_ref[...] = dmid
    go = tn(o_ref[...], dmid.astype(bf16)).astype(bf16)
    for h in range(parts):
        gw_refs[h][0, :, 0:dim] = go[64 * h : 64 * h + 54]


def scores_back_kernel(
    dmid_ref, mix_ref, keep_ref, ex_ref, el_ref, q_ref, k_ref, v_ref, qw_ref, p_ref, pv_ref, *refs, parts, part
):
    heads = mix_ref.shape[1] // PITCH
    n = heads * PITCH
    if part == 0:
        w_refs, refs = refs[:parts], refs[parts:]
        do_ref, gq_ref, gk_ref, gv_ref, g0_ref, g1_ref, wo_ref, dw_ref, dp_ref, dt_ref = refs
        wo_ref[...] = jnp.zeros_like(wo_ref)
        load_weight(wo_ref, w_refs, 3)
        f = dmid_ref[...].astype(bf16)
        keep = keep_ref[0:1, :]
        do_ref[...] = (nt(f, wo_ref[...]) * keep).astype(bf16)
        for ref in (gk_ref, gv_ref, g0_ref, g1_ref):
            ref[...] = jnp.zeros_like(ref)
    else:
        do_ref, *sums, gq_ref, gkb_ref, gvb_ref, gt_ref, gk_ref, gv_ref, g0_ref, g1_ref, dw_ref, dp_ref, dt_ref = refs
        for ref, old in zip((gk_ref, gv_ref, g0_ref, g1_ref), sums):
            ref[...] = old[...]
    first, last = (0, EARLY) if part == 0 else (EARLY, SIDE)
    for y in range(first, last):
        do = do_ref[PITCH * y : PITCH * (y + 1), :].astype(f32)
        at = n * (y - first)
        dw_ref[at : at + n, :] = (tiled(do, heads) * mix_ref[1]).astype(bf16)
    groups = [(b, b + first // BUNCH, y, count) for b, (y, count) in enumerate(bunches(first, last))]
    for b, _, y, count in groups:
        at = n * (y - first)
        dp_ref[b, :, 0 : n * count] = nt(v_ref[...], dw_ref[at : at + n * count, :])
    for b, whole_b, y, count in groups:
        for at in range(0, n * count, 128):
            dp = dp_ref[b, :, at : at + 128]
            p = p_ref[whole_b, :, at : at + 128].astype(f32)
            dt_ref[b, :, at : at + 128] = (p * (dp - jnp.sum(dp * p, axis=0, keepdims=True))).astype(bf16)
    gv, gk = gv_ref[...], gk_ref[...]
    for b, whole_b, y, count in groups:
        at = n * (y - first)
        gv = gv + nn(p_ref[whole_b, :, 0 : n * count], dw_ref[at : at + n * count, :])
        gk = gk + nn(dt_ref[b, :, 0 : n * count], qw_ref[n * y : n * (y + count), :])
    gv_ref[...] = gv
    gk_ref[...] = gk
    for b, _, y, count in groups:
        dk = tn(dt_ref[b, :, 0 : n * count], k_ref[...])
        for u in range(count):
            mine = dk[n * u : n * (u + 1)]
            at = PITCH * (y + u)
            gq_ref[at - PITCH * first : at - PITCH * first + PITCH, :] = over_heads(mine * mix_ref[0], heads).astype(bf16)
            g0_ref[...] += mine * tiled(q_ref[at : at + PITCH, :].astype(f32), heads)
    for y in range(first, last):
        do = do_ref[PITCH * y : PITCH * (y + 1), :].astype(f32)
        g1_ref[...] += pv_ref[n * y : n * (y + 1), :].astype(f32) * tiled(do, heads)
    if part == 0:
        return
    gkb_ref[...] = gk_ref[...].astype(bf16)
    gvb_ref[...] = gv_ref[...].astype(bf16)
    ex, el = ex_ref[...], el_ref[...]
    for i, ref in enumerate((g0_ref, g1_ref)):
        hi, lo = split2(ref[...])
        hi, lo = split2(nn(hi, el) + nn(lo, el))
        if i == 0:
            gt_ref[i] = (tn(ex, hi) + tn(ex, lo)) * HD**-0.5
        else:
            gt_ref[i] = tn(hi, ex) + tn(lo, ex)


def weights_back_kernel(
    x_ref, a_ref, dmid_ref, norm_ref, gn2_ref, gqa_ref, gqb_ref, gk_ref, gv_ref, gt_ref, y_ref, *refs, parts
):
    w_refs, refs = refs[:parts], refs[parts:]
    both_ref, gw_refs, refs = refs[0], refs[1 : 1 + parts], refs[1 + parts :]
    ws_ref, tmp_ref, flat_ref, sm_ref = refs
    heads = gt_ref.shape[1]
    dim = x_ref.shape[1]
    ws_ref[...] = jnp.zeros_like(ws_ref)
    for b in range(3):
        load_weight(ws_ref.at[b], w_refs, b)
    gq = jnp.concatenate([gqa_ref[...], gqb_ref[...]], axis=0)
    gk, gv = gk_ref[...], gv_ref[...]
    a = a_ref[...]
    da = nn(gq, ws_ref[0]) + nn(gk, ws_ref[1]) + nn(gv, ws_ref[2])
    z, inv = ln_stats(x_ref[...])
    flat_ref[...] = jnp.zeros_like(flat_ref)
    flat_ref[0:1, 0:dim] = jnp.sum(da * z, axis=0, keepdims=True)
    flat_ref[1:2, 0:dim] = jnp.sum(da, axis=0, keepdims=True)
    flat_ref[2:4, 0:dim] = gn2_ref[0:2, :]
    for i in range(2):
        flat_ref[8 : 8 + heads, 128 * i : 128 * i + heads] = gt_ref[i]
    sm_ref[...] = jnp.zeros_like(sm_ref)
    in_free_lanes(flat_ref[0:4, :], sm_ref, 0)
    mix = flat_ref[8 : 8 + heads, :]
    first = iota(mix.shape, 1) < 128
    mix = jnp.where(first, mix, 0.0) + pltpu.roll(jnp.where(first, 0.0, mix), 128 + heads, 1)
    sm_ref[24 : 24 + heads, :] = pltpu.roll(mix, FREE, 1)
    small = jnp.where(iota((54, 256), 1) >= FREE, sm_ref[0:54, :], 0.0).astype(bf16)
    for h in range(parts):
        gw_refs[h][0] = small
    for b, g in enumerate((gq, gk, gv)):
        gw = tn(g, a).astype(bf16)
        for h in range(parts):
            gw_refs[h][b, :, 0:dim] = gw[64 * h : 64 * h + 54]
    tmp_ref[...] = dmid_ref[...] + ln_back(da, z, inv, norm_ref[0:1, :])
    for y in range(SIDE):
        both_ref[1, SIDE * y : SIDE * (y + 1), :] = tmp_ref[PITCH * y : PITCH * y + SIDE, :].astype(bf16)
    both_ref[0] = y_ref[...]


def cast_kernel(m_hbm, out_ref, m_ref, sem):
    copy = pltpu.make_async_copy(m_hbm, m_ref, sem)
    copy.start()
    copy.wait()
    for i in range(out_ref.shape[0]):
        out_ref[i] = m_ref[:, i, :].astype(bf16)


def stack_kernel(*refs):
    for k, ref in enumerate(refs[:-1]):
        refs[-1][k] = ref[...]


def slots_of(sources):
    found = []
    for i, ref in enumerate(sources):
        ranks = [ref] if i % 2 == 0 else [ref.at[k] for k in range(ref.shape[0])]
        found += [rank[own] for rank in ranks for own in range(rank.shape[0])]
    return found


def pick(sel_ref, b, slots):
    dim = slots[0].shape[1]
    block = None
    for i, slot in enumerate(slots):
        term = sel_ref[b, i : i + 1, 0:dim] * slot.astype(f32)
        block = term if block is None else block + term
    return block.astype(bf16)


def select_attn_kernel(sel_ref, *refs):
    slots = slots_of(refs[:-1])
    for b in range(4):
        refs[-1][b] = pick(sel_ref, b, slots)


def select_ffn_kernel(sel_ref, conv_ref, *refs):
    slots, ffn_ref = slots_of(refs[:-1]), refs[-1]
    for b in range(8):
        ffn_ref[b] = pick(sel_ref, 4 + b, slots)
    hi, lo = split2(conv_ref[...])
    ffn_ref[8] = jnp.zeros_like(ffn_ref[8])
    ffn_ref[8, 0:9] = hi
    ffn_ref[8, 16:25] = lo


def total(refs, at):
    acc = refs[0][at].astype(f32)
    for ref in refs[1:]:
        acc = acc + ref[at].astype(f32)
    return acc


def half_sum_kernel(a_ref, b_ref, out_ref):
    out_ref[...] = (a_ref[...].astype(f32) + b_ref[...].astype(f32)).astype(bf16)


def spread_ffn_kernel(slot_ref, scal, *refs):
    ffn_refs, out_ref = refs[:-1], refs[-1]
    pairs, _, per = out_ref.shape[:3]
    out_ref[...] = jnp.zeros_like(out_ref)
    for b in range(9):
        block = total(ffn_refs, b)
        k, j, i = spot(slot_ref[3 + b], per)
        out_ref[k ^ scal[5], j ^ scal[4], i, :, 0:FREE] = block[:, 0:FREE].astype(bf16)
        if b == 0:
            wide = block[:, FREE:].astype(bf16)
    for k in range(pairs):
        for j in range(2):
            out_ref[k, j, 0, :, FREE:] = wide


def spread_attn_kernel(sel_ref, old_ref, *refs, parts):
    attn, outs = refs[:parts], refs[parts:]
    half, per = outs[0].shape[:2]
    blocks = [total(attn, b) for b in range(3)]
    wide = blocks[0][:, FREE:].astype(bf16)
    blocks = [block[:, 0:FREE] for block in blocks]
    for i, ref in enumerate(outs):
        for k in range(half):
            pair = half * (i % 2) + k
            for own in range(per):
                old = old_ref[pair, i // 2, own]
                at = (i // 2 * 2 * half + pair) * per + own
                low = old[:, 0:FREE].astype(f32)
                for b in range(3):
                    low = low + sel_ref[b, at : at + 1, 0:FREE] * blocks[b]
                ref[k, own] = old
                ref[k, own, :, 0:FREE] = low.astype(bf16)
            ref[k, 1, :, FREE:] = wide


def place_sum_kernel(own_ref, other_ref, *outs):
    for k, out_ref in enumerate(outs):
        out_ref[...] = (own_ref[k].astype(f32) + other_ref[k].astype(f32)).astype(out_ref.dtype)


def adam(w, g, one, two, rate, decay):
    one_new = 0.5 * one + 0.5 * g
    two_new = 0.5 * two + 0.5 * g * g
    hat_one = one_new / (1.0 - 0.5**3)
    hat_two = two_new / (1.0 - 0.5**3)
    return w - rate * (hat_one / (jnp.sqrt(hat_two) + 1e-08) + decay * w), one_new, two_new


def update_kernel(*refs):
    got, refs = refs[:-28], refs[-28:]
    ins, outs, (g_ref, sm_ref, flat_ref) = refs[0:12], refs[12:25], refs[25:]
    per, rows = got[0].shape[:2]
    dim = ins[0].shape[2]
    for i in range(per):
        g = total(got, i)
        g_ref[:, i, :] = g[:, 0:dim]
        sm_ref[i, 0:rows, :] = g
    w, one, two = adam(ins[0][...], g_ref[...], ins[1][...], ins[2][...], 0.06, 0.05)
    outs[0][...], outs[1][...], outs[2][...], outs[3][...] = w, one, two, w.astype(bf16)
    heads = ins[6].shape[0]
    flat_ref[0:9, :] = from_free_lanes(sm_ref.at[0], 0, 9)
    flat_ref[16:20, :] = from_free_lanes(sm_ref.at[1], 0, 4)
    mix = pltpu.roll(sm_ref[1, 24 : 24 + heads, :], 256 - FREE, 1)
    flat_ref[32 : 32 + heads, :] = mix
    flat_ref[48 : 48 + heads, :] = pltpu.roll(mix, 256 - heads, 1)
    outs[4][...], outs[5][...], outs[6][...] = adam(
        ins[3][...], flat_ref[16:20, 0:dim], ins[4][...], ins[5][...], 0.2, 0.0
    )
    for i in range(2):
        w, one, two = adam(
            ins[6][:, i, :], flat_ref[16 * (i + 2) : 16 * (i + 2) + heads, 0:heads], ins[7][:, i, :], ins[8][:, i, :],
            0.2, 0.0,
        )
        outs[7][:, i, :], outs[8][:, i, :], outs[9][:, i, :] = w, one, two
    outs[10][...], outs[11][...], outs[12][...] = adam(
        ins[9][...], flat_ref[0:9, 0:dim], ins[10][...], ins[11][...], 0.2, 0.05
    )


def assemble_kernel(scal, *refs):
    ins, outs, (all_ref,) = refs[:-3], refs[-3:-1], refs[-1:]
    parts, tokens = len(ins), ins[0].shape[1]
    step = 32
    shape = (parts * step, parts * step)
    row, col = iota(shape, 0), iota(shape, 1)
    bits = parts.bit_length() - 1
    pick = ((row >> bits == col & (step - 1)) & (row & (parts - 1) == col >> 5)).astype(bf16)
    full = all_ref.shape[1]
    for k in range(parts):
        all_ref[k, tokens // step * step : full, :] = jnp.zeros((full - tokens // step * step, all_ref.shape[2]), bf16)
    for i, out_ref in enumerate(outs):
        for k, ref in enumerate(ins):
            all_ref[scal[0] ^ k, 0:tokens, :] = ref[i]
        for at in range(0, tokens, step):
            mixed = nn(pick, jnp.concatenate([all_ref[k, at : at + step, :] for k in range(parts)], axis=0))
            for t in range(min(step, tokens - at)):
                out_ref[at + t] = mixed[parts * t : parts * (t + 1)]


VM = pl.BlockSpec(memory_space=pltpu.VMEM)
SM = pl.BlockSpec(memory_space=pltpu.SMEM)
SDS = jax.ShapeDtypeStruct


def call(body, name, n_scalar, n_in, out_shape, scratch=(), mb=16, micros=1, **kw):
    return pl.pallas_call(
        functools.partial(body, **kw) if kw else body,
        in_specs=[SM] * n_scalar + [VM] * n_in,
        out_specs=[VM] * len(out_shape),
        out_shape=out_shape,
        scratch_shapes=scratch,
        compiler_params=pltpu.CompilerParams(vmem_limit_bytes=mb << 20),
        cost_estimate=pl.CostEstimate(flops=micros * 1000000000, transcendentals=0, bytes_accessed=micros * 3000000),
        name=name,
    )


def prep(scal, block_slot, tokens, cotangent, norm_params, talk, parts, pairs, slots):
    tok, dim = tokens.shape[1], tokens.shape[2]
    pad = SIDE * PITCH
    heads = talk.shape[1]
    n = heads * PITCH
    full = lambda *s: pl.BlockSpec(s, lambda i, sc, bs: (0,) * len(s))
    return pl.pallas_call(
        functools.partial(prep_kernel, pairs=pairs),
        grid_spec=pltpu.PrefetchScalarGridSpec(
            num_scalar_prefetch=2,
            grid=(1,),
            in_specs=[
                pl.BlockSpec((1, tok, dim), lambda i, sc, bs: (sc[0], 0, 0)),
                pl.BlockSpec((1, tok, dim), lambda i, sc, bs: (sc[0], 0, 0)),
                full(*norm_params.shape),
                full(*talk.shape),
            ],
            out_specs=[full(pad, dim), full(pad, dim), full(pad, dim), full(2, n, 256), full(pad, 128),
                full(parts + 2, 256), full(n, heads), full(256, heads),
                full(12, slots, 256),
            ],
            scratch_shapes=[pltpu.VMEM((tok, dim), f32)],
        ),
        out_shape=[SDS((pad, dim), f32), SDS((pad, dim), bf16), SDS((pad, dim), f32), SDS((2, n, 256), f32),
                   SDS((pad, 128), f32), SDS((parts + 2, 256), f32), SDS((n, heads), bf16), SDS((256, heads), bf16),
                   SDS((12, slots, 256), f32)],
        compiler_params=pltpu.CompilerParams(vmem_limit_bytes=16 << 20),
        cost_estimate=pl.CostEstimate(flops=1000000000, transcendentals=0, bytes_accessed=3000000),
        name="prep",
    )(scal, block_slot, tokens, cotangent, norm_params, talk)


def attn_fwd(x, a, mix, bias, keep, w):
    pad, dim = x.shape
    n = mix.shape[1]
    grid = (len(bunches(0, SIDE)), pad, n * BUNCH)
    return call(
        attn_fwd_kernel, "attn_fwd", 0, 5 + len(w),
        [SDS((pad, dim), f32)] + [SDS((pad, 256), bf16)] * 4
        + [SDS((SIDE * n, 256), bf16), SDS(grid, bf16), SDS((SIDE * n, 256), bf16)],
        [pltpu.VMEM((4, 256, dim), bf16), pltpu.VMEM(grid, f32)],
        mb=24, micros=1, parts=len(w),
    )(x, a, mix, bias, keep, *w)


def ffn_first(mid, dy, norm_params, keep, w):
    pad, dim = mid.shape
    count = len(w)
    lanes = [(count, 256, dim)] * 2 + [(count, pad, 256)] * 2
    grids = [pltpu.VMEM((count, 2, pad + 2 * MARGIN, 128), f32)] * 2
    return call(
        ffn_first_kernel, "ffn_first", 0, 4 + count,
        [SDS((pad, dim), f32), SDS((pad, 128), f32), SDS((pad, dim), bf16), SDS((pad, dim), bf16)]
        + [SDS(t, bf16) for t in lanes] + [SDS((count, 9, 256), f32)],
        grids + [pltpu.VMEM((count, 9, 256), f32)],
        mb=24, micros=3, parts=count,
    )(mid, dy, norm_params, keep, *w)


def ffn_last(mid, dy, norm_params, keep, o, first, w):
    pad, dim = mid.shape
    late = len(w)
    parts = first[4].shape[0] + late
    grids = [pltpu.VMEM((late, 2, pad + 2 * MARGIN, 128), f32)] * 2
    return call(
        ffn_last_kernel, "ffn_last", 0, 14 + late,
        [SDS((SIDE * SIDE, dim), bf16), SDS((pad, dim), f32), SDS((8, dim), f32)] + [SDS((9, 54, 256), bf16)] * parts,
        [pltpu.VMEM((late, 256, dim), bf16)] * 2 + [pltpu.VMEM((late, pad, 256), bf16)] * 2
        + [pltpu.VMEM((late, 9, 256), f32)] + grids
        + [
            pltpu.VMEM((late, 9, 256), f32), pltpu.VMEM((pad, dim), f32), pltpu.VMEM((parts, 56, 256), f32),
            pltpu.VMEM((pad, dim), f32),
        ],
        mb=24, micros=4, parts=parts, late=late,
    )(mid, dy, norm_params, keep, o, *first, *w)


def scores_back(dmid, mix, keep, ex, el, q, k, v, qw, p, pv, more, part):
    pad, dim = dmid.shape
    n = mix.shape[1]
    heads = n // PITCH
    sums = [SDS((pad, 256), f32)] * 2 + [SDS((n, 256), f32)] * 2
    count = EARLY if part == 0 else SIDE - EARLY
    half = SDS((PITCH * count, 256), bf16)
    if part == 0:
        outs = [SDS((pad, 256), bf16), half] + sums
        scratch = [pltpu.VMEM((256, dim), bf16)]
    else:
        outs = [half] + [SDS((pad, 256), bf16)] * 2 + [SDS((2, heads, heads), f32)]
        scratch = [pltpu.VMEM(t.shape, f32) for t in sums]
    scratch += [
        pltpu.VMEM((n * count, 256), bf16), pltpu.VMEM((-(-count // BUNCH), pad, n * BUNCH), f32),
        pltpu.VMEM((-(-count // BUNCH), pad, n * BUNCH), bf16),
    ]
    return call(
        scores_back_kernel, "scores_back", 0, 11 + len(more), outs, scratch,
        mb=24, micros=4, parts=len(more), part=part,
    )(dmid, mix, keep, ex, el, q, k, v, qw, p, pv, *more)


def weights_back(x, a, dmid, norm_params, gn2, gqa, gqb, gk, gv, gt, out, w):
    pad, dim = x.shape
    return call(
        weights_back_kernel, "weights_back", 0, 11 + len(w),
        [SDS((2, SIDE * SIDE, dim), bf16)] + [SDS((3, 54, 256), bf16)] * len(w),
        [pltpu.VMEM((3, 256, dim), bf16), pltpu.VMEM((pad, dim), f32), pltpu.VMEM((24, 256), f32),
         pltpu.VMEM((56, 256), f32)],
        mb=24, micros=3, parts=len(w),
    )(x, a, dmid, norm_params, gn2, gqa, gqb, gk, gv, gt, out, *w)


def permute(x, axis, k):
    return lax.ppermute(x, axis, [(i, i ^ k) for i in range(lax.axis_size(axis))])


def swap(t):
    return jnp.swapaxes(t, 0, 1)


def whole(*shape):
    return pl.BlockSpec(shape, lambda i: (0,) * len(shape))


def staged(body, name, ins, outs, scratch=(), micros=1):
    return pl.pallas_call(
        body,
        grid=(1,),
        in_specs=[VM] * len(ins),
        out_specs=[whole(*t.shape) for t in outs],
        out_shape=outs,
        scratch_shapes=scratch,
        compiler_params=pltpu.CompilerParams(vmem_limit_bytes=16 << 20),
        cost_estimate=pl.CostEstimate(flops=micros * 1000000000, transcendentals=0, bytes_accessed=micros * 3000000),
        name=name,
    )(*ins)


def local(
    tokens, cotangent, image_count, subnet_heads, subnet_width, block_slot,
    master, master_m1, master_m2, norm_params, norm_m1, norm_m2, talk, talk_m1, talk_m2, conv, conv_m1, conv_m2,
):
    slots, rows, dim = master.shape
    parts = lax.axis_size("head")
    ranks = lax.axis_size("dp")
    place_id = lax.axis_index("head").astype(jnp.int32)
    rank = lax.axis_index("dp").astype(jnp.int32)
    scal = jnp.concatenate(
        [place_id[None], image_count, subnet_heads, subnet_width, (rank % 2)[None], (rank // 2)[None]]
    )
    mine = pl.pallas_call(
        cast_kernel,
        grid=(1,),
        in_specs=[pl.BlockSpec(memory_space=pltpu.HBM)],
        out_specs=whole(slots, rows, dim),
        out_shape=SDS((slots, rows, dim), bf16),
        scratch_shapes=[pltpu.VMEM((rows, slots, dim), f32), pltpu.SemaphoreType.DMA],
        compiler_params=pltpu.CompilerParams(vmem_limit_bytes=16 << 20),
        name="cast",
    )(swap(master))
    pairs = ranks // 2
    half = pairs // 2
    near, far = range(1, half), range(half, pairs)
    apart = {k: permute(mine, "dp", 2 * k) for k in (*far, *near)}
    near_other = permute(mine, "dp", 1)
    apart[1], near_other = lax.optimization_barrier((apart[1], near_other))
    apart[half], tokens, cotangent, talk_in = lax.optimization_barrier((apart[half], tokens, cotangent, talk))
    (far_own,) = call(stack_kernel, "stack", 0, pairs - 1, [SDS((pairs - 1, slots, rows, dim), bf16)])(
        *[apart[k] for k in range(1, pairs)]
    )
    far_other = permute(far_own, "dp", 1)
    x, a, dy, mix, bias, keep, ex, el, sel = prep(
        scal, block_slot, tokens, cotangent, norm_params, talk_in, parts, pairs, ranks * slots
    )
    far_other, x = lax.optimization_barrier((far_other, x))
    sources = (mine, far_own, near_other, far_other)
    (attn_w,) = call(select_attn_kernel, "select_attn", 0, 5, [SDS((4, rows, dim), bf16)])(sel, *sources)
    (ffn_w,) = call(select_ffn_kernel, "select_ffn", 0, 6, [SDS((9, rows, dim), bf16)])(sel, conv, *sources)
    attn_2, attn_1 = permute(attn_w, "head", 2), permute(attn_w, "head", 1)
    attn_3 = permute(attn_2, "head", 1)
    attn_w = [attn_w, attn_1, attn_2, attn_3]
    ffn_2, ffn_1 = permute(ffn_w, "head", 2), permute(ffn_w, "head", 1)
    mid, q, k, v, o, qw, p, pv = attn_fwd(x, a, mix, bias, keep, attn_w)
    mid, ffn_2 = lax.optimization_barrier((mid, ffn_2))
    ffn_3 = permute(ffn_2, "head", 1)
    first = list(ffn_first(mid, dy, norm_params, keep, [ffn_w, ffn_1]))
    first[0], ffn_3 = lax.optimization_barrier((first[0], ffn_3))
    out, dmid, gn2, *ffn_g = ffn_last(mid, dy, norm_params, keep, o, first, [ffn_2, ffn_3])
    ffn_3 = permute(ffn_g[3], "head", 1)
    do, gqa, *sums = scores_back(dmid, mix, keep, ex, el, q, k, v, qw, p, pv, attn_w, 0)
    do, ffn_3 = lax.optimization_barrier((do, ffn_3))
    (summed,) = call(half_sum_kernel, "half_sum", 0, 2, [SDS(ffn_3.shape, bf16)])(ffn_g[2], ffn_3)
    ffn_g[1], summed = lax.optimization_barrier((ffn_g[1], summed))
    ffn_2, ffn_1 = permute(summed, "head", 2), permute(ffn_g[1], "head", 1)
    gqb, gk, gv, gt = scores_back(dmid, mix, keep, ex, el, q, k, v, qw, p, pv, [do, *sums], 1)
    both, *attn_g = weights_back(x, a, dmid, norm_params, gn2, gqa, gqb, gk, gv, gt, out, attn_w)
    attn_1, attn_3 = permute(attn_g[1], "head", 1), permute(attn_g[3], "head", 1)
    (summed,) = call(half_sum_kernel, "half_sum", 0, 2, [SDS(attn_3.shape, bf16)])(attn_g[2], attn_3)
    both, ffn_2 = lax.optimization_barrier((both, ffn_2))
    attn_2 = permute(summed, "head", 2)
    both_2, both_1 = permute(both, "head", 2), permute(both, "head", 1)
    both_3 = permute(both_2, "head", 1)
    (message,) = call(
        spread_ffn_kernel, "spread_ffn", 2, 3, [SDS((ranks // 2, 2, slots, rows, 256), bf16)]
    )(block_slot, scal, ffn_g[0], ffn_1, ffn_2)
    near_own, far_own, near_other, far_other = call(
        spread_attn_kernel, "spread_attn", 0, 5, [SDS((half,) + message.shape[2:], bf16)] * 4, parts=3,
    )(sel, message, attn_g[0], attn_1, attn_2)
    slot_shape = (slots, rows, 256)
    far_other = permute(far_other, "dp", 1)
    near_other = permute(near_other, "dp", 1)
    far_sum = call(place_sum_kernel, "place_sum", 0, 2, [SDS(slot_shape, bf16)] * half)(far_own, far_other)
    far_sum = [permute(far_sum[k - half], "dp", 2 * k) for k in far]
    own, *near_sum = call(
        place_sum_kernel, "place_sum", 0, 2, [SDS(slot_shape, f32)] + [SDS(slot_shape, bf16)] * (half - 1)
    )(near_own, near_other)
    got = [own] + [permute(near_sum[k - 1], "dp", 2 * k) for k in near] + far_sum
    shape = SDS((tokens.shape[1], parts, dim), f32)
    output, token_grad = pl.pallas_call(
        assemble_kernel,
        grid=(1,),
        in_specs=[SM] + [whole(*both.shape)] * parts,
        out_specs=[whole(*shape.shape)] * 2,
        out_shape=[shape, shape],
        scratch_shapes=[pltpu.VMEM((parts, 224, dim), bf16)],
        compiler_params=pltpu.CompilerParams(vmem_limit_bytes=16 << 20),
        cost_estimate=pl.CostEstimate(flops=1000000000, transcendentals=0, bytes_accessed=3000000),
        name="assemble",
    )(scal, both, both_1, both_2, both_3)
    got[-1], output, token_grad = lax.optimization_barrier((got[-1], output, token_grad))
    state = [
        swap(master), swap(master_m1), swap(master_m2), norm_params, norm_m1, norm_m2,
        swap(talk), swap(talk_m1), swap(talk_m2), conv, conv_m1, conv_m2,
    ]
    shapes = [SDS(t.shape, f32) for t in state]
    shapes.insert(3, SDS(state[0].shape, bf16))
    new = staged(
        update_kernel, "update", [*got, *state], shapes,
        [pltpu.VMEM((rows, slots, dim), f32), pltpu.VMEM((slots, 64, 256), f32), pltpu.VMEM((64, 256), f32)],
    )
    new = [swap(t) if t.ndim == 3 else t for t in new]
    return (swap(output), swap(token_grad), *new)


def solution(mesh):
    in_specs = (
        P("dp", None, None),
        P("dp", None, None),
        P("dp"),
        P(),
        P(),
        P(),
        P("dp", None, "head"),
        P("dp", None, "head"),
        P("dp", None, "head"),
        P(),
        P(),
        P(),
        P(),
        P(),
        P(),
        P(None, "head"),
        P(None, "head"),
        P(None, "head"),
    )
    out_specs = (
        P("dp", None, None),
        P("dp", None, None),
        P("dp", None, "head"),
        P("dp", None, "head"),
        P("dp", None, "head"),
        P("dp", None, "head"),
        P(),
        P(),
        P(),
        P(),
        P(),
        P(),
        P(None, "head"),
        P(None, "head"),
        P(None, "head"),
    )
    return jax.shard_map(local, mesh=mesh, in_specs=in_specs, out_specs=out_specs, check_vma=False)
```

```python
import functools
import jax
import jax.numpy as jnp
from jax import lax
from jax.experimental import pallas as pl
from jax.experimental.pallas import tpu as pltpu
from jax.sharding import PartitionSpec as P

HD = 18
SIDE = 14
PITCH = 16
MARGIN = 24
BUNCH = 4
EARLY = 4


def bunches(first, last):
    return [(y, min(BUNCH, last - y)) for y in range(first, last, BUNCH)]

FREE = 216
WIDE = 40
norm_eps = 1e-05
bf16 = jnp.bfloat16
f32 = jnp.float32


def nn(a, b):
    return lax.dot_general(a, b, (((1,), (0,)), ((), ())), preferred_element_type=f32)


def nt(a, b):
    return lax.dot_general(a, b, (((1,), (1,)), ((), ())), preferred_element_type=f32)


def tn(a, b):
    return lax.dot_general(a, b, (((0,), (0,)), ((), ())), preferred_element_type=f32)


def iota(shape, dim):
    return lax.broadcasted_iota(jnp.int32, shape, dim)


def split2(v):
    hi = v.astype(bf16)
    return hi, (v - hi.astype(f32)).astype(bf16)


def real_rows(shape):
    return (iota(shape, 0) & (PITCH - 1)) < SIDE


def lane_head(shape, dim, place):
    lane = iota(shape, dim)
    rest = lane & 63
    head = ((lane >> 6) ^ place) * 3 + (rest >= 18).astype(jnp.int32) + (rest >= 36).astype(jnp.int32)
    return jnp.where(rest < 54, head, -1)


def true_head(rows, place):
    head = rows >> 4
    part = (head >= 3).astype(jnp.int32) + (head >= 6).astype(jnp.int32) + (head >= 9).astype(jnp.int32)
    return (part ^ place) * 3 + (head - 3 * part)


def spot(slot, per):
    bits = per.bit_length() - 1
    return slot >> (bits + 1), (slot >> bits) & 1, slot & (per - 1)


def prep_kernel(
    scal, slot_ref, tok_ref, cot_ref, norm_ref, talk_ref, x_ref, a_ref, dy_ref, mix_ref, bias_ref, keep_ref, ex_ref, el_ref, sel_ref, tmp_ref, *, pairs
):
    x_ref[...] = jnp.zeros_like(x_ref)
    dy_ref[...] = jnp.zeros_like(dy_ref)
    valid = (scal[0] < scal[1]).astype(f32)
    tmp_ref[...] = tok_ref[0].astype(f32)
    for y in range(SIDE):
        x_ref[PITCH * y : PITCH * y + SIDE, :] = tmp_ref[SIDE * y : SIDE * (y + 1), :]
        dy_ref[PITCH * y : PITCH * y + SIDE, :] = cot_ref[0, SIDE * y : SIDE * (y + 1), :] * valid
    x = x_ref[...]
    centred = x - jnp.mean(x, axis=-1, keepdims=True)
    inv = lax.rsqrt(jnp.mean(centred * centred, axis=-1, keepdims=True) + norm_eps)
    a = centred * inv * norm_ref[0:1, :] + norm_ref[1:2, :]
    a_ref[...] = jnp.where(real_rows(a.shape), a, 0.0).astype(bf16)
    heads = talk_ref.shape[1]
    n = heads * PITCH
    ex = (true_head(iota((n, heads), 0), scal[0]) == iota((n, heads), 1)).astype(bf16)
    el = (lane_head((256, heads), 0, scal[0]) == iota((256, heads), 1)).astype(bf16)
    for i in range(2):
        both = []
        for part in split2(talk_ref[i]):
            if i == 0:
                both.append(nt(nn(ex, part).astype(bf16), el))
            else:
                both.append(nt(nt(ex, part).astype(bf16), el))
        mix_ref[i] = (both[0] + both[1]) * (HD**-0.5 if i == 0 else 1.0)
    bias_ref[...] = jnp.where(real_rows(bias_ref.shape), 0.0, -1e30)
    lanes = lane_head((1, 256), 1, scal[0])
    keep_ref[0:1, :] = ((lanes >= 0) & (lanes < scal[2])).astype(f32)
    lane = iota((1, 256), 1)
    for k in range(keep_ref.shape[0] - 2):
        unit = ((k ^ scal[0]) * 4 + (lane >> 6)) * 54 + (lane & 63)
        keep_ref[1 + k : 2 + k, :] = (unit < scal[3]).astype(f32)
    keep_ref[keep_ref.shape[0] - 1 :, :] = jnp.broadcast_to(valid, (1, 256))
    ex_ref[...] = ex
    el_ref[...] = el
    blocks, slots = sel_ref.shape[:2]
    per = slots // (2 * pairs)
    for b in range(blocks):
        pair, place, own = spot(slot_ref[b], per)
        at = ((place ^ scal[4]) * pairs + (pair ^ scal[5])) * per + own
        sel_ref[b] = (iota(sel_ref.shape[1:], 0) == at).astype(f32)


def load_weight(dst_ref, w_refs, b):
    for k, w_ref in enumerate(w_refs):
        dst_ref[64 * k : 64 * k + 54, :] = w_ref[b]
        dst_ref[64 * k + 54 : 64 * k + 64, :] = jnp.zeros((10, dst_ref.shape[1]), bf16)


def tiled(rows, heads):
    return jnp.concatenate([rows] * heads, axis=0)


def over_heads(rows, heads):
    return jnp.sum(rows.reshape(heads, PITCH, rows.shape[1]), axis=0)


def attn_fwd_kernel(x_ref, a_ref, mix_ref, bias_ref, keep_ref, *refs, parts):
    w_refs, refs = refs[:parts], refs[parts:]
    mid_ref, q_ref, k_ref, v_ref, o_ref, qw_ref, p_ref, pv_ref, ws_ref, t_ref = refs
    heads = mix_ref.shape[1] // PITCH
    a = a_ref[...]
    for b, dst in enumerate((q_ref, k_ref, v_ref)):
        load_weight(ws_ref.at[b], w_refs, b)
        dst[...] = nt(a, ws_ref[b]).astype(bf16)
    load_weight(ws_ref.at[3], w_refs, 3)
    keep = keep_ref[0:1, :]

    n = heads * PITCH
    for y in range(SIDE):
        q = q_ref[PITCH * y : PITCH * (y + 1), :].astype(f32)
        qw_ref[n * y : n * (y + 1), :] = (tiled(q, heads) * mix_ref[0]).astype(bf16)
    for b, (y, count) in enumerate(bunches(0, SIDE)):
        t_ref[b, :, 0 : n * count] = nt(k_ref[...], qw_ref[n * y : n * (y + count), :])
    for b, (y, count) in enumerate(bunches(0, SIDE)):
        for at in range(0, n * count, 128):
            t = t_ref[b, :, at : at + 128] + bias_ref[...]
            e = jnp.exp(t - jnp.max(t, axis=0, keepdims=True))
            p_ref[b, :, at : at + 128] = (e * (1.0 / jnp.sum(e, axis=0, keepdims=True))).astype(bf16)
    for b, (first, count) in enumerate(bunches(0, SIDE)):
        pv = tn(p_ref[b, :, 0 : n * count], v_ref[...])
        pv_ref[n * first : n * (first + count), :] = pv.astype(bf16)
        for u in range(count):
            o = over_heads(pv[n * u : n * (u + 1)] * mix_ref[1], heads)
            o_ref[PITCH * (first + u) : PITCH * (first + u + 1), :] = (o * keep).astype(bf16)
    mid_ref[...] = x_ref[...] + nn(o_ref[...], ws_ref[3])


def ln_stats(v):
    centred = v - jnp.mean(v, axis=-1, keepdims=True)
    inv = lax.rsqrt(jnp.mean(centred * centred, axis=-1, keepdims=True) + norm_eps)
    return centred * inv, inv


def ln_back(grad, scaled, inv, gain):
    gs = grad * gain
    return inv * (
        gs - jnp.mean(gs, axis=-1, keepdims=True) - scaled * jnp.mean(gs * scaled, axis=-1, keepdims=True)
    )


def in_free_lanes(flat, dst_ref, first_row):
    rows = flat.shape[0]
    for j in range(6):
        dst_ref[first_row + rows * j : first_row + rows * (j + 1), :] = pltpu.roll(flat, (FREE - WIDE * j) % 256, 1)


def from_free_lanes(src_ref, first_row, rows):
    lane = iota((rows, 256), 1)
    flat = jnp.zeros((rows, 256), f32)
    for j in range(6):
        moved = pltpu.roll(src_ref[first_row + rows * j : first_row + rows * (j + 1), :], (WIDE * j - FREE) % 256, 1)
        flat = flat + jnp.where((lane >= WIDE * j) & (lane < WIDE * (j + 1)), moved, 0.0)
    return flat


def place(rows=216):
    shape = (rows, 256)
    lane = iota(shape, 1)
    rest = lane & 63
    return ((iota(shape, 0) == (lane >> 6) * 54 + rest) & (rest < 54)).astype(bf16)


def up(w_ref, w, e, win_ref, wdn_ref, h_ref, d_ref, cv_ref):
    tokens, dim = w.shape
    pad = MARGIN
    for j in range(4):
        at = 64 * j
        win_ref[at : at + 54, :] = w_ref[j]
        wdn_ref[at : at + 54, :] = w_ref[4 + j]
        win_ref[at + 54 : at + 64, :] = jnp.zeros((10, dim), bf16)
        wdn_ref[at + 54 : at + 64, :] = jnp.zeros((10, dim), bf16)
    both = nn(w_ref[8], place(dim))
    cv_ref[...] = both[0:9] + both[16:25]
    hidden = nt(w, win_ref[...])
    dgate = nt(e, wdn_ref[...])
    zero = jnp.zeros((pad, 128), f32)
    for half in range(2):
        mine = slice(128 * half, 128 * (half + 1))
        for ref, value in ((h_ref, hidden), (d_ref, dgate)):
            ref[half, 0:pad, :] = zero
            ref[half, pad + tokens :, :] = zero
            ref[half, pad : pad + tokens, :] = value[:, mine]


def middle(keep, h_ref, d_ref, gate_ref, dh_ref, cv_ref, gcv_ref):
    tokens = gate_ref.shape[0]
    pad = MARGIN
    for half in range(2):
        cols = slice(128 * half, 128 * (half + 1))
        on = keep[:, cols]
        act = None
        for t in range(9):
            off = pad + PITCH * (t // 3 - 1) + t % 3 - 1
            term = cv_ref[t : t + 1, cols] * h_ref[half, off : off + tokens, :]
            act = term if act is None else act + term
        sig = 0.5 * jnp.tanh(0.5 * act) + 0.5
        silu = act * sig
        gate_ref[:, cols] = (silu * on).astype(bf16)
        dact = d_ref[half, pad : pad + tokens, :] * on * (silu + sig * (1.0 - silu))
        d_ref[half, pad : pad + tokens, :] = dact
        dh = None
        for t in range(9):
            shift = PITCH * (t // 3 - 1) + t % 3 - 1
            gcv_ref[t : t + 1, cols] = jnp.sum(
                dact * h_ref[half, pad + shift : pad + shift + tokens, :], axis=0, keepdims=True
            )
            term = cv_ref[t : t + 1, cols] * d_ref[half, pad - shift : pad - shift + tokens, :]
            dh = term if dh is None else dh + term
        dh_ref[:, cols] = dh.astype(bf16)


def ffn_first_kernel(mid_ref, dy_ref, norm_ref, keep_ref, *refs, parts):
    w_refs, refs = refs[:parts], refs[parts:]
    z_ref, inv_ref, w_ref, e_ref, win_ref, wdn_ref, gate_ref, dh_ref, gcv_ref, h_ref, d_ref, cv_ref = refs
    z, inv = ln_stats(mid_ref[...])
    z_ref[...] = z
    inv_ref[...] = jnp.broadcast_to(inv, inv_ref.shape)
    w = jnp.where(real_rows(z.shape), z * norm_ref[2:3, :] + norm_ref[3:4, :], 0.0).astype(bf16)
    e = dy_ref[...].astype(bf16)
    w_ref[...] = w
    e_ref[...] = e
    for k in range(parts):
        up(w_refs[k], w, e, win_ref.at[k], wdn_ref.at[k], h_ref.at[k], d_ref.at[k], cv_ref.at[k])
    for k in range(parts):
        middle(
            keep_ref[1 + k : 2 + k, :], h_ref.at[k], d_ref.at[k], gate_ref.at[k], dh_ref.at[k], cv_ref.at[k], gcv_ref.at[k]
        )


def ffn_last_kernel(
    mid_ref, dy_ref, norm_ref, keep_ref, o_ref, z_ref, inv_ref, w_ref, e_ref, *refs, parts, late
):
    early = parts - late
    wins, wdns, gates, dhs, gcvs = refs[:5]
    last_refs, refs = refs[5 : 5 + late], refs[5 + late :]
    out_ref, dmid_ref, gn_ref = refs[:3]
    gw_refs, refs = refs[3 : 3 + parts], refs[3 + parts :]
    win_ref, wdn_ref, gate_ref, dh_ref, gcv_ref, h_ref, d_ref, cv_ref, tmp_ref, sm_ref, dw_ref = refs
    w, e = w_ref[...], e_ref[...]
    dim = w.shape[1]
    wins, wdns, gates, dhs, gcvs = [
        [ref.at[i] for i in range(early)] + [own.at[i] for i in range(late)]
        for ref, own in ((wins, win_ref), (wdns, wdn_ref), (gates, gate_ref), (dhs, dh_ref), (gcvs, gcv_ref))
    ]

    def back(h):
        gi = tn(dhs[h][...], w).astype(bf16)
        gd = tn(gates[h][...], e).astype(bf16)
        for j in range(4):
            gw_refs[h][1 + j, :, 0:dim] = gi[64 * j : 64 * j + 54]
            gw_refs[h][5 + j, :, 0:dim] = gd[64 * j : 64 * j + 54]

    for i in range(late):
        up(last_refs[i], w, e, win_ref.at[i], wdn_ref.at[i], h_ref.at[i], d_ref.at[i], cv_ref.at[i])
    for h in range(early):
        back(h)
    for i in range(late):
        middle(
            keep_ref[1 + early + i : 2 + early + i, :], h_ref.at[i], d_ref.at[i], gate_ref.at[i], dh_ref.at[i], cv_ref.at[i], gcv_ref.at[i]
        )
    dw_ref[...] = sum(nn(dhs[h][...], wins[h][...]) for h in range(parts))
    valid = keep_ref[parts + 1 : parts + 2, 0:1]
    tmp_ref[...] = (mid_ref[...] + sum(nn(gates[h][...], wdns[h][...]) for h in range(parts))) * valid
    free = iota((54, 256), 1) >= FREE
    pm = place(256)
    for h in range(parts):
        if h >= early:
            back(h)
        in_free_lanes(nt(gcvs[h][...].astype(bf16), pm), sm_ref.at[h], 0)
        gw_refs[h][0] = jnp.where(free, sm_ref[h, 0:54, :], 0.0).astype(bf16)
    for y in range(SIDE):
        out_ref[SIDE * y : SIDE * (y + 1), :] = tmp_ref[PITCH * y : PITCH * y + SIDE, :].astype(bf16)
    z, inv = z_ref[...], inv_ref[:, 0:1]
    dw = jnp.where(real_rows(z.shape), dw_ref[...], 0.0)
    gn_ref[...] = jnp.zeros_like(gn_ref)
    gn_ref[0:1, :] = jnp.sum(dw * z, axis=0, keepdims=True)
    gn_ref[1:2, :] = jnp.sum(dw, axis=0, keepdims=True)
    dmid = dy_ref[...] + ln_back(dw, z, inv, norm_ref[2:3, :])
    dmid_ref[...] = dmid
    go = tn(o_ref[...], dmid.astype(bf16)).astype(bf16)
    for h in range(parts):
        gw_refs[h][0, :, 0:dim] = go[64 * h : 64 * h + 54]


def scores_back_kernel(
    dmid_ref, mix_ref, keep_ref, ex_ref, el_ref, q_ref, k_ref, v_ref, qw_ref, p_ref, pv_ref, *refs, parts, part
):
    heads = mix_ref.shape[1] // PITCH
    n = heads * PITCH
    if part == 0:
        w_refs, refs = refs[:parts], refs[parts:]
        do_ref, gq_ref, gk_ref, gv_ref, g0_ref, g1_ref, wo_ref, dw_ref, dp_ref, dt_ref = refs
        load_weight(wo_ref, w_refs, 3)
        f = dmid_ref[...].astype(bf16)
        keep = keep_ref[0:1, :]
        do_ref[...] = (nt(f, wo_ref[...]) * keep).astype(bf16)
        for ref in (gk_ref, gv_ref, g0_ref, g1_ref):
            ref[...] = jnp.zeros_like(ref)
    else:
        do_ref, *sums, gq_ref, gkb_ref, gvb_ref, gt_ref, gk_ref, gv_ref, g0_ref, g1_ref, dw_ref, dp_ref, dt_ref = refs
        for ref, old in zip((gk_ref, gv_ref, g0_ref, g1_ref), sums):
            ref[...] = old[...]
    first, last = (0, EARLY) if part == 0 else (EARLY, SIDE)
    for y in range(first, last):
        do = do_ref[PITCH * y : PITCH * (y + 1), :].astype(f32)
        at = n * (y - first)
        dw_ref[at : at + n, :] = (tiled(do, heads) * mix_ref[1]).astype(bf16)
    groups = [(b, b + first // BUNCH, y, count) for b, (y, count) in enumerate(bunches(first, last))]
    for b, _, y, count in groups:
        at = n * (y - first)
        dp_ref[b, :, 0 : n * count] = nt(v_ref[...], dw_ref[at : at + n * count, :])
    for b, whole_b, y, count in groups:
        for at in range(0, n * count, 128):
            dp = dp_ref[b, :, at : at + 128]
            p = p_ref[whole_b, :, at : at + 128].astype(f32)
            dt_ref[b, :, at : at + 128] = (p * (dp - jnp.sum(dp * p, axis=0, keepdims=True))).astype(bf16)
    gv, gk = gv_ref[...], gk_ref[...]
    for b, whole_b, y, count in groups:
        at = n * (y - first)
        gv = gv + nn(p_ref[whole_b, :, 0 : n * count], dw_ref[at : at + n * count, :])
        gk = gk + nn(dt_ref[b, :, 0 : n * count], qw_ref[n * y : n * (y + count), :])
    gv_ref[...] = gv
    gk_ref[...] = gk
    for b, _, y, count in groups:
        dk = tn(dt_ref[b, :, 0 : n * count], k_ref[...])
        for u in range(count):
            mine = dk[n * u : n * (u + 1)]
            at = PITCH * (y + u)
            gq_ref[at - PITCH * first : at - PITCH * first + PITCH, :] = over_heads(mine * mix_ref[0], heads).astype(bf16)
            g0_ref[...] += mine * tiled(q_ref[at : at + PITCH, :].astype(f32), heads)
    for y in range(first, last):
        do = do_ref[PITCH * y : PITCH * (y + 1), :].astype(f32)
        g1_ref[...] += pv_ref[n * y : n * (y + 1), :].astype(f32) * tiled(do, heads)
    if part == 0:
        return
    gkb_ref[...] = gk_ref[...].astype(bf16)
    gvb_ref[...] = gv_ref[...].astype(bf16)
    ex, el = ex_ref[...], el_ref[...]
    for i, ref in enumerate((g0_ref, g1_ref)):
        hi, lo = split2(ref[...])
        hi, lo = split2(nn(hi, el) + nn(lo, el))
        if i == 0:
            gt_ref[i] = (tn(ex, hi) + tn(ex, lo)) * HD**-0.5
        else:
            gt_ref[i] = tn(hi, ex) + tn(lo, ex)


def weights_back_kernel(
    x_ref, a_ref, dmid_ref, norm_ref, gn2_ref, gqa_ref, gqb_ref, gk_ref, gv_ref, gt_ref, y_ref, *refs, parts
):
    w_refs, refs = refs[:parts], refs[parts:]
    both_ref, gw_refs, refs = refs[0], refs[1 : 1 + parts], refs[1 + parts :]
    ws_ref, tmp_ref, flat_ref, sm_ref = refs
    heads = gt_ref.shape[1]
    dim = x_ref.shape[1]
    for b in range(3):
        load_weight(ws_ref.at[b], w_refs, b)
    gq = jnp.concatenate([gqa_ref[...], gqb_ref[...]], axis=0)
    gk, gv = gk_ref[...], gv_ref[...]
    a = a_ref[...]
    da = nn(gq, ws_ref[0]) + nn(gk, ws_ref[1]) + nn(gv, ws_ref[2])
    z, inv = ln_stats(x_ref[...])
    flat_ref[...] = jnp.zeros_like(flat_ref)
    flat_ref[0:1, 0:dim] = jnp.sum(da * z, axis=0, keepdims=True)
    flat_ref[1:2, 0:dim] = jnp.sum(da, axis=0, keepdims=True)
    flat_ref[2:4, 0:dim] = gn2_ref[0:2, :]
    for i in range(2):
        flat_ref[8 : 8 + heads, 128 * i : 128 * i + heads] = gt_ref[i]
    sm_ref[...] = jnp.zeros_like(sm_ref)
    in_free_lanes(flat_ref[0:4, :], sm_ref, 0)
    mix = flat_ref[8 : 8 + heads, :]
    first = iota(mix.shape, 1) < 128
    mix = jnp.where(first, mix, 0.0) + pltpu.roll(jnp.where(first, 0.0, mix), 128 + heads, 1)
    sm_ref[24 : 24 + heads, :] = pltpu.roll(mix, FREE, 1)
    small = jnp.where(iota((54, 256), 1) >= FREE, sm_ref[0:54, :], 0.0).astype(bf16)
    for h in range(parts):
        gw_refs[h][0] = small
    for b, g in enumerate((gq, gk, gv)):
        gw = tn(g, a).astype(bf16)
        for h in range(parts):
            gw_refs[h][b, :, 0:dim] = gw[64 * h : 64 * h + 54]
    tmp_ref[...] = dmid_ref[...] + ln_back(da, z, inv, norm_ref[0:1, :])
    for y in range(SIDE):
        both_ref[1, SIDE * y : SIDE * (y + 1), :] = tmp_ref[PITCH * y : PITCH * y + SIDE, :].astype(bf16)
    both_ref[0] = y_ref[...]


def cast_kernel(m_hbm, out_ref, m_ref, sem):
    copy = pltpu.make_async_copy(m_hbm, m_ref, sem)
    copy.start()
    copy.wait()
    for i in range(out_ref.shape[0]):
        out_ref[i] = m_ref[:, i, :].astype(bf16)


def stack_kernel(*refs):
    for k, ref in enumerate(refs[:-1]):
        refs[-1][k] = ref[...]


def slots_of(sources):
    found = []
    for i, ref in enumerate(sources):
        ranks = [ref] if i % 2 == 0 else [ref.at[k] for k in range(ref.shape[0])]
        found += [rank[own] for rank in ranks for own in range(rank.shape[0])]
    return found


def pick(sel_ref, b, slots):
    dim = slots[0].shape[1]
    block = None
    for i, slot in enumerate(slots):
        term = sel_ref[b, i : i + 1, 0:dim] * slot.astype(f32)
        block = term if block is None else block + term
    return block.astype(bf16)


def select_attn_kernel(sel_ref, *refs):
    slots = slots_of(refs[:-1])
    for b in range(4):
        refs[-1][b] = pick(sel_ref, b, slots)


def select_ffn_kernel(sel_ref, conv_ref, *refs):
    slots, ffn_ref = slots_of(refs[:-1]), refs[-1]
    for b in range(8):
        ffn_ref[b] = pick(sel_ref, 4 + b, slots)
    hi, lo = split2(conv_ref[...])
    ffn_ref[8] = jnp.zeros_like(ffn_ref[8])
    ffn_ref[8, 0:9] = hi
    ffn_ref[8, 16:25] = lo


def total(refs, at):
    acc = refs[0][at].astype(f32)
    for ref in refs[1:]:
        acc = acc + ref[at].astype(f32)
    return acc


def half_sum_kernel(a_ref, b_ref, out_ref):
    out_ref[...] = (a_ref[...].astype(f32) + b_ref[...].astype(f32)).astype(bf16)


def spread_ffn_kernel(slot_ref, scal, *refs):
    ffn_refs, out_ref = refs[:-1], refs[-1]
    pairs, _, per = out_ref.shape[:3]
    out_ref[...] = jnp.zeros_like(out_ref)
    for b in range(9):
        block = total(ffn_refs, b)
        k, j, i = spot(slot_ref[3 + b], per)
        out_ref[k ^ scal[5], j ^ scal[4], i, :, 0:FREE] = block[:, 0:FREE].astype(bf16)
        if b == 0:
            wide = block[:, FREE:].astype(bf16)
    for k in range(pairs):
        for j in range(2):
            out_ref[k, j, 0, :, FREE:] = wide


def spread_attn_kernel(sel_ref, old_ref, *refs, parts):
    attn, outs = refs[:parts], refs[parts:]
    half, per = outs[0].shape[:2]
    blocks = [total(attn, b) for b in range(3)]
    wide = blocks[0][:, FREE:].astype(bf16)
    blocks = [block[:, 0:FREE] for block in blocks]
    for i, ref in enumerate(outs):
        for k in range(half):
            pair = half * (i % 2) + k
            for own in range(per):
                old = old_ref[pair, i // 2, own]
                at = (i // 2 * 2 * half + pair) * per + own
                low = old[:, 0:FREE].astype(f32)
                for b in range(3):
                    low = low + sel_ref[b, at : at + 1, 0:FREE] * blocks[b]
                ref[k, own] = old
                ref[k, own, :, 0:FREE] = low.astype(bf16)
            ref[k, 1, :, FREE:] = wide


def place_sum_kernel(own_ref, other_ref, *outs):
    for k, out_ref in enumerate(outs):
        out_ref[...] = (own_ref[k].astype(f32) + other_ref[k].astype(f32)).astype(out_ref.dtype)


def adam(w, g, one, two, rate, decay):
    one_new = 0.5 * one + 0.5 * g
    two_new = 0.5 * two + 0.5 * g * g
    hat_one = one_new / (1.0 - 0.5**3)
    hat_two = two_new / (1.0 - 0.5**3)
    return w - rate * (hat_one / (jnp.sqrt(hat_two) + 1e-08) + decay * w), one_new, two_new


def update_kernel(*refs):
    got, refs = refs[:-28], refs[-28:]
    ins, outs, (g_ref, sm_ref, flat_ref) = refs[0:12], refs[12:25], refs[25:]
    per, rows = got[0].shape[:2]
    dim = ins[0].shape[2]
    for i in range(per):
        g = total(got, i)
        g_ref[:, i, :] = g[:, 0:dim]
        sm_ref[i, 0:rows, :] = g
    w, one, two = adam(ins[0][...], g_ref[...], ins[1][...], ins[2][...], 0.06, 0.05)
    outs[0][...], outs[1][...], outs[2][...], outs[3][...] = w, one, two, w.astype(bf16)
    heads = ins[6].shape[0]
    flat_ref[0:9, :] = from_free_lanes(sm_ref.at[0], 0, 9)
    flat_ref[16:20, :] = from_free_lanes(sm_ref.at[1], 0, 4)
    mix = pltpu.roll(sm_ref[1, 24 : 24 + heads, :], 256 - FREE, 1)
    flat_ref[32 : 32 + heads, :] = mix
    flat_ref[48 : 48 + heads, :] = pltpu.roll(mix, 256 - heads, 1)
    outs[4][...], outs[5][...], outs[6][...] = adam(
        ins[3][...], flat_ref[16:20, 0:dim], ins[4][...], ins[5][...], 0.2, 0.0
    )
    for i in range(2):
        w, one, two = adam(
            ins[6][:, i, :], flat_ref[16 * (i + 2) : 16 * (i + 2) + heads, 0:heads], ins[7][:, i, :], ins[8][:, i, :],
            0.2, 0.0,
        )
        outs[7][:, i, :], outs[8][:, i, :], outs[9][:, i, :] = w, one, two
    outs[10][...], outs[11][...], outs[12][...] = adam(
        ins[9][...], flat_ref[0:9, 0:dim], ins[10][...], ins[11][...], 0.2, 0.05
    )


def assemble_kernel(scal, *refs):
    ins, outs, (all_ref,) = refs[:-3], refs[-3:-1], refs[-1:]
    parts, tokens = len(ins), ins[0].shape[1]
    step = 32
    shape = (parts * step, parts * step)
    row, col = iota(shape, 0), iota(shape, 1)
    bits = parts.bit_length() - 1
    pick = ((row >> bits == col & (step - 1)) & (row & (parts - 1) == col >> 5)).astype(bf16)
    full = all_ref.shape[1]
    for k in range(parts):
        all_ref[k, tokens // step * step : full, :] = jnp.zeros((full - tokens // step * step, all_ref.shape[2]), bf16)
    for i, out_ref in enumerate(outs):
        for k, ref in enumerate(ins):
            all_ref[scal[0] ^ k, 0:tokens, :] = ref[i]
        for at in range(0, tokens, step):
            mixed = nn(pick, jnp.concatenate([all_ref[k, at : at + step, :] for k in range(parts)], axis=0))
            for t in range(min(step, tokens - at)):
                out_ref[at + t] = mixed[parts * t : parts * (t + 1)]


VM = pl.BlockSpec(memory_space=pltpu.VMEM)
SM = pl.BlockSpec(memory_space=pltpu.SMEM)
SDS = jax.ShapeDtypeStruct


def call(body, name, n_scalar, n_in, out_shape, scratch=(), mb=16, micros=1, **kw):
    return pl.pallas_call(
        functools.partial(body, **kw) if kw else body,
        in_specs=[SM] * n_scalar + [VM] * n_in,
        out_specs=[VM] * len(out_shape),
        out_shape=out_shape,
        scratch_shapes=scratch,
        compiler_params=pltpu.CompilerParams(vmem_limit_bytes=mb << 20),
        cost_estimate=pl.CostEstimate(flops=micros * 1000000000, transcendentals=0, bytes_accessed=micros * 3000000),
        name=name,
    )


def prep(scal, block_slot, tokens, cotangent, norm_params, talk, parts, pairs, slots):
    tok, dim = tokens.shape[1], tokens.shape[2]
    pad = SIDE * PITCH
    heads = talk.shape[1]
    n = heads * PITCH
    full = lambda *s: pl.BlockSpec(s, lambda i, sc, bs: (0,) * len(s))
    return pl.pallas_call(
        functools.partial(prep_kernel, pairs=pairs),
        grid_spec=pltpu.PrefetchScalarGridSpec(
            num_scalar_prefetch=2,
            grid=(1,),
            in_specs=[
                pl.BlockSpec((1, tok, dim), lambda i, sc, bs: (sc[0], 0, 0)),
                pl.BlockSpec((1, tok, dim), lambda i, sc, bs: (sc[0], 0, 0)),
                full(*norm_params.shape),
                full(*talk.shape),
            ],
            out_specs=[full(pad, dim), full(pad, dim), full(pad, dim), full(2, n, 256), full(pad, 128),
                full(parts + 2, 256), full(n, heads), full(256, heads),
                full(12, slots, 256),
            ],
            scratch_shapes=[pltpu.VMEM((tok, dim), f32)],
        ),
        out_shape=[SDS((pad, dim), f32), SDS((pad, dim), bf16), SDS((pad, dim), f32), SDS((2, n, 256), f32),
                   SDS((pad, 128), f32), SDS((parts + 2, 256), f32), SDS((n, heads), bf16), SDS((256, heads), bf16),
                   SDS((12, slots, 256), f32)],
        compiler_params=pltpu.CompilerParams(vmem_limit_bytes=16 << 20),
        cost_estimate=pl.CostEstimate(flops=1000000000, transcendentals=0, bytes_accessed=3000000),
        name="prep",
    )(scal, block_slot, tokens, cotangent, norm_params, talk)


def attn_fwd(x, a, mix, bias, keep, w):
    pad, dim = x.shape
    n = mix.shape[1]
    grid = (len(bunches(0, SIDE)), pad, n * BUNCH)
    return call(
        attn_fwd_kernel, "attn_fwd", 0, 5 + len(w),
        [SDS((pad, dim), f32)] + [SDS((pad, 256), bf16)] * 4
        + [SDS((SIDE * n, 256), bf16), SDS(grid, bf16), SDS((SIDE * n, 256), bf16)],
        [pltpu.VMEM((4, 256, dim), bf16), pltpu.VMEM(grid, f32)],
        mb=24, micros=1, parts=len(w),
    )(x, a, mix, bias, keep, *w)


def ffn_first(mid, dy, norm_params, keep, w):
    pad, dim = mid.shape
    count = len(w)
    lanes = [(count, 256, dim)] * 2 + [(count, pad, 256)] * 2
    grids = [pltpu.VMEM((count, 2, pad + 2 * MARGIN, 128), f32)] * 2
    return call(
        ffn_first_kernel, "ffn_first", 0, 4 + count,
        [SDS((pad, dim), f32), SDS((pad, 128), f32), SDS((pad, dim), bf16), SDS((pad, dim), bf16)]
        + [SDS(t, bf16) for t in lanes] + [SDS((count, 9, 256), f32)],
        grids + [pltpu.VMEM((count, 9, 256), f32)],
        mb=24, micros=3, parts=count,
    )(mid, dy, norm_params, keep, *w)


def ffn_last(mid, dy, norm_params, keep, o, first, w):
    pad, dim = mid.shape
    late = len(w)
    parts = first[4].shape[0] + late
    grids = [pltpu.VMEM((late, 2, pad + 2 * MARGIN, 128), f32)] * 2
    return call(
        ffn_last_kernel, "ffn_last", 0, 14 + late,
        [SDS((SIDE * SIDE, dim), bf16), SDS((pad, dim), f32), SDS((8, dim), f32)] + [SDS((9, 54, 256), bf16)] * parts,
        [pltpu.VMEM((late, 256, dim), bf16)] * 2 + [pltpu.VMEM((late, pad, 256), bf16)] * 2
        + [pltpu.VMEM((late, 9, 256), f32)] + grids
        + [
            pltpu.VMEM((late, 9, 256), f32), pltpu.VMEM((pad, dim), f32), pltpu.VMEM((parts, 56, 256), f32),
            pltpu.VMEM((pad, dim), f32),
        ],
        mb=24, micros=4, parts=parts, late=late,
    )(mid, dy, norm_params, keep, o, *first, *w)


def scores_back(dmid, mix, keep, ex, el, q, k, v, qw, p, pv, more, part):
    pad, dim = dmid.shape
    n = mix.shape[1]
    heads = n // PITCH
    sums = [SDS((pad, 256), f32)] * 2 + [SDS((n, 256), f32)] * 2
    count = EARLY if part == 0 else SIDE - EARLY
    half = SDS((PITCH * count, 256), bf16)
    if part == 0:
        outs = [SDS((pad, 256), bf16), half] + sums
        scratch = [pltpu.VMEM((256, dim), bf16)]
    else:
        outs = [half] + [SDS((pad, 256), bf16)] * 2 + [SDS((2, heads, heads), f32)]
        scratch = [pltpu.VMEM(t.shape, f32) for t in sums]
    scratch += [
        pltpu.VMEM((n * count, 256), bf16), pltpu.VMEM((-(-count // BUNCH), pad, n * BUNCH), f32),
        pltpu.VMEM((-(-count // BUNCH), pad, n * BUNCH), bf16),
    ]
    return call(
        scores_back_kernel, "scores_back", 0, 11 + len(more), outs, scratch,
        mb=24, micros=4, parts=len(more), part=part,
    )(dmid, mix, keep, ex, el, q, k, v, qw, p, pv, *more)


def weights_back(x, a, dmid, norm_params, gn2, gqa, gqb, gk, gv, gt, out, w):
    pad, dim = x.shape
    return call(
        weights_back_kernel, "weights_back", 0, 11 + len(w),
        [SDS((2, SIDE * SIDE, dim), bf16)] + [SDS((3, 54, 256), bf16)] * len(w),
        [pltpu.VMEM((3, 256, dim), bf16), pltpu.VMEM((pad, dim), f32), pltpu.VMEM((24, 256), f32),
         pltpu.VMEM((56, 256), f32)],
        mb=24, micros=3, parts=len(w),
    )(x, a, dmid, norm_params, gn2, gqa, gqb, gk, gv, gt, out, *w)


def permute(x, axis, k):
    return lax.ppermute(x, axis, [(i, i ^ k) for i in range(lax.axis_size(axis))])


def swap(t):
    return jnp.swapaxes(t, 0, 1)


def whole(*shape):
    return pl.BlockSpec(shape, lambda i: (0,) * len(shape))


def staged(body, name, ins, outs, scratch=(), micros=1):
    return pl.pallas_call(
        body,
        grid=(1,),
        in_specs=[VM] * len(ins),
        out_specs=[whole(*t.shape) for t in outs],
        out_shape=outs,
        scratch_shapes=scratch,
        compiler_params=pltpu.CompilerParams(vmem_limit_bytes=16 << 20),
        cost_estimate=pl.CostEstimate(flops=micros * 1000000000, transcendentals=0, bytes_accessed=micros * 3000000),
        name=name,
    )(*ins)


def local(
    tokens, cotangent, image_count, subnet_heads, subnet_width, block_slot,
    master, master_m1, master_m2, norm_params, norm_m1, norm_m2, talk, talk_m1, talk_m2, conv, conv_m1, conv_m2,
):
    slots, rows, dim = master.shape
    parts = lax.axis_size("head")
    ranks = lax.axis_size("dp")
    place_id = lax.axis_index("head").astype(jnp.int32)
    rank = lax.axis_index("dp").astype(jnp.int32)
    scal = jnp.concatenate(
        [place_id[None], image_count, subnet_heads, subnet_width, (rank % 2)[None], (rank // 2)[None]]
    )
    mine = pl.pallas_call(
        cast_kernel,
        grid=(1,),
        in_specs=[pl.BlockSpec(memory_space=pltpu.HBM)],
        out_specs=whole(slots, rows, dim),
        out_shape=SDS((slots, rows, dim), bf16),
        scratch_shapes=[pltpu.VMEM((rows, slots, dim), f32), pltpu.SemaphoreType.DMA],
        compiler_params=pltpu.CompilerParams(vmem_limit_bytes=16 << 20),
        name="cast",
    )(swap(master))
    pairs = ranks // 2
    half = pairs // 2
    near, far = range(1, half), range(half, pairs)
    apart = {k: permute(mine, "dp", 2 * k) for k in (*far, *near)}
    near_other = permute(mine, "dp", 1)
    apart[1], near_other = lax.optimization_barrier((apart[1], near_other))
    apart[half], tokens, cotangent, talk_in = lax.optimization_barrier((apart[half], tokens, cotangent, talk))
    (far_own,) = call(stack_kernel, "stack", 0, pairs - 1, [SDS((pairs - 1, slots, rows, dim), bf16)])(
        *[apart[k] for k in range(1, pairs)]
    )
    far_other = permute(far_own, "dp", 1)
    x, a, dy, mix, bias, keep, ex, el, sel = prep(
        scal, block_slot, tokens, cotangent, norm_params, talk_in, parts, pairs, ranks * slots
    )
    far_other, x = lax.optimization_barrier((far_other, x))
    sources = (mine, far_own, near_other, far_other)
    (attn_w,) = call(select_attn_kernel, "select_attn", 0, 5, [SDS((4, rows, dim), bf16)])(sel, *sources)
    (ffn_w,) = call(select_ffn_kernel, "select_ffn", 0, 6, [SDS((9, rows, dim), bf16)])(sel, conv, *sources)
    attn_2, attn_1 = permute(attn_w, "head", 2), permute(attn_w, "head", 1)
    attn_3 = permute(attn_2, "head", 1)
    attn_w = [attn_w, attn_1, attn_2, attn_3]
    ffn_2, ffn_1 = permute(ffn_w, "head", 2), permute(ffn_w, "head", 1)
    mid, q, k, v, o, qw, p, pv = attn_fwd(x, a, mix, bias, keep, attn_w)
    mid, ffn_2 = lax.optimization_barrier((mid, ffn_2))
    ffn_3 = permute(ffn_2, "head", 1)
    first = list(ffn_first(mid, dy, norm_params, keep, [ffn_w, ffn_1]))
    first[0], ffn_3 = lax.optimization_barrier((first[0], ffn_3))
    out, dmid, gn2, *ffn_g = ffn_last(mid, dy, norm_params, keep, o, first, [ffn_2, ffn_3])
    ffn_3 = permute(ffn_g[3], "head", 1)
    do, gqa, *sums = scores_back(dmid, mix, keep, ex, el, q, k, v, qw, p, pv, attn_w, 0)
    do, ffn_3 = lax.optimization_barrier((do, ffn_3))
    (summed,) = call(half_sum_kernel, "half_sum", 0, 2, [SDS(ffn_3.shape, bf16)])(ffn_g[2], ffn_3)
    ffn_g[1], summed = lax.optimization_barrier((ffn_g[1], summed))
    ffn_2, ffn_1 = permute(summed, "head", 2), permute(ffn_g[1], "head", 1)
    gqb, gk, gv, gt = scores_back(dmid, mix, keep, ex, el, q, k, v, qw, p, pv, [do, *sums], 1)
    both, *attn_g = weights_back(x, a, dmid, norm_params, gn2, gqa, gqb, gk, gv, gt, out, attn_w)
    attn_1, attn_3 = permute(attn_g[1], "head", 1), permute(attn_g[3], "head", 1)
    (summed,) = call(half_sum_kernel, "half_sum", 0, 2, [SDS(attn_3.shape, bf16)])(attn_g[2], attn_3)
    both, summed = lax.optimization_barrier((both, summed))
    attn_2 = permute(summed, "head", 2)
    both_2, both_1 = permute(both, "head", 2), permute(both, "head", 1)
    both_3 = permute(both_2, "head", 1)
    (message,) = call(
        spread_ffn_kernel, "spread_ffn", 2, 3, [SDS((ranks // 2, 2, slots, rows, 256), bf16)]
    )(block_slot, scal, ffn_g[0], ffn_1, ffn_2)
    near_own, far_own, near_other, far_other = call(
        spread_attn_kernel, "spread_attn", 0, 5, [SDS((half,) + message.shape[2:], bf16)] * 4, parts=3,
    )(sel, message, attn_g[0], attn_1, attn_2)
    slot_shape = (slots, rows, 256)
    far_other = permute(far_other, "dp", 1)
    near_other = permute(near_other, "dp", 1)
    far_sum = call(place_sum_kernel, "place_sum", 0, 2, [SDS(slot_shape, bf16)] * half)(far_own, far_other)
    far_sum = [permute(far_sum[k - half], "dp", 2 * k) for k in far]
    own, *near_sum = call(
        place_sum_kernel, "place_sum", 0, 2, [SDS(slot_shape, f32)] + [SDS(slot_shape, bf16)] * (half - 1)
    )(near_own, near_other)
    got = [own] + [permute(near_sum[k - 1], "dp", 2 * k) for k in near] + far_sum
    shape = SDS((tokens.shape[1], parts, dim), f32)
    output, token_grad = pl.pallas_call(
        assemble_kernel,
        grid=(1,),
        in_specs=[SM] + [whole(*both.shape)] * parts,
        out_specs=[whole(*shape.shape)] * 2,
        out_shape=[shape, shape],
        scratch_shapes=[pltpu.VMEM((parts, 224, dim), bf16)],
        compiler_params=pltpu.CompilerParams(vmem_limit_bytes=16 << 20),
        cost_estimate=pl.CostEstimate(flops=1000000000, transcendentals=0, bytes_accessed=3000000),
        name="assemble",
    )(scal, both, both_1, both_2, both_3)
    got[-1], output, token_grad = lax.optimization_barrier((got[-1], output, token_grad))
    state = [
        swap(master), swap(master_m1), swap(master_m2), norm_params, norm_m1, norm_m2,
        swap(talk), swap(talk_m1), swap(talk_m2), conv, conv_m1, conv_m2,
    ]
    shapes = [SDS(t.shape, f32) for t in state]
    shapes.insert(3, SDS(state[0].shape, bf16))
    new = staged(
        update_kernel, "update", [*got, *state], shapes,
        [pltpu.VMEM((rows, slots, dim), f32), pltpu.VMEM((slots, 64, 256), f32), pltpu.VMEM((64, 256), f32)],
    )
    new = [swap(t) if t.ndim == 3 else t for t in new]
    return (swap(output), swap(token_grad), *new)


def solution(mesh):
    in_specs = (
        P("dp", None, None),
        P("dp", None, None),
        P("dp"),
        P(),
        P(),
        P(),
        P("dp", None, "head"),
        P("dp", None, "head"),
        P("dp", None, "head"),
        P(),
        P(),
        P(),
        P(),
        P(),
        P(),
        P(None, "head"),
        P(None, "head"),
        P(None, "head"),
    )
    out_specs = (
        P("dp", None, None),
        P("dp", None, None),
        P("dp", None, "head"),
        P("dp", None, "head"),
        P("dp", None, "head"),
        P("dp", None, "head"),
        P(),
        P(),
        P(),
        P(),
        P(),
        P(),
        P(None, "head"),
        P(None, "head"),
        P(None, "head"),
    )
    return jax.shard_map(local, mesh=mesh, in_specs=in_specs, out_specs=out_specs, check_vma=False)
```
